32 devices in a mesh: fsdp: 32 (over z, y, x, core).
Axes of the slice: x: 2, y: 2, z: 4, core: 2. Of those that a mesh axis runs over, the one named last changes fastest.
Arguments:
- tokens: bfloat16 [4096, 2048], P('fsdp'), may hold values from -6 to 6
- segments: int32 [2, 2048], replicated, may hold values from 0 to 15, never falling along the last dimension, each value on 1 to 1024 neighbouring positions
- routes: int32 [4096, 8], P('fsdp'), may hold values from 0 to 15, all different within a row; in each aligned block of 128 rows (0 to 127, 128 to 255, ...) at most 128 rows name the same one
- gates: float32 [4096, 8], P('fsdp'), may hold values from 0.25 to 0.75
- sequence_adapter_index: int32 [2], replicated, may hold values from 0 to 7
- attention_norm_gain: bfloat16 [2048], replicated, may hold values from 0.5 to 1.5
- query_norm_gain: bfloat16 [128], replicated, may hold values from 0.25 to 1.75
- key_norm_gain: bfloat16 [128], replicated, may hold values from 0.25 to 1.75
- query_weight: bfloat16 [2048, 2048], P('fsdp'), may hold values from -0.125 to 0.125
- key_weight: bfloat16 [2048, 2048], P('fsdp'), may hold values from -0.125 to 0.125
- value_weight: bfloat16 [2048, 2048], P('fsdp'), may hold values from -0.125 to 0.125
- output_weight: bfloat16 [2048, 2048], P('fsdp'), may hold values from -0.5 to 0.5
- adapter_down_factors: bfloat16 [8, 4, 2048, 16], P(None, None, 'fsdp'), may hold values from -0.125 to 0.125
- adapter_up_factors: bfloat16 [8, 4, 16, 2048], P(None, None, None, 'fsdp'), may hold values from -0.75 to 0.75
- expert_norm_gain: bfloat16 [2048], replicated, may hold values from 0.5 to 1.5
- expert_gate_weight: bfloat16 [32, 2048, 512], P('fsdp'), may hold values from -0.125 to 0.125
- expert_up_weight: bfloat16 [32, 2048, 512], P('fsdp'), may hold values from -0.125 to 0.125
- expert_down_weight: bfloat16 [32, 512, 2048], P('fsdp'), may hold values from -0.1875 to 0.1875
- output_gradient: bfloat16 [4096, 2048], P('fsdp'), may hold values from -6 to 6
Outputs:
- output: bfloat16 [4096, 2048], P('fsdp')
- grad_tokens: bfloat16 [4096, 2048], P('fsdp')
- grad_lora_down: float32 [8, 4, 2048, 16], P(None, None, 'fsdp')
- grad_lora_up: float32 [8, 4, 16, 2048], P(None, None, None, 'fsdp')
The draws below stay inside these ranges and needn't reach their ends.
Inputs may be any that keep to these rules, and one draw needn't show every extreme that they name: `segments`: segment numbers never fall along a sequence; a document holds at most 1024 positions, and one holds exactly that many. `routes`: A row names 8 different experts. In the rows of one device no expert is named by more than 128 rows, a bound that some block reaches.
All inputs are finite; a program needn't handle non-finite values.
Results may differ from the reference program's by a relative error of at most 0.018.
Values may be sent and summed in bfloat16 or wider, within the bound.
A program may use at most 384 MiB of HBM per device.

```python
import math
import jax
import jax.numpy as jnp
import numpy as np
from jax import lax

MODEL_WIDTH = 2048
HEAD_DIM = 128
FFE = 1024
TOPK = 8
ADAPTER_RANK = 16
ADAPTER_COUNT = 8
SEQ_LEN = 2048
TOK_DEV = 128
HALF = 512
EXPERTS = 16
SLABS = 32
CAP = 128
SEQS = 2
TOKENS = 4096


def level_of(rng, extent, cuts, least, high):
    level, own = 1.0, jax.random.fold_in(rng, 6)
    for axis_at, blocks in cuts:
        steps = jnp.exp(jax.random.uniform(jax.random.fold_in(own, axis_at), (blocks,), jnp.float32, least / len(cuts), high / len(cuts)))
        level = level * jnp.repeat(steps, extent[axis_at] // blocks).reshape([-1 if axis == axis_at else 1 for axis in range(len(extent))])
    return level


def length_profile(count, total, limit, lean):
    portions = [(1 << 20) // math.isqrt(standing ** lean) + 1 for standing in range(2, count + 1)]
    spare, counts = total - limit - (count - 1), [1] * (count - 1)
    while spare > 0:
        movable = [i for i in range(count - 1) if counts[i] < limit]
        whole, budget = sum([portions[i] for i in movable]), spare
        for i in movable:
            more = min(limit - counts[i], max(1, budget * portions[i] // whole), spare)
            counts[i] = counts[i] + more
            spare = spare - more
    return np.array([limit] + counts)


def ragged_sizes(stream_key, count, total, limit, slope):
    if count == 2:
        one = jax.random.randint(stream_key, (), max(1, total - limit), min(limit, total - 1) + 1)
        return jnp.stack([one, total - one])
    sizes = jnp.asarray(length_profile(count, total, limit, slope), jnp.int32)
    twos = (count - 1) // 2
    source_of, receiver = sizes[1:1 + 2 * twos:2], sizes[2:2 + 2 * twos:2]
    margin = jnp.minimum(source_of - 1, limit - receiver)
    moved = jax.random.randint(jax.random.fold_in(stream_key, 1), (twos,), 0, 1 << 20) % (margin + 1)
    sizes = sizes.at[1:1 + 2 * twos:2].set(source_of - moved).at[2:2 + 2 * twos:2].set(receiver + moved)
    return sizes[jax.random.permutation(jax.random.fold_in(stream_key, 2), count)]


def shared_out(rng, own, number, rows, number_of, top, most, lean):
    order = jax.random.permutation(rng, number_of)
    crowded, common = shares(number_of, rows * top, most, lean, True), shares(number_of, rows * top, most, lean, False)
    places = jnp.arange(number_of)

    def named(tallies, rotation):
        used = int((tallies > 0).sum())
        fixed = max(1, used // 4)
        shifted = fixed + (places - fixed + rotation * (used - fixed)) % max(1, number_of - fixed)
        return jnp.zeros((number_of,), jnp.int32).at[order[jnp.where(places < fixed, places, shifted)]].set(jnp.asarray(tallies, jnp.int32))

    tallies = jnp.where(number % 4 == 0, named(crowded, number // 4), named(common, number - number // 4 - 1))
    mixed = jax.random.permutation(jax.random.fold_in(own, 3), number_of)
    donor, taker = mixed[0:number_of // 2 * 2:2], mixed[1:number_of // 2 * 2:2]
    slack = jnp.minimum(tallies[donor] - 1, most - tallies[taker]) // 2
    slack = jnp.where((donor == order[0]) | (taker == order[0]) | (tallies[taker] == 0), 0, jnp.maximum(slack, 0))
    shifted = jax.random.randint(jax.random.fold_in(own, 4), (number_of // 2,), 0, 1 << 20) % (slack + 1)
    tallies = tallies.at[donor].add(-shifted).at[taker].add(shifted)
    members = jnp.searchsorted(jnp.cumsum(tallies), jnp.arange(rows * top), side="right").astype(jnp.int32)
    listing = members.reshape(top, rows).T
    listing = listing[jax.random.permutation(jax.random.fold_in(own, 1), rows)]
    rotation = jax.random.randint(jax.random.fold_in(own, 2), (rows, 1), 0, top)
    return jnp.take_along_axis(listing, (jnp.arange(top)[None, :] + rotation) % top, axis=1)


def shares(count, total, reach, skew, full):
    weights = [(1 << 20) // math.isqrt(standing ** skew) + 1 for standing in range(1, count + 1)]
    largest = reach if full else min(reach, max(-(-total // count), total * weights[0] // sum(weights)))
    least = 1 if total - largest >= count - 1 else 0
    given, rest = [largest] + [least] * (count - 1), total - largest - least * (count - 1)
    while rest > 0:
        candidates = [i for i in range(1, count) if given[i] < largest] or [i for i in range(1, count) if given[i] < reach]
        mass, budget = sum([weights[i] for i in candidates]), rest
        for i in candidates:
            more = min(reach - given[i], max(1, budget * weights[i] // mass), rest)
            given[i] = given[i] + more
            rest = rest - more
    return np.array(given)


def noise(rng, extent, deviation, limit, split=(), kind=jnp.bfloat16):
    entries = jax.random.normal(rng, extent, jnp.float32) * deviation
    if len(split) > 0:
        entries = level_of(rng, extent, split, -0.22, 0.18) * entries
    return jnp.clip(entries, min=-limit, max=limit).astype(kind)


def setup_inputs(seed: int = 0) -> dict:
    splits = jax.random.split(jax.random.key(seed), 20)
    tokens = noise(splits[0], (TOKENS, MODEL_WIDTH), 1.0, 6.0, ((0, 32),))
    segments = jax.vmap(lambda own: jnp.searchsorted(jnp.cumsum(ragged_sizes(own, 16, SEQ_LEN, SEQ_LEN // 2, 2)), jnp.arange(SEQ_LEN), side="right"))(jax.random.split(splits[1], SEQS)).reshape((SEQS, SEQ_LEN)).astype(jnp.int32)
    routes_keys = jax.random.split(jax.random.fold_in(splits[2], 1), TOKENS // TOK_DEV)
    routes_turns = jax.random.permutation(jax.random.fold_in(splits[2], 3), TOKENS // TOK_DEV)
    routes = jax.vmap(lambda own, number: shared_out(jax.random.fold_in(splits[2], 2), own, number, TOK_DEV, EXPERTS, TOPK, CAP, 1))(routes_keys, routes_turns).reshape((TOKENS, TOPK))
    gates = jnp.clip(0.25 + 0.5 * jax.random.uniform(splits[3], (TOKENS, TOPK), jnp.float32) ** level_of(splits[3], (TOKENS, TOPK), ((0, 32),), -0.2, 0.2), 0.25, 0.75)
    sequence_adapter_index = jax.random.randint(splits[4], (SEQS,), 0, ADAPTER_COUNT).astype(jnp.int32)
    attention_norm_gain = jnp.clip(1.0 + 0.1 * jax.random.normal(splits[5], (MODEL_WIDTH,), jnp.float32), 0.5, 1.5).astype(jnp.bfloat16)
    query_norm_gain = jnp.clip(1.0 + 0.15 * jax.random.normal(splits[6], (HEAD_DIM,), jnp.float32), 0.25, 1.75).astype(jnp.bfloat16)
    key_norm_gain = jnp.clip(1.0 + 0.15 * jax.random.normal(splits[7], (HEAD_DIM,), jnp.float32), 0.25, 1.75).astype(jnp.bfloat16)
    query_weight = noise(splits[8], (MODEL_WIDTH, MODEL_WIDTH), MODEL_WIDTH ** -0.5, 0.125, ((0, 32),))
    key_weight = noise(splits[9], (MODEL_WIDTH, MODEL_WIDTH), MODEL_WIDTH ** -0.5, 0.125, ((0, 32),))
    value_weight = noise(splits[10], (MODEL_WIDTH, MODEL_WIDTH), MODEL_WIDTH ** -0.5, 0.125, ((0, 32),))
    output_weight = noise(splits[11], (MODEL_WIDTH, MODEL_WIDTH), (MODEL_WIDTH // 16) ** -0.5, 0.5, ((0, 32),))
    adapter_down_factors = noise(splits[12], (ADAPTER_COUNT, 4, MODEL_WIDTH, ADAPTER_RANK), MODEL_WIDTH ** -0.5, 0.125, ((2, 32),))
    adapter_up_factors = noise(splits[13], (ADAPTER_COUNT, 4, ADAPTER_RANK, MODEL_WIDTH), (4 * ADAPTER_RANK) ** -0.5, 0.75, ((3, 32),))
    expert_norm_gain = jnp.clip(1.0 + 0.1 * jax.random.normal(splits[14], (MODEL_WIDTH,), jnp.float32), 0.5, 1.5).astype(jnp.bfloat16)
    expert_gate_weight = noise(splits[15], (SLABS, MODEL_WIDTH, HALF), MODEL_WIDTH ** -0.5, 0.125, ((0, 32),))
    expert_up_weight = noise(splits[16], (SLABS, MODEL_WIDTH, HALF), MODEL_WIDTH ** -0.5, 0.125, ((0, 32),))
    expert_down_weight = noise(splits[17], (SLABS, HALF, MODEL_WIDTH), FFE ** -0.5, 0.1875, ((0, 32),))
    output_gradient = noise(splits[18], (TOKENS, MODEL_WIDTH), 1.0, 6.0, ((0, 32),))
    return {"tokens": tokens, "segments": segments, "routes": routes, "gates": gates, "sequence_adapter_index": sequence_adapter_index, "attention_norm_gain": attention_norm_gain, "query_norm_gain": query_norm_gain, "key_norm_gain": key_norm_gain, "query_weight": query_weight, "key_weight": key_weight, "value_weight": value_weight, "output_weight": output_weight, "adapter_down_factors": adapter_down_factors, "adapter_up_factors": adapter_up_factors, "expert_norm_gain": expert_norm_gain, "expert_gate_weight": expert_gate_weight, "expert_up_weight": expert_up_weight, "expert_down_weight": expert_down_weight, "output_gradient": output_gradient}


epsilon = 1e-06
rope_base = 50000.0

@jax.custom_vjp
def low(v):
    return lax.optimization_barrier(v.astype(jnp.bfloat16)).astype(jnp.float32)

@jax.custom_vjp
def low_back(v):
    return v

def low_keep(v):
    return (low(v), None)

def low_pass(kept, grad):
    return (grad,)

def back_keep(v):
    return (v, None)

def back_low(kept, grad):
    return (low(grad),)
low.defvjp(low_keep, low_pass)
low_back.defvjp(back_keep, back_low)

def product(left, right):
    return jnp.matmul(left, right, precision=lax.Precision.HIGHEST)

def rms_scale(rows, gain):
    return rows * lax.rsqrt(lax.optimization_barrier(jnp.mean(rows * rows, axis=-1, keepdims=True)) + epsilon) * gain

def rope_tables(positions):
    half = HEAD_DIM // 2
    frequency = rope_base ** (-(jnp.arange(half, dtype=jnp.float32) * 2.0 / HEAD_DIM))
    angle = positions[:, None] * frequency[None, :]
    return (jnp.cos(angle)[:, None, :], jnp.sin(angle)[:, None, :])

def rotate(rows, cosine, sine):
    half = rows.shape[-1] // 2
    first = rows[..., :half]
    second = rows[..., half:]
    return jnp.concatenate([first * cosine - second * sine, second * cosine + first * sine], axis=-1)

def reference(tokens, segments, routes, gates, sequence_adapter_index, attention_norm_gain, query_norm_gain, key_norm_gain, query_weight, key_weight, value_weight, output_weight, adapter_down_factors, adapter_up_factors, expert_norm_gain, expert_gate_weight, expert_up_weight, expert_down_weight, output_gradient):
    matrices = [matrix.astype(jnp.float32) for matrix in (query_weight, key_weight, value_weight, output_weight)]
    attn_scale = attention_norm_gain.astype(jnp.float32)
    query_scale = query_norm_gain.astype(jnp.float32)
    key_scale = key_norm_gain.astype(jnp.float32)
    ffn_scale = expert_norm_gain.astype(jnp.float32)
    slab_gate = expert_gate_weight.astype(jnp.float32)
    slab_up = expert_up_weight.astype(jnp.float32)
    slab_down = expert_down_weight.astype(jnp.float32)
    cosine, sine = rope_tables(jnp.arange(SEQ_LEN, dtype=jnp.float32))
    scale = 1.0 / math.sqrt(HEAD_DIM)
    heads = MODEL_WIDTH // HEAD_DIM
    chosen = (routes[:, :, None] == jnp.arange(EXPERTS, dtype=jnp.int32)[None, None, :]).astype(jnp.float32)
    coeff = lax.optimization_barrier(jnp.sum(gates[:, :, None] * chosen, axis=1))

    def layer_forward(rows_all, down_all, up_all):

        def attend(rows, segment, adapter):
            down_own = down_all[adapter]
            up_own = up_all[adapter]

            def project(inputs, index):
                inner = low_back(low(product(inputs, down_own[index])))
                return low_back(product(inputs, matrices[index]) + product(inner, up_own[index]))
            normed = low(rms_scale(rows, attn_scale))
            query_heads = project(normed, 0).reshape(SEQ_LEN, heads, HEAD_DIM)
            key_heads = project(normed, 1).reshape(SEQ_LEN, heads, HEAD_DIM)
            value = low(project(normed, 2)).reshape(SEQ_LEN, heads, HEAD_DIM)
            query = low(rotate(rms_scale(query_heads, query_scale), cosine, sine))
            key = low(rotate(rms_scale(key_heads, key_scale), cosine, sine))
            scores = low_back(jnp.einsum('shd,thd->hst', query, key, precision=lax.Precision.HIGHEST) * scale)
            allowed = (segment[:, None] == segment[None, :])[None]
            probs = jax.nn.softmax(jnp.where(allowed, scores, -1e+30), axis=-1)
            mixed = low_back(low(jnp.einsum('hst,thd->shd', low(probs), value, precision=lax.Precision.HIGHEST)))
            return rows + project(mixed.reshape(SEQ_LEN, MODEL_WIDTH), 3)

        def sequence_step(carry, pieces):
            rows, segment, adapter = pieces
            return (carry, attend(rows, segment, adapter))
        _, middle = lax.scan(jax.checkpoint(sequence_step), jnp.zeros((), jnp.float32), (rows_all.reshape(SEQS, SEQ_LEN, MODEL_WIDTH), segments, sequence_adapter_index))
        middle = middle.reshape(TOKENS, MODEL_WIDTH)
        normed_ffn = low(rms_scale(middle, ffn_scale))

        def slab_step(total, slab):
            inputs = low_back(normed_ffn)
            gate_part = low_back(product(inputs, slab_gate[slab]))
            up_part = low_back(product(inputs, slab_up[slab]))
            hidden = low(jax.nn.silu(gate_part) * up_part)
            part = low_back(low(product(hidden, slab_down[slab])))
            weight = lax.dynamic_index_in_dim(coeff, slab // 2, 1, keepdims=False)
            return (total + weight[:, None] * part, None)
        moe, _ = lax.scan(jax.checkpoint(slab_step), jnp.zeros((TOKENS, MODEL_WIDTH), jnp.float32), jnp.arange(SLABS, dtype=jnp.int32))
        return middle + moe
    output, layer_backward = jax.vjp(layer_forward, tokens.astype(jnp.float32), adapter_down_factors.astype(jnp.float32), adapter_up_factors.astype(jnp.float32))
    grad_tokens, grad_down, grad_up = layer_backward(output_gradient.astype(jnp.float32))
    return (output.astype(jnp.bfloat16), grad_tokens.astype(jnp.bfloat16), grad_down, grad_up)
```

```python
import math

import jax
import jax.numpy as jnp
from jax import lax
from jax.sharding import PartitionSpec as P

HEAD_DIM = 128
TOPK = 8
ADAPTER_COUNT = 8
SEQ_LEN = 2048


epsilon = 1e-06
rope_base = 50000.0


def from_partner(value, axis, distance):
    mask = 2**distance
    pairs = [(source, source ^ mask) for source in range(lax.axis_size(axis))]
    return lax.ppermute(value, axis, pairs)


def matmul(left, right):
    return jnp.dot(left, right, preferred_element_type=jnp.float32)


def rms_scale(rows, gain):
    return rows * lax.rsqrt(jnp.mean(rows * rows, axis=-1, keepdims=True) + epsilon) * gain


def rms_back(rows, gain, upstream):
    inverse = lax.rsqrt(jnp.mean(rows * rows, axis=-1, keepdims=True) + epsilon)
    unit = rows * inverse
    scaled = upstream * gain
    return inverse * (scaled - unit * jnp.mean(scaled * unit, axis=-1, keepdims=True))


def rope_tables(positions):
    half = HEAD_DIM // 2
    frequency = rope_base ** (-(jnp.arange(half, dtype=jnp.float32) * 2.0 / HEAD_DIM))
    angle = positions[:, None] * frequency[None, :]
    return (jnp.cos(angle)[:, None, :], jnp.sin(angle)[:, None, :])


def rotate(rows, cosine, sine):
    half = rows.shape[-1] // 2
    first = rows[..., :half]
    second = rows[..., half:]
    return jnp.concatenate(
        [first * cosine - second * sine, second * cosine + first * sine], axis=-1
    )


def rotate_back(upstream, cosine, sine):
    half = upstream.shape[-1] // 2
    first = upstream[..., :half]
    second = upstream[..., half:]
    return jnp.concatenate(
        [first * cosine + second * sine, second * cosine - first * sine], axis=-1
    )


def pick(table, index):
    return lax.dynamic_index_in_dim(table, index, 0, keepdims=False)


def shards(
    tokens,
    segments,
    routes,
    gates,
    sequence_adapter_index,
    attention_norm_gain,
    query_norm_gain,
    key_norm_gain,
    query_weight,
    key_weight,
    value_weight,
    output_weight,
    adapter_down_factors,
    adapter_up_factors,
    expert_norm_gain,
    expert_gate_weight,
    expert_up_weight,
    expert_down_weight,
    output_gradient,
):
    rows_dev = tokens.shape[0]
    width = tokens.shape[1]
    heads = width // HEAD_DIM
    group = SEQ_LEN // rows_dev
    level_list = group.bit_length() - 1
    device = lax.axis_index("fsdp")
    place = device % group
    sequence = device // group
    segment_row = pick(segments, sequence)
    own_segment = lax.dynamic_slice_in_dim(segment_row, place * rows_dev, rows_dev)
    adapter = pick(sequence_adapter_index, sequence)
    scale = 1.0 / math.sqrt(HEAD_DIM)
    cosine, sine = rope_tables(
        (place * rows_dev + jnp.arange(rows_dev, dtype=jnp.int32)).astype(jnp.float32)
    )
    attn_scale = attention_norm_gain.astype(jnp.float32)
    query_scale = query_norm_gain.astype(jnp.float32)
    key_scale = key_norm_gain.astype(jnp.float32)
    ffn_scale = expert_norm_gain.astype(jnp.float32)
    gathered = (
        lax.all_gather(query_weight, "fsdp", axis=0, tiled=True),
        lax.all_gather(key_weight, "fsdp", axis=0, tiled=True),
        lax.all_gather(value_weight, "fsdp", axis=0, tiled=True),
        lax.all_gather(output_weight, "fsdp", axis=0, tiled=True),
        lax.all_gather(adapter_down_factors, "fsdp", axis=2, tiled=True),
        lax.all_gather(adapter_up_factors, "fsdp", axis=3, tiled=True),
    )
    matrices = gathered[:4]
    down_own = pick(gathered[4], adapter)
    up_own = pick(gathered[5], adapter)

    def project(inputs, index):
        inner = matmul(inputs, down_own[index]).astype(jnp.bfloat16)
        return (matmul(inputs, matrices[index]) + matmul(inner, up_own[index]), inner)

    rows = tokens.astype(jnp.float32)
    normed = rms_scale(rows, attn_scale).astype(jnp.bfloat16)
    query_proj, query_inner = project(normed, 0)
    key_proj, key_inner = project(normed, 1)
    value_proj, value_inner = project(normed, 2)
    query_heads = query_proj.reshape(rows_dev, heads, HEAD_DIM)
    key_heads = key_proj.reshape(rows_dev, heads, HEAD_DIM)
    query_rot = rotate(rms_scale(query_heads, query_scale), cosine, sine).astype(jnp.bfloat16)
    key_rot = (
        rotate(rms_scale(key_heads, key_scale), cosine, sine)
        .astype(jnp.bfloat16)
        .reshape(rows_dev, width)
    )
    value_low = value_proj.astype(jnp.bfloat16)
    held_keys = key_rot
    held_values = value_low
    for level in range(level_list):
        other_keys, other_values = from_partner((held_keys, held_values), "fsdp", level)
        upper_bit = place // (1 << level) % 2 == 1
        held_keys = jnp.where(
            upper_bit,
            jnp.concatenate([other_keys, held_keys], axis=0),
            jnp.concatenate([held_keys, other_keys], axis=0),
        )
        held_values = jnp.where(
            upper_bit,
            jnp.concatenate([other_values, held_values], axis=0),
            jnp.concatenate([held_values, other_values], axis=0),
        )
    keys_all = held_keys.reshape(SEQ_LEN, heads, HEAD_DIM)
    values_all = held_values.reshape(SEQ_LEN, heads, HEAD_DIM)
    allowed = (own_segment[:, None] == segment_row[None, :])[None]

    def masked_scores():
        raw = (
            jnp.einsum("thd,shd->hts", query_rot, keys_all, preferred_element_type=jnp.float32)
            * scale
        )
        return jnp.where(allowed, raw, -1e30)

    scores = masked_scores()
    maximum = jnp.max(scores, axis=-1, keepdims=True)
    weights = jnp.exp(scores - maximum)
    total = jnp.sum(weights, axis=-1, keepdims=True)
    probs = weights / total
    log_total = maximum + jnp.log(total)
    mixed = jnp.einsum(
        "hts,shd->thd", probs.astype(jnp.bfloat16), values_all, preferred_element_type=jnp.float32
    )
    mixed = mixed.astype(jnp.bfloat16).reshape(rows_dev, width)
    attn_proj, out_inner = project(mixed, 3)
    middle = rows + attn_proj
    normed_ffn = rms_scale(middle, ffn_scale).astype(jnp.bfloat16)
    experts = lax.axis_size("fsdp") // 2
    capacity = 2 * rows_dev * TOPK // experts
    flat_routes = routes.reshape(-1)
    onehot = (flat_routes[:, None] == jnp.arange(experts, dtype=jnp.int32)[None, :]).astype(
        jnp.int32
    )
    slot = jnp.sum(jnp.cumsum(onehot, axis=0) * onehot, axis=1) - 1
    target = flat_routes * capacity + slot

    def spread(entries):
        buffer = jnp.zeros((experts * capacity, width), jnp.bfloat16).at[target].set(entries)
        buffer = buffer.reshape(experts, 1, capacity, width)
        return jnp.broadcast_to(buffer, (experts, 2, capacity, width)).reshape(
            2 * experts, capacity, width
        )

    def collect(returned):
        halves = returned.reshape(experts, 2, capacity, width).astype(jnp.float32)
        summed = (halves[:, 0] + halves[:, 1]).reshape(experts * capacity, width)
        return summed[target].reshape(rows_dev, TOPK, width)

    slab_gate = expert_gate_weight[0]
    slab_up = expert_up_weight[0]
    slab_down = expert_down_weight[0]
    dispatched = lax.all_to_all(
        spread(jnp.repeat(normed_ffn, TOPK, axis=0)),
        "fsdp",
        split_axis=0,
        concat_axis=0,
        tiled=True,
    )
    gate_part = jnp.einsum("scd,dh->sch", dispatched, slab_gate, preferred_element_type=jnp.float32)
    up_part = jnp.einsum("scd,dh->sch", dispatched, slab_up, preferred_element_type=jnp.float32)
    hidden = (jax.nn.silu(gate_part) * up_part).astype(jnp.bfloat16)
    produced = jnp.einsum(
        "sch,hd->scd", hidden, slab_down, preferred_element_type=jnp.float32
    ).astype(jnp.bfloat16)
    returned = lax.all_to_all(produced, "fsdp", split_axis=0, concat_axis=0, tiled=True)
    moe = jnp.sum(gates[:, :, None] * collect(returned), axis=1)
    output = (middle + moe).astype(jnp.bfloat16)
    upstream = output_gradient.astype(jnp.float32)
    grad_parts = (
        (gates[:, :, None] * upstream[:, None, :])
        .astype(jnp.bfloat16)
        .reshape(rows_dev * TOPK, width)
    )
    grad_sent = lax.all_to_all(spread(grad_parts), "fsdp", split_axis=0, concat_axis=0, tiled=True)
    grad_hidden = jnp.einsum(
        "scd,hd->sch", grad_sent, slab_down, preferred_element_type=jnp.float32
    )
    sigmoid = jax.nn.sigmoid(gate_part)
    grad_gate = (grad_hidden * up_part * sigmoid * (1.0 + gate_part * (1.0 - sigmoid))).astype(
        jnp.bfloat16
    )
    grad_up = (grad_hidden * gate_part * sigmoid).astype(jnp.bfloat16)
    grad_inputs = jnp.einsum(
        "sch,dh->scd", grad_gate, slab_gate, preferred_element_type=jnp.float32
    )
    grad_inputs = (
        grad_inputs
        + jnp.einsum("sch,dh->scd", grad_up, slab_up, preferred_element_type=jnp.float32)
    ).astype(jnp.bfloat16)
    grad_back = lax.all_to_all(grad_inputs, "fsdp", split_axis=0, concat_axis=0, tiled=True)
    grad_ffn = jnp.sum(collect(grad_back), axis=1)
    grad_middle = upstream + rms_back(middle, ffn_scale, grad_ffn)
    grad_attn = grad_middle.astype(jnp.bfloat16)
    regathered = (
        lax.all_gather(query_weight, "fsdp", axis=0, tiled=True),
        lax.all_gather(key_weight, "fsdp", axis=0, tiled=True),
        lax.all_gather(value_weight, "fsdp", axis=0, tiled=True),
        lax.all_gather(output_weight, "fsdp", axis=0, tiled=True),
        lax.all_gather(adapter_down_factors, "fsdp", axis=2, tiled=True),
        lax.all_gather(adapter_up_factors, "fsdp", axis=3, tiled=True),
    )
    back_matrices = regathered[:4]
    back_down = pick(regathered[4], adapter)
    back_up = pick(regathered[5], adapter)

    def project_back(inputs, inner, upstream_low, index):
        grad_inner = matmul(upstream_low, back_up[index].T).astype(jnp.bfloat16)
        grad_input = matmul(upstream_low, back_matrices[index].T) + matmul(
            grad_inner, back_down[index].T
        )
        return (grad_input, matmul(inputs.T, grad_inner), matmul(inner.T, upstream_low))

    grad_mixed_full, down_output, up_output = project_back(mixed, out_inner, grad_attn, 3)
    grad_mixed = grad_mixed_full.astype(jnp.bfloat16).reshape(rows_dev, heads, HEAD_DIM)
    probs = jnp.exp(masked_scores() - log_total)
    grad_probs = jnp.einsum(
        "thd,shd->hts", grad_mixed, values_all, preferred_element_type=jnp.float32
    )
    grad_scores = (
        probs * (grad_probs - jnp.sum(probs * grad_probs, axis=-1, keepdims=True))
    ).astype(jnp.bfloat16)
    grad_query = (
        jnp.einsum("hts,shd->thd", grad_scores, keys_all, preferred_element_type=jnp.float32)
        * scale
    )
    grad_keys_part = (
        jnp.einsum("hts,thd->shd", grad_scores, query_rot, preferred_element_type=jnp.float32)
        * scale
    )
    grad_keys_part = grad_keys_part.reshape(group, rows_dev, width)
    grad_values_part = jnp.einsum(
        "hts,thd->shd", probs.astype(jnp.bfloat16), grad_mixed, preferred_element_type=jnp.float32
    )
    grad_values_part = grad_values_part.reshape(group, rows_dev, width)
    for level in reversed(range(level_list)):
        size_half = 1 << level
        upper_bit = place // size_half % 2 == 1
        keep_keys = jnp.where(upper_bit, grad_keys_part[size_half:], grad_keys_part[:size_half])
        send_keys = jnp.where(upper_bit, grad_keys_part[:size_half], grad_keys_part[size_half:])
        keep_values = jnp.where(
            upper_bit, grad_values_part[size_half:], grad_values_part[:size_half]
        )
        send_values = jnp.where(
            upper_bit, grad_values_part[:size_half], grad_values_part[size_half:]
        )
        got_keys, got_values = (
            from_partner(send_keys.astype(jnp.bfloat16), "fsdp", level).astype(send_keys.dtype),
            from_partner(send_values.astype(jnp.bfloat16), "fsdp", level).astype(send_values.dtype),
        )
        grad_keys_part = keep_keys + got_keys
        grad_values_part = keep_values + got_values
    grad_keys = grad_keys_part[0]
    grad_values = grad_values_part[0]
    grad_value_proj = grad_values.astype(jnp.bfloat16)
    grad_key_proj = rms_back(
        key_heads,
        key_scale,
        rotate_back(grad_keys.reshape(rows_dev, heads, HEAD_DIM), cosine, sine),
    )
    grad_key_proj = grad_key_proj.reshape(rows_dev, width).astype(jnp.bfloat16)
    grad_query_proj = rms_back(query_heads, query_scale, rotate_back(grad_query, cosine, sine))
    grad_query_proj = grad_query_proj.reshape(rows_dev, width).astype(jnp.bfloat16)
    grad_from_query, down_query, up_query = project_back(normed, query_inner, grad_query_proj, 0)
    grad_from_key, down_key, up_key = project_back(normed, key_inner, grad_key_proj, 1)
    grad_from_value, down_value, up_value = project_back(normed, value_inner, grad_value_proj, 2)
    grad_normed = grad_from_query + grad_from_key + grad_from_value
    grad_tokens = (grad_middle + rms_back(rows, attn_scale, grad_normed)).astype(jnp.bfloat16)
    down_terms = jnp.stack([down_query, down_key, down_value, down_output])
    up_terms = jnp.stack([up_query, up_key, up_value, up_output])
    selected = (jnp.arange(ADAPTER_COUNT, dtype=jnp.int32) == adapter).astype(jnp.float32)[
        :, None, None, None
    ]
    grad_down, grad_up = (
        lax.psum_scatter(selected * down_terms[None], "fsdp", scatter_dimension=2, tiled=True),
        lax.psum_scatter(selected * up_terms[None], "fsdp", scatter_dimension=3, tiled=True),
    )
    return (output, grad_tokens, grad_down, grad_up)

def own_columns(value, axis, groups):
    return lax.all_to_all(value, axis, split_axis=1, concat_axis=0, tiled=True, axis_index_groups=groups)


def heads_plan(
    tokens,
    segments,
    routes,
    gates,
    sequence_adapter_index,
    attention_norm_gain,
    query_norm_gain,
    key_norm_gain,
    query_weight,
    key_weight,
    value_weight,
    output_weight,
    adapter_down_factors,
    adapter_up_factors,
    expert_norm_gain,
    expert_gate_weight,
    expert_up_weight,
    expert_down_weight,
    output_gradient,
):
    bf, f32 = jnp.bfloat16, jnp.float32
    devices = lax.axis_size("fsdp")
    rows_dev, width = tokens.shape
    group = SEQ_LEN // rows_dev
    seqs = segments.shape[0]
    experts = devices // 2
    rank = adapter_down_factors.shape[3]
    slots = 4 * rank
    own_rows = query_weight.shape[0]
    device = lax.axis_index("fsdp")
    place = device % group
    sequence = device // group
    groups = [list(range(s * group, (s + 1) * group)) for s in range(seqs)]
    scale = 1.0 / math.sqrt(HEAD_DIM)
    segment_row = pick(segments, sequence)
    cosine, sine = rope_tables(jnp.arange(SEQ_LEN, dtype=jnp.int32).astype(f32))
    cosine, sine = cosine[:, 0], sine[:, 0]
    attn_scale = attention_norm_gain.astype(f32)
    query_scale = query_norm_gain.astype(f32)
    key_scale = key_norm_gain.astype(f32)
    ffn_scale = expert_norm_gain.astype(f32)

    downs = jnp.take(adapter_down_factors, sequence_adapter_index, axis=0)
    ups = jnp.take(adapter_up_factors, sequence_adapter_index, axis=0)
    pair = jnp.concatenate(
        [
            downs.transpose(2, 0, 1, 3).reshape(own_rows, seqs * slots),
            ups.transpose(3, 0, 1, 2).reshape(own_rows, seqs * slots),
        ],
        axis=1,
    )
    factors = lax.all_gather(pair, "fsdp", axis=0, tiled=True)
    down_own = lax.dynamic_slice_in_dim(factors, sequence * slots, slots, 1)
    up_own = lax.dynamic_slice_in_dim(factors, (seqs + sequence) * slots, slots, 1)
    up_head = lax.dynamic_slice_in_dim(up_own, place * HEAD_DIM, HEAD_DIM, 0)

    rows = tokens.astype(f32)
    normed = rms_scale(rows, attn_scale).astype(bf)
    normed_all = lax.all_gather(normed, "fsdp", axis=0, tiled=True, axis_index_groups=groups)

    stacked = jnp.concatenate([query_weight, key_weight, value_weight], axis=0)
    copies = [stacked]
    for other in range(1, seqs):
        copies.append(
            lax.ppermute(
                stacked, "fsdp", [(i, (i + other * group) % devices) for i in range(devices)]
            )
        )
    mine = own_columns(jnp.concatenate(copies, axis=0), "fsdp", groups)
    mine = mine.reshape(group, seqs, 3, own_rows, HEAD_DIM)
    order = (sequence - jnp.arange(seqs)) % seqs
    mine = jnp.take(mine, order, axis=1).transpose(2, 1, 0, 3, 4).reshape(3, width, HEAD_DIM)
    output_matrix = lax.all_gather(output_weight, "fsdp", axis=0, tiled=True)

    inner_all = matmul(normed_all, down_own).astype(bf)

    def project(index):
        inner = inner_all[:, index * rank : (index + 1) * rank]
        up = up_head[:, index * rank : (index + 1) * rank]
        return matmul(normed_all, mine[index]) + matmul(inner, up.T)

    query_proj, key_proj, value_proj = project(0), project(1), project(2)
    query = rotate(rms_scale(query_proj, query_scale), cosine, sine).astype(bf)
    key = rotate(rms_scale(key_proj, key_scale), cosine, sine).astype(bf)
    value = value_proj.astype(bf)
    allowed = segment_row[:, None] == segment_row[None, :]
    scores = jnp.where(allowed, matmul(query, key.T) * scale, -1e30)
    maximum = jnp.max(scores, axis=-1, keepdims=True)
    weights = jnp.exp(scores - maximum)
    total = jnp.sum(weights, axis=-1, keepdims=True)
    probs = weights / total
    probs_low = probs.astype(bf)
    mixed_head = matmul(probs_low, value).astype(bf)
    mixed = lax.all_to_all(
        mixed_head.reshape(group, rows_dev, HEAD_DIM),
        "fsdp",
        split_axis=0,
        concat_axis=0,
        axis_index_groups=groups,
        tiled=True,
    )
    mixed = mixed.transpose(1, 0, 2).reshape(rows_dev, width)
    down_out = down_own[:, 3 * rank :]
    up_out = up_own[:, 3 * rank :]
    out_inner = matmul(mixed, down_out).astype(bf)
    middle = rows + matmul(mixed, output_matrix) + matmul(out_inner, up_out.T)
    normed_ffn = rms_scale(middle, ffn_scale).astype(bf)

    chosen = (routes[:, :, None] == jnp.arange(experts, dtype=jnp.int32)).astype(f32)
    coeff = jnp.sum(gates[:, :, None] * chosen, axis=1)
    coeff_all = lax.all_gather(coeff.T, "fsdp", axis=0, tiled=False)
    coeff_own = lax.dynamic_index_in_dim(coeff_all, device // 2, 1, keepdims=False).reshape(-1, 1)
    slab_gate = expert_gate_weight[0]
    slab_up = expert_up_weight[0]
    slab_down = expert_down_weight[0]
    upstream_all = lax.all_gather(output_gradient, "fsdp", axis=0, tiled=True)
    inputs = lax.all_gather(normed_ffn, "fsdp", axis=0, tiled=True)
    gate_part = matmul(inputs, slab_gate)
    up_part = matmul(inputs, slab_up)
    sigmoid = jax.nn.sigmoid(gate_part)
    hidden = (gate_part * sigmoid * up_part).astype(bf)
    part = (coeff_own * matmul(hidden, slab_down)).astype(bf)
    grad_part = (coeff_own * upstream_all.astype(f32)).astype(bf)
    grad_hidden = matmul(grad_part, slab_down.T)
    grad_gate = (grad_hidden * up_part * sigmoid * (1.0 + gate_part * (1.0 - sigmoid))).astype(bf)
    grad_up = (grad_hidden * gate_part * sigmoid).astype(bf)
    grad_slab = (matmul(grad_gate, slab_gate.T) + matmul(grad_up, slab_up.T)).astype(bf)
    grad_ffn = lax.psum_scatter(grad_slab, "fsdp", scatter_dimension=0, tiled=True).astype(f32)
    moe = lax.psum_scatter(part, "fsdp", scatter_dimension=0, tiled=True).astype(f32)
    output = (middle + moe).astype(bf)
    upstream = output_gradient.astype(f32)
    grad_middle = upstream + rms_back(middle, ffn_scale, grad_ffn)
    grad_attn = grad_middle.astype(bf)

    grad_inner_out = matmul(grad_attn, up_out).astype(bf)
    grad_mixed = matmul(grad_attn, output_matrix.T) + matmul(grad_inner_out, down_out.T)
    grad_mixed = own_columns(grad_mixed.astype(bf), "fsdp", groups)
    up_out_terms = matmul(out_inner.T, grad_attn)
    down_out_terms = matmul(grad_inner_out.T, mixed)

    grad_probs = matmul(grad_mixed, value.T)
    grad_scores = (
        probs * (grad_probs - jnp.sum(probs * grad_probs, axis=-1, keepdims=True))
    ).astype(bf)
    grad_query = matmul(grad_scores, key) * scale
    grad_key = matmul(grad_scores.T, query) * scale
    grad_value = matmul(probs_low.T, grad_mixed)
    back = jnp.concatenate(
        [
            rms_back(query_proj, query_scale, rotate_back(grad_query, cosine, sine)).astype(bf),
            rms_back(key_proj, key_scale, rotate_back(grad_key, cosine, sine)).astype(bf),
            grad_value.astype(bf),
        ],
        axis=1,
    )
    grad_partial = sum(
        matmul(back[:, j * HEAD_DIM : (j + 1) * HEAD_DIM], mine[j].T) for j in range(3)
    ).astype(bf)
    inner_partial = jnp.concatenate(
        [
            matmul(back[:, j * HEAD_DIM : (j + 1) * HEAD_DIM], up_head[:, j * rank : (j + 1) * rank])
            for j in range(3)
        ],
        axis=1,
    )
    grad_sum = lax.psum_scatter(
        grad_partial, "fsdp", scatter_dimension=0, tiled=True, axis_index_groups=groups
    ).astype(f32)
    inner_sum = lax.psum_scatter(
        jnp.pad(inner_partial, ((0, 0), (0, 128 - 3 * rank))),
        "fsdp",
        scatter_dimension=0,
        tiled=True,
        axis_index_groups=groups,
    )
    grad_inner = inner_sum[:, : 3 * rank].astype(bf)
    grad_normed = grad_sum + matmul(grad_inner, down_own[:, : 3 * rank].T)
    grad_tokens = (grad_middle + rms_back(rows, attn_scale, grad_normed)).astype(bf)

    up_head_terms = jnp.concatenate(
        [
            matmul(
                inner_all[:, j * rank : (j + 1) * rank].T,
                back[:, j * HEAD_DIM : (j + 1) * HEAD_DIM],
            )
            for j in range(3)
        ],
        axis=0,
    )
    down_terms = jnp.concatenate([matmul(grad_inner.T, normed), down_out_terms], axis=0)
    head_slot = (jnp.arange(group) == place).astype(f32)
    up_terms = jnp.concatenate(
        [
            (up_head_terms[:, None, :] * head_slot[None, :, None]).reshape(3 * rank, width),
            up_out_terms,
        ],
        axis=0,
    )
    terms = jnp.concatenate([down_terms, up_terms], axis=0)
    terms = lax.all_to_all(
        terms.reshape(2 * slots, devices, own_rows).transpose(1, 0, 2),
        "fsdp",
        split_axis=0,
        concat_axis=0,
        tiled=True,
    )
    terms = jnp.sum(terms.reshape(seqs, group, 2 * slots, own_rows), axis=1)
    selected = (
        jnp.arange(ADAPTER_COUNT, dtype=jnp.int32)[:, None] == sequence_adapter_index[None, :]
    ).astype(f32)
    spread = jnp.sum(selected[:, :, None, None] * terms[None], axis=1)
    spread = spread.reshape(ADAPTER_COUNT, 2, 4, rank, own_rows)
    grad_down = spread[:, 0].transpose(0, 1, 3, 2)
    grad_up = spread[:, 1]
    return (output, grad_tokens, grad_down, grad_up)


def solution(mesh):
    plan = heads_plan if mesh.shape["fsdp"] == 32 else shards
    in_specs = (
        P("fsdp", None),
        P(),
        P("fsdp", None),
        P("fsdp", None),
        P(),
        P(),
        P(),
        P(),
        P("fsdp", None),
        P("fsdp", None),
        P("fsdp", None),
        P("fsdp", None),
        P(None, None, "fsdp", None),
        P(None, None, None, "fsdp"),
        P(),
        P("fsdp", None, None),
        P("fsdp", None, None),
        P("fsdp", None, None),
        P("fsdp", None),
    )
    out_specs = (
        P("fsdp", None),
        P("fsdp", None),
        P(None, None, "fsdp", None),
        P(None, None, None, "fsdp"),
    )
    return jax.shard_map(plan, mesh=mesh, in_specs=in_specs, out_specs=out_specs, check_vma=False)
```

```python
import functools
import math

import jax
import jax.numpy as jnp
from jax import lax
from jax.experimental import pallas as pl
from jax.experimental.pallas import tpu as pltpu
from jax.sharding import PartitionSpec as P

HEAD_DIM = 128
TOPK = 8
ADAPTER_COUNT = 8
SEQ_LEN = 2048


epsilon = 1e-06
rope_base = 50000.0


def from_partner(value, axis, distance):
    mask = 2**distance
    pairs = [(source, source ^ mask) for source in range(lax.axis_size(axis))]
    return lax.ppermute(value, axis, pairs)


def matmul(left, right):
    return jnp.dot(left, right, preferred_element_type=jnp.float32)


def rms_scale(rows, gain):
    return rows * lax.rsqrt(jnp.mean(rows * rows, axis=-1, keepdims=True) + epsilon) * gain


def rms_back(rows, gain, upstream):
    inverse = lax.rsqrt(jnp.mean(rows * rows, axis=-1, keepdims=True) + epsilon)
    unit = rows * inverse
    scaled = upstream * gain
    return inverse * (scaled - unit * jnp.mean(scaled * unit, axis=-1, keepdims=True))


def rope_tables(positions):
    half = HEAD_DIM // 2
    frequency = rope_base ** (-(jnp.arange(half, dtype=jnp.float32) * 2.0 / HEAD_DIM))
    angle = positions[:, None] * frequency[None, :]
    return (jnp.cos(angle)[:, None, :], jnp.sin(angle)[:, None, :])


def rotate(rows, cosine, sine):
    half = rows.shape[-1] // 2
    first = rows[..., :half]
    second = rows[..., half:]
    return jnp.concatenate(
        [first * cosine - second * sine, second * cosine + first * sine], axis=-1
    )


def rotate_back(upstream, cosine, sine):
    half = upstream.shape[-1] // 2
    first = upstream[..., :half]
    second = upstream[..., half:]
    return jnp.concatenate(
        [first * cosine + second * sine, second * cosine - first * sine], axis=-1
    )


def pick(table, index):
    return lax.dynamic_index_in_dim(table, index, 0, keepdims=False)


def shards(
    tokens,
    segments,
    routes,
    gates,
    sequence_adapter_index,
    attention_norm_gain,
    query_norm_gain,
    key_norm_gain,
    query_weight,
    key_weight,
    value_weight,
    output_weight,
    adapter_down_factors,
    adapter_up_factors,
    expert_norm_gain,
    expert_gate_weight,
    expert_up_weight,
    expert_down_weight,
    output_gradient,
):
    rows_dev = tokens.shape[0]
    width = tokens.shape[1]
    heads = width // HEAD_DIM
    group = SEQ_LEN // rows_dev
    level_list = group.bit_length() - 1
    device = lax.axis_index("fsdp")
    place = device % group
    sequence = device // group
    segment_row = pick(segments, sequence)
    own_segment = lax.dynamic_slice_in_dim(segment_row, place * rows_dev, rows_dev)
    adapter = pick(sequence_adapter_index, sequence)
    scale = 1.0 / math.sqrt(HEAD_DIM)
    cosine, sine = rope_tables(
        (place * rows_dev + jnp.arange(rows_dev, dtype=jnp.int32)).astype(jnp.float32)
    )
    attn_scale = attention_norm_gain.astype(jnp.float32)
    query_scale = query_norm_gain.astype(jnp.float32)
    key_scale = key_norm_gain.astype(jnp.float32)
    ffn_scale = expert_norm_gain.astype(jnp.float32)
    gathered = (
        lax.all_gather(query_weight, "fsdp", axis=0, tiled=True),
        lax.all_gather(key_weight, "fsdp", axis=0, tiled=True),
        lax.all_gather(value_weight, "fsdp", axis=0, tiled=True),
        lax.all_gather(output_weight, "fsdp", axis=0, tiled=True),
        lax.all_gather(adapter_down_factors, "fsdp", axis=2, tiled=True),
        lax.all_gather(adapter_up_factors, "fsdp", axis=3, tiled=True),
    )
    matrices = gathered[:4]
    down_own = pick(gathered[4], adapter)
    up_own = pick(gathered[5], adapter)

    def project(inputs, index):
        inner = matmul(inputs, down_own[index]).astype(jnp.bfloat16)
        return (matmul(inputs, matrices[index]) + matmul(inner, up_own[index]), inner)

    rows = tokens.astype(jnp.float32)
    normed = rms_scale(rows, attn_scale).astype(jnp.bfloat16)
    query_proj, query_inner = project(normed, 0)
    key_proj, key_inner = project(normed, 1)
    value_proj, value_inner = project(normed, 2)
    query_heads = query_proj.reshape(rows_dev, heads, HEAD_DIM)
    key_heads = key_proj.reshape(rows_dev, heads, HEAD_DIM)
    query_rot = rotate(rms_scale(query_heads, query_scale), cosine, sine).astype(jnp.bfloat16)
    key_rot = (
        rotate(rms_scale(key_heads, key_scale), cosine, sine)
        .astype(jnp.bfloat16)
        .reshape(rows_dev, width)
    )
    value_low = value_proj.astype(jnp.bfloat16)
    held_keys = key_rot
    held_values = value_low
    for level in range(level_list):
        other_keys, other_values = from_partner((held_keys, held_values), "fsdp", level)
        upper_bit = place // (1 << level) % 2 == 1
        held_keys = jnp.where(
            upper_bit,
            jnp.concatenate([other_keys, held_keys], axis=0),
            jnp.concatenate([held_keys, other_keys], axis=0),
        )
        held_values = jnp.where(
            upper_bit,
            jnp.concatenate([other_values, held_values], axis=0),
            jnp.concatenate([held_values, other_values], axis=0),
        )
    keys_all = held_keys.reshape(SEQ_LEN, heads, HEAD_DIM)
    values_all = held_values.reshape(SEQ_LEN, heads, HEAD_DIM)
    allowed = (own_segment[:, None] == segment_row[None, :])[None]

    def masked_scores():
        raw = (
            jnp.einsum("thd,shd->hts", query_rot, keys_all, preferred_element_type=jnp.float32)
            * scale
        )
        return jnp.where(allowed, raw, -1e30)

    scores = masked_scores()
    maximum = jnp.max(scores, axis=-1, keepdims=True)
    weights = jnp.exp(scores - maximum)
    total = jnp.sum(weights, axis=-1, keepdims=True)
    probs = weights / total
    log_total = maximum + jnp.log(total)
    mixed = jnp.einsum(
        "hts,shd->thd", probs.astype(jnp.bfloat16), values_all, preferred_element_type=jnp.float32
    )
    mixed = mixed.astype(jnp.bfloat16).reshape(rows_dev, width)
    attn_proj, out_inner = project(mixed, 3)
    middle = rows + attn_proj
    normed_ffn = rms_scale(middle, ffn_scale).astype(jnp.bfloat16)
    experts = lax.axis_size("fsdp") // 2
    capacity = 2 * rows_dev * TOPK // experts
    flat_routes = routes.reshape(-1)
    onehot = (flat_routes[:, None] == jnp.arange(experts, dtype=jnp.int32)[None, :]).astype(
        jnp.int32
    )
    slot = jnp.sum(jnp.cumsum(onehot, axis=0) * onehot, axis=1) - 1
    target = flat_routes * capacity + slot

    def spread(entries):
        buffer = jnp.zeros((experts * capacity, width), jnp.bfloat16).at[target].set(entries)
        buffer = buffer.reshape(experts, 1, capacity, width)
        return jnp.broadcast_to(buffer, (experts, 2, capacity, width)).reshape(
            2 * experts, capacity, width
        )

    def collect(returned):
        halves = returned.reshape(experts, 2, capacity, width).astype(jnp.float32)
        summed = (halves[:, 0] + halves[:, 1]).reshape(experts * capacity, width)
        return summed[target].reshape(rows_dev, TOPK, width)

    slab_gate = expert_gate_weight[0]
    slab_up = expert_up_weight[0]
    slab_down = expert_down_weight[0]
    dispatched = lax.all_to_all(
        spread(jnp.repeat(normed_ffn, TOPK, axis=0)),
        "fsdp",
        split_axis=0,
        concat_axis=0,
        tiled=True,
    )
    gate_part = jnp.einsum("scd,dh->sch", dispatched, slab_gate, preferred_element_type=jnp.float32)
    up_part = jnp.einsum("scd,dh->sch", dispatched, slab_up, preferred_element_type=jnp.float32)
    hidden = (jax.nn.silu(gate_part) * up_part).astype(jnp.bfloat16)
    produced = jnp.einsum(
        "sch,hd->scd", hidden, slab_down, preferred_element_type=jnp.float32
    ).astype(jnp.bfloat16)
    returned = lax.all_to_all(produced, "fsdp", split_axis=0, concat_axis=0, tiled=True)
    moe = jnp.sum(gates[:, :, None] * collect(returned), axis=1)
    output = (middle + moe).astype(jnp.bfloat16)
    upstream = output_gradient.astype(jnp.float32)
    grad_parts = (
        (gates[:, :, None] * upstream[:, None, :])
        .astype(jnp.bfloat16)
        .reshape(rows_dev * TOPK, width)
    )
    grad_sent = lax.all_to_all(spread(grad_parts), "fsdp", split_axis=0, concat_axis=0, tiled=True)
    grad_hidden = jnp.einsum(
        "scd,hd->sch", grad_sent, slab_down, preferred_element_type=jnp.float32
    )
    sigmoid = jax.nn.sigmoid(gate_part)
    grad_gate = (grad_hidden * up_part * sigmoid * (1.0 + gate_part * (1.0 - sigmoid))).astype(
        jnp.bfloat16
    )
    grad_up = (grad_hidden * gate_part * sigmoid).astype(jnp.bfloat16)
    grad_inputs = jnp.einsum(
        "sch,dh->scd", grad_gate, slab_gate, preferred_element_type=jnp.float32
    )
    grad_inputs = (
        grad_inputs
        + jnp.einsum("sch,dh->scd", grad_up, slab_up, preferred_element_type=jnp.float32)
    ).astype(jnp.bfloat16)
    grad_back = lax.all_to_all(grad_inputs, "fsdp", split_axis=0, concat_axis=0, tiled=True)
    grad_ffn = jnp.sum(collect(grad_back), axis=1)
    grad_middle = upstream + rms_back(middle, ffn_scale, grad_ffn)
    grad_attn = grad_middle.astype(jnp.bfloat16)
    regathered = (
        lax.all_gather(query_weight, "fsdp", axis=0, tiled=True),
        lax.all_gather(key_weight, "fsdp", axis=0, tiled=True),
        lax.all_gather(value_weight, "fsdp", axis=0, tiled=True),
        lax.all_gather(output_weight, "fsdp", axis=0, tiled=True),
        lax.all_gather(adapter_down_factors, "fsdp", axis=2, tiled=True),
        lax.all_gather(adapter_up_factors, "fsdp", axis=3, tiled=True),
    )
    back_matrices = regathered[:4]
    back_down = pick(regathered[4], adapter)
    back_up = pick(regathered[5], adapter)

    def project_back(inputs, inner, upstream_low, index):
        grad_inner = matmul(upstream_low, back_up[index].T).astype(jnp.bfloat16)
        grad_input = matmul(upstream_low, back_matrices[index].T) + matmul(
            grad_inner, back_down[index].T
        )
        return (grad_input, matmul(inputs.T, grad_inner), matmul(inner.T, upstream_low))

    grad_mixed_full, down_output, up_output = project_back(mixed, out_inner, grad_attn, 3)
    grad_mixed = grad_mixed_full.astype(jnp.bfloat16).reshape(rows_dev, heads, HEAD_DIM)
    probs = jnp.exp(masked_scores() - log_total)
    grad_probs = jnp.einsum(
        "thd,shd->hts", grad_mixed, values_all, preferred_element_type=jnp.float32
    )
    grad_scores = (
        probs * (grad_probs - jnp.sum(probs * grad_probs, axis=-1, keepdims=True))
    ).astype(jnp.bfloat16)
    grad_query = (
        jnp.einsum("hts,shd->thd", grad_scores, keys_all, preferred_element_type=jnp.float32)
        * scale
    )
    grad_keys_part = (
        jnp.einsum("hts,thd->shd", grad_scores, query_rot, preferred_element_type=jnp.float32)
        * scale
    )
    grad_keys_part = grad_keys_part.reshape(group, rows_dev, width)
    grad_values_part = jnp.einsum(
        "hts,thd->shd", probs.astype(jnp.bfloat16), grad_mixed, preferred_element_type=jnp.float32
    )
    grad_values_part = grad_values_part.reshape(group, rows_dev, width)
    for level in reversed(range(level_list)):
        size_half = 1 << level
        upper_bit = place // size_half % 2 == 1
        keep_keys = jnp.where(upper_bit, grad_keys_part[size_half:], grad_keys_part[:size_half])
        send_keys = jnp.where(upper_bit, grad_keys_part[:size_half], grad_keys_part[size_half:])
        keep_values = jnp.where(
            upper_bit, grad_values_part[size_half:], grad_values_part[:size_half]
        )
        send_values = jnp.where(
            upper_bit, grad_values_part[:size_half], grad_values_part[size_half:]
        )
        got_keys, got_values = (
            from_partner(send_keys.astype(jnp.bfloat16), "fsdp", level).astype(send_keys.dtype),
            from_partner(send_values.astype(jnp.bfloat16), "fsdp", level).astype(send_values.dtype),
        )
        grad_keys_part = keep_keys + got_keys
        grad_values_part = keep_values + got_values
    grad_keys = grad_keys_part[0]
    grad_values = grad_values_part[0]
    grad_value_proj = grad_values.astype(jnp.bfloat16)
    grad_key_proj = rms_back(
        key_heads,
        key_scale,
        rotate_back(grad_keys.reshape(rows_dev, heads, HEAD_DIM), cosine, sine),
    )
    grad_key_proj = grad_key_proj.reshape(rows_dev, width).astype(jnp.bfloat16)
    grad_query_proj = rms_back(query_heads, query_scale, rotate_back(grad_query, cosine, sine))
    grad_query_proj = grad_query_proj.reshape(rows_dev, width).astype(jnp.bfloat16)
    grad_from_query, down_query, up_query = project_back(normed, query_inner, grad_query_proj, 0)
    grad_from_key, down_key, up_key = project_back(normed, key_inner, grad_key_proj, 1)
    grad_from_value, down_value, up_value = project_back(normed, value_inner, grad_value_proj, 2)
    grad_normed = grad_from_query + grad_from_key + grad_from_value
    grad_tokens = (grad_middle + rms_back(rows, attn_scale, grad_normed)).astype(jnp.bfloat16)
    down_terms = jnp.stack([down_query, down_key, down_value, down_output])
    up_terms = jnp.stack([up_query, up_key, up_value, up_output])
    selected = (jnp.arange(ADAPTER_COUNT, dtype=jnp.int32) == adapter).astype(jnp.float32)[
        :, None, None, None
    ]
    grad_down, grad_up = (
        lax.psum_scatter(selected * down_terms[None], "fsdp", scatter_dimension=2, tiled=True),
        lax.psum_scatter(selected * up_terms[None], "fsdp", scatter_dimension=3, tiled=True),
    )
    return (output, grad_tokens, grad_down, grad_up)


MESH = pl.DeviceIdType.MESH
LEVELS = 4
CHIPS = 16


class Place:
    def __init__(self):
        self.me = me = lax.axis_index("fsdp")
        self.core = me % 2
        self.x = me // 2 % 2
        self.y = me // 4 % 2
        self.z = me // 8
        self.sibling = me + 1 - 2 * self.core
        self.across_x = me + 2 - 4 * self.x
        self.across_y = me + 4 - 8 * self.y

    def level(self, i):
        upper = self.z // 2
        inner = self.z * (1 - upper) + (3 - self.z) * upper
        turn = i + inner * (1 - 2 * i) * (1 - i // 2)
        return turn + upper * (3 - 2 * turn)

    def chip(self, half, side, level):
        flip = 1 - 2 * side
        y = self.y + (1 - half) * side * (1 - 2 * self.y)
        x = self.x + half * side * (1 - 2 * self.x)
        return level * 4 + y * 2 + x

    def chip_at(self, dx, dy, level):
        y = self.y + dy * (1 - 2 * self.y)
        x = self.x + dx * (1 - 2 * self.x)
        return level * 4 + y * 2 + x

    def first(self, half):
        return self.across_y * (1 - half) + self.across_x * half

    def last(self, half):
        return self.across_x * (1 - half) + self.across_y * half


def scatter_kernel(rows, work, source, out, own, sib, cross_out, cross_in, z_out, z_in, first_out, first_in, total,
                   own_sem, sib_send, sib_recv, cross_send, cross_recv, z_send, z_recv, first_send, first_recv):
    place = Place()
    half_rows = rows // 2
    f32, bf = jnp.float32, jnp.bfloat16

    def local(o):
        return pltpu.make_async_copy(source.at[2 * o + place.core], own.at[o], own_sem.at[o])

    def to_sibling(o):
        return pltpu.make_async_remote_copy(
            src_ref=source.at[2 * o + 1 - place.core], dst_ref=sib.at[o], send_sem=sib_send.at[o],
            recv_sem=sib_recv.at[o], device_id=(place.sibling,), device_id_type=MESH)

    def across(h, k, level):
        return pltpu.make_async_remote_copy(
            src_ref=cross_out.at[h, k, level], dst_ref=cross_in.at[h, k, level], send_sem=cross_send.at[h, k, level],
            recv_sem=cross_recv.at[h, k, level], device_id=(place.last(h),), device_id_type=MESH)

    def along(h, k, level, up):
        return pltpu.make_async_remote_copy(
            src_ref=z_out.at[h, k, level], dst_ref=z_in.at[up, h, k, level], send_sem=z_send.at[h, k, level],
            recv_sem=z_recv.at[up, h, k, level], device_id=(place.me - 8 + 16 * up,), device_id_type=MESH)

    def first(h):
        return pltpu.make_async_remote_copy(
            src_ref=first_out.at[h], dst_ref=first_in.at[h], send_sem=first_send.at[h],
            recv_sem=first_recv.at[h], device_id=(place.first(h),), device_id_type=MESH)

    def both(o, h):
        part = pl.ds(h * half_rows, half_rows)
        return own[o, part].astype(f32) + sib[o, part].astype(f32)

    @pl.loop(0, CHIPS)
    def _(q):
        o = place.chip_at(q % 2, q // 2 % 2, place.level(3 - q // 4))
        local(o).start()
        to_sibling(o).start()

    @pl.loop(0, CHIPS + 4)
    def _(t):
        @pl.when(t < CHIPS)
        def _():
            level = place.level(3 - t // 4)
            dx, dy = t % 2, t // 2 % 2
            o = place.chip_at(dx, dy, level)
            local(o).wait()
            to_sibling(o).wait_recv()
            for h, away, k in ((0, dx, dy), (1, dy, dx)):
                @pl.when(away == 1)
                def _():
                    cross_out[h, k, level] = both(o, h).astype(bf)
                    across(h, k, level).start()

        @pl.when(t >= 4)
        def _():
            i, h, k = (t - 4) // 4, t % 2, t // 2 % 2
            level = place.level(3 - i)
            o = place.chip(h, k, level)
            across(h, k, level).wait_recv()
            total[...] = both(o, h) + cross_in[h, k, level].astype(f32)

            @pl.when((level >= place.z) & (place.z > 0))
            def _():
                along(h, k, level, 1).wait_recv()
                total[...] += z_in[1, h, k, level].astype(f32)

            @pl.when((level <= place.z) & (place.z < LEVELS - 1))
            def _():
                along(h, k, level, 0).wait_recv()
                total[...] += z_in[0, h, k, level].astype(f32)

            @pl.when(level > place.z)
            def _():
                z_out[h, k, level] = total[...].astype(bf)
                along(h, k, level, 1).start()

            @pl.when(level < place.z)
            def _():
                z_out[h, k, level] = total[...].astype(bf)
                along(h, k, level, 0).start()

            @pl.when((level == place.z) & (k == 1))
            def _():
                first_out[h] = total[...].astype(bf)
                first(h).start()

            @pl.when((level == place.z) & (k == 0))
            def _():
                out[pl.ds(h * half_rows, half_rows)] = total[...]

        if work is not None:
            work(t)

    for h in range(2):
        first(h).wait_recv()
        out[pl.ds(h * half_rows, half_rows)] += first_in[h].astype(f32)

    @pl.loop(0, CHIPS)
    def _(q):
        o = place.chip_at(q % 2, q // 2 % 2, place.level(3 - q // 4))
        to_sibling(o).wait_send()
        h, k, level = q % 2, q // 2 % 2, q // 4
        across(h, k, level).wait_send()

        @pl.when(level > place.z)
        def _():
            along(h, k, level, 1).wait_send()

        @pl.when(level < place.z)
        def _():
            along(h, k, level, 0).wait_send()

    for h in range(2):
        first(h).wait_send()


def scatter_scratch(rows, width):
    bf = jnp.bfloat16
    dma = pltpu.SemaphoreType.DMA
    piece = (rows // 2, width)
    return [
        pltpu.VMEM((CHIPS, rows, width), bf),
        pltpu.VMEM((CHIPS, rows, width), bf),
        pltpu.VMEM((2, 2, LEVELS) + piece, bf),
        pltpu.VMEM((2, 2, LEVELS) + piece, bf),
        pltpu.VMEM((2, 2, LEVELS) + piece, bf),
        pltpu.VMEM((2, 2, 2, LEVELS) + piece, bf),
        pltpu.VMEM((2,) + piece, bf),
        pltpu.VMEM((2,) + piece, bf),
        pltpu.VMEM(piece, jnp.float32),
        dma((CHIPS,)), dma((CHIPS,)), dma((CHIPS,)),
        dma((2, 2, LEVELS)), dma((2, 2, LEVELS)),
        dma((2, 2, LEVELS)), dma((2, 2, 2, LEVELS)),
        dma((2,)), dma((2,)),
    ]


def scatter_all(partial):
    devices, rows, width = partial.shape
    return pl.pallas_call(
        functools.partial(scatter_kernel, rows, None),
        out_shape=jax.ShapeDtypeStruct((rows, width), jnp.float32),
        in_specs=[pl.BlockSpec(memory_space=pl.ANY)],
        out_specs=pl.BlockSpec(memory_space=pltpu.VMEM),
        scratch_shapes=scatter_scratch(rows, width),
        compiler_params=pltpu.CompilerParams(has_side_effects=True, vmem_limit_bytes=48 << 20),
        name="scatter_all",
    )(partial)


def expert_kernel(rows, x_ref, gate_w, up_w, down_w, coeff, part_out, a_out, b_out,
                  held, part_buf, a_buf, b_buf, own_sem, send, recv, out_sem):
    place = Place()
    half_rows = rows // 2
    f32, bf = jnp.float32, jnp.bfloat16
    me = place.me
    UP, DOWN, LAST, SIB, FIRST = range(5)

    def move(h, o, kind, target):
        d = 2 * o + place.core
        part = pl.ds(h * half_rows, half_rows)
        return pltpu.make_async_remote_copy(
            src_ref=held.at[d, part], dst_ref=held.at[d, part], send_sem=send.at[kind, h, o],
            recv_sem=recv.at[1 if kind == SIB else 0, h, o], device_id=(target,), device_id_type=MESH)

    def arrived(h, o, sib):
        d = 2 * o + (1 - place.core if sib else place.core)
        part = pl.ds(h * half_rows, half_rows)
        pltpu.make_async_remote_copy(
            src_ref=held.at[d, part], dst_ref=held.at[d, part], send_sem=send.at[SIB, h, o],
            recv_sem=recv.at[1 if sib else 0, h, o], device_id=(place.sibling,), device_id_type=MESH).wait_recv()

    def spread(h, o, level, act):
        @pl.when((level <= place.z) & (place.z < LEVELS - 1))
        def _():
            act(move(h, o, UP, me + 8))

        @pl.when((level >= place.z) & (place.z > 0))
        def _():
            act(move(h, o, DOWN, me - 8))

        act(move(h, o, LAST, place.last(h)))
        act(move(h, o, SIB, place.sibling))

    start = lambda copy: copy.start()
    done = lambda copy: copy.wait_send()
    own = pltpu.make_async_copy(x_ref, held.at[me], own_sem)
    own.start()
    own.wait()
    mine = me // 2
    for h in range(2):
        move(h, mine, FIRST, place.first(h)).start()
        spread(h, mine, place.z, start)
    for h in range(2):
        o = place.chip(h, 1, place.z)
        arrived(h, o, False)
        spread(h, o, place.z, start)

    def cross(q):
        level, dx, dy = place.level(q // 4), q % 2, q // 2 % 2
        o = place.chip_at(dx, dy, level)
        for h, away in ((0, dx), (1, dy)):
            @pl.when(away == 1)
            def _():
                arrived(h, o, False)
                move(h, o, SIB, place.sibling).start()

    def outputs(t, slot):
        o = place.chip_at(t % 2, t // 2 % 2, place.level(t // 4))
        two = pl.ds(2 * o, 2)
        return (
            pltpu.make_async_copy(part_buf.at[slot], part_out.at[two], out_sem.at[slot, 0]),
            pltpu.make_async_copy(a_buf.at[slot], a_out.at[two], out_sem.at[slot, 1]),
            pltpu.make_async_copy(b_buf.at[slot], b_out.at[two], out_sem.at[slot, 2]),
        )

    @pl.loop(0, CHIPS)
    def _(t):
        @pl.when(t < CHIPS - 4)
        def _():
            level, h, k = place.level(1 + t // 4), t % 2, t // 2 % 2
            o = place.chip(h, k, level)
            arrived(h, o, False)
            spread(h, o, level, start)

        @pl.when(t + 1 < CHIPS)
        def _():
            cross(t + 1)

        o = place.chip_at(t % 2, t // 2 % 2, place.level(t // 4))
        for h in range(2):
            arrived(h, o, True)
        slot = t % 2

        @pl.when(t >= 2)
        def _():
            for copy in outputs(t - 2, slot):
                copy.wait()

        x = held[pl.ds(2 * o, 2)].reshape(2 * rows, -1)
        gate = jnp.dot(x, gate_w[...], preferred_element_type=f32)
        up = jnp.dot(x, up_w[...], preferred_element_type=f32)
        sig = jax.nn.sigmoid(gate)
        silu = gate * sig
        hidden = (silu * up).astype(bf)
        a_buf[slot] = (up * sig * (1.0 + gate * (1.0 - sig))).reshape(2, rows, -1)
        b_buf[slot] = silu.reshape(2, rows, -1)
        c = coeff[pl.ds(2 * o, 2)].reshape(2 * rows, 1)
        part = jnp.dot(hidden, down_w[...], preferred_element_type=f32)
        part_buf[slot] = (c * part).astype(bf).reshape(2, rows, -1)
        for copy in outputs(t, slot):
            copy.start()

    for t in (CHIPS - 2, CHIPS - 1):
        for copy in outputs(t, t % 2):
            copy.wait()

    for h in range(2):
        move(h, mine, FIRST, place.first(h)).wait_send()
        spread(h, mine, place.z, done)
        spread(h, place.chip(h, 1, place.z), place.z, done)

    @pl.loop(0, CHIPS)
    def _(t):
        @pl.when(t < CHIPS - 4)
        def _():
            level, h, k = place.level(1 + t // 4), t % 2, t // 2 % 2
            spread(h, place.chip(h, k, level), level, done)

        dx, dy = t % 2, t // 2 % 2
        o = place.chip_at(dx, dy, place.level(t // 4))
        for h, away in ((0, dx), (1, dy)):
            @pl.when(away == 1)
            def _():
                move(h, o, SIB, place.sibling).wait_send()


def experts_forward(x, gate_w, up_w, down_w, coeff):
    rows, width = x.shape
    devices, hidden = coeff.shape[0], gate_w.shape[1]
    bf, f32 = jnp.bfloat16, jnp.float32
    dma = pltpu.SemaphoreType.DMA
    vmem, anywhere = pl.BlockSpec(memory_space=pltpu.VMEM), pl.BlockSpec(memory_space=pl.ANY)
    return pl.pallas_call(
        functools.partial(expert_kernel, rows),
        out_shape=(
            jax.ShapeDtypeStruct((devices, rows, width), bf),
            jax.ShapeDtypeStruct((devices, rows, hidden), f32),
            jax.ShapeDtypeStruct((devices, rows, hidden), f32),
        ),
        in_specs=[anywhere, vmem, vmem, vmem, vmem],
        out_specs=(anywhere, anywhere, anywhere),
        scratch_shapes=[
            pltpu.VMEM((devices, rows, width), bf),
            pltpu.VMEM((2, 2, rows, width), bf),
            pltpu.VMEM((2, 2, rows, hidden), f32),
            pltpu.VMEM((2, 2, rows, hidden), f32),
            dma, dma((5, 2, CHIPS)), dma((2, 2, CHIPS)), dma((2, 3)),
        ],
        compiler_params=pltpu.CompilerParams(has_side_effects=True, vmem_limit_bytes=56 << 20),
        name="experts_forward",
    )(x, gate_w, up_w, down_w, coeff)


def backward_kernel(rows, source, upstream, a_in, b_in, gate_w, up_w, down_w, coeff, out, grad_out, *scratch):
    scatter, (u_buf, a_buf, b_buf, g_buf, in_sem, out_sem) = scratch[:-6], scratch[-6:]
    f32, bf = jnp.float32, jnp.bfloat16
    flip = (((1,), (1,)), ((), ()))

    def inputs(t, slot):
        two = pl.ds(2 * t, 2)
        return (
            pltpu.make_async_copy(upstream.at[two], u_buf.at[slot], in_sem.at[slot, 0]),
            pltpu.make_async_copy(a_in.at[two], a_buf.at[slot], in_sem.at[slot, 1]),
            pltpu.make_async_copy(b_in.at[two], b_buf.at[slot], in_sem.at[slot, 2]),
        )

    def output(t, slot):
        return pltpu.make_async_copy(g_buf.at[slot], grad_out.at[pl.ds(2 * t, 2)], out_sem.at[slot])

    def work(t):
        @pl.when(t == 0)
        def _():
            for copy in inputs(0, 0):
                copy.start()

        @pl.when(t < CHIPS)
        def _():
            slot = t % 2

            @pl.when(t + 1 < CHIPS)
            def _():
                for copy in inputs(t + 1, 1 - slot):
                    copy.start()

            for copy in inputs(t, slot):
                copy.wait()

            @pl.when(t >= 2)
            def _():
                output(t - 2, slot).wait()

            c = coeff[pl.ds(2 * t, 2)].reshape(2 * rows, 1)
            part = (c * u_buf[slot].reshape(2 * rows, -1).astype(f32)).astype(bf)
            grad_hidden = lax.dot_general(part, down_w[...], flip, preferred_element_type=f32)
            grad_gate = (grad_hidden * a_buf[slot].reshape(2 * rows, -1)).astype(bf)
            grad_up = (grad_hidden * b_buf[slot].reshape(2 * rows, -1)).astype(bf)
            grad = lax.dot_general(grad_gate, gate_w[...], flip, preferred_element_type=f32)
            grad += lax.dot_general(grad_up, up_w[...], flip, preferred_element_type=f32)
            g_buf[slot] = grad.astype(bf).reshape(2, rows, -1)
            output(t, slot).start()

    scatter_kernel(rows, work, source, out, *scatter)
    for t in (CHIPS - 2, CHIPS - 1):
        output(t, t % 2).wait()


def scatter_beside_backward(partial, upstream, a, b, gate_w, up_w, down_w, coeff):
    devices, rows, width = partial.shape
    hidden = gate_w.shape[1]
    bf, f32 = jnp.bfloat16, jnp.float32
    dma = pltpu.SemaphoreType.DMA
    vmem, anywhere = pl.BlockSpec(memory_space=pltpu.VMEM), pl.BlockSpec(memory_space=pl.ANY)
    return pl.pallas_call(
        functools.partial(backward_kernel, rows),
        out_shape=(
            jax.ShapeDtypeStruct((rows, width), f32),
            jax.ShapeDtypeStruct((devices, rows, width), bf),
        ),
        in_specs=[anywhere] * 4 + [vmem] * 4,
        out_specs=(vmem, anywhere),
        scratch_shapes=scatter_scratch(rows, width) + [
            pltpu.VMEM((2, 2, rows, width), bf),
            pltpu.VMEM((2, 2, rows, hidden), f32),
            pltpu.VMEM((2, 2, rows, hidden), f32),
            pltpu.VMEM((2, 2, rows, width), bf),
            dma((2, 3)), dma((2,)),
        ],
        compiler_params=pltpu.CompilerParams(has_side_effects=True, vmem_limit_bytes=60 << 20),
        name="scatter_backward",
    )(partial, upstream, a, b, gate_w, up_w, down_w, coeff)


def own_columns(value, axis, groups):
    return lax.all_to_all(value, axis, split_axis=1, concat_axis=0, tiled=True, axis_index_groups=groups)


def heads_plan(
    tokens,
    segments,
    routes,
    gates,
    sequence_adapter_index,
    attention_norm_gain,
    query_norm_gain,
    key_norm_gain,
    query_weight,
    key_weight,
    value_weight,
    output_weight,
    adapter_down_factors,
    adapter_up_factors,
    expert_norm_gain,
    expert_gate_weight,
    expert_up_weight,
    expert_down_weight,
    output_gradient,
):
    bf, f32 = jnp.bfloat16, jnp.float32
    devices = lax.axis_size("fsdp")
    rows_dev, width = tokens.shape
    group = SEQ_LEN // rows_dev
    seqs = segments.shape[0]
    experts = devices // 2
    rank = adapter_down_factors.shape[3]
    slots = 4 * rank
    own_rows = query_weight.shape[0]
    device = lax.axis_index("fsdp")
    place = device % group
    sequence = device // group
    groups = [list(range(s * group, (s + 1) * group)) for s in range(seqs)]
    scale = 1.0 / math.sqrt(HEAD_DIM)
    segment_row = pick(segments, sequence)
    cosine, sine = rope_tables(jnp.arange(SEQ_LEN, dtype=jnp.int32).astype(f32))
    cosine, sine = cosine[:, 0], sine[:, 0]
    attn_scale = attention_norm_gain.astype(f32)
    query_scale = query_norm_gain.astype(f32)
    key_scale = key_norm_gain.astype(f32)
    ffn_scale = expert_norm_gain.astype(f32)

    downs = jnp.take(adapter_down_factors, sequence_adapter_index, axis=0)
    ups = jnp.take(adapter_up_factors, sequence_adapter_index, axis=0)
    pair = jnp.concatenate(
        [
            downs.transpose(2, 0, 1, 3).reshape(own_rows, seqs * slots),
            ups.transpose(3, 0, 1, 2).reshape(own_rows, seqs * slots),
        ],
        axis=1,
    )
    factors = lax.all_gather(pair, "fsdp", axis=0, tiled=True)
    down_own = lax.dynamic_slice_in_dim(factors, sequence * slots, slots, 1)
    up_own = lax.dynamic_slice_in_dim(factors, (seqs + sequence) * slots, slots, 1)
    up_head = lax.dynamic_slice_in_dim(up_own, place * HEAD_DIM, HEAD_DIM, 0)

    rows = tokens.astype(f32)
    normed = rms_scale(rows, attn_scale).astype(bf)
    normed_all = lax.all_gather(normed, "fsdp", axis=0, tiled=True, axis_index_groups=groups)

    stacked = jnp.concatenate([query_weight, key_weight, value_weight], axis=0)
    copies = [stacked]
    for other in range(1, seqs):
        copies.append(
            lax.ppermute(
                stacked, "fsdp", [(i, (i + other * group) % devices) for i in range(devices)]
            )
        )
    mine = own_columns(jnp.concatenate(copies, axis=0), "fsdp", groups)
    mine = mine.reshape(group, seqs, 3, own_rows, HEAD_DIM)
    order = (sequence - jnp.arange(seqs)) % seqs
    mine = jnp.take(mine, order, axis=1).transpose(2, 1, 0, 3, 4).reshape(3, width, HEAD_DIM)
    output_matrix = lax.all_gather(output_weight, "fsdp", axis=0, tiled=True)

    inner_all = matmul(normed_all, down_own).astype(bf)

    def project(index):
        inner = inner_all[:, index * rank : (index + 1) * rank]
        up = up_head[:, index * rank : (index + 1) * rank]
        return matmul(normed_all, mine[index]) + matmul(inner, up.T)

    query_proj, key_proj, value_proj = project(0), project(1), project(2)
    query = rotate(rms_scale(query_proj, query_scale), cosine, sine).astype(bf)
    key = rotate(rms_scale(key_proj, key_scale), cosine, sine).astype(bf)
    value = value_proj.astype(bf)
    allowed = segment_row[:, None] == segment_row[None, :]
    scores = jnp.where(allowed, matmul(query, key.T) * scale, -1e30)
    maximum = jnp.max(scores, axis=-1, keepdims=True)
    weights = jnp.exp(scores - maximum)
    total = jnp.sum(weights, axis=-1, keepdims=True)
    probs = weights / total
    probs_low = probs.astype(bf)
    mixed_head = matmul(probs_low, value).astype(bf)
    mixed = lax.all_to_all(
        mixed_head.reshape(group, rows_dev, HEAD_DIM),
        "fsdp",
        split_axis=0,
        concat_axis=0,
        axis_index_groups=groups,
        tiled=True,
    )
    mixed = mixed.transpose(1, 0, 2).reshape(rows_dev, width)
    down_out = down_own[:, 3 * rank :]
    up_out = up_own[:, 3 * rank :]
    out_inner = matmul(mixed, down_out).astype(bf)
    middle = rows + matmul(mixed, output_matrix) + matmul(out_inner, up_out.T)
    normed_ffn = rms_scale(middle, ffn_scale).astype(bf)

    chosen = (routes[:, :, None] == jnp.arange(experts, dtype=jnp.int32)).astype(f32)
    coeff = jnp.sum(gates[:, :, None] * chosen, axis=1)
    coeff_all = lax.all_gather(coeff.T, "fsdp", axis=0, tiled=False)
    coeff_own = lax.dynamic_index_in_dim(coeff_all, device // 2, 1, keepdims=False).reshape(-1, 1)
    slab_gate = expert_gate_weight[0]
    slab_up = expert_up_weight[0]
    slab_down = expert_down_weight[0]
    upstream_all = lax.all_gather(output_gradient, "fsdp", axis=0, tiled=True)
    coeff_own = coeff_own.reshape(devices, rows_dev, 1)
    part, keep_gate, keep_up = experts_forward(normed_ffn, slab_gate, slab_up, slab_down, coeff_own)
    moe, grad_slab = scatter_beside_backward(
        part,
        upstream_all.reshape(devices, rows_dev, width),
        keep_gate,
        keep_up,
        slab_gate,
        slab_up,
        slab_down,
        coeff_own,
    )
    grad_ffn = scatter_all(grad_slab)
    output = (middle + moe).astype(bf)
    upstream = output_gradient.astype(f32)
    grad_middle = upstream + rms_back(middle, ffn_scale, grad_ffn)
    grad_attn = grad_middle.astype(bf)

    grad_inner_out = matmul(grad_attn, up_out).astype(bf)
    grad_mixed = matmul(grad_attn, output_matrix.T) + matmul(grad_inner_out, down_out.T)
    grad_mixed = own_columns(grad_mixed.astype(bf), "fsdp", groups)
    up_out_terms = matmul(out_inner.T, grad_attn)
    down_out_terms = matmul(grad_inner_out.T, mixed)

    grad_probs = matmul(grad_mixed, value.T)
    grad_scores = (
        probs * (grad_probs - jnp.sum(probs * grad_probs, axis=-1, keepdims=True))
    ).astype(bf)
    grad_query = matmul(grad_scores, key) * scale
    grad_key = matmul(grad_scores.T, query) * scale
    grad_value = matmul(probs_low.T, grad_mixed)
    back = jnp.concatenate(
        [
            rms_back(query_proj, query_scale, rotate_back(grad_query, cosine, sine)).astype(bf),
            rms_back(key_proj, key_scale, rotate_back(grad_key, cosine, sine)).astype(bf),
            grad_value.astype(bf),
        ],
        axis=1,
    )
    grad_partial = sum(
        matmul(back[:, j * HEAD_DIM : (j + 1) * HEAD_DIM], mine[j].T) for j in range(3)
    ).astype(bf)
    inner_partial = jnp.concatenate(
        [
            matmul(back[:, j * HEAD_DIM : (j + 1) * HEAD_DIM], up_head[:, j * rank : (j + 1) * rank])
            for j in range(3)
        ],
        axis=1,
    )
    grad_sum = lax.psum_scatter(
        grad_partial, "fsdp", scatter_dimension=0, tiled=True, axis_index_groups=groups
    ).astype(f32)
    inner_sum = lax.psum_scatter(
        jnp.pad(inner_partial, ((0, 0), (0, 128 - 3 * rank))),
        "fsdp",
        scatter_dimension=0,
        tiled=True,
        axis_index_groups=groups,
    )
    grad_inner = inner_sum[:, : 3 * rank].astype(bf)
    grad_normed = grad_sum + matmul(grad_inner, down_own[:, : 3 * rank].T)
    grad_tokens = (grad_middle + rms_back(rows, attn_scale, grad_normed)).astype(bf)

    up_head_terms = jnp.concatenate(
        [
            matmul(
                inner_all[:, j * rank : (j + 1) * rank].T,
                back[:, j * HEAD_DIM : (j + 1) * HEAD_DIM],
            )
            for j in range(3)
        ],
        axis=0,
    )
    down_terms = jnp.concatenate([matmul(grad_inner.T, normed), down_out_terms], axis=0)
    head_slot = (jnp.arange(group) == place).astype(f32)
    up_terms = jnp.concatenate(
        [
            (up_head_terms[:, None, :] * head_slot[None, :, None]).reshape(3 * rank, width),
            up_out_terms,
        ],
        axis=0,
    )
    terms = jnp.concatenate([down_terms, up_terms], axis=0)
    terms = lax.all_to_all(
        terms.reshape(2 * slots, devices, own_rows).transpose(1, 0, 2),
        "fsdp",
        split_axis=0,
        concat_axis=0,
        tiled=True,
    )
    terms = jnp.sum(terms.reshape(seqs, group, 2 * slots, own_rows), axis=1)
    selected = (
        jnp.arange(ADAPTER_COUNT, dtype=jnp.int32)[:, None] == sequence_adapter_index[None, :]
    ).astype(f32)
    spread = jnp.sum(selected[:, :, None, None] * terms[None], axis=1)
    spread = spread.reshape(ADAPTER_COUNT, 2, 4, rank, own_rows)
    grad_down = spread[:, 0].transpose(0, 1, 3, 2)
    grad_up = spread[:, 1]
    return (output, grad_tokens, grad_down, grad_up)


def solution(mesh):
    plan = heads_plan if mesh.shape["fsdp"] == LEVELS * 8 else shards
    in_specs = (
        P("fsdp", None),
        P(),
        P("fsdp", None),
        P("fsdp", None),
        P(),
        P(),
        P(),
        P(),
        P("fsdp", None),
        P("fsdp", None),
        P("fsdp", None),
        P("fsdp", None),
        P(None, None, "fsdp", None),
        P(None, None, None, "fsdp"),
        P(),
        P("fsdp", None, None),
        P("fsdp", None, None),
        P("fsdp", None, None),
        P("fsdp", None),
    )
    out_specs = (
        P("fsdp", None),
        P("fsdp", None),
        P(None, None, "fsdp", None),
        P(None, None, None, "fsdp"),
    )
    return jax.shard_map(plan, mesh=mesh, in_specs=in_specs, out_specs=out_specs, check_vma=False)
```

```python
import functools
import math

import jax
import jax.numpy as jnp
from jax import lax
from jax.experimental import pallas as pl
from jax.experimental.pallas import tpu as pltpu
from jax.sharding import PartitionSpec as P

HEAD_DIM = 128
TOPK = 8
ADAPTER_COUNT = 8
SEQ_LEN = 2048


epsilon = 1e-06
rope_base = 50000.0


def from_partner(value, axis, distance):
    mask = 2**distance
    pairs = [(source, source ^ mask) for source in range(lax.axis_size(axis))]
    return lax.ppermute(value, axis, pairs)


def matmul(left, right):
    return jnp.dot(left, right, preferred_element_type=jnp.float32)


def rms_scale(rows, gain):
    return rows * lax.rsqrt(jnp.mean(rows * rows, axis=-1, keepdims=True) + epsilon) * gain


def rms_back(rows, gain, upstream):
    inverse = lax.rsqrt(jnp.mean(rows * rows, axis=-1, keepdims=True) + epsilon)
    unit = rows * inverse
    scaled = upstream * gain
    return inverse * (scaled - unit * jnp.mean(scaled * unit, axis=-1, keepdims=True))


def rope_tables(positions):
    half = HEAD_DIM // 2
    frequency = rope_base ** (-(jnp.arange(half, dtype=jnp.float32) * 2.0 / HEAD_DIM))
    angle = positions[:, None] * frequency[None, :]
    return (jnp.cos(angle)[:, None, :], jnp.sin(angle)[:, None, :])


def rotate(rows, cosine, sine):
    half = rows.shape[-1] // 2
    first = rows[..., :half]
    second = rows[..., half:]
    return jnp.concatenate(
        [first * cosine - second * sine, second * cosine + first * sine], axis=-1
    )


def rotate_back(upstream, cosine, sine):
    half = upstream.shape[-1] // 2
    first = upstream[..., :half]
    second = upstream[..., half:]
    return jnp.concatenate(
        [first * cosine + second * sine, second * cosine - first * sine], axis=-1
    )


def pick(table, index):
    return lax.dynamic_index_in_dim(table, index, 0, keepdims=False)


def shards(
    tokens,
    segments,
    routes,
    gates,
    sequence_adapter_index,
    attention_norm_gain,
    query_norm_gain,
    key_norm_gain,
    query_weight,
    key_weight,
    value_weight,
    output_weight,
    adapter_down_factors,
    adapter_up_factors,
    expert_norm_gain,
    expert_gate_weight,
    expert_up_weight,
    expert_down_weight,
    output_gradient,
):
    rows_dev = tokens.shape[0]
    width = tokens.shape[1]
    heads = width // HEAD_DIM
    group = SEQ_LEN // rows_dev
    level_list = group.bit_length() - 1
    device = lax.axis_index("fsdp")
    place = device % group
    sequence = device // group
    segment_row = pick(segments, sequence)
    own_segment = lax.dynamic_slice_in_dim(segment_row, place * rows_dev, rows_dev)
    adapter = pick(sequence_adapter_index, sequence)
    scale = 1.0 / math.sqrt(HEAD_DIM)
    cosine, sine = rope_tables(
        (place * rows_dev + jnp.arange(rows_dev, dtype=jnp.int32)).astype(jnp.float32)
    )
    attn_scale = attention_norm_gain.astype(jnp.float32)
    query_scale = query_norm_gain.astype(jnp.float32)
    key_scale = key_norm_gain.astype(jnp.float32)
    ffn_scale = expert_norm_gain.astype(jnp.float32)
    gathered = (
        lax.all_gather(query_weight, "fsdp", axis=0, tiled=True),
        lax.all_gather(key_weight, "fsdp", axis=0, tiled=True),
        lax.all_gather(value_weight, "fsdp", axis=0, tiled=True),
        lax.all_gather(output_weight, "fsdp", axis=0, tiled=True),
        lax.all_gather(adapter_down_factors, "fsdp", axis=2, tiled=True),
        lax.all_gather(adapter_up_factors, "fsdp", axis=3, tiled=True),
    )
    matrices = gathered[:4]
    down_own = pick(gathered[4], adapter)
    up_own = pick(gathered[5], adapter)

    def project(inputs, index):
        inner = matmul(inputs, down_own[index]).astype(jnp.bfloat16)
        return (matmul(inputs, matrices[index]) + matmul(inner, up_own[index]), inner)

    rows = tokens.astype(jnp.float32)
    normed = rms_scale(rows, attn_scale).astype(jnp.bfloat16)
    query_proj, query_inner = project(normed, 0)
    key_proj, key_inner = project(normed, 1)
    value_proj, value_inner = project(normed, 2)
    query_heads = query_proj.reshape(rows_dev, heads, HEAD_DIM)
    key_heads = key_proj.reshape(rows_dev, heads, HEAD_DIM)
    query_rot = rotate(rms_scale(query_heads, query_scale), cosine, sine).astype(jnp.bfloat16)
    key_rot = (
        rotate(rms_scale(key_heads, key_scale), cosine, sine)
        .astype(jnp.bfloat16)
        .reshape(rows_dev, width)
    )
    value_low = value_proj.astype(jnp.bfloat16)
    held_keys = key_rot
    held_values = value_low
    for level in range(level_list):
        other_keys, other_values = from_partner((held_keys, held_values), "fsdp", level)
        upper_bit = place // (1 << level) % 2 == 1
        held_keys = jnp.where(
            upper_bit,
            jnp.concatenate([other_keys, held_keys], axis=0),
            jnp.concatenate([held_keys, other_keys], axis=0),
        )
        held_values = jnp.where(
            upper_bit,
            jnp.concatenate([other_values, held_values], axis=0),
            jnp.concatenate([held_values, other_values], axis=0),
        )
    keys_all = held_keys.reshape(SEQ_LEN, heads, HEAD_DIM)
    values_all = held_values.reshape(SEQ_LEN, heads, HEAD_DIM)
    allowed = (own_segment[:, None] == segment_row[None, :])[None]

    def masked_scores():
        raw = (
            jnp.einsum("thd,shd->hts", query_rot, keys_all, preferred_element_type=jnp.float32)
            * scale
        )
        return jnp.where(allowed, raw, -1e30)

    scores = masked_scores()
    maximum = jnp.max(scores, axis=-1, keepdims=True)
    weights = jnp.exp(scores - maximum)
    total = jnp.sum(weights, axis=-1, keepdims=True)
    probs = weights / total
    log_total = maximum + jnp.log(total)
    mixed = jnp.einsum(
        "hts,shd->thd", probs.astype(jnp.bfloat16), values_all, preferred_element_type=jnp.float32
    )
    mixed = mixed.astype(jnp.bfloat16).reshape(rows_dev, width)
    attn_proj, out_inner = project(mixed, 3)
    middle = rows + attn_proj
    normed_ffn = rms_scale(middle, ffn_scale).astype(jnp.bfloat16)
    experts = lax.axis_size("fsdp") // 2
    capacity = 2 * rows_dev * TOPK // experts
    flat_routes = routes.reshape(-1)
    onehot = (flat_routes[:, None] == jnp.arange(experts, dtype=jnp.int32)[None, :]).astype(
        jnp.int32
    )
    slot = jnp.sum(jnp.cumsum(onehot, axis=0) * onehot, axis=1) - 1
    target = flat_routes * capacity + slot

    def spread(entries):
        buffer = jnp.zeros((experts * capacity, width), jnp.bfloat16).at[target].set(entries)
        buffer = buffer.reshape(experts, 1, capacity, width)
        return jnp.broadcast_to(buffer, (experts, 2, capacity, width)).reshape(
            2 * experts, capacity, width
        )

    def collect(returned):
        halves = returned.reshape(experts, 2, capacity, width).astype(jnp.float32)
        summed = (halves[:, 0] + halves[:, 1]).reshape(experts * capacity, width)
        return summed[target].reshape(rows_dev, TOPK, width)

    slab_gate = expert_gate_weight[0]
    slab_up = expert_up_weight[0]
    slab_down = expert_down_weight[0]
    dispatched = lax.all_to_all(
        spread(jnp.repeat(normed_ffn, TOPK, axis=0)),
        "fsdp",
        split_axis=0,
        concat_axis=0,
        tiled=True,
    )
    gate_part = jnp.einsum("scd,dh->sch", dispatched, slab_gate, preferred_element_type=jnp.float32)
    up_part = jnp.einsum("scd,dh->sch", dispatched, slab_up, preferred_element_type=jnp.float32)
    hidden = (jax.nn.silu(gate_part) * up_part).astype(jnp.bfloat16)
    produced = jnp.einsum(
        "sch,hd->scd", hidden, slab_down, preferred_element_type=jnp.float32
    ).astype(jnp.bfloat16)
    returned = lax.all_to_all(produced, "fsdp", split_axis=0, concat_axis=0, tiled=True)
    moe = jnp.sum(gates[:, :, None] * collect(returned), axis=1)
    output = (middle + moe).astype(jnp.bfloat16)
    upstream = output_gradient.astype(jnp.float32)
    grad_parts = (
        (gates[:, :, None] * upstream[:, None, :])
        .astype(jnp.bfloat16)
        .reshape(rows_dev * TOPK, width)
    )
    grad_sent = lax.all_to_all(spread(grad_parts), "fsdp", split_axis=0, concat_axis=0, tiled=True)
    grad_hidden = jnp.einsum(
        "scd,hd->sch", grad_sent, slab_down, preferred_element_type=jnp.float32
    )
    sigmoid = jax.nn.sigmoid(gate_part)
    grad_gate = (grad_hidden * up_part * sigmoid * (1.0 + gate_part * (1.0 - sigmoid))).astype(
        jnp.bfloat16
    )
    grad_up = (grad_hidden * gate_part * sigmoid).astype(jnp.bfloat16)
    grad_inputs = jnp.einsum(
        "sch,dh->scd", grad_gate, slab_gate, preferred_element_type=jnp.float32
    )
    grad_inputs = (
        grad_inputs
        + jnp.einsum("sch,dh->scd", grad_up, slab_up, preferred_element_type=jnp.float32)
    ).astype(jnp.bfloat16)
    grad_back = lax.all_to_all(grad_inputs, "fsdp", split_axis=0, concat_axis=0, tiled=True)
    grad_ffn = jnp.sum(collect(grad_back), axis=1)
    grad_middle = upstream + rms_back(middle, ffn_scale, grad_ffn)
    grad_attn = grad_middle.astype(jnp.bfloat16)
    regathered = (
        lax.all_gather(query_weight, "fsdp", axis=0, tiled=True),
        lax.all_gather(key_weight, "fsdp", axis=0, tiled=True),
        lax.all_gather(value_weight, "fsdp", axis=0, tiled=True),
        lax.all_gather(output_weight, "fsdp", axis=0, tiled=True),
        lax.all_gather(adapter_down_factors, "fsdp", axis=2, tiled=True),
        lax.all_gather(adapter_up_factors, "fsdp", axis=3, tiled=True),
    )
    back_matrices = regathered[:4]
    back_down = pick(regathered[4], adapter)
    back_up = pick(regathered[5], adapter)

    def project_back(inputs, inner, upstream_low, index):
        grad_inner = matmul(upstream_low, back_up[index].T).astype(jnp.bfloat16)
        grad_input = matmul(upstream_low, back_matrices[index].T) + matmul(
            grad_inner, back_down[index].T
        )
        return (grad_input, matmul(inputs.T, grad_inner), matmul(inner.T, upstream_low))

    grad_mixed_full, down_output, up_output = project_back(mixed, out_inner, grad_attn, 3)
    grad_mixed = grad_mixed_full.astype(jnp.bfloat16).reshape(rows_dev, heads, HEAD_DIM)
    probs = jnp.exp(masked_scores() - log_total)
    grad_probs = jnp.einsum(
        "thd,shd->hts", grad_mixed, values_all, preferred_element_type=jnp.float32
    )
    grad_scores = (
        probs * (grad_probs - jnp.sum(probs * grad_probs, axis=-1, keepdims=True))
    ).astype(jnp.bfloat16)
    grad_query = (
        jnp.einsum("hts,shd->thd", grad_scores, keys_all, preferred_element_type=jnp.float32)
        * scale
    )
    grad_keys_part = (
        jnp.einsum("hts,thd->shd", grad_scores, query_rot, preferred_element_type=jnp.float32)
        * scale
    )
    grad_keys_part = grad_keys_part.reshape(group, rows_dev, width)
    grad_values_part = jnp.einsum(
        "hts,thd->shd", probs.astype(jnp.bfloat16), grad_mixed, preferred_element_type=jnp.float32
    )
    grad_values_part = grad_values_part.reshape(group, rows_dev, width)
    for level in reversed(range(level_list)):
        size_half = 1 << level
        upper_bit = place // size_half % 2 == 1
        keep_keys = jnp.where(upper_bit, grad_keys_part[size_half:], grad_keys_part[:size_half])
        send_keys = jnp.where(upper_bit, grad_keys_part[:size_half], grad_keys_part[size_half:])
        keep_values = jnp.where(
            upper_bit, grad_values_part[size_half:], grad_values_part[:size_half]
        )
        send_values = jnp.where(
            upper_bit, grad_values_part[:size_half], grad_values_part[size_half:]
        )
        got_keys, got_values = (
            from_partner(send_keys.astype(jnp.bfloat16), "fsdp", level).astype(send_keys.dtype),
            from_partner(send_values.astype(jnp.bfloat16), "fsdp", level).astype(send_values.dtype),
        )
        grad_keys_part = keep_keys + got_keys
        grad_values_part = keep_values + got_values
    grad_keys = grad_keys_part[0]
    grad_values = grad_values_part[0]
    grad_value_proj = grad_values.astype(jnp.bfloat16)
    grad_key_proj = rms_back(
        key_heads,
        key_scale,
        rotate_back(grad_keys.reshape(rows_dev, heads, HEAD_DIM), cosine, sine),
    )
    grad_key_proj = grad_key_proj.reshape(rows_dev, width).astype(jnp.bfloat16)
    grad_query_proj = rms_back(query_heads, query_scale, rotate_back(grad_query, cosine, sine))
    grad_query_proj = grad_query_proj.reshape(rows_dev, width).astype(jnp.bfloat16)
    grad_from_query, down_query, up_query = project_back(normed, query_inner, grad_query_proj, 0)
    grad_from_key, down_key, up_key = project_back(normed, key_inner, grad_key_proj, 1)
    grad_from_value, down_value, up_value = project_back(normed, value_inner, grad_value_proj, 2)
    grad_normed = grad_from_query + grad_from_key + grad_from_value
    grad_tokens = (grad_middle + rms_back(rows, attn_scale, grad_normed)).astype(jnp.bfloat16)
    down_terms = jnp.stack([down_query, down_key, down_value, down_output])
    up_terms = jnp.stack([up_query, up_key, up_value, up_output])
    selected = (jnp.arange(ADAPTER_COUNT, dtype=jnp.int32) == adapter).astype(jnp.float32)[
        :, None, None, None
    ]
    grad_down, grad_up = (
        lax.psum_scatter(selected * down_terms[None], "fsdp", scatter_dimension=2, tiled=True),
        lax.psum_scatter(selected * up_terms[None], "fsdp", scatter_dimension=3, tiled=True),
    )
    return (output, grad_tokens, grad_down, grad_up)


MESH = pl.DeviceIdType.MESH
LEVELS = 4
CHIPS = 16


class Place:
    def __init__(self):
        self.me = me = lax.axis_index("fsdp")
        self.core = me % 2
        self.x = me // 2 % 2
        self.y = me // 4 % 2
        self.z = me // 8
        self.sibling = me + 1 - 2 * self.core
        self.across_x = me + 2 - 4 * self.x
        self.across_y = me + 4 - 8 * self.y

    def level(self, i):
        upper = self.z // 2
        inner = self.z * (1 - upper) + (3 - self.z) * upper
        turn = i + inner * (1 - 2 * i) * (1 - i // 2)
        return turn + upper * (3 - 2 * turn)

    def chip(self, half, side, level):
        flip = 1 - 2 * side
        y = self.y + (1 - half) * side * (1 - 2 * self.y)
        x = self.x + half * side * (1 - 2 * self.x)
        return level * 4 + y * 2 + x

    def chip_at(self, dx, dy, level):
        y = self.y + dy * (1 - 2 * self.y)
        x = self.x + dx * (1 - 2 * self.x)
        return level * 4 + y * 2 + x

    def first(self, half):
        return self.across_y * (1 - half) + self.across_x * half

    def last(self, half):
        return self.across_x * (1 - half) + self.across_y * half


def scatter_kernel(rows, work, source, out, own, sib, cross_out, cross_in, z_out, z_in, first_out, first_in, total,
                   own_sem, sib_send, sib_recv, cross_send, cross_recv, z_send, z_recv, first_send, first_recv):
    place = Place()
    half_rows = rows // 2
    f32, bf = jnp.float32, jnp.bfloat16

    def local(o):
        return pltpu.make_async_copy(source.at[2 * o + place.core], own.at[o], own_sem.at[o])

    def to_sibling(o):
        return pltpu.make_async_remote_copy(
            src_ref=source.at[2 * o + 1 - place.core], dst_ref=sib.at[o], send_sem=sib_send.at[o],
            recv_sem=sib_recv.at[o], device_id=(place.sibling,), device_id_type=MESH)

    def across(h, k, level):
        return pltpu.make_async_remote_copy(
            src_ref=cross_out.at[h, k, level], dst_ref=cross_in.at[h, k, level], send_sem=cross_send.at[h, k, level],
            recv_sem=cross_recv.at[h, k, level], device_id=(place.last(h),), device_id_type=MESH)

    def along(h, k, level, up):
        return pltpu.make_async_remote_copy(
            src_ref=z_out.at[h, k, level], dst_ref=z_in.at[up, h, k, level], send_sem=z_send.at[h, k, level],
            recv_sem=z_recv.at[up, h, k, level], device_id=(place.me - 8 + 16 * up,), device_id_type=MESH)

    def first(h):
        return pltpu.make_async_remote_copy(
            src_ref=first_out.at[h], dst_ref=first_in.at[h], send_sem=first_send.at[h],
            recv_sem=first_recv.at[h], device_id=(place.first(h),), device_id_type=MESH)

    def both(o, h):
        part = pl.ds(h * half_rows, half_rows)
        return own[o, part].astype(f32) + sib[o, part].astype(f32)

    @pl.loop(0, CHIPS)
    def _(q):
        o = place.chip_at(q % 2, q // 2 % 2, place.level(3 - q // 4))
        local(o).start()
        to_sibling(o).start()

    @pl.loop(0, CHIPS + 4)
    def _(t):
        @pl.when(t < CHIPS)
        def _():
            level = place.level(3 - t // 4)
            dx, dy = t % 2, t // 2 % 2
            o = place.chip_at(dx, dy, level)
            local(o).wait()
            to_sibling(o).wait_recv()
            for h, away, k in ((0, dx, dy), (1, dy, dx)):
                @pl.when(away == 1)
                def _():
                    cross_out[h, k, level] = both(o, h).astype(bf)
                    across(h, k, level).start()

        @pl.when(t >= 4)
        def _():
            i, h, k = (t - 4) // 4, t % 2, t // 2 % 2
            level = place.level(3 - i)
            o = place.chip(h, k, level)
            across(h, k, level).wait_recv()
            total[...] = both(o, h) + cross_in[h, k, level].astype(f32)

            @pl.when((level >= place.z) & (place.z > 0))
            def _():
                along(h, k, level, 1).wait_recv()
                total[...] += z_in[1, h, k, level].astype(f32)

            @pl.when((level <= place.z) & (place.z < LEVELS - 1))
            def _():
                along(h, k, level, 0).wait_recv()
                total[...] += z_in[0, h, k, level].astype(f32)

            @pl.when(level > place.z)
            def _():
                z_out[h, k, level] = total[...].astype(bf)
                along(h, k, level, 1).start()

            @pl.when(level < place.z)
            def _():
                z_out[h, k, level] = total[...].astype(bf)
                along(h, k, level, 0).start()

            @pl.when((level == place.z) & (k == 1))
            def _():
                first_out[h] = total[...].astype(bf)
                first(h).start()

            @pl.when((level == place.z) & (k == 0))
            def _():
                out[pl.ds(h * half_rows, half_rows)] = total[...]

        if work is not None:
            work(t)

    for h in range(2):
        first(h).wait_recv()
        out[pl.ds(h * half_rows, half_rows)] += first_in[h].astype(f32)

    @pl.loop(0, CHIPS)
    def _(q):
        o = place.chip_at(q % 2, q // 2 % 2, place.level(3 - q // 4))
        to_sibling(o).wait_send()
        h, k, level = q % 2, q // 2 % 2, q // 4
        across(h, k, level).wait_send()

        @pl.when(level > place.z)
        def _():
            along(h, k, level, 1).wait_send()

        @pl.when(level < place.z)
        def _():
            along(h, k, level, 0).wait_send()

    for h in range(2):
        first(h).wait_send()


def scatter_scratch(rows, width):
    bf = jnp.bfloat16
    dma = pltpu.SemaphoreType.DMA
    piece = (rows // 2, width)
    return [
        pltpu.VMEM((CHIPS, rows, width), bf),
        pltpu.VMEM((CHIPS, rows, width), bf),
        pltpu.VMEM((2, 2, LEVELS) + piece, bf),
        pltpu.VMEM((2, 2, LEVELS) + piece, bf),
        pltpu.VMEM((2, 2, LEVELS) + piece, bf),
        pltpu.VMEM((2, 2, 2, LEVELS) + piece, bf),
        pltpu.VMEM((2,) + piece, bf),
        pltpu.VMEM((2,) + piece, bf),
        pltpu.VMEM(piece, jnp.float32),
        dma((CHIPS,)), dma((CHIPS,)), dma((CHIPS,)),
        dma((2, 2, LEVELS)), dma((2, 2, LEVELS)),
        dma((2, 2, LEVELS)), dma((2, 2, 2, LEVELS)),
        dma((2,)), dma((2,)),
    ]


def scatter_all(partial):
    devices, rows, width = partial.shape
    return pl.pallas_call(
        functools.partial(scatter_kernel, rows, None),
        out_shape=jax.ShapeDtypeStruct((rows, width), jnp.float32),
        in_specs=[pl.BlockSpec(memory_space=pl.ANY)],
        out_specs=pl.BlockSpec(memory_space=pltpu.VMEM),
        scratch_shapes=scatter_scratch(rows, width),
        compiler_params=pltpu.CompilerParams(has_side_effects=True, vmem_limit_bytes=48 << 20),
        name="scatter_all",
    )(partial)


def expert_kernel(rows, x_ref, gate_w, up_w, down_w, coeff, part_out, a_out, b_out,
                  held, part_buf, a_buf, b_buf, own_sem, send, recv, out_sem):
    place = Place()
    half_rows = rows // 2
    f32, bf = jnp.float32, jnp.bfloat16
    me = place.me
    UP, DOWN, LAST, SIB, FIRST = range(5)

    def move(h, o, kind, target):
        d = 2 * o + place.core
        part = pl.ds(h * half_rows, half_rows)
        return pltpu.make_async_remote_copy(
            src_ref=held.at[d, part], dst_ref=held.at[d, part], send_sem=send.at[kind, h, o],
            recv_sem=recv.at[1 if kind == SIB else 0, h, o], device_id=(target,), device_id_type=MESH)

    def arrived(h, o, sib):
        d = 2 * o + (1 - place.core if sib else place.core)
        part = pl.ds(h * half_rows, half_rows)
        pltpu.make_async_remote_copy(
            src_ref=held.at[d, part], dst_ref=held.at[d, part], send_sem=send.at[SIB, h, o],
            recv_sem=recv.at[1 if sib else 0, h, o], device_id=(place.sibling,), device_id_type=MESH).wait_recv()

    def spread(h, o, level, act):
        @pl.when((level <= place.z) & (place.z < LEVELS - 1))
        def _():
            act(move(h, o, UP, me + 8))

        @pl.when((level >= place.z) & (place.z > 0))
        def _():
            act(move(h, o, DOWN, me - 8))

        act(move(h, o, LAST, place.last(h)))
        act(move(h, o, SIB, place.sibling))

    start = lambda copy: copy.start()
    done = lambda copy: copy.wait_send()
    own = pltpu.make_async_copy(x_ref, held.at[me], own_sem)
    own.start()
    own.wait()
    mine = me // 2
    for h in range(2):
        move(h, mine, FIRST, place.first(h)).start()
        spread(h, mine, place.z, start)
    for h in range(2):
        o = place.chip(h, 1, place.z)
        arrived(h, o, False)
        spread(h, o, place.z, start)

    def cross(q):
        level, dx, dy = place.level(q // 4), q % 2, q // 2 % 2
        o = place.chip_at(dx, dy, level)
        for h, away in ((0, dx), (1, dy)):
            @pl.when(away == 1)
            def _():
                arrived(h, o, False)
                move(h, o, SIB, place.sibling).start()

    def outputs(t, slot):
        o = place.chip_at(t % 2, t // 2 % 2, place.level(t // 4))
        two = pl.ds(2 * o, 2)
        return (
            pltpu.make_async_copy(part_buf.at[slot], part_out.at[two], out_sem.at[slot, 0]),
            pltpu.make_async_copy(a_buf.at[slot], a_out.at[two], out_sem.at[slot, 1]),
            pltpu.make_async_copy(b_buf.at[slot], b_out.at[two], out_sem.at[slot, 2]),
        )

    @pl.loop(0, CHIPS)
    def _(t):
        @pl.when(t < CHIPS - 4)
        def _():
            level, h, k = place.level(1 + t // 4), t % 2, t // 2 % 2
            o = place.chip(h, k, level)
            arrived(h, o, False)
            spread(h, o, level, start)

        @pl.when(t + 1 < CHIPS)
        def _():
            cross(t + 1)

        o = place.chip_at(t % 2, t // 2 % 2, place.level(t // 4))
        for h in range(2):
            arrived(h, o, True)
        slot = t % 2

        @pl.when(t >= 2)
        def _():
            for copy in outputs(t - 2, slot):
                copy.wait()

        x = held[pl.ds(2 * o, 2)].reshape(2 * rows, -1)
        gate = jnp.dot(x, gate_w[...], preferred_element_type=f32)
        up = jnp.dot(x, up_w[...], preferred_element_type=f32)
        sig = jax.nn.sigmoid(gate)
        silu = gate * sig
        hidden = (silu * up).astype(bf)
        a_buf[slot] = (up * sig * (1.0 + gate * (1.0 - sig))).reshape(2, rows, -1)
        b_buf[slot] = silu.reshape(2, rows, -1)
        c = coeff[pl.ds(2 * o, 2)].reshape(2 * rows, 1)
        part = jnp.dot(hidden, down_w[...], preferred_element_type=f32)
        part_buf[slot] = (c * part).astype(bf).reshape(2, rows, -1)
        for copy in outputs(t, slot):
            copy.start()

    for t in (CHIPS - 2, CHIPS - 1):
        for copy in outputs(t, t % 2):
            copy.wait()

    for h in range(2):
        move(h, mine, FIRST, place.first(h)).wait_send()
        spread(h, mine, place.z, done)
        spread(h, place.chip(h, 1, place.z), place.z, done)

    @pl.loop(0, CHIPS)
    def _(t):
        @pl.when(t < CHIPS - 4)
        def _():
            level, h, k = place.level(1 + t // 4), t % 2, t // 2 % 2
            spread(h, place.chip(h, k, level), level, done)

        dx, dy = t % 2, t // 2 % 2
        o = place.chip_at(dx, dy, place.level(t // 4))
        for h, away in ((0, dx), (1, dy)):
            @pl.when(away == 1)
            def _():
                move(h, o, SIB, place.sibling).wait_send()


def experts_forward(x, gate_w, up_w, down_w, coeff):
    rows, width = x.shape
    devices, hidden = coeff.shape[0], gate_w.shape[1]
    bf, f32 = jnp.bfloat16, jnp.float32
    dma = pltpu.SemaphoreType.DMA
    vmem, anywhere = pl.BlockSpec(memory_space=pltpu.VMEM), pl.BlockSpec(memory_space=pl.ANY)
    return pl.pallas_call(
        functools.partial(expert_kernel, rows),
        out_shape=(
            jax.ShapeDtypeStruct((devices, rows, width), bf),
            jax.ShapeDtypeStruct((devices, rows, hidden), f32),
            jax.ShapeDtypeStruct((devices, rows, hidden), f32),
        ),
        in_specs=[anywhere, vmem, vmem, vmem, vmem],
        out_specs=(anywhere, anywhere, anywhere),
        scratch_shapes=[
            pltpu.VMEM((devices, rows, width), bf),
            pltpu.VMEM((2, 2, rows, width), bf),
            pltpu.VMEM((2, 2, rows, hidden), f32),
            pltpu.VMEM((2, 2, rows, hidden), f32),
            dma, dma((5, 2, CHIPS)), dma((2, 2, CHIPS)), dma((2, 3)),
        ],
        compiler_params=pltpu.CompilerParams(has_side_effects=True, vmem_limit_bytes=56 << 20),
        name="experts_forward",
    )(x, gate_w, up_w, down_w, coeff)


def backward_kernel(rows, source, upstream, a_in, b_in, gate_w, up_w, down_w, coeff, out, grad_out, *scratch):
    scatter, (u_buf, a_buf, b_buf, g_buf, in_sem, out_sem) = scratch[:-6], scratch[-6:]
    f32, bf = jnp.float32, jnp.bfloat16
    flip = (((1,), (1,)), ((), ()))

    def inputs(t, slot):
        two = pl.ds(2 * t, 2)
        return (
            pltpu.make_async_copy(upstream.at[two], u_buf.at[slot], in_sem.at[slot, 0]),
            pltpu.make_async_copy(a_in.at[two], a_buf.at[slot], in_sem.at[slot, 1]),
            pltpu.make_async_copy(b_in.at[two], b_buf.at[slot], in_sem.at[slot, 2]),
        )

    def output(t, slot):
        return pltpu.make_async_copy(g_buf.at[slot], grad_out.at[pl.ds(2 * t, 2)], out_sem.at[slot])

    def work(t):
        @pl.when(t == 0)
        def _():
            for copy in inputs(0, 0):
                copy.start()

        @pl.when(t < CHIPS)
        def _():
            slot = t % 2

            @pl.when(t + 1 < CHIPS)
            def _():
                for copy in inputs(t + 1, 1 - slot):
                    copy.start()

            for copy in inputs(t, slot):
                copy.wait()

            @pl.when(t >= 2)
            def _():
                output(t - 2, slot).wait()

            c = coeff[pl.ds(2 * t, 2)].reshape(2 * rows, 1)
            part = (c * u_buf[slot].reshape(2 * rows, -1).astype(f32)).astype(bf)
            grad_hidden = lax.dot_general(part, down_w[...], flip, preferred_element_type=f32)
            grad_gate = (grad_hidden * a_buf[slot].reshape(2 * rows, -1)).astype(bf)
            grad_up = (grad_hidden * b_buf[slot].reshape(2 * rows, -1)).astype(bf)
            grad = lax.dot_general(grad_gate, gate_w[...], flip, preferred_element_type=f32)
            grad += lax.dot_general(grad_up, up_w[...], flip, preferred_element_type=f32)
            g_buf[slot] = grad.astype(bf).reshape(2, rows, -1)
            output(t, slot).start()

    scatter_kernel(rows, work, source, out, *scatter)
    for t in (CHIPS - 2, CHIPS - 1):
        output(t, t % 2).wait()


def scatter_beside_backward(partial, upstream, a, b, gate_w, up_w, down_w, coeff):
    devices, rows, width = partial.shape
    hidden = gate_w.shape[1]
    bf, f32 = jnp.bfloat16, jnp.float32
    dma = pltpu.SemaphoreType.DMA
    vmem, anywhere = pl.BlockSpec(memory_space=pltpu.VMEM), pl.BlockSpec(memory_space=pl.ANY)
    return pl.pallas_call(
        functools.partial(backward_kernel, rows),
        out_shape=(
            jax.ShapeDtypeStruct((rows, width), f32),
            jax.ShapeDtypeStruct((devices, rows, width), bf),
        ),
        in_specs=[anywhere] * 4 + [vmem] * 4,
        out_specs=(vmem, anywhere),
        scratch_shapes=scatter_scratch(rows, width) + [
            pltpu.VMEM((2, 2, rows, width), bf),
            pltpu.VMEM((2, 2, rows, hidden), f32),
            pltpu.VMEM((2, 2, rows, hidden), f32),
            pltpu.VMEM((2, 2, rows, width), bf),
            dma((2, 3)), dma((2,)),
        ],
        compiler_params=pltpu.CompilerParams(has_side_effects=True, vmem_limit_bytes=60 << 20),
        name="scatter_backward",
    )(partial, upstream, a, b, gate_w, up_w, down_w, coeff)


def front_kernel(rows, rank, normed, heads_w, pair, coeff, cosine, sine, query_gain, key_gain, q_seg, k_seg,
                 mixed, weights, query_out, key_out, value_out, query_proj, key_proj, inner_out, coeff_out,
                 held, mixed_buf,
                 local_sem, send, recv, w_send, w_recv, pair_send, pair_recv, c_send, c_recv, m_send, m_recv, m_local):
    place = Place()
    f32, bf = jnp.float32, jnp.bfloat16
    me, core = place.me, place.core
    group = held.shape[0]
    base, p = me // group * group, me % group
    other = (me + group) % (2 * group)
    other_base = group - base
    half = rows // 2
    depth = weights.shape[1]
    wide = 3 * 128
    z = place.z % 2
    across_z = me + 8 - 16 * z
    chip = p // 2

    FIRST, ALONG, LAST, SIB = range(4)

    def chip_at(h, k, far):
        flip = place.chip(h, k, 0)
        zz = z + far * (1 - 2 * z)
        return zz * 4 + flip

    def move(h, o, kind, target):
        piece = held.at[2 * o + core, pl.ds(h * half, half)]
        return pltpu.make_async_remote_copy(
            src_ref=piece, dst_ref=piece, send_sem=send.at[kind, h, o],
            recv_sem=recv.at[1 if kind == SIB else 0, h, o], device_id=(target,), device_id_type=MESH)

    def arrived(h, o, sibling):
        piece = held.at[2 * o + (1 - core if sibling else core), pl.ds(h * half, half)]
        pltpu.make_async_remote_copy(
            src_ref=piece, dst_ref=piece, send_sem=send.at[SIB, h, o],
            recv_sem=recv.at[1 if sibling else 0, h, o], device_id=(place.sibling,), device_id_type=MESH).wait_recv()

    def to_heads(q):
        return pltpu.make_async_remote_copy(
            src_ref=heads_w.at[q % group], dst_ref=weights.at[me, :, pl.ds(0, wide)], send_sem=w_send.at[q],
            recv_sem=w_recv.at[me], device_id=(q,), device_id_type=MESH)

    def to_expert(q):
        return pltpu.make_async_remote_copy(
            src_ref=coeff.at[q // 2], dst_ref=coeff_out.at[me], send_sem=c_send.at[q],
            recv_sem=c_recv.at[me], device_id=(q,), device_id_type=MESH)

    def pair_over(q, side):
        row = (me + side * group) % (2 * group)
        piece = weights.at[row, :, pl.ds(wide, 128)]
        return pltpu.make_async_remote_copy(
            src_ref=piece, dst_ref=piece, send_sem=pair_send.at[side, q],
            recv_sem=pair_recv.at[row], device_id=(base + q,), device_id_type=MESH)

    pair_other = pltpu.make_async_remote_copy(
        src_ref=pair.at[other // group], dst_ref=weights.at[me, :, pl.ds(wide, 128)], send_sem=pair_send.at[2, 0],
        recv_sem=pair_recv.at[me], device_id=(other,), device_id_type=MESH)
    locals_ = [
        pltpu.make_async_copy(normed, held.at[p], local_sem.at[0]),
        pltpu.make_async_copy(pair.at[me // group], weights.at[me, :, pl.ds(wide, 128)], local_sem.at[1]),
        pltpu.make_async_copy(heads_w.at[p], weights.at[me, :, pl.ds(0, wide)], local_sem.at[2]),
        pltpu.make_async_copy(coeff.at[me // 2], coeff_out.at[me], local_sem.at[3]),
    ]
    for copy in locals_:
        copy.start()
    pair_other.start()

    @pl.loop(0, group)
    def _(i):
        to_heads(other_base + (p + i) % group).start()

    locals_[0].wait()
    for h in range(2):
        move(h, chip, FIRST, place.first(h)).start()
        move(h, chip, ALONG, across_z).start()
    for h in range(2):
        move(h, chip, LAST, place.last(h)).start()
        move(h, chip, SIB, place.sibling).start()
    locals_[1].wait()

    @pl.loop(1, group)
    def _(i):
        pair_over((p + i) % group, 0).start()
        to_heads(base + (p + i) % group).start()

    @pl.loop(1, 2 * group)
    def _(i):
        to_expert((me + i) % (2 * group)).start()

    pltpu.make_async_remote_copy(
        src_ref=pair.at[0], dst_ref=weights.at[other, :, pl.ds(wide, 128)], send_sem=pair_send.at[2, 0],
        recv_sem=pair_recv.at[other], device_id=(other,), device_id_type=MESH).wait_recv()

    @pl.loop(1, group)
    def _(i):
        pair_over((p + i) % group, 1).start()

    for h in range(2):
        o = chip_at(h, 1, 0)
        arrived(h, o, False)
        move(h, o, ALONG, across_z).start()
        move(h, o, LAST, place.last(h)).start()
        move(h, o, SIB, place.sibling).start()
    for k in range(2):
        for h in range(2):
            o = chip_at(h, k, 1)
            arrived(h, o, False)
            move(h, o, LAST, place.last(h)).start()
            move(h, o, SIB, place.sibling).start()
    for far in range(2):
        for k in range(2):
            for h in range(2):
                dx, dy = (1, k) if h == 0 else (k, 1)
                o = (z + far * (1 - 2 * z)) * 4 + place.chip_at(dx, dy, 0)
                arrived(h, o, False)
                move(h, o, SIB, place.sibling).start()
    for copy in locals_[2:]:
        copy.wait()

    @pl.loop(1, 2 * group)
    def _(i):
        q = (me + i) % (2 * group)
        pltpu.make_async_remote_copy(
            src_ref=heads_w.at[0], dst_ref=weights.at[q, :, pl.ds(0, wide)], send_sem=w_send.at[q],
            recv_sem=w_recv.at[q], device_id=(q,), device_id_type=MESH).wait_recv()
        pltpu.make_async_remote_copy(
            src_ref=coeff.at[0], dst_ref=coeff_out.at[q], send_sem=c_send.at[q],
            recv_sem=c_recv.at[q], device_id=(q,), device_id_type=MESH).wait_recv()

        @pl.when(q != other)
        def _():
            pltpu.make_async_remote_copy(
                src_ref=pair.at[0], dst_ref=weights.at[q, :, pl.ds(wide, 128)], send_sem=pair_send.at[2, 0],
                recv_sem=pair_recv.at[q], device_id=(other,), device_id_type=MESH).wait_recv()

    @pl.loop(0, group // 2)
    def _(o):
        for h in range(2):
            arrived(h, o, True)

    span = 2 * rows
    seq = group * rows
    up_own = weights[pl.ds(2 * p, 2), :, pl.ds(wide, 128)].reshape(2 * depth, 128)
    up_own = pltpu.roll(up_own.astype(f32), 64, 1).astype(bf)
    flip = (((1,), (1,)), ((), ()))
    scale = 1.0 / math.sqrt(128)

    @pl.loop(0, group // 2)
    def _(b):
        at = pl.ds(pl.multiple_of(b * span, span), span)
        x = held[pl.ds(2 * b, 2)].reshape(span, -1)
        acc = jnp.dot(x, weights[...].reshape(2 * group * depth, wide + 128), preferred_element_type=f32)
        inner = acc[:, wide:].astype(bf)
        inner_out[at] = inner
        owner = lax.broadcasted_iota(jnp.int32, inner.shape, 1) // rank

        def projected(j):
            low = jnp.where(owner == j, inner.astype(f32), 0.0).astype(bf)
            return acc[:, j * 128 : (j + 1) * 128] + lax.dot_general(low, up_own, flip, preferred_element_type=f32)

        for j, (gain, raw, rot) in enumerate(((query_gain, query_proj, query_out), (key_gain, key_proj, key_out))):
            value = projected(j)
            raw[at] = value
            unit = value * lax.rsqrt(jnp.mean(value * value, axis=-1, keepdims=True) + epsilon) * gain[...]
            rot[at] = (unit * cosine[at] + pltpu.roll(unit, 64, 1) * sine[at]).astype(bf)
        value_out[at] = projected(2).astype(bf)

    def to_token(q):
        return pltpu.make_async_remote_copy(
            src_ref=mixed_buf.at[q], dst_ref=mixed.at[:, pl.ds(p * 128, 128)], send_sem=m_send.at[q],
            recv_sem=m_recv.at[p], device_id=(base + q,), device_id_type=MESH)

    keep = pltpu.make_async_copy(mixed_buf.at[p], mixed.at[:, pl.ds(p * 128, 128)], m_local)

    @pl.loop(0, group // 2)
    def _(b):
        at = pl.ds(pl.multiple_of(b * span, span), span)
        scores = lax.dot_general(query_out[at], key_out[...], flip, preferred_element_type=f32)
        weight = jnp.where(q_seg[at] == k_seg[...], jnp.exp2(scores * (scale * math.log2(math.e))), 0.0)
        total = jnp.sum(weight, axis=-1, keepdims=True)
        value = jnp.dot(weight.astype(bf), value_out[...], preferred_element_type=f32) / total
        mixed_buf[pl.ds(2 * b, 2)] = value.astype(bf).reshape(2, rows, 128)
        for side in range(2):
            q = 2 * b + side

            @pl.when(q != p)
            def _():
                to_token(q).start()

            @pl.when(q == p)
            def _():
                keep.start()

    keep.wait()

    @pl.loop(1, group)
    def _(i):
        q = (p + i) % group
        pltpu.make_async_remote_copy(
            src_ref=mixed_buf.at[q], dst_ref=mixed.at[:, pl.ds(q * 128, 128)], send_sem=m_send.at[q],
            recv_sem=m_recv.at[q], device_id=(base + q,), device_id_type=MESH).wait_recv()

    pair_other.wait_send()
    for h in range(2):
        move(h, chip, FIRST, place.first(h)).wait_send()
        for far in range(2):
            for k in range(2):
                o = chip_at(h, k, far)
                if far == 0:
                    move(h, o, ALONG, across_z).wait_send()
                move(h, o, LAST, place.last(h)).wait_send()
                move(h, o, SIB, place.sibling).wait_send()
                dx, dy = (1, k) if h == 0 else (k, 1)
                o = (z + far * (1 - 2 * z)) * 4 + place.chip_at(dx, dy, 0)
                move(h, o, SIB, place.sibling).wait_send()

    @pl.loop(1, group)
    def _(i):
        q = (p + i) % group
        pair_over(q, 0).wait_send()
        pair_over(q, 1).wait_send()
        to_token(q).wait_send()

    @pl.loop(1, 2 * group)
    def _(i):
        q = (me + i) % (2 * group)
        to_heads(q).wait_send()
        to_expert(q).wait_send()


def front(normed, heads_w, pair, coeff, cosine, sine, query_gain, key_gain, q_seg, k_seg, rank):
    rows, width = normed.shape
    group, depth = heads_w.shape[0], heads_w.shape[1]
    devices, seq = 2 * group, rows * group
    bf, f32 = jnp.bfloat16, jnp.float32
    dma = pltpu.SemaphoreType.DMA
    vmem, anywhere = pl.BlockSpec(memory_space=pltpu.VMEM), pl.BlockSpec(memory_space=pl.ANY)
    head = jax.ShapeDtypeStruct((seq, 128), bf)
    raw = jax.ShapeDtypeStruct((seq, 128), f32)
    return pl.pallas_call(
        functools.partial(front_kernel, rows, rank),
        out_shape=(
            jax.ShapeDtypeStruct((rows, width), bf),
            jax.ShapeDtypeStruct((devices, depth, 512), bf),
            head, head, head, raw, raw, head,
            jax.ShapeDtypeStruct((devices, 1, rows), f32),
        ),
        in_specs=[anywhere] * 4 + [vmem] * 6,
        out_specs=(vmem,) * 9,
        scratch_shapes=[
            pltpu.VMEM((group, rows, width), bf),
            pltpu.VMEM((group, rows, 128), bf),
            dma((4,)), dma((4, 2, group // 2)), dma((2, 2, group // 2)),
            dma((devices,)), dma((devices,)), dma((3, group)), dma((devices,)),
            dma((devices,)), dma((devices,)), dma((group,)), dma((group,)), dma,
        ],
        compiler_params=pltpu.CompilerParams(has_side_effects=True, vmem_limit_bytes=56 << 20),
        name="front",
    )(normed, heads_w, pair, coeff, cosine, sine, query_gain, key_gain, q_seg, k_seg)


def back_kernel(rows, rank, grad_mixed, weights, query, key, value, query_proj, key_proj, inner, cosine, sine,
                query_gain, key_gain, q_seg, k_seg, out, up_terms,
                grads, key_t, grad_key, grad_value, heads, result, sib, cross_out, cross_in, z_out, z_in, first_out, first_in,
                a_send, a_recv, a_local, sib_send, sib_recv, cross_send, cross_recv, z_send, z_recv, first_send, first_recv):
    place = Place()
    f32, bf = jnp.float32, jnp.bfloat16
    me, core = place.me, place.core
    group = grads.shape[0]
    depth = weights.shape[1]
    base, p = me // group * group, me % group
    half, span, seq = rows // 2, 2 * rows, rows * group
    width = out.shape[1] - 128
    z = place.z % 2
    across_z = me + 8 - 16 * z
    flip = (((1,), (1,)), ((), ()))
    tall = (((0,), (0,)), ((), ()))
    scale = 1.0 / math.sqrt(128)

    def to_head(q):
        return pltpu.make_async_remote_copy(
            src_ref=grad_mixed.at[:, pl.ds(q * 128, 128)], dst_ref=grads.at[p], send_sem=a_send.at[q],
            recv_sem=a_recv.at[p], device_id=(base + q,), device_id_type=MESH)

    def from_token(q):
        return pltpu.make_async_remote_copy(
            src_ref=grad_mixed.at[:, pl.ds(q * 128, 128)], dst_ref=grads.at[q], send_sem=a_send.at[q],
            recv_sem=a_recv.at[q], device_id=(base + q,), device_id_type=MESH)

    keep = pltpu.make_async_copy(grad_mixed.at[:, pl.ds(p * 128, 128)], grads.at[p], a_local)
    keep.start()

    @pl.loop(1, group)
    def _(i):
        to_head((p + i) % group).start()

    key_t[...] = key[...].astype(f32).T.astype(bf)
    grad_key[...] = jnp.zeros_like(grad_key)
    grad_value[...] = jnp.zeros_like(grad_value)
    keep.wait()

    def raw_grad(raw, gain, turned, at):
        back = turned * cosine[at] - pltpu.roll(turned, 64, 1) * sine[at]
        rows_ = raw[at]
        inverse = lax.rsqrt(jnp.mean(rows_ * rows_, axis=-1, keepdims=True) + epsilon)
        unit = rows_ * inverse
        scaled = back * gain[...]
        return (inverse * (scaled - unit * jnp.mean(scaled * unit, axis=-1, keepdims=True))).astype(bf)

    @pl.loop(0, group // 2)
    def _(b):
        at = pl.ds(pl.multiple_of(b * span, span), span)
        for side in range(2):
            q = 2 * b + side

            @pl.when(q != p)
            def _():
                from_token(q).wait_recv()

        ours = query[at]
        grad = grads[pl.ds(2 * b, 2)].reshape(span, 128)
        scores = lax.dot_general(key[...], ours, flip, preferred_element_type=f32)
        weight = jnp.where(k_seg[...] == q_seg[:, at], jnp.exp2(scores * (scale * math.log2(math.e))), 0.0)
        probs = weight * (1.0 / jnp.sum(weight, axis=0, keepdims=True))
        grad_probs = lax.dot_general(value[...], grad, flip, preferred_element_type=f32)
        mean = jnp.sum(probs * grad_probs, axis=0, keepdims=True)
        grad_scores = (probs * (grad_probs - mean)).astype(bf)
        grad_key[...] += jnp.dot(grad_scores, ours, preferred_element_type=f32)
        grad_value[...] += jnp.dot(probs.astype(bf), grad, preferred_element_type=f32)
        grad_query = jnp.dot(key_t[...], grad_scores, preferred_element_type=f32).T * scale
        heads[at, 0:128] = raw_grad(query_proj, query_gain, grad_query, at)

    up_own = weights[pl.ds(2 * p, 2), :, 384:512].reshape(2 * depth, 128)
    up_own = pltpu.roll(up_own.astype(f32), 64, 1).astype(bf)

    @pl.loop(0, group // 2)
    def _(b):
        at = pl.ds(pl.multiple_of(b * span, span), span)
        heads[at, 128:256] = raw_grad(key_proj, key_gain, grad_key[at] * scale, at)
        heads[at, 256:384] = grad_value[at].astype(bf)

    def to_sibling(c):
        return pltpu.make_async_remote_copy(
            src_ref=result.at[c, 1 - core], dst_ref=sib.at[c], send_sem=sib_send.at[c],
            recv_sem=sib_recv.at[c], device_id=(place.sibling,), device_id_type=MESH)

    def across(h, k, far):
        return pltpu.make_async_remote_copy(
            src_ref=cross_out.at[h, k, far], dst_ref=cross_in.at[h, k, far], send_sem=cross_send.at[h, k, far],
            recv_sem=cross_recv.at[h, k, far], device_id=(place.last(h),), device_id_type=MESH)

    def along(h, k):
        return pltpu.make_async_remote_copy(
            src_ref=z_out.at[h, k], dst_ref=z_in.at[h, k], send_sem=z_send.at[h, k],
            recv_sem=z_recv.at[h, k], device_id=(across_z,), device_id_type=MESH)

    def first(h):
        return pltpu.make_async_remote_copy(
            src_ref=first_out.at[h], dst_ref=first_in.at[h], send_sem=first_send.at[h],
            recv_sem=first_recv.at[h], device_id=(place.first(h),), device_id_type=MESH)

    def both(c, h):
        part = pl.ds(h * half, half)
        return result[c, core, part].astype(f32) + sib[c, part].astype(f32)

    def pair_sum(c):
        far, dx, dy = 1 - c // 4, c % 2, c // 2 % 2
        to_sibling(c).wait_recv()
        for h, away, k in ((0, dx, dy), (1, dy, dx)):
            @pl.when(away == 1)
            def _():
                cross_out[h, k, far] = both(c, h).astype(bf)
                across(h, k, far).start()

    @pl.loop(0, group // 2 + 1)
    def _(c):
        @pl.when(c < group // 2)
        def _():
            far, dx, dy = 1 - c // 4, c % 2, c // 2 % 2
            o = (z + far * (1 - 2 * z)) * 4 + place.chip_at(dx, dy, 0)
            mine = heads[pl.ds(pl.multiple_of(o * span, span), span), :]
            matrix = weights[...].reshape(2 * group * depth, 512)[:, 0:384]
            part = lax.dot_general(mine, matrix, flip, preferred_element_type=f32)
            result[c, :, :, 0:width] = part.astype(bf).reshape(2, rows, width)
            low = jnp.zeros((span, 128), f32)
            owner = lax.broadcasted_iota(jnp.int32, low.shape, 1) // rank
            for j in range(3):
                term = jnp.dot(mine[:, j * 128 : (j + 1) * 128], up_own, preferred_element_type=f32)
                low = jnp.where(owner == j, term, low)
            result[c, :, :, width:] = low.astype(bf).reshape(2, rows, 128)
            to_sibling(c).start()

        @pl.when(c >= 1)
        def _():
            pair_sum(c - 1)

    @pl.loop(0, group // 2)
    def _(e):
        far, k, h = 1 - e // 4, e // 2 % 2, e % 2
        c = (1 - far) * 4 + k * (2 - h)
        across(h, k, far).wait_recv()
        total = both(c, h) + cross_in[h, k, far].astype(f32)

        @pl.when(far == 1)
        def _():
            z_out[h, k] = total.astype(bf)
            along(h, k).start()

        @pl.when(far == 0)
        def _():
            along(h, k).wait_recv()
            whole = total + z_in[h, k].astype(f32)

            @pl.when(k == 1)
            def _():
                first_out[h] = whole.astype(bf)
                first(h).start()

            @pl.when(k == 0)
            def _():
                out[pl.ds(h * half, half)] = whole

    owner = lax.broadcasted_iota(jnp.int32, (128, 128), 0) // rank
    up = jnp.zeros((128, 128), f32)
    for j in range(3):
        term = lax.dot_general(inner[...], heads[:, j * 128 : (j + 1) * 128], tall, preferred_element_type=f32)
        up = jnp.where(owner == j, term, up)
    up_terms[...] = up
    for h in range(2):
        first(h).wait_recv()
        out[pl.ds(h * half, half)] += first_in[h].astype(f32)

    @pl.loop(1, group)
    def _(i):
        to_head((p + i) % group).wait_send()

    @pl.loop(0, group // 2)
    def _(c):
        to_sibling(c).wait_send()
        across(c % 2, c // 2 % 2, c // 4).wait_send()

        @pl.when(c < 4)
        def _():
            along(c % 2, c // 2).wait_send()

        @pl.when(c < 2)
        def _():
            first(c).wait_send()


def back(grad_mixed, weights, query, key, value, query_proj, key_proj, inner, cosine, sine,
         query_gain, key_gain, q_seg, k_seg, rank):
    rows, width = grad_mixed.shape
    seq = query.shape[0]
    group = seq // rows
    bf, f32 = jnp.bfloat16, jnp.float32
    dma = pltpu.SemaphoreType.DMA
    vmem = pl.BlockSpec(memory_space=pltpu.VMEM)
    wide = width + 128
    piece = (rows // 2, wide)
    return pl.pallas_call(
        functools.partial(back_kernel, rows, rank),
        out_shape=(jax.ShapeDtypeStruct((rows, wide), f32), jax.ShapeDtypeStruct((128, 128), f32)),
        in_specs=[vmem] * 14,
        out_specs=(vmem, vmem),
        scratch_shapes=[
            pltpu.VMEM((group, rows, 128), bf),
            pltpu.VMEM((128, seq), bf),
            pltpu.VMEM((seq, 128), f32),
            pltpu.VMEM((seq, 128), f32),
            pltpu.VMEM((seq, 384), bf),
            pltpu.VMEM((group // 2, 2, rows, wide), bf),
            pltpu.VMEM((group // 2, rows, wide), bf),
            pltpu.VMEM((2, 2, 2) + piece, bf),
            pltpu.VMEM((2, 2, 2) + piece, bf),
            pltpu.VMEM((2, 2) + piece, bf),
            pltpu.VMEM((2, 2) + piece, bf),
            pltpu.VMEM((2,) + piece, bf),
            pltpu.VMEM((2,) + piece, bf),
            dma((group,)), dma((group,)), dma, dma((group // 2,)), dma((group // 2,)),
            dma((2, 2, 2)), dma((2, 2, 2)), dma((2, 2)), dma((2, 2)), dma((2,)), dma((2,)),
        ],
        compiler_params=pltpu.CompilerParams(has_side_effects=True, vmem_limit_bytes=60 << 20),
        name="back",
    )(grad_mixed, weights, query, key, value, query_proj, key_proj, inner, cosine, sine,
      query_gain, key_gain, q_seg, k_seg)


def heads_plan(
    tokens,
    segments,
    routes,
    gates,
    sequence_adapter_index,
    attention_norm_gain,
    query_norm_gain,
    key_norm_gain,
    query_weight,
    key_weight,
    value_weight,
    output_weight,
    adapter_down_factors,
    adapter_up_factors,
    expert_norm_gain,
    expert_gate_weight,
    expert_up_weight,
    expert_down_weight,
    output_gradient,
):
    bf, f32 = jnp.bfloat16, jnp.float32
    devices = lax.axis_size("fsdp")
    rows_dev, width = tokens.shape
    group = SEQ_LEN // rows_dev
    seqs = segments.shape[0]
    experts = devices // 2
    rank = adapter_down_factors.shape[3]
    slots = 4 * rank
    own_rows = query_weight.shape[0]
    device = lax.axis_index("fsdp")
    place = device % group
    sequence = device // group
    groups = [list(range(s * group, (s + 1) * group)) for s in range(seqs)]
    scale = 1.0 / math.sqrt(HEAD_DIM)
    segment_row = pick(segments, sequence)
    cosine, sine = rope_tables(jnp.arange(SEQ_LEN, dtype=jnp.int32).astype(f32))
    cosine, sine = cosine[:, 0], sine[:, 0]
    attn_scale = attention_norm_gain.astype(f32)
    query_scale = query_norm_gain.astype(f32)
    key_scale = key_norm_gain.astype(f32)
    ffn_scale = expert_norm_gain.astype(f32)

    downs = jnp.take(adapter_down_factors, sequence_adapter_index, axis=0)
    ups = jnp.take(adapter_up_factors, sequence_adapter_index, axis=0)
    pair = jnp.concatenate(
        [
            downs.transpose(0, 2, 1, 3).reshape(seqs, own_rows, slots),
            ups.transpose(0, 3, 1, 2).reshape(seqs, own_rows, slots),
        ],
        axis=2,
    )
    heads_w = jnp.concatenate(
        [
            weight.reshape(own_rows, group, HEAD_DIM)
            for weight in (query_weight, key_weight, value_weight)
        ],
        axis=2,
    ).transpose(1, 0, 2)
    chosen = (routes[:, :, None] == jnp.arange(experts, dtype=jnp.int32)).astype(f32)
    coeff = jnp.sum(gates[:, :, None] * chosen, axis=1)
    rows = tokens.astype(f32)
    normed = rms_scale(rows, attn_scale).astype(bf)
    output_matrix = lax.all_gather(output_weight, "fsdp", axis=0, tiled=True)
    turns = (jnp.concatenate([cosine, cosine], axis=1), jnp.concatenate([-sine, sine], axis=1))
    head_gains = (query_scale.reshape(1, HEAD_DIM), key_scale.reshape(1, HEAD_DIM))
    tall, flat = segment_row.reshape(SEQ_LEN, 1), segment_row.reshape(1, SEQ_LEN)
    mixed, head_weights, query, key, value, query_proj, key_proj, inner_all, coeff_own = front(
        normed, heads_w, pair, coeff.T.reshape(experts, 1, rows_dev), *turns, *head_gains, tall, flat, rank
    )
    weights = head_weights.reshape(width, 4 * HEAD_DIM)
    down_own = weights[:, 3 * HEAD_DIM : 3 * HEAD_DIM + slots]
    up_own = weights[:, 3 * HEAD_DIM + slots :]
    down_out = down_own[:, 3 * rank :]
    up_out = up_own[:, 3 * rank :]
    out_inner = matmul(mixed, down_out).astype(bf)
    middle = rows + matmul(mixed, output_matrix) + matmul(out_inner, up_out.T)
    normed_ffn = rms_scale(middle, ffn_scale).astype(bf)

    slab_gate = expert_gate_weight[0]
    slab_up = expert_up_weight[0]
    slab_down = expert_down_weight[0]
    upstream_all = lax.all_gather(output_gradient, "fsdp", axis=0, tiled=True)
    coeff_own = coeff_own.reshape(devices, rows_dev, 1)
    part, keep_gate, keep_up = experts_forward(normed_ffn, slab_gate, slab_up, slab_down, coeff_own)
    moe, grad_slab = scatter_beside_backward(
        part,
        upstream_all.reshape(devices, rows_dev, width),
        keep_gate,
        keep_up,
        slab_gate,
        slab_up,
        slab_down,
        coeff_own,
    )
    grad_ffn = scatter_all(grad_slab)
    output = (middle + moe).astype(bf)
    upstream = output_gradient.astype(f32)
    grad_middle = upstream + rms_back(middle, ffn_scale, grad_ffn)
    grad_attn = grad_middle.astype(bf)

    grad_inner_out = matmul(grad_attn, up_out).astype(bf)
    grad_mixed = matmul(grad_attn, output_matrix.T) + matmul(grad_inner_out, down_out.T)
    grad_mixed = grad_mixed.astype(bf)
    up_out_terms = matmul(out_inner.T, grad_attn)
    down_out_terms = matmul(grad_inner_out.T, mixed)

    sums, up_head_terms = back(
        grad_mixed, head_weights, query, key, value, query_proj, key_proj, inner_all,
        *turns, *head_gains, flat, tall, rank,
    )
    up_head_terms = up_head_terms[: 3 * rank]
    grad_sum, grad_inner = sums[:, :width], sums[:, width : width + 3 * rank].astype(bf)
    grad_normed = grad_sum + matmul(grad_inner, down_own[:, : 3 * rank].T)
    grad_tokens = (grad_middle + rms_back(rows, attn_scale, grad_normed)).astype(bf)

    down_terms = jnp.concatenate([matmul(grad_inner.T, normed), down_out_terms], axis=0)
    head_slot = (jnp.arange(group) == place).astype(f32)
    up_terms = jnp.concatenate(
        [
            (up_head_terms[:, None, :] * head_slot[None, :, None]).reshape(3 * rank, width),
            up_out_terms,
        ],
        axis=0,
    )
    terms = jnp.concatenate([down_terms, up_terms], axis=0)
    terms = lax.all_to_all(
        terms.reshape(2 * slots, devices, own_rows).transpose(1, 0, 2),
        "fsdp",
        split_axis=0,
        concat_axis=0,
        tiled=True,
    )
    terms = jnp.sum(terms.reshape(seqs, group, 2 * slots, own_rows), axis=1)
    selected = (
        jnp.arange(ADAPTER_COUNT, dtype=jnp.int32)[:, None] == sequence_adapter_index[None, :]
    ).astype(f32)
    spread = jnp.sum(selected[:, :, None, None] * terms[None], axis=1)
    spread = spread.reshape(ADAPTER_COUNT, 2, 4, rank, own_rows)
    grad_down = spread[:, 0].transpose(0, 1, 3, 2)
    grad_up = spread[:, 1]
    return (output, grad_tokens, grad_down, grad_up)


def solution(mesh):
    plan = heads_plan if mesh.shape["fsdp"] == LEVELS * 8 else shards
    in_specs = (
        P("fsdp", None),
        P(),
        P("fsdp", None),
        P("fsdp", None),
        P(),
        P(),
        P(),
        P(),
        P("fsdp", None),
        P("fsdp", None),
        P("fsdp", None),
        P("fsdp", None),
        P(None, None, "fsdp", None),
        P(None, None, None, "fsdp"),
        P(),
        P("fsdp", None, None),
        P("fsdp", None, None),
        P("fsdp", None, None),
        P("fsdp", None),
    )
    out_specs = (
        P("fsdp", None),
        P("fsdp", None),
        P(None, None, "fsdp", None),
        P(None, None, None, "fsdp"),
    )
    return jax.shard_map(plan, mesh=mesh, in_specs=in_specs, out_specs=out_specs, check_vma=False)
```

```python
import functools
import math

import jax
import jax.numpy as jnp
import numpy as np
from jax import lax
from jax.experimental import pallas as pl
from jax.experimental.pallas import tpu as pltpu
from jax.sharding import PartitionSpec as P

HEAD_DIM = 128
TOPK = 8
ADAPTER_COUNT = 8
SEQ_LEN = 2048


epsilon = 1e-06
rope_base = 50000.0


def from_partner(value, axis, distance):
    mask = 2**distance
    pairs = [(source, source ^ mask) for source in range(lax.axis_size(axis))]
    return lax.ppermute(value, axis, pairs)


def matmul(left, right):
    return jnp.dot(left, right, preferred_element_type=jnp.float32)


def rms_scale(rows, gain):
    return rows * lax.rsqrt(jnp.mean(rows * rows, axis=-1, keepdims=True) + epsilon) * gain


def rms_back(rows, gain, upstream):
    inverse = lax.rsqrt(jnp.mean(rows * rows, axis=-1, keepdims=True) + epsilon)
    unit = rows * inverse
    scaled = upstream * gain
    return inverse * (scaled - unit * jnp.mean(scaled * unit, axis=-1, keepdims=True))


def rope_tables(positions):
    half = HEAD_DIM // 2
    frequency = rope_base ** (-(jnp.arange(half, dtype=jnp.float32) * 2.0 / HEAD_DIM))
    angle = positions[:, None] * frequency[None, :]
    return (jnp.cos(angle)[:, None, :], jnp.sin(angle)[:, None, :])


def rotate(rows, cosine, sine):
    half = rows.shape[-1] // 2
    first = rows[..., :half]
    second = rows[..., half:]
    return jnp.concatenate(
        [first * cosine - second * sine, second * cosine + first * sine], axis=-1
    )


def rotate_back(upstream, cosine, sine):
    half = upstream.shape[-1] // 2
    first = upstream[..., :half]
    second = upstream[..., half:]
    return jnp.concatenate(
        [first * cosine + second * sine, second * cosine - first * sine], axis=-1
    )


def pick(table, index):
    return lax.dynamic_index_in_dim(table, index, 0, keepdims=False)


def shards(
    tokens,
    segments,
    routes,
    gates,
    sequence_adapter_index,
    attention_norm_gain,
    query_norm_gain,
    key_norm_gain,
    query_weight,
    key_weight,
    value_weight,
    output_weight,
    adapter_down_factors,
    adapter_up_factors,
    expert_norm_gain,
    expert_gate_weight,
    expert_up_weight,
    expert_down_weight,
    output_gradient,
):
    rows_dev = tokens.shape[0]
    width = tokens.shape[1]
    heads = width // HEAD_DIM
    group = SEQ_LEN // rows_dev
    level_list = group.bit_length() - 1
    device = lax.axis_index("fsdp")
    place = device % group
    sequence = device // group
    segment_row = pick(segments, sequence)
    own_segment = lax.dynamic_slice_in_dim(segment_row, place * rows_dev, rows_dev)
    adapter = pick(sequence_adapter_index, sequence)
    scale = 1.0 / math.sqrt(HEAD_DIM)
    cosine, sine = rope_tables(
        (place * rows_dev + jnp.arange(rows_dev, dtype=jnp.int32)).astype(jnp.float32)
    )
    attn_scale = attention_norm_gain.astype(jnp.float32)
    query_scale = query_norm_gain.astype(jnp.float32)
    key_scale = key_norm_gain.astype(jnp.float32)
    ffn_scale = expert_norm_gain.astype(jnp.float32)
    gathered = (
        lax.all_gather(query_weight, "fsdp", axis=0, tiled=True),
        lax.all_gather(key_weight, "fsdp", axis=0, tiled=True),
        lax.all_gather(value_weight, "fsdp", axis=0, tiled=True),
        lax.all_gather(output_weight, "fsdp", axis=0, tiled=True),
        lax.all_gather(adapter_down_factors, "fsdp", axis=2, tiled=True),
        lax.all_gather(adapter_up_factors, "fsdp", axis=3, tiled=True),
    )
    matrices = gathered[:4]
    down_own = pick(gathered[4], adapter)
    up_own = pick(gathered[5], adapter)

    def project(inputs, index):
        inner = matmul(inputs, down_own[index]).astype(jnp.bfloat16)
        return (matmul(inputs, matrices[index]) + matmul(inner, up_own[index]), inner)

    rows = tokens.astype(jnp.float32)
    normed = rms_scale(rows, attn_scale).astype(jnp.bfloat16)
    query_proj, query_inner = project(normed, 0)
    key_proj, key_inner = project(normed, 1)
    value_proj, value_inner = project(normed, 2)
    query_heads = query_proj.reshape(rows_dev, heads, HEAD_DIM)
    key_heads = key_proj.reshape(rows_dev, heads, HEAD_DIM)
    query_rot = rotate(rms_scale(query_heads, query_scale), cosine, sine).astype(jnp.bfloat16)
    key_rot = (
        rotate(rms_scale(key_heads, key_scale), cosine, sine)
        .astype(jnp.bfloat16)
        .reshape(rows_dev, width)
    )
    value_low = value_proj.astype(jnp.bfloat16)
    held_keys = key_rot
    held_values = value_low
    for level in range(level_list):
        other_keys, other_values = from_partner((held_keys, held_values), "fsdp", level)
        upper_bit = place // (1 << level) % 2 == 1
        held_keys = jnp.where(
            upper_bit,
            jnp.concatenate([other_keys, held_keys], axis=0),
            jnp.concatenate([held_keys, other_keys], axis=0),
        )
        held_values = jnp.where(
            upper_bit,
            jnp.concatenate([other_values, held_values], axis=0),
            jnp.concatenate([held_values, other_values], axis=0),
        )
    keys_all = held_keys.reshape(SEQ_LEN, heads, HEAD_DIM)
    values_all = held_values.reshape(SEQ_LEN, heads, HEAD_DIM)
    allowed = (own_segment[:, None] == segment_row[None, :])[None]

    def masked_scores():
        raw = (
            jnp.einsum("thd,shd->hts", query_rot, keys_all, preferred_element_type=jnp.float32)
            * scale
        )
        return jnp.where(allowed, raw, -1e30)

    scores = masked_scores()
    maximum = jnp.max(scores, axis=-1, keepdims=True)
    weights = jnp.exp(scores - maximum)
    total = jnp.sum(weights, axis=-1, keepdims=True)
    probs = weights / total
    log_total = maximum + jnp.log(total)
    mixed = jnp.einsum(
        "hts,shd->thd", probs.astype(jnp.bfloat16), values_all, preferred_element_type=jnp.float32
    )
    mixed = mixed.astype(jnp.bfloat16).reshape(rows_dev, width)
    attn_proj, out_inner = project(mixed, 3)
    middle = rows + attn_proj
    normed_ffn = rms_scale(middle, ffn_scale).astype(jnp.bfloat16)
    experts = lax.axis_size("fsdp") // 2
    capacity = 2 * rows_dev * TOPK // experts
    flat_routes = routes.reshape(-1)
    onehot = (flat_routes[:, None] == jnp.arange(experts, dtype=jnp.int32)[None, :]).astype(
        jnp.int32
    )
    slot = jnp.sum(jnp.cumsum(onehot, axis=0) * onehot, axis=1) - 1
    target = flat_routes * capacity + slot

    def spread(entries):
        buffer = jnp.zeros((experts * capacity, width), jnp.bfloat16).at[target].set(entries)
        buffer = buffer.reshape(experts, 1, capacity, width)
        return jnp.broadcast_to(buffer, (experts, 2, capacity, width)).reshape(
            2 * experts, capacity, width
        )

    def collect(returned):
        halves = returned.reshape(experts, 2, capacity, width).astype(jnp.float32)
        summed = (halves[:, 0] + halves[:, 1]).reshape(experts * capacity, width)
        return summed[target].reshape(rows_dev, TOPK, width)

    slab_gate = expert_gate_weight[0]
    slab_up = expert_up_weight[0]
    slab_down = expert_down_weight[0]
    dispatched = lax.all_to_all(
        spread(jnp.repeat(normed_ffn, TOPK, axis=0)),
        "fsdp",
        split_axis=0,
        concat_axis=0,
        tiled=True,
    )
    gate_part = jnp.einsum("scd,dh->sch", dispatched, slab_gate, preferred_element_type=jnp.float32)
    up_part = jnp.einsum("scd,dh->sch", dispatched, slab_up, preferred_element_type=jnp.float32)
    hidden = (jax.nn.silu(gate_part) * up_part).astype(jnp.bfloat16)
    produced = jnp.einsum(
        "sch,hd->scd", hidden, slab_down, preferred_element_type=jnp.float32
    ).astype(jnp.bfloat16)
    returned = lax.all_to_all(produced, "fsdp", split_axis=0, concat_axis=0, tiled=True)
    moe = jnp.sum(gates[:, :, None] * collect(returned), axis=1)
    output = (middle + moe).astype(jnp.bfloat16)
    upstream = output_gradient.astype(jnp.float32)
    grad_parts = (
        (gates[:, :, None] * upstream[:, None, :])
        .astype(jnp.bfloat16)
        .reshape(rows_dev * TOPK, width)
    )
    grad_sent = lax.all_to_all(spread(grad_parts), "fsdp", split_axis=0, concat_axis=0, tiled=True)
    grad_hidden = jnp.einsum(
        "scd,hd->sch", grad_sent, slab_down, preferred_element_type=jnp.float32
    )
    sigmoid = jax.nn.sigmoid(gate_part)
    grad_gate = (grad_hidden * up_part * sigmoid * (1.0 + gate_part * (1.0 - sigmoid))).astype(
        jnp.bfloat16
    )
    grad_up = (grad_hidden * gate_part * sigmoid).astype(jnp.bfloat16)
    grad_inputs = jnp.einsum(
        "sch,dh->scd", grad_gate, slab_gate, preferred_element_type=jnp.float32
    )
    grad_inputs = (
        grad_inputs
        + jnp.einsum("sch,dh->scd", grad_up, slab_up, preferred_element_type=jnp.float32)
    ).astype(jnp.bfloat16)
    grad_back = lax.all_to_all(grad_inputs, "fsdp", split_axis=0, concat_axis=0, tiled=True)
    grad_ffn = jnp.sum(collect(grad_back), axis=1)
    grad_middle = upstream + rms_back(middle, ffn_scale, grad_ffn)
    grad_attn = grad_middle.astype(jnp.bfloat16)
    regathered = (
        lax.all_gather(query_weight, "fsdp", axis=0, tiled=True),
        lax.all_gather(key_weight, "fsdp", axis=0, tiled=True),
        lax.all_gather(value_weight, "fsdp", axis=0, tiled=True),
        lax.all_gather(output_weight, "fsdp", axis=0, tiled=True),
        lax.all_gather(adapter_down_factors, "fsdp", axis=2, tiled=True),
        lax.all_gather(adapter_up_factors, "fsdp", axis=3, tiled=True),
    )
    back_matrices = regathered[:4]
    back_down = pick(regathered[4], adapter)
    back_up = pick(regathered[5], adapter)

    def project_back(inputs, inner, upstream_low, index):
        grad_inner = matmul(upstream_low, back_up[index].T).astype(jnp.bfloat16)
        grad_input = matmul(upstream_low, back_matrices[index].T) + matmul(
            grad_inner, back_down[index].T
        )
        return (grad_input, matmul(inputs.T, grad_inner), matmul(inner.T, upstream_low))

    grad_mixed_full, down_output, up_output = project_back(mixed, out_inner, grad_attn, 3)
    grad_mixed = grad_mixed_full.astype(jnp.bfloat16).reshape(rows_dev, heads, HEAD_DIM)
    probs = jnp.exp(masked_scores() - log_total)
    grad_probs = jnp.einsum(
        "thd,shd->hts", grad_mixed, values_all, preferred_element_type=jnp.float32
    )
    grad_scores = (
        probs * (grad_probs - jnp.sum(probs * grad_probs, axis=-1, keepdims=True))
    ).astype(jnp.bfloat16)
    grad_query = (
        jnp.einsum("hts,shd->thd", grad_scores, keys_all, preferred_element_type=jnp.float32)
        * scale
    )
    grad_keys_part = (
        jnp.einsum("hts,thd->shd", grad_scores, query_rot, preferred_element_type=jnp.float32)
        * scale
    )
    grad_keys_part = grad_keys_part.reshape(group, rows_dev, width)
    grad_values_part = jnp.einsum(
        "hts,thd->shd", probs.astype(jnp.bfloat16), grad_mixed, preferred_element_type=jnp.float32
    )
    grad_values_part = grad_values_part.reshape(group, rows_dev, width)
    for level in reversed(range(level_list)):
        size_half = 1 << level
        upper_bit = place // size_half % 2 == 1
        keep_keys = jnp.where(upper_bit, grad_keys_part[size_half:], grad_keys_part[:size_half])
        send_keys = jnp.where(upper_bit, grad_keys_part[:size_half], grad_keys_part[size_half:])
        keep_values = jnp.where(
            upper_bit, grad_values_part[size_half:], grad_values_part[:size_half]
        )
        send_values = jnp.where(
            upper_bit, grad_values_part[:size_half], grad_values_part[size_half:]
        )
        got_keys, got_values = (
            from_partner(send_keys.astype(jnp.bfloat16), "fsdp", level).astype(send_keys.dtype),
            from_partner(send_values.astype(jnp.bfloat16), "fsdp", level).astype(send_values.dtype),
        )
        grad_keys_part = keep_keys + got_keys
        grad_values_part = keep_values + got_values
    grad_keys = grad_keys_part[0]
    grad_values = grad_values_part[0]
    grad_value_proj = grad_values.astype(jnp.bfloat16)
    grad_key_proj = rms_back(
        key_heads,
        key_scale,
        rotate_back(grad_keys.reshape(rows_dev, heads, HEAD_DIM), cosine, sine),
    )
    grad_key_proj = grad_key_proj.reshape(rows_dev, width).astype(jnp.bfloat16)
    grad_query_proj = rms_back(query_heads, query_scale, rotate_back(grad_query, cosine, sine))
    grad_query_proj = grad_query_proj.reshape(rows_dev, width).astype(jnp.bfloat16)
    grad_from_query, down_query, up_query = project_back(normed, query_inner, grad_query_proj, 0)
    grad_from_key, down_key, up_key = project_back(normed, key_inner, grad_key_proj, 1)
    grad_from_value, down_value, up_value = project_back(normed, value_inner, grad_value_proj, 2)
    grad_normed = grad_from_query + grad_from_key + grad_from_value
    grad_tokens = (grad_middle + rms_back(rows, attn_scale, grad_normed)).astype(jnp.bfloat16)
    down_terms = jnp.stack([down_query, down_key, down_value, down_output])
    up_terms = jnp.stack([up_query, up_key, up_value, up_output])
    selected = (jnp.arange(ADAPTER_COUNT, dtype=jnp.int32) == adapter).astype(jnp.float32)[
        :, None, None, None
    ]
    grad_down, grad_up = (
        lax.psum_scatter(selected * down_terms[None], "fsdp", scatter_dimension=2, tiled=True),
        lax.psum_scatter(selected * up_terms[None], "fsdp", scatter_dimension=3, tiled=True),
    )
    return (output, grad_tokens, grad_down, grad_up)


epsilon = 1e-06
MESH = pl.DeviceIdType.MESH
LEVELS = 4
CHIPS = 16


class Place:
    def __init__(self):
        self.me = me = lax.axis_index("fsdp")
        self.core = me % 2
        self.x = me // 2 % 2
        self.y = me // 4 % 2
        self.z = me // 8
        self.sibling = me + 1 - 2 * self.core
        self.across_x = me + 2 - 4 * self.x
        self.across_y = me + 4 - 8 * self.y

    def level(self, i):
        upper = self.z // 2
        inner = self.z * (1 - upper) + (3 - self.z) * upper
        turn = i + inner * (1 - 2 * i) * (1 - i // 2)
        return turn + upper * (3 - 2 * turn)

    def chip(self, half, side, level):
        flip = 1 - 2 * side
        y = self.y + (1 - half) * side * (1 - 2 * self.y)
        x = self.x + half * side * (1 - 2 * self.x)
        return level * 4 + y * 2 + x

    def chip_at(self, dx, dy, level):
        y = self.y + dy * (1 - 2 * self.y)
        x = self.x + dx * (1 - 2 * self.x)
        return level * 4 + y * 2 + x

    def first(self, half):
        return self.across_y * (1 - half) + self.across_x * half

    def last(self, half):
        return self.across_x * (1 - half) + self.across_y * half


def scatter_kernel(rows, work, source, out, own, sib, cross_out, cross_in, z_out, z_in, first_out, first_in, total,
                   own_sem, sib_send, sib_recv, cross_send, cross_recv, z_send, z_recv, first_send, first_recv):
    place = Place()
    half_rows = rows // 2
    f32, bf = jnp.float32, jnp.bfloat16

    def local(o):
        return pltpu.make_async_copy(source.at[2 * o + place.core], own.at[o], own_sem.at[o])

    def to_sibling(o):
        return pltpu.make_async_remote_copy(
            src_ref=source.at[2 * o + 1 - place.core], dst_ref=sib.at[o], send_sem=sib_send.at[o],
            recv_sem=sib_recv.at[o], device_id=(place.sibling,), device_id_type=MESH)

    def across(h, k, level):
        return pltpu.make_async_remote_copy(
            src_ref=cross_out.at[h, k, level], dst_ref=cross_in.at[h, k, level], send_sem=cross_send.at[h, k, level],
            recv_sem=cross_recv.at[h, k, level], device_id=(place.last(h),), device_id_type=MESH)

    def along(h, k, level, up):
        return pltpu.make_async_remote_copy(
            src_ref=z_out.at[h, k, level], dst_ref=z_in.at[up, h, k, level], send_sem=z_send.at[h, k, level],
            recv_sem=z_recv.at[up, h, k, level], device_id=(place.me - 8 + 16 * up,), device_id_type=MESH)

    def first(h):
        return pltpu.make_async_remote_copy(
            src_ref=first_out.at[h], dst_ref=first_in.at[h], send_sem=first_send.at[h],
            recv_sem=first_recv.at[h], device_id=(place.first(h),), device_id_type=MESH)

    def both(o, h):
        part = pl.ds(h * half_rows, half_rows)
        return own[o, part].astype(f32) + sib[o, part].astype(f32)

    @pl.loop(0, CHIPS)
    def _(q):
        o = place.chip_at(q % 2, q // 2 % 2, place.level(3 - q // 4))
        local(o).start()
        to_sibling(o).start()

    @pl.loop(0, CHIPS + 4)
    def _(t):
        @pl.when(t < CHIPS)
        def _():
            level = place.level(3 - t // 4)
            dx, dy = t % 2, t // 2 % 2
            o = place.chip_at(dx, dy, level)
            local(o).wait()
            to_sibling(o).wait_recv()
            for h, away, k in ((0, dx, dy), (1, dy, dx)):
                @pl.when(away == 1)
                def _():
                    cross_out[h, k, level] = both(o, h).astype(bf)
                    across(h, k, level).start()

        @pl.when(t >= 4)
        def _():
            i, h, k = (t - 4) // 4, t % 2, t // 2 % 2
            level = place.level(3 - i)
            o = place.chip(h, k, level)
            across(h, k, level).wait_recv()
            total[...] = both(o, h) + cross_in[h, k, level].astype(f32)

            @pl.when((level >= place.z) & (place.z > 0))
            def _():
                along(h, k, level, 1).wait_recv()
                total[...] += z_in[1, h, k, level].astype(f32)

            @pl.when((level <= place.z) & (place.z < LEVELS - 1))
            def _():
                along(h, k, level, 0).wait_recv()
                total[...] += z_in[0, h, k, level].astype(f32)

            @pl.when(level > place.z)
            def _():
                z_out[h, k, level] = total[...].astype(bf)
                along(h, k, level, 1).start()

            @pl.when(level < place.z)
            def _():
                z_out[h, k, level] = total[...].astype(bf)
                along(h, k, level, 0).start()

            @pl.when((level == place.z) & (k == 1))
            def _():
                first_out[h] = total[...].astype(bf)
                first(h).start()

            @pl.when((level == place.z) & (k == 0))
            def _():
                out[pl.ds(h * half_rows, half_rows)] = total[...]

        if work is not None:
            work(t)

    for h in range(2):
        first(h).wait_recv()
        out[pl.ds(h * half_rows, half_rows)] += first_in[h].astype(f32)

    @pl.loop(0, CHIPS)
    def _(q):
        o = place.chip_at(q % 2, q // 2 % 2, place.level(3 - q // 4))
        to_sibling(o).wait_send()
        h, k, level = q % 2, q // 2 % 2, q // 4
        across(h, k, level).wait_send()

        @pl.when(level > place.z)
        def _():
            along(h, k, level, 1).wait_send()

        @pl.when(level < place.z)
        def _():
            along(h, k, level, 0).wait_send()

    for h in range(2):
        first(h).wait_send()


def scatter_scratch(rows, width):
    bf = jnp.bfloat16
    dma = pltpu.SemaphoreType.DMA
    piece = (rows // 2, width)
    return [
        pltpu.VMEM((CHIPS, rows, width), bf),
        pltpu.VMEM((CHIPS, rows, width), bf),
        pltpu.VMEM((2, 2, LEVELS) + piece, bf),
        pltpu.VMEM((2, 2, LEVELS) + piece, bf),
        pltpu.VMEM((2, 2, LEVELS) + piece, bf),
        pltpu.VMEM((2, 2, 2, LEVELS) + piece, bf),
        pltpu.VMEM((2,) + piece, bf),
        pltpu.VMEM((2,) + piece, bf),
        pltpu.VMEM(piece, jnp.float32),
        dma((CHIPS,)), dma((CHIPS,)), dma((CHIPS,)),
        dma((2, 2, LEVELS)), dma((2, 2, LEVELS)),
        dma((2, 2, LEVELS)), dma((2, 2, 2, LEVELS)),
        dma((2,)), dma((2,)),
    ]


def scatter_all(partial):
    devices, rows, width = partial.shape
    return pl.pallas_call(
        functools.partial(scatter_kernel, rows, None),
        out_shape=jax.ShapeDtypeStruct((rows, width), jnp.float32),
        in_specs=[pl.BlockSpec(memory_space=pl.ANY)],
        out_specs=pl.BlockSpec(memory_space=pltpu.VMEM),
        scratch_shapes=scatter_scratch(rows, width),
        compiler_params=pltpu.CompilerParams(has_side_effects=True, vmem_limit_bytes=48 << 20),
        name="scatter_all",
    )(partial)


def experts_kernel(rows, x_ref, up_ref, gate_w, up_w, down_w, coeff, out, part_out, gathered,
                   block, part_buf, result, sib, cross_out, cross_in, hold, z_in, first_out, first_in, total,
                   local_sem, load_sem, part_sem, send, recv, sib_send, sib_recv, cross_send, cross_recv,
                   z_send, z_recv, first_send, first_recv):
    place = Place()
    half = rows // 2
    f32, bf = jnp.float32, jnp.bfloat16
    flip = (((1,), (1,)), ((), ()))
    me, core = place.me, place.core
    upper = place.z // 2
    inner = place.z * (1 - upper) + (3 - place.z) * upper
    UP, DOWN, LAST, SIB, FIRST = range(5)

    def move(n, h, o, kind, target):
        piece = gathered.at[2 * o + core, h, n]
        return pltpu.make_async_remote_copy(
            src_ref=piece, dst_ref=piece, send_sem=send.at[kind, n, h, o],
            recv_sem=recv.at[1 if kind == SIB else 0, n, h, o], device_id=(target,), device_id_type=MESH)

    def arrived(n, h, o, sibling):
        piece = gathered.at[2 * o + (1 - core if sibling else core), h, n]
        pltpu.make_async_remote_copy(
            src_ref=piece, dst_ref=piece, send_sem=send.at[SIB, n, h, o],
            recv_sem=recv.at[1 if sibling else 0, n, h, o], device_id=(place.sibling,), device_id_type=MESH).wait_recv()

    def column(n, h, o, level, act):
        @pl.when((level <= place.z) & (place.z < LEVELS - 1))
        def _():
            act(move(n, h, o, UP, me + 8))

        @pl.when((level >= place.z) & (place.z > 0))
        def _():
            act(move(n, h, o, DOWN, me - 8))

    def spread(n, h, o, level, act):
        column(n, h, o, level, act)
        act(move(n, h, o, LAST, place.last(h)))
        act(move(n, h, o, SIB, place.sibling))

    def to_sibling(u):
        slot = u % 2
        return pltpu.make_async_remote_copy(
            src_ref=result.at[slot, 1 - core], dst_ref=sib.at[slot], send_sem=sib_send.at[slot],
            recv_sem=sib_recv.at[slot], device_id=(place.sibling,), device_id_type=MESH)

    def across(h, k, i):
        return pltpu.make_async_remote_copy(
            src_ref=cross_out.at[h, k, i % 2], dst_ref=cross_in.at[h, k, i], send_sem=cross_send.at[h, k, i],
            recv_sem=cross_recv.at[h, k, i], device_id=(place.last(h),), device_id_type=MESH)

    def along(h, k, level, up, slot):
        return pltpu.make_async_remote_copy(
            src_ref=hold.at[h, k, level], dst_ref=z_in.at[h, k, slot], send_sem=z_send.at[h, k, level],
            recv_sem=z_recv.at[h, k, slot], device_id=(me - 8 + 16 * up,), device_id_type=MESH)

    def first(h):
        return pltpu.make_async_remote_copy(
            src_ref=first_out.at[h], dst_ref=first_in.at[h], send_sem=first_send.at[h],
            recv_sem=first_recv.at[h], device_id=(place.first(h),), device_id_type=MESH)

    def down_slot(level):
        ends = 1 - jnp.minimum(jnp.abs(level - (place.z - 1)), 1)
        return level + ends * (LEVELS - level)

    def order(u):
        return u % 2, u // 2 % 2, place.level(u // 4)

    start = lambda copy: copy.start()
    done = lambda copy: copy.wait_send()
    mine = me // 2
    own = [
        pltpu.make_async_copy(ref.at[pl.ds(h * half, half)], gathered.at[me, h, n], local_sem.at[n, h])
        for n, ref in enumerate((x_ref, up_ref)) for h in range(2)
    ]
    for copy in own:
        copy.start()
    for copy in own:
        copy.wait()
    pieces = [(n, h) for n in range(2) for h in range(2)]
    for n, h in pieces:
        column(n, h, mine, place.z, start)
        move(n, h, mine, FIRST, place.first(h)).start()
    for n, h in pieces:
        move(n, h, mine, LAST, place.last(h)).start()
        move(n, h, mine, SIB, place.sibling).start()
    for n, h in pieces:
        o = place.chip(h, 1, place.z)
        arrived(n, h, o, False)
        spread(n, h, o, place.z, start)

    def cross_arrivals(q):
        dx, dy, level = order(q)
        o = place.chip_at(dx, dy, level)
        for h, away in ((0, dx), (1, dy)):
            @pl.when(away == 1)
            def _():
                for n in range(2):
                    arrived(n, h, o, False)
                    move(n, h, o, SIB, place.sibling).start()

    def keep_part(u):
        dx, dy, level = order(u)
        o = place.chip_at(dx, dy, level)
        return pltpu.make_async_copy(part_buf.at[u % 2], part_out.at[o], part_sem.at[u % 2])

    def compute(u):
        dx, dy, level = order(u)
        o = place.chip_at(dx, dy, level)
        for n, h in pieces:
            arrived(n, h, o, True)
        load = pltpu.make_async_copy(gathered.at[pl.ds(2 * o, 2)], block, load_sem)
        load.start()

        @pl.when(u >= 2)
        def _():
            to_sibling(u - 2).wait_send()

        load.wait()
        slot = u % 2
        c = coeff[pl.ds(2 * o, 2)].reshape(2 * rows, 1)
        x = block[:, :, 0].reshape(2 * rows, -1)
        gate = jnp.dot(x, gate_w[...], preferred_element_type=f32)
        up = jnp.dot(x, up_w[...], preferred_element_type=f32)
        sig = jax.nn.sigmoid(gate)
        silu = gate * sig
        hidden = (silu * up).astype(bf)
        part = (c * jnp.dot(hidden, down_w[...], preferred_element_type=f32)).astype(bf)
        part = part.reshape(2, 2, half, -1)
        result[slot, 0, 1] = part[0]
        result[slot, 1, 1] = part[1]
        upstream = (c * block[:, :, 1].reshape(2 * rows, -1).astype(f32)).astype(bf)
        grad_hidden = lax.dot_general(upstream, down_w[...], flip, preferred_element_type=f32)
        grad_gate = (grad_hidden * up * sig * (1.0 + gate * (1.0 - sig))).astype(bf)
        grad_up = (grad_hidden * silu).astype(bf)
        grad = lax.dot_general(grad_gate, gate_w[...], flip, preferred_element_type=f32)
        grad += lax.dot_general(grad_up, up_w[...], flip, preferred_element_type=f32)
        grad = grad.astype(bf).reshape(2, 2, half, -1)
        result[slot, 0, 0] = grad[0]
        result[slot, 1, 0] = grad[1]

    def pair_sum(u):
        dx, dy, level = order(u)
        i, slot = u // 4, u % 2
        to_sibling(u).wait_recv()

        def pair(n, h):
            return (result[slot, core, n, h].astype(f32) + sib[slot, n, h].astype(f32)).astype(bf)

        for h, away, k in ((0, dx, dy), (1, dy, dx)):
            @pl.when(away == 1)
            def _():
                @pl.when(i >= 2)
                def _():
                    across(h, k, i - 2).wait_send()

                cross_out[h, k, i % 2] = pair(0, h)
                across(h, k, i).start()

            @pl.when(away == 0)
            def _():
                hold[h, k, level] = pair(0, h)

        @pl.when(u >= 2)
        def _():
            keep_part(u - 2).wait()

        for h in range(2):
            part_buf[slot, h] = pair(1, h)
        keep_part(u).start()

    def column_event(e):
        late = e // 8
        i_end = e // 4
        j_end = e % 4
        i_mid = (e // 4) * (1 - late) + (2 + e % 2) * late
        j_mid = (e % 4) * (1 - late) + ((e - 8) // 2) * late
        turn_end = i_end + 1 - 4 * (i_end // 3)
        level_end = turn_end + upper * (3 - 2 * turn_end)
        turn_mid = 2 - i_mid + (i_mid // 2) * 3 - (i_mid // 3) * 2
        level_mid = turn_mid + upper * (3 - 2 * turn_mid)
        j = j_end + inner * (j_mid - j_end)
        level = level_end + inner * (level_mid - level_end)
        return j % 2, j // 2, level

    def column_sum(e):
        h, k, level = column_event(e)
        turn = level + upper * (3 - 2 * level)
        i = turn + inner * (1 - 2 * turn) * (1 - jnp.minimum(turn // 2, 1))
        across(h, k, i).wait_recv()
        total[...] = hold[h, k, level].astype(f32) + cross_in[h, k, i].astype(f32)

        @pl.when((level >= place.z) & (place.z > 0))
        def _():
            along(h, k, level, 1, level).wait_recv()
            total[...] += z_in[h, k, level].astype(f32)

        @pl.when((level < place.z) & (place.z < LEVELS - 1))
        def _():
            along(h, k, level, 0, level).wait_recv()
            total[...] += z_in[h, k, level].astype(f32)

        @pl.when((level == place.z) & (place.z < LEVELS - 1))
        def _():
            along(h, k, level, 0, LEVELS).wait_recv()
            total[...] += z_in[h, k, LEVELS].astype(f32)

        @pl.when(level > place.z)
        def _():
            hold[h, k, level] = total[...].astype(bf)
            along(h, k, level, 1, level).start()

        @pl.when(level < place.z)
        def _():
            hold[h, k, level] = total[...].astype(bf)
            along(h, k, level, 0, down_slot(level)).start()

        @pl.when((level == place.z) & (k == 1))
        def _():
            first_out[h] = total[...].astype(bf)
            first(h).start()

        @pl.when((level == place.z) & (k == 0))
        def _():
            out[h] = total[...]

    @pl.loop(0, 2 * CHIPS - 1)
    def _(u):
        @pl.when((u >= 1) & (u < CHIPS - 3))
        def _():
            t = u - 1
            level, h, k = place.level(1 + t // 4), t % 2, t // 2 % 2
            o = place.chip(h, k, level)
            for n in range(2):
                arrived(n, h, o, False)
                spread(n, h, o, level, start)

        @pl.when(u + 1 < CHIPS)
        def _():
            cross_arrivals(u + 1)

        @pl.when(u < CHIPS)
        def _():
            compute(u)

        @pl.when((u >= 1) & (u <= CHIPS))
        def _():
            pair_sum(u - 1)

        @pl.when(u < CHIPS)
        def _():
            to_sibling(u).start()

        e = u - 7 - 8 * inner

        @pl.when((e >= 0) & (e < CHIPS))
        def _():
            column_sum(e)

    for h in range(2):
        first(h).wait_recv()
        out[h] += first_in[h].astype(f32)

    for n, h in pieces:
        move(n, h, mine, FIRST, place.first(h)).wait_send()
        spread(n, h, mine, place.z, done)
        spread(n, h, place.chip(h, 1, place.z), place.z, done)
    for h in range(2):
        first(h).wait_send()
    for u in (CHIPS - 2, CHIPS - 1):
        to_sibling(u).wait_send()
        keep_part(u).wait()

    @pl.loop(0, CHIPS)
    def _(t):
        h, k = t % 2, t // 2 % 2

        @pl.when(t < CHIPS - 4)
        def _():
            level = place.level(1 + t // 4)
            for n in range(2):
                spread(n, h, place.chip(h, k, level), level, done)

        dx, dy, level = order(t)
        o = place.chip_at(dx, dy, level)
        for side, away in ((0, dx), (1, dy)):
            @pl.when(away == 1)
            def _():
                for n in range(2):
                    move(n, side, o, SIB, place.sibling).wait_send()

        @pl.when(t >= 8)
        def _():
            across(h, k, t // 4).wait_send()

        level = t // 4

        @pl.when(level > place.z)
        def _():
            along(h, k, level, 1, level).wait_send()

        @pl.when(level < place.z)
        def _():
            along(h, k, level, 0, down_slot(level)).wait_send()


def experts_pass(x, upstream, gate_w, up_w, down_w, coeff):
    rows, width = x.shape
    devices = coeff.shape[0]
    half = rows // 2
    bf, f32 = jnp.bfloat16, jnp.float32
    dma = pltpu.SemaphoreType.DMA
    vmem, anywhere = pl.BlockSpec(memory_space=pltpu.VMEM), pl.BlockSpec(memory_space=pl.ANY)
    piece = (half, width)
    grad, part, _ = pl.pallas_call(
        functools.partial(experts_kernel, rows),
        out_shape=(
            jax.ShapeDtypeStruct((2,) + piece, f32),
            jax.ShapeDtypeStruct((CHIPS, 2) + piece, bf),
            jax.ShapeDtypeStruct((devices, 2, 2) + piece, bf),
        ),
        in_specs=[anywhere, anywhere, vmem, vmem, vmem, vmem],
        out_specs=(vmem, anywhere, anywhere),
        scratch_shapes=[
            pltpu.VMEM((2, 2, 2) + piece, bf),
            pltpu.VMEM((2, 2) + piece, bf),
            pltpu.VMEM((2, 2, 2, 2) + piece, bf),
            pltpu.VMEM((2, 2, 2) + piece, bf),
            pltpu.VMEM((2, 2, 2) + piece, bf),
            pltpu.VMEM((2, 2, LEVELS) + piece, bf),
            pltpu.VMEM((2, 2, LEVELS) + piece, bf),
            pltpu.VMEM((2, 2, LEVELS + 1) + piece, bf),
            pltpu.VMEM((2,) + piece, bf),
            pltpu.VMEM((2,) + piece, bf),
            pltpu.VMEM(piece, f32),
            dma((2, 2)), dma, dma((2,)), dma((5, 2, 2, CHIPS)), dma((2, 2, 2, CHIPS)), dma((2,)), dma((2,)),
            dma((2, 2, LEVELS)), dma((2, 2, LEVELS)),
            dma((2, 2, LEVELS)), dma((2, 2, LEVELS + 1)), dma((2,)), dma((2,)),
        ],
        compiler_params=pltpu.CompilerParams(has_side_effects=True, vmem_limit_bytes=56 << 20),
        name="experts",
    )(x, upstream, gate_w, up_w, down_w, coeff)
    return grad.reshape(rows, width), part


def front_kernel(rows, rank, picked, tokens, rows_gain, heads_w, downs, ups, routes, gates, out_w, near, far_turn,
                 query_gain, key_gain, ffn_gain, q_seg, k_seg,
                 middle, normed_ffn, normed, mixed, out_inner, weights, query_out, key_out, value_out,
                 query_proj, key_proj, inner_out, coeff_out, cosine, sine, out_all,
                 held, mixed_buf, pair, coeff, wo,
                 local_sem, send, recv, w_send, w_recv, pair_send, pair_recv, c_send, c_recv, m_send, m_recv, m_local,
                 g_send, g_recv, keep_sem):
    place = Place()
    f32, bf = jnp.float32, jnp.bfloat16
    me, core = place.me, place.core
    group = held.shape[0]
    base, p = me // group * group, me % group
    other = (me + group) % (2 * group)
    other_base = group - base
    half = rows // 2
    depth = weights.shape[1]
    wide = 3 * 128
    z = place.z % 2
    across_z = me + 8 - 16 * z
    chip = p // 2

    FIRST, ALONG, LAST, SIB = range(4)

    def chip_at(h, k, far):
        flip = place.chip(h, k, 0)
        zz = z + far * (1 - 2 * z)
        return zz * 4 + flip

    def move(h, o, kind, target):
        piece = held.at[2 * o + core, pl.ds(h * half, half)]
        return pltpu.make_async_remote_copy(
            src_ref=piece, dst_ref=piece, send_sem=send.at[kind, h, o],
            recv_sem=recv.at[1 if kind == SIB else 0, h, o], device_id=(target,), device_id_type=MESH)

    def arrived(h, o, sibling):
        piece = held.at[2 * o + (1 - core if sibling else core), pl.ds(h * half, half)]
        pltpu.make_async_remote_copy(
            src_ref=piece, dst_ref=piece, send_sem=send.at[SIB, h, o],
            recv_sem=recv.at[1 if sibling else 0, h, o], device_id=(place.sibling,), device_id_type=MESH).wait_recv()

    def to_heads(q):
        return pltpu.make_async_remote_copy(
            src_ref=heads_w.at[q % group], dst_ref=weights.at[me, :, pl.ds(0, wide)], send_sem=w_send.at[q],
            recv_sem=w_recv.at[me], device_id=(q,), device_id_type=MESH)

    def to_expert(q):
        return pltpu.make_async_remote_copy(
            src_ref=coeff.at[q // 2], dst_ref=coeff_out.at[me], send_sem=c_send.at[q],
            recv_sem=c_recv.at[me], device_id=(q,), device_id_type=MESH)

    def pair_over(q, side):
        row = (me + side * group) % (2 * group)
        piece = weights.at[row, :, pl.ds(wide, 128)]
        return pltpu.make_async_remote_copy(
            src_ref=piece, dst_ref=piece, send_sem=pair_send.at[side, q],
            recv_sem=pair_recv.at[row], device_id=(base + q,), device_id_type=MESH)

    pair_other = pltpu.make_async_remote_copy(
        src_ref=pair.at[other // group], dst_ref=weights.at[me, :, pl.ds(wide, 128)], send_sem=pair_send.at[2, 0],
        recv_sem=pair_recv.at[me], device_id=(other,), device_id_type=MESH)
    UP, DOWN, G_LAST, G_SIB, G_FIRST = range(5)

    def g_move(h, o, kind, target):
        piece = wo.at[2 * o + core, h]
        return pltpu.make_async_remote_copy(
            src_ref=piece, dst_ref=piece, send_sem=g_send.at[kind, h, o],
            recv_sem=g_recv.at[1 if kind == G_SIB else 0, h, o], device_id=(target,), device_id_type=MESH)

    def g_arrived(h, o, sibling):
        piece = wo.at[2 * o + (1 - core if sibling else core), h]
        pltpu.make_async_remote_copy(
            src_ref=piece, dst_ref=piece, send_sem=g_send.at[G_SIB, h, o],
            recv_sem=g_recv.at[1 if sibling else 0, h, o], device_id=(place.sibling,), device_id_type=MESH).wait_recv()

    def g_column(h, o, level, act):
        @pl.when((level <= place.z) & (place.z < LEVELS - 1))
        def _():
            act(g_move(h, o, UP, me + 8))

        @pl.when((level >= place.z) & (place.z > 0))
        def _():
            act(g_move(h, o, DOWN, me - 8))

    def g_spread(h, o, level, act):
        g_column(h, o, level, act)
        act(g_move(h, o, G_LAST, place.last(h)))
        act(g_move(h, o, G_SIB, place.sibling))

    def g_level(t):
        level, h, k = place.level(1 + t // 4), t % 2, t // 2 % 2
        o = place.chip(h, k, level)
        g_arrived(h, o, False)
        g_spread(h, o, level, start)

    def g_cross(q):
        dx, dy = q % 2, q // 2 % 2
        o = place.chip_at(dx, dy, place.level(q // 4))
        for h, away in ((0, dx), (1, dy)):
            @pl.when(away == 1)
            def _():
                g_arrived(h, o, False)
                g_move(h, o, G_SIB, place.sibling).start()

    start = lambda copy: copy.start()
    done = lambda copy: copy.wait_send()
    own_chip = me // 2
    own_copies = [
        pltpu.make_async_copy(heads_w.at[p], weights.at[me, :, pl.ds(0, wide)], local_sem.at[0]),
        pltpu.make_async_copy(out_w.at[pl.ds(0, depth // 2)], wo.at[me, 0], local_sem.at[1]),
        pltpu.make_async_copy(out_w.at[pl.ds(depth // 2, depth // 2)], wo.at[me, 1], local_sem.at[2]),
    ]
    for copy in own_copies:
        copy.start()
    ours = tokens[...].astype(f32)
    low = (ours * lax.rsqrt(jnp.mean(ours * ours, axis=-1, keepdims=True) + epsilon) * rows_gain[...]).astype(bf)
    held[p] = low
    normed[...] = low
    for h in range(2):
        move(h, chip, FIRST, place.first(h)).start()
        move(h, chip, ALONG, across_z).start()
    for h in range(2):
        move(h, chip, LAST, place.last(h)).start()
        move(h, chip, SIB, place.sibling).start()

    for s in range(2):
        down, up = downs[picked[s]].astype(f32), ups[picked[s]].astype(f32)
        down = jnp.concatenate([down[j] for j in range(4)], axis=1)
        up = jnp.concatenate([up[j] for j in range(4)], axis=0).T
        pair[s] = jnp.concatenate([down, up], axis=1).astype(bf)
    weights[me, :, wide:] = pair[me // group]
    pair_other.start()

    @pl.loop(0, group)
    def _(i):
        to_heads(other_base + (p + i) % group).start()

    lane = lax.broadcasted_iota(jnp.int32, (rows, 128), 1)
    gate = jnp.zeros((rows, 128), f32)
    for k in range(routes.shape[1]):
        gate += jnp.where(lane == routes[:, k : k + 1], gates[:, k : k + 1], 0.0)
    gate = gate.T
    for e in range(coeff.shape[0]):
        coeff[e] = gate[e : e + 1]
    coeff_out[me] = coeff[me // 2]

    @pl.loop(1, group)
    def _(i):
        pair_over((p + i) % group, 0).start()
        to_heads(base + (p + i) % group).start()

    @pl.loop(1, 2 * group)
    def _(i):
        to_expert((me + i) % (2 * group)).start()

    for copy in own_copies[1:]:
        copy.wait()
    for h in range(2):
        g_column(h, own_chip, place.z, start)
        g_move(h, own_chip, G_FIRST, place.first(h)).start()
    for h in range(2):
        g_move(h, own_chip, G_LAST, place.last(h)).start()
        g_move(h, own_chip, G_SIB, place.sibling).start()

    pltpu.make_async_remote_copy(
        src_ref=pair.at[0], dst_ref=weights.at[other, :, pl.ds(wide, 128)], send_sem=pair_send.at[2, 0],
        recv_sem=pair_recv.at[other], device_id=(other,), device_id_type=MESH).wait_recv()

    @pl.loop(1, group)
    def _(i):
        pair_over((p + i) % group, 1).start()

    for h in range(2):
        o = chip_at(h, 1, 0)
        arrived(h, o, False)
        move(h, o, ALONG, across_z).start()
        move(h, o, LAST, place.last(h)).start()
        move(h, o, SIB, place.sibling).start()
    for k in range(2):
        for h in range(2):
            o = chip_at(h, k, 1)
            arrived(h, o, False)
            move(h, o, LAST, place.last(h)).start()
            move(h, o, SIB, place.sibling).start()
    for h in range(2):
        o = place.chip(h, 1, place.z)
        g_arrived(h, o, False)
        g_spread(h, o, place.z, start)

    @pl.loop(0, group)
    def _(i):
        at = pl.ds(pl.multiple_of(i * rows, rows), rows)
        c, s = far_turn[0, pl.ds(i, 1)], far_turn[1, pl.ds(i, 1)]
        cosine[at] = c * near[0] - s * near[1]
        turn = s * near[0] + c * near[1]
        sine[at] = jnp.where(lane < 64, -turn, turn)

    for far in range(2):
        for k in range(2):
            for h in range(2):
                dx, dy = (1, k) if h == 0 else (k, 1)
                o = (z + far * (1 - 2 * z)) * 4 + place.chip_at(dx, dy, 0)
                arrived(h, o, False)
                move(h, o, SIB, place.sibling).start()
    own_copies[0].wait()

    @pl.loop(0, 4)
    def _(t):
        g_level(t)


    @pl.loop(1, 2 * group)
    def _(i):
        q = (me + i) % (2 * group)
        pltpu.make_async_remote_copy(
            src_ref=heads_w.at[0], dst_ref=weights.at[q, :, pl.ds(0, wide)], send_sem=w_send.at[q],
            recv_sem=w_recv.at[q], device_id=(q,), device_id_type=MESH).wait_recv()
        pltpu.make_async_remote_copy(
            src_ref=coeff.at[0], dst_ref=coeff_out.at[q], send_sem=c_send.at[q],
            recv_sem=c_recv.at[q], device_id=(q,), device_id_type=MESH).wait_recv()

        @pl.when(q != other)
        def _():
            pltpu.make_async_remote_copy(
                src_ref=pair.at[0], dst_ref=weights.at[q, :, pl.ds(wide, 128)], send_sem=pair_send.at[2, 0],
                recv_sem=pair_recv.at[q], device_id=(other,), device_id_type=MESH).wait_recv()

    @pl.loop(0, group // 2)
    def _(o):
        for h in range(2):
            arrived(h, o, True)

    @pl.loop(4, 8)
    def _(t):
        g_level(t)

    span = 2 * rows
    seq = group * rows
    up_own = weights[pl.ds(2 * p, 2), :, pl.ds(wide, 128)].reshape(2 * depth, 128)
    up_own = pltpu.roll(up_own.astype(f32), 64, 1).astype(bf)
    flip = (((1,), (1,)), ((), ()))
    scale = 1.0 / math.sqrt(128)

    @pl.loop(0, group // 2)
    def _(b):
        at = pl.ds(pl.multiple_of(b * span, span), span)
        x = held[pl.ds(2 * b, 2)].reshape(span, -1)
        acc = jnp.dot(x, weights[...].reshape(2 * group * depth, wide + 128), preferred_element_type=f32)
        inner = acc[:, wide:].astype(bf)
        inner_out[at] = inner
        owner = lax.broadcasted_iota(jnp.int32, inner.shape, 1) // rank

        def projected(j):
            low = jnp.where(owner == j, inner.astype(f32), 0.0).astype(bf)
            return acc[:, j * 128 : (j + 1) * 128] + lax.dot_general(low, up_own, flip, preferred_element_type=f32)

        for j, (gain, raw, rot) in enumerate(((query_gain, query_proj, query_out), (key_gain, key_proj, key_out))):
            value = projected(j)
            raw[at] = value
            unit = value * lax.rsqrt(jnp.mean(value * value, axis=-1, keepdims=True) + epsilon) * gain[...]
            rot[at] = (unit * cosine[at] + pltpu.roll(unit, 64, 1) * sine[at]).astype(bf)
        value_out[at] = projected(2).astype(bf)

        @pl.when(b % 2 == 0)
        def _():
            g_level(8 + b // 2)

    def to_token(q):
        return pltpu.make_async_remote_copy(
            src_ref=mixed_buf.at[q], dst_ref=mixed.at[:, pl.ds(p * 128, 128)], send_sem=m_send.at[q],
            recv_sem=m_recv.at[p], device_id=(base + q,), device_id_type=MESH)

    keep = pltpu.make_async_copy(mixed_buf.at[p], mixed.at[:, pl.ds(p * 128, 128)], m_local)

    @pl.loop(0, group // 2)
    def _(b):
        at = pl.ds(pl.multiple_of(b * span, span), span)
        scores = lax.dot_general(query_out[at], key_out[...], flip, preferred_element_type=f32)
        weight = jnp.where(q_seg[at] == k_seg[...], jnp.exp2(scores * (scale * math.log2(math.e))), 0.0)
        total = jnp.sum(weight, axis=-1, keepdims=True)
        value = jnp.dot(weight.astype(bf), value_out[...], preferred_element_type=f32) / total
        mixed_buf[pl.ds(2 * b, 2)] = value.astype(bf).reshape(2, rows, 128)
        for side in range(2):
            q = 2 * b + side

            @pl.when(q != p)
            def _():
                to_token(q).start()

            @pl.when(q == p)
            def _():
                keep.start()

        g_cross(2 * b)
        g_cross(2 * b + 1)

    keep.wait()

    @pl.loop(1, group)
    def _(i):
        q = (p + i) % group
        pltpu.make_async_remote_copy(
            src_ref=mixed_buf.at[q], dst_ref=mixed.at[:, pl.ds(q * 128, 128)], send_sem=m_send.at[q],
            recv_sem=m_recv.at[q], device_id=(base + q,), device_id_type=MESH).wait_recv()

    @pl.loop(0, CHIPS)
    def _(o):
        for h in range(2):
            g_arrived(h, o, True)

    keep_out = pltpu.make_async_copy(wo, out_all, keep_sem)
    keep_out.start()
    ours = mixed[...]
    matrix = weights[:, :, wide:].reshape(2 * group * depth, 128)
    lane = lax.broadcasted_iota(jnp.int32, (rows, 128), 1)
    inner = jnp.dot(ours, matrix, preferred_element_type=f32)
    inner = jnp.where(lane // rank == 3, inner, 0.0).astype(bf)
    out_inner[...] = inner
    shifted = pltpu.roll(inner.astype(f32), 64, 1).astype(bf)
    total = tokens[...].astype(f32) + jnp.dot(ours, wo[...].reshape(2 * group * depth, -1), preferred_element_type=f32)
    total = total + lax.dot_general(shifted, matrix, flip, preferred_element_type=f32)
    middle[...] = total
    unit = total * lax.rsqrt(jnp.mean(total * total, axis=-1, keepdims=True) + epsilon)
    normed_ffn[...] = (unit * ffn_gain[...]).astype(bf)

    keep_out.wait()
    for h in range(2):
        g_move(h, own_chip, G_FIRST, place.first(h)).wait_send()
        g_spread(h, own_chip, place.z, done)
        g_spread(h, place.chip(h, 1, place.z), place.z, done)

    @pl.loop(0, CHIPS)
    def _(t):
        @pl.when(t < CHIPS - 4)
        def _():
            level, h, k = place.level(1 + t // 4), t % 2, t // 2 % 2
            g_spread(h, place.chip(h, k, level), level, done)

        dx, dy = t % 2, t // 2 % 2
        o = place.chip_at(dx, dy, place.level(t // 4))
        for h, away in ((0, dx), (1, dy)):
            @pl.when(away == 1)
            def _():
                g_move(h, o, G_SIB, place.sibling).wait_send()

    pair_other.wait_send()
    for h in range(2):
        move(h, chip, FIRST, place.first(h)).wait_send()
        for far in range(2):
            for k in range(2):
                o = chip_at(h, k, far)
                if far == 0:
                    move(h, o, ALONG, across_z).wait_send()
                move(h, o, LAST, place.last(h)).wait_send()
                move(h, o, SIB, place.sibling).wait_send()
                dx, dy = (1, k) if h == 0 else (k, 1)
                o = (z + far * (1 - 2 * z)) * 4 + place.chip_at(dx, dy, 0)
                move(h, o, SIB, place.sibling).wait_send()

    @pl.loop(1, group)
    def _(i):
        q = (p + i) % group
        pair_over(q, 0).wait_send()
        pair_over(q, 1).wait_send()
        to_token(q).wait_send()

    @pl.loop(1, 2 * group)
    def _(i):
        q = (me + i) % (2 * group)
        to_heads(q).wait_send()
        to_expert(q).wait_send()


def turn_tables(rows, group):
    frequency = rope_base ** (-(np.arange(64, dtype=np.float32) * np.float32(2.0 / 128)))
    frequency = np.concatenate([frequency, frequency]).astype(np.float64)
    tables = []
    for positions in (np.arange(rows), np.arange(group) * rows):
        angle = positions[:, None] * frequency[None, :]
        tables.append(np.stack([np.cos(angle), np.sin(angle)]).astype(np.float32))
    return tables


def front(picked, tokens, rows_gain, heads_w, downs, ups, routes, gates, out_w, query_gain, key_gain, ffn_gain, q_seg, k_seg):
    rows, width = tokens.shape
    group, depth = heads_w.shape[0], heads_w.shape[1]
    rank = downs.shape[3]
    devices, seq = 2 * group, rows * group
    bf, f32 = jnp.bfloat16, jnp.float32
    dma = pltpu.SemaphoreType.DMA
    vmem, anywhere = pl.BlockSpec(memory_space=pltpu.VMEM), pl.BlockSpec(memory_space=pl.ANY)
    head = jax.ShapeDtypeStruct((seq, 128), bf)
    raw = jax.ShapeDtypeStruct((seq, 128), f32)
    mine = jax.ShapeDtypeStruct((rows, width), bf)
    near, far_turn = turn_tables(rows, group)
    return pl.pallas_call(
        functools.partial(front_kernel, rows, rank),
        out_shape=(
            jax.ShapeDtypeStruct((rows, width), f32), mine, mine, mine,
            jax.ShapeDtypeStruct((rows, 128), bf),
            jax.ShapeDtypeStruct((devices, depth, 512), bf),
            head, head, head, raw, raw, head,
            jax.ShapeDtypeStruct((devices, 1, rows), f32),
            raw, raw,
            jax.ShapeDtypeStruct((devices, 2, depth // 2, width), bf),
        ),
        in_specs=[pl.BlockSpec(memory_space=pltpu.SMEM), vmem, vmem, anywhere, vmem, vmem, vmem, vmem, anywhere]
        + [vmem] * 7,
        out_specs=(vmem,) * 15 + (anywhere,),
        scratch_shapes=[
            pltpu.VMEM((group, rows, width), bf),
            pltpu.VMEM((group, rows, 128), bf),
            pltpu.VMEM((2, depth, 128), bf),
            pltpu.VMEM((group, 1, rows), f32),
            pltpu.VMEM((devices, 2, depth // 2, width), bf),
            dma((3,)), dma((4, 2, group // 2)), dma((2, 2, group // 2)),
            dma((devices,)), dma((devices,)), dma((3, group)), dma((devices,)),
            dma((devices,)), dma((devices,)), dma((group,)), dma((group,)), dma,
            dma((5, 2, CHIPS)), dma((2, 2, CHIPS)), dma,
        ],
        compiler_params=pltpu.CompilerParams(has_side_effects=True, vmem_limit_bytes=60 << 20),
        name="front",
    )(picked, tokens, rows_gain, heads_w, downs, ups, routes, gates, out_w, jnp.asarray(near), jnp.asarray(far_turn),
      query_gain, key_gain, ffn_gain, q_seg, k_seg)


def back_kernel(rows, rank, grad_mixed, part, weights, query, key, value, query_proj, key_proj, inner, cosine, sine,
                query_gain, key_gain, q_seg, k_seg, rows_in, normed, rows_gain, grad_middle, middle, early,
                grad_rows, output, factors, out, up_terms, part_sum, late, early_in, late_in, owned,
                e_send, e_recv, l_send, l_recv, f_send, f_recv, t_local,
                grads, key_t, grad_key, grad_value, heads, result, sib, cross_out, cross_in, z_out, z_in, first_out, first_in,
                held, part_in, part_z, part_total, part_first_out, part_first_in,
                held_sem, pc_send, pc_recv, pz_send, pz_recv, pf_send, pf_recv,
                a_send, a_recv, a_local, sib_send, sib_recv, cross_send, cross_recv, z_send, z_recv, first_send, first_recv):
    place = Place()
    f32, bf = jnp.float32, jnp.bfloat16
    me, core = place.me, place.core
    group = grads.shape[0]
    depth = weights.shape[1]
    base, p = me // group * group, me % group
    half, span, seq = rows // 2, 2 * rows, rows * group
    width = out.shape[1] - 128
    z = place.z % 2
    across_z = me + 8 - 16 * z
    flip = (((1,), (1,)), ((), ()))
    tall = (((0,), (0,)), ((), ()))
    scale = 1.0 / math.sqrt(128)

    def keep_piece(h, k, level):
        return pltpu.make_async_copy(part.at[place.chip(h, k, level), h], held.at[h, k, level], held_sem.at[h, k, level])

    def part_across(h, k, level):
        dx, dy = (1, k) if h == 0 else (k, 1)
        return pltpu.make_async_remote_copy(
            src_ref=part.at[place.chip_at(dx, dy, level), h], dst_ref=part_in.at[h, k, level],
            send_sem=pc_send.at[h, k, level], recv_sem=pc_recv.at[h, k, level],
            device_id=(place.last(h),), device_id_type=MESH)

    def crossed(h, k, level):
        return pltpu.make_async_remote_copy(
            src_ref=held.at[h, k, level], dst_ref=part_in.at[h, k, level], send_sem=pc_send.at[h, k, level],
            recv_sem=pc_recv.at[h, k, level], device_id=(place.last(h),), device_id_type=MESH)

    def part_along(h, k, level, up, slot):
        return pltpu.make_async_remote_copy(
            src_ref=held.at[h, k, level], dst_ref=part_z.at[h, k, slot], send_sem=pz_send.at[h, k, level],
            recv_sem=pz_recv.at[h, k, slot], device_id=(me - 8 + 16 * up,), device_id_type=MESH)

    def part_first(h):
        return pltpu.make_async_remote_copy(
            src_ref=part_first_out.at[h], dst_ref=part_first_in.at[h], send_sem=pf_send.at[h],
            recv_sem=pf_recv.at[h], device_id=(place.first(h),), device_id_type=MESH)

    def down_slot(level):
        ends = 1 - jnp.minimum(jnp.abs(level - (place.z - 1)), 1)
        return level + ends * (LEVELS - level)

    def part_event(e):
        h, k, level = e % 2, e // 2 % 2, place.level(3 - e // 4)
        keep_piece(h, k, level).wait()
        crossed(h, k, level).wait_recv()
        total = held[h, k, level].astype(f32) + part_in[h, k, level].astype(f32)
        part_total[...] = total

        @pl.when((level >= place.z) & (place.z > 0))
        def _():
            part_along(h, k, level, 1, level).wait_recv()
            part_total[...] += part_z[h, k, level].astype(f32)

        @pl.when((level < place.z) & (place.z < LEVELS - 1))
        def _():
            part_along(h, k, level, 0, level).wait_recv()
            part_total[...] += part_z[h, k, level].astype(f32)

        @pl.when((level == place.z) & (place.z < LEVELS - 1))
        def _():
            part_along(h, k, level, 0, LEVELS).wait_recv()
            part_total[...] += part_z[h, k, LEVELS].astype(f32)

        @pl.when(level > place.z)
        def _():
            held[h, k, level] = part_total[...].astype(bf)
            part_along(h, k, level, 1, level).start()

        @pl.when(level < place.z)
        def _():
            held[h, k, level] = part_total[...].astype(bf)
            part_along(h, k, level, 0, down_slot(level)).start()

        @pl.when((level == place.z) & (k == 1))
        def _():
            part_first_out[h] = part_total[...].astype(bf)
            part_first(h).start()

        @pl.when((level == place.z) & (k == 0))
        def _():
            part_sum[h] = part_total[...]

    def to_head(q):
        return pltpu.make_async_remote_copy(
            src_ref=grad_mixed.at[:, pl.ds(q * 128, 128)], dst_ref=grads.at[p], send_sem=a_send.at[q],
            recv_sem=a_recv.at[p], device_id=(base + q,), device_id_type=MESH)

    def from_token(q):
        return pltpu.make_async_remote_copy(
            src_ref=grad_mixed.at[:, pl.ds(q * 128, 128)], dst_ref=grads.at[q], send_sem=a_send.at[q],
            recv_sem=a_recv.at[q], device_id=(base + q,), device_id_type=MESH)

    keep = pltpu.make_async_copy(grad_mixed.at[:, pl.ds(p * 128, 128)], grads.at[p], a_local)
    keep.start()

    def early_to(q, frm):
        return pltpu.make_async_remote_copy(
            src_ref=early.at[:, pl.ds(q * 128, 128)], dst_ref=early_in.at[frm], send_sem=e_send.at[q],
            recv_sem=e_recv.at[frm], device_id=(base + q,), device_id_type=MESH)

    def late_to(q, frm):
        return pltpu.make_async_remote_copy(
            src_ref=late.at[:, pl.ds(q * 128, 128)], dst_ref=late_in.at[frm], send_sem=l_send.at[q],
            recv_sem=l_recv.at[frm], device_id=(base + q,), device_id_type=MESH)

    def to_owner(side, q, frm):
        return pltpu.make_async_remote_copy(
            src_ref=owned, dst_ref=factors.at[frm], send_sem=f_send.at[side],
            recv_sem=f_recv.at[frm], device_id=(q,), device_id_type=MESH)

    early_keep = pltpu.make_async_copy(early.at[:, pl.ds(p * 128, 128)], early_in.at[p], t_local.at[0])
    late_keep = pltpu.make_async_copy(late.at[:, pl.ds(p * 128, 128)], late_in.at[p], t_local.at[1])
    owned_keep = pltpu.make_async_copy(owned, factors.at[me // group], t_local.at[2])
    early_keep.start()

    @pl.loop(1, group)
    def _(i):
        to_head((p + i) % group).start()

    @pl.loop(1, group)
    def _(i):
        early_to((p + i) % group, p).start()

    @pl.loop(0, 4)
    def _(i):
        level = place.level(3 - i)
        for k in range(2):
            for h in range(2):
                part_across(h, k, level).start()
                keep_piece(h, k, level).start()

    key_t[...] = key[...].astype(f32).T.astype(bf)
    grad_key[...] = jnp.zeros_like(grad_key)
    grad_value[...] = jnp.zeros_like(grad_value)
    keep.wait()

    def raw_grad(raw, gain, turned, at):
        back = turned * cosine[at] - pltpu.roll(turned, 64, 1) * sine[at]
        rows_ = raw[at]
        inverse = lax.rsqrt(jnp.mean(rows_ * rows_, axis=-1, keepdims=True) + epsilon)
        unit = rows_ * inverse
        scaled = back * gain[...]
        return (inverse * (scaled - unit * jnp.mean(scaled * unit, axis=-1, keepdims=True))).astype(bf)

    @pl.loop(0, group // 2)
    def _(b):
        at = pl.ds(pl.multiple_of(b * span, span), span)
        for side in range(2):
            q = 2 * b + side

            @pl.when(q != p)
            def _():
                from_token(q).wait_recv()

        ours = query[at]
        grad = grads[pl.ds(2 * b, 2)].reshape(span, 128)
        scores = lax.dot_general(key[...], ours, flip, preferred_element_type=f32)
        weight = jnp.where(k_seg[...] == q_seg[:, at], jnp.exp2(scores * (scale * math.log2(math.e))), 0.0)
        probs = weight * (1.0 / jnp.sum(weight, axis=0, keepdims=True))
        grad_probs = lax.dot_general(value[...], grad, flip, preferred_element_type=f32)
        mean = jnp.sum(probs * grad_probs, axis=0, keepdims=True)
        grad_scores = (probs * (grad_probs - mean)).astype(bf)
        grad_key[...] += jnp.dot(grad_scores, ours, preferred_element_type=f32)
        grad_value[...] += jnp.dot(probs.astype(bf), grad, preferred_element_type=f32)
        grad_query = jnp.dot(key_t[...], grad_scores, preferred_element_type=f32).T * scale
        heads[at, 0:128] = raw_grad(query_proj, query_gain, grad_query, at)
        part_event(b)

    up_own = weights[pl.ds(2 * p, 2), :, 384:512].reshape(2 * depth, 128)
    up_own = pltpu.roll(up_own.astype(f32), 64, 1).astype(bf)

    @pl.loop(0, group // 2)
    def _(b):
        at = pl.ds(pl.multiple_of(b * span, span), span)
        heads[at, 128:256] = raw_grad(key_proj, key_gain, grad_key[at] * scale, at)
        heads[at, 256:384] = grad_value[at].astype(bf)

    def to_sibling(c):
        return pltpu.make_async_remote_copy(
            src_ref=result.at[c, 1 - core], dst_ref=sib.at[c], send_sem=sib_send.at[c],
            recv_sem=sib_recv.at[c], device_id=(place.sibling,), device_id_type=MESH)

    def across(h, k, far):
        return pltpu.make_async_remote_copy(
            src_ref=cross_out.at[h, k, far], dst_ref=cross_in.at[h, k, far], send_sem=cross_send.at[h, k, far],
            recv_sem=cross_recv.at[h, k, far], device_id=(place.last(h),), device_id_type=MESH)

    def along(h, k):
        return pltpu.make_async_remote_copy(
            src_ref=z_out.at[h, k], dst_ref=z_in.at[h, k], send_sem=z_send.at[h, k],
            recv_sem=z_recv.at[h, k], device_id=(across_z,), device_id_type=MESH)

    def first(h):
        return pltpu.make_async_remote_copy(
            src_ref=first_out.at[h], dst_ref=first_in.at[h], send_sem=first_send.at[h],
            recv_sem=first_recv.at[h], device_id=(place.first(h),), device_id_type=MESH)

    def both(c, h):
        part = pl.ds(h * half, half)
        return result[c, core, part].astype(f32) + sib[c, part].astype(f32)

    def pair_sum(c):
        far, dx, dy = 1 - c // 4, c % 2, c // 2 % 2
        to_sibling(c).wait_recv()
        for h, away, k in ((0, dx, dy), (1, dy, dx)):
            @pl.when(away == 1)
            def _():
                cross_out[h, k, far] = both(c, h).astype(bf)
                across(h, k, far).start()

    @pl.loop(0, group // 2 + 1)
    def _(c):
        @pl.when(c < group // 2)
        def _():
            far, dx, dy = 1 - c // 4, c % 2, c // 2 % 2
            o = (z + far * (1 - 2 * z)) * 4 + place.chip_at(dx, dy, 0)
            mine = heads[pl.ds(pl.multiple_of(o * span, span), span), :]
            matrix = weights[...].reshape(2 * group * depth, 512)[:, 0:384]
            part = lax.dot_general(mine, matrix, flip, preferred_element_type=f32)
            result[c, :, :, 0:width] = part.astype(bf).reshape(2, rows, width)
            low = jnp.zeros((span, 128), f32)
            owner = lax.broadcasted_iota(jnp.int32, low.shape, 1) // rank
            for j in range(3):
                term = jnp.dot(mine[:, j * 128 : (j + 1) * 128], up_own, preferred_element_type=f32)
                low = jnp.where(owner == j, term, low)
            result[c, :, :, width:] = low.astype(bf).reshape(2, rows, 128)
            to_sibling(c).start()

        @pl.when(c >= 1)
        def _():
            pair_sum(c - 1)
            part_event(group // 2 + c - 1)

    @pl.loop(0, group // 2)
    def _(e):
        far, k, h = 1 - e // 4, e // 2 % 2, e % 2
        c = (1 - far) * 4 + k * (2 - h)
        across(h, k, far).wait_recv()
        total = both(c, h) + cross_in[h, k, far].astype(f32)

        @pl.when(far == 1)
        def _():
            z_out[h, k] = total.astype(bf)
            along(h, k).start()

        @pl.when(far == 0)
        def _():
            along(h, k).wait_recv()
            whole = total + z_in[h, k].astype(f32)

            @pl.when(k == 1)
            def _():
                first_out[h] = whole.astype(bf)
                first(h).start()

            @pl.when(k == 0)
            def _():
                out[pl.ds(h * half, half)] = whole

    owner = lax.broadcasted_iota(jnp.int32, (128, 128), 0) // rank
    up = jnp.zeros((128, 128), f32)
    for j in range(3):
        term = lax.dot_general(inner[...], heads[:, j * 128 : (j + 1) * 128], tall, preferred_element_type=f32)
        up = jnp.where(owner == j, term, up)
    up_terms[...] = up
    for h in range(2):
        first(h).wait_recv()
        out[pl.ds(h * half, half)] += first_in[h].astype(f32)
    lane = lax.broadcasted_iota(jnp.int32, (rows, 128), 1)
    grad_inner = jnp.where(lane < 3 * rank, out[:, width:], 0.0).astype(bf)
    late[...] = lax.dot_general(grad_inner, normed[...], tall, preferred_element_type=f32)[: 3 * rank]
    late_keep.start()

    @pl.loop(1, group)
    def _(i):
        late_to((p + i) % group, p).start()

    downs = weights[:, :, 384:512].reshape(2 * group * depth, 128)
    grad_normed = out[:, 0:width] + lax.dot_general(grad_inner, downs, flip, preferred_element_type=f32)
    ours = rows_in[...].astype(f32)
    inverse = lax.rsqrt(jnp.mean(ours * ours, axis=-1, keepdims=True) + epsilon)
    unit = ours * inverse
    scaled = grad_normed * rows_gain[...]
    grad = inverse * (scaled - unit * jnp.mean(scaled * unit, axis=-1, keepdims=True))
    grad_rows[...] = (grad_middle[...] + grad).astype(bf)
    early_keep.wait()
    late_keep.wait()

    @pl.loop(1, group)
    def _(i):
        q = (p + i) % group
        early_to(q, q).wait_recv()
        late_to(q, q).wait_recv()

    sums = jnp.sum(early_in[...], axis=0)
    owned[0 : 3 * rank] = jnp.sum(late_in[...], axis=0)
    owned[3 * rank : 4 * rank] = sums[:rank]
    owned[4 * rank : 7 * rank] = up_terms[0 : 3 * rank]
    owned[7 * rank : 8 * rank] = sums[rank:]
    for side in range(2):
        q = 2 * p + side

        @pl.when(q != me)
        def _():
            to_owner(side, q, me // group).start()

        @pl.when(q == me)
        def _():
            owned_keep.start()

    for h in range(2):
        part_first(h).wait_recv()
        side = pl.ds(h * half, half)
        output[side] = (middle[side] + part_sum[h] + part_first_in[h].astype(f32)).astype(bf)
    for s in range(2):
        source = s * group + me // 2

        @pl.when(source != me)
        def _():
            to_owner(0, source, s).wait_recv()

        @pl.when(source == me)
        def _():
            owned_keep.wait()

    @pl.loop(1, group)
    def _(i):
        to_head((p + i) % group).wait_send()
        early_to((p + i) % group, p).wait_send()
        late_to((p + i) % group, p).wait_send()

    for side in range(2):
        @pl.when(2 * p + side != me)
        def _():
            to_owner(side, 2 * p + side, me // group).wait_send()

    for h in range(2):
        part_first(h).wait_send()

    @pl.loop(0, 4)
    def _(level):
        for k in range(2):
            for h in range(2):
                part_across(h, k, level).wait_send()

                @pl.when(level > place.z)
                def _():
                    part_along(h, k, level, 1, level).wait_send()

                @pl.when(level < place.z)
                def _():
                    part_along(h, k, level, 0, down_slot(level)).wait_send()

    @pl.loop(0, group // 2)
    def _(c):
        to_sibling(c).wait_send()
        across(c % 2, c // 2 % 2, c // 4).wait_send()

        @pl.when(c < 4)
        def _():
            along(c % 2, c // 2).wait_send()

        @pl.when(c < 2)
        def _():
            first(c).wait_send()


def back(grad_mixed, part, weights, query, key, value, query_proj, key_proj, inner, cosine, sine,
         query_gain, key_gain, q_seg, k_seg, rows_in, normed, rows_gain, grad_middle, middle, early, rank):
    rows, width = grad_mixed.shape
    seq = query.shape[0]
    group = seq // rows
    bf, f32 = jnp.bfloat16, jnp.float32
    dma = pltpu.SemaphoreType.DMA
    vmem = pl.BlockSpec(memory_space=pltpu.VMEM)
    wide = width + 128
    piece = (rows // 2, wide)
    own = part.shape[2:]
    return pl.pallas_call(
        functools.partial(back_kernel, rows, rank),
        out_shape=(
            jax.ShapeDtypeStruct((rows, width), bf),
            jax.ShapeDtypeStruct((rows, width), bf),
            jax.ShapeDtypeStruct((2, 8 * rank, 128), f32),
        ),
        in_specs=[vmem, pl.BlockSpec(memory_space=pl.ANY)] + [vmem] * 19,
        out_specs=(vmem, vmem, vmem),
        scratch_shapes=[
            pltpu.VMEM((rows, wide), f32),
            pltpu.VMEM((128, 128), f32),
            pltpu.VMEM((2,) + own, f32),
            pltpu.VMEM((3 * rank, width), f32),
            pltpu.VMEM((group, 2 * rank, 128), f32),
            pltpu.VMEM((group, 3 * rank, 128), f32),
            pltpu.VMEM((8 * rank, 128), f32),
            dma((group,)), dma((group,)), dma((group,)), dma((group,)), dma((2,)), dma((2,)), dma((3,)),
            pltpu.VMEM((group, rows, 128), bf),
            pltpu.VMEM((128, seq), bf),
            pltpu.VMEM((seq, 128), f32),
            pltpu.VMEM((seq, 128), f32),
            pltpu.VMEM((seq, 384), bf),
            pltpu.VMEM((group // 2, 2, rows, wide), bf),
            pltpu.VMEM((group // 2, rows, wide), bf),
            pltpu.VMEM((2, 2, 2) + piece, bf),
            pltpu.VMEM((2, 2, 2) + piece, bf),
            pltpu.VMEM((2, 2) + piece, bf),
            pltpu.VMEM((2, 2) + piece, bf),
            pltpu.VMEM((2,) + piece, bf),
            pltpu.VMEM((2,) + piece, bf),
            pltpu.VMEM((2, 2, LEVELS) + own, bf),
            pltpu.VMEM((2, 2, LEVELS) + own, bf),
            pltpu.VMEM((2, 2, LEVELS + 1) + own, bf),
            pltpu.VMEM(own, f32),
            pltpu.VMEM((2,) + own, bf),
            pltpu.VMEM((2,) + own, bf),
            dma((2, 2, LEVELS)), dma((2, 2, LEVELS)), dma((2, 2, LEVELS)), dma((2, 2, LEVELS)), dma((2, 2, LEVELS + 1)),
            dma((2,)), dma((2,)),
            dma((group,)), dma((group,)), dma, dma((group // 2,)), dma((group // 2,)),
            dma((2, 2, 2)), dma((2, 2, 2)), dma((2, 2)), dma((2, 2)), dma((2,)), dma((2,)),
        ],
        compiler_params=pltpu.CompilerParams(has_side_effects=True, vmem_limit_bytes=63 << 20),
        name="back",
    )(grad_mixed, part, weights, query, key, value, query_proj, key_proj, inner, cosine, sine,
      query_gain, key_gain, q_seg, k_seg, rows_in, normed, rows_gain, grad_middle, middle, early)


def heads_plan(
    tokens,
    segments,
    routes,
    gates,
    sequence_adapter_index,
    attention_norm_gain,
    query_norm_gain,
    key_norm_gain,
    query_weight,
    key_weight,
    value_weight,
    output_weight,
    adapter_down_factors,
    adapter_up_factors,
    expert_norm_gain,
    expert_gate_weight,
    expert_up_weight,
    expert_down_weight,
    output_gradient,
):
    bf, f32 = jnp.bfloat16, jnp.float32
    devices = lax.axis_size("fsdp")
    rows_dev, width = tokens.shape
    group = SEQ_LEN // rows_dev
    seqs = segments.shape[0]
    rank = adapter_down_factors.shape[3]
    slots = 4 * rank
    own_rows = query_weight.shape[0]
    device = lax.axis_index("fsdp")
    sequence = device // group
    segment_row = pick(segments, sequence)
    attn_scale = attention_norm_gain.astype(f32)
    query_scale = query_norm_gain.astype(f32)
    key_scale = key_norm_gain.astype(f32)
    ffn_scale = expert_norm_gain.astype(f32)

    heads_w = jnp.concatenate(
        [
            weight.reshape(own_rows, group, HEAD_DIM)
            for weight in (query_weight, key_weight, value_weight)
        ],
        axis=2,
    ).transpose(1, 0, 2)
    head_gains = (query_scale.reshape(1, HEAD_DIM), key_scale.reshape(1, HEAD_DIM))
    tall, flat = segment_row.reshape(SEQ_LEN, 1), segment_row.reshape(1, SEQ_LEN)
    (middle, normed_ffn, normed, mixed, out_inner, head_weights, query, key, value, query_proj, key_proj, inner_all,
     coeff_own, *turns, output_matrix) = front(
        sequence_adapter_index, tokens, attn_scale.reshape(1, width), heads_w, adapter_down_factors,
        adapter_up_factors, routes, gates, output_weight, *head_gains, ffn_scale.reshape(1, width), tall, flat,
    )
    output_matrix = output_matrix.reshape(width, width)
    out_inner = out_inner[:, 3 * rank : slots]
    weights = head_weights.reshape(width, 4 * HEAD_DIM)
    down_out = weights[:, 3 * HEAD_DIM + 3 * rank : 3 * HEAD_DIM + slots]
    up_out = weights[:, 3 * HEAD_DIM + slots + 3 * rank :]

    slab_gate = expert_gate_weight[0]
    slab_up = expert_up_weight[0]
    slab_down = expert_down_weight[0]
    coeff_own = coeff_own.reshape(devices, rows_dev, 1)
    grad_ffn, part = experts_pass(normed_ffn, output_gradient, slab_gate, slab_up, slab_down, coeff_own)
    upstream = output_gradient.astype(f32)
    grad_middle = upstream + rms_back(middle, ffn_scale, grad_ffn)
    grad_attn = grad_middle.astype(bf)

    grad_inner_out = matmul(grad_attn, up_out).astype(bf)
    grad_mixed = matmul(grad_attn, output_matrix.T) + matmul(grad_inner_out, down_out.T)
    grad_mixed = grad_mixed.astype(bf)
    up_out_terms = matmul(out_inner.T, grad_attn)
    down_out_terms = matmul(grad_inner_out.T, mixed)

    grad_tokens, output, terms = back(
        grad_mixed, part, head_weights, query, key, value, query_proj, key_proj, inner_all,
        *turns, *head_gains, flat, tall,
        tokens, normed, attn_scale.reshape(1, width), grad_middle, middle,
        jnp.concatenate([down_out_terms, up_out_terms], axis=0), rank,
    )
    terms = lax.dynamic_slice_in_dim(terms, device % 2 * own_rows, own_rows, 2)
    selected = (
        jnp.arange(ADAPTER_COUNT, dtype=jnp.int32)[:, None] == sequence_adapter_index[None, :]
    ).astype(f32)
    spread = jnp.sum(selected[:, :, None, None] * terms[None], axis=1)
    spread = spread.reshape(ADAPTER_COUNT, 2, 4, rank, own_rows)
    grad_down = spread[:, 0].transpose(0, 1, 3, 2)
    grad_up = spread[:, 1]
    return (output, grad_tokens, grad_down, grad_up)


def solution(mesh):
    plan = heads_plan if mesh.shape["fsdp"] == LEVELS * 8 else shards
    in_specs = (
        P("fsdp", None),
        P(),
        P("fsdp", None),
        P("fsdp", None),
        P(),
        P(),
        P(),
        P(),
        P("fsdp", None),
        P("fsdp", None),
        P("fsdp", None),
        P("fsdp", None),
        P(None, None, "fsdp", None),
        P(None, None, None, "fsdp"),
        P(),
        P("fsdp", None, None),
        P("fsdp", None, None),
        P("fsdp", None, None),
        P("fsdp", None),
    )
    out_specs = (
        P("fsdp", None),
        P("fsdp", None),
        P(None, None, "fsdp", None),
        P(None, None, None, "fsdp"),
    )
    return jax.shard_map(plan, mesh=mesh, in_specs=in_specs, out_specs=out_specs, check_vma=False)
```

```python
import functools
import math

import jax
import jax.numpy as jnp
import numpy as np
from jax import lax
from jax.experimental import pallas as pl
from jax.experimental.pallas import tpu as pltpu
from jax.sharding import PartitionSpec as P

HEAD_DIM = 128
TOPK = 8
ADAPTER_COUNT = 8
SEQ_LEN = 2048


epsilon = 1e-06
rope_base = 50000.0


def from_partner(value, axis, distance):
    mask = 2**distance
    pairs = [(source, source ^ mask) for source in range(lax.axis_size(axis))]
    return lax.ppermute(value, axis, pairs)


def matmul(left, right):
    return jnp.dot(left, right, preferred_element_type=jnp.float32)


def rms_scale(rows, gain):
    return rows * lax.rsqrt(jnp.mean(rows * rows, axis=-1, keepdims=True) + epsilon) * gain


def rms_back(rows, gain, upstream):
    inverse = lax.rsqrt(jnp.mean(rows * rows, axis=-1, keepdims=True) + epsilon)
    unit = rows * inverse
    scaled = upstream * gain
    return inverse * (scaled - unit * jnp.mean(scaled * unit, axis=-1, keepdims=True))


def rope_tables(positions):
    half = HEAD_DIM // 2
    frequency = rope_base ** (-(jnp.arange(half, dtype=jnp.float32) * 2.0 / HEAD_DIM))
    angle = positions[:, None] * frequency[None, :]
    return (jnp.cos(angle)[:, None, :], jnp.sin(angle)[:, None, :])


def rotate(rows, cosine, sine):
    half = rows.shape[-1] // 2
    first = rows[..., :half]
    second = rows[..., half:]
    return jnp.concatenate(
        [first * cosine - second * sine, second * cosine + first * sine], axis=-1
    )


def rotate_back(upstream, cosine, sine):
    half = upstream.shape[-1] // 2
    first = upstream[..., :half]
    second = upstream[..., half:]
    return jnp.concatenate(
        [first * cosine + second * sine, second * cosine - first * sine], axis=-1
    )


def pick(table, index):
    return lax.dynamic_index_in_dim(table, index, 0, keepdims=False)


def shards(
    tokens,
    segments,
    routes,
    gates,
    sequence_adapter_index,
    attention_norm_gain,
    query_norm_gain,
    key_norm_gain,
    query_weight,
    key_weight,
    value_weight,
    output_weight,
    adapter_down_factors,
    adapter_up_factors,
    expert_norm_gain,
    expert_gate_weight,
    expert_up_weight,
    expert_down_weight,
    output_gradient,
):
    rows_dev = tokens.shape[0]
    width = tokens.shape[1]
    heads = width // HEAD_DIM
    group = SEQ_LEN // rows_dev
    level_list = group.bit_length() - 1
    device = lax.axis_index("fsdp")
    place = device % group
    sequence = device // group
    segment_row = pick(segments, sequence)
    own_segment = lax.dynamic_slice_in_dim(segment_row, place * rows_dev, rows_dev)
    adapter = pick(sequence_adapter_index, sequence)
    scale = 1.0 / math.sqrt(HEAD_DIM)
    cosine, sine = rope_tables(
        (place * rows_dev + jnp.arange(rows_dev, dtype=jnp.int32)).astype(jnp.float32)
    )
    attn_scale = attention_norm_gain.astype(jnp.float32)
    query_scale = query_norm_gain.astype(jnp.float32)
    key_scale = key_norm_gain.astype(jnp.float32)
    ffn_scale = expert_norm_gain.astype(jnp.float32)
    gathered = (
        lax.all_gather(query_weight, "fsdp", axis=0, tiled=True),
        lax.all_gather(key_weight, "fsdp", axis=0, tiled=True),
        lax.all_gather(value_weight, "fsdp", axis=0, tiled=True),
        lax.all_gather(output_weight, "fsdp", axis=0, tiled=True),
        lax.all_gather(adapter_down_factors, "fsdp", axis=2, tiled=True),
        lax.all_gather(adapter_up_factors, "fsdp", axis=3, tiled=True),
    )
    matrices = gathered[:4]
    down_own = pick(gathered[4], adapter)
    up_own = pick(gathered[5], adapter)

    def project(inputs, index):
        inner = matmul(inputs, down_own[index]).astype(jnp.bfloat16)
        return (matmul(inputs, matrices[index]) + matmul(inner, up_own[index]), inner)

    rows = tokens.astype(jnp.float32)
    normed = rms_scale(rows, attn_scale).astype(jnp.bfloat16)
    query_proj, query_inner = project(normed, 0)
    key_proj, key_inner = project(normed, 1)
    value_proj, value_inner = project(normed, 2)
    query_heads = query_proj.reshape(rows_dev, heads, HEAD_DIM)
    key_heads = key_proj.reshape(rows_dev, heads, HEAD_DIM)
    query_rot = rotate(rms_scale(query_heads, query_scale), cosine, sine).astype(jnp.bfloat16)
    key_rot = (
        rotate(rms_scale(key_heads, key_scale), cosine, sine)
        .astype(jnp.bfloat16)
        .reshape(rows_dev, width)
    )
    value_low = value_proj.astype(jnp.bfloat16)
    held_keys = key_rot
    held_values = value_low
    for level in range(level_list):
        other_keys, other_values = from_partner((held_keys, held_values), "fsdp", level)
        upper_bit = place // (1 << level) % 2 == 1
        held_keys = jnp.where(
            upper_bit,
            jnp.concatenate([other_keys, held_keys], axis=0),
            jnp.concatenate([held_keys, other_keys], axis=0),
        )
        held_values = jnp.where(
            upper_bit,
            jnp.concatenate([other_values, held_values], axis=0),
            jnp.concatenate([held_values, other_values], axis=0),
        )
    keys_all = held_keys.reshape(SEQ_LEN, heads, HEAD_DIM)
    values_all = held_values.reshape(SEQ_LEN, heads, HEAD_DIM)
    allowed = (own_segment[:, None] == segment_row[None, :])[None]

    def masked_scores():
        raw = (
            jnp.einsum("thd,shd->hts", query_rot, keys_all, preferred_element_type=jnp.float32)
            * scale
        )
        return jnp.where(allowed, raw, -1e30)

    scores = masked_scores()
    maximum = jnp.max(scores, axis=-1, keepdims=True)
    weights = jnp.exp(scores - maximum)
    total = jnp.sum(weights, axis=-1, keepdims=True)
    probs = weights / total
    log_total = maximum + jnp.log(total)
    mixed = jnp.einsum(
        "hts,shd->thd", probs.astype(jnp.bfloat16), values_all, preferred_element_type=jnp.float32
    )
    mixed = mixed.astype(jnp.bfloat16).reshape(rows_dev, width)
    attn_proj, out_inner = project(mixed, 3)
    middle = rows + attn_proj
    normed_ffn = rms_scale(middle, ffn_scale).astype(jnp.bfloat16)
    experts = lax.axis_size("fsdp") // 2
    capacity = 2 * rows_dev * TOPK // experts
    flat_routes = routes.reshape(-1)
    onehot = (flat_routes[:, None] == jnp.arange(experts, dtype=jnp.int32)[None, :]).astype(
        jnp.int32
    )
    slot = jnp.sum(jnp.cumsum(onehot, axis=0) * onehot, axis=1) - 1
    target = flat_routes * capacity + slot

    def spread(entries):
        buffer = jnp.zeros((experts * capacity, width), jnp.bfloat16).at[target].set(entries)
        buffer = buffer.reshape(experts, 1, capacity, width)
        return jnp.broadcast_to(buffer, (experts, 2, capacity, width)).reshape(
            2 * experts, capacity, width
        )

    def collect(returned):
        halves = returned.reshape(experts, 2, capacity, width).astype(jnp.float32)
        summed = (halves[:, 0] + halves[:, 1]).reshape(experts * capacity, width)
        return summed[target].reshape(rows_dev, TOPK, width)

    slab_gate = expert_gate_weight[0]
    slab_up = expert_up_weight[0]
    slab_down = expert_down_weight[0]
    dispatched = lax.all_to_all(
        spread(jnp.repeat(normed_ffn, TOPK, axis=0)),
        "fsdp",
        split_axis=0,
        concat_axis=0,
        tiled=True,
    )
    gate_part = jnp.einsum("scd,dh->sch", dispatched, slab_gate, preferred_element_type=jnp.float32)
    up_part = jnp.einsum("scd,dh->sch", dispatched, slab_up, preferred_element_type=jnp.float32)
    hidden = (jax.nn.silu(gate_part) * up_part).astype(jnp.bfloat16)
    produced = jnp.einsum(
        "sch,hd->scd", hidden, slab_down, preferred_element_type=jnp.float32
    ).astype(jnp.bfloat16)
    returned = lax.all_to_all(produced, "fsdp", split_axis=0, concat_axis=0, tiled=True)
    moe = jnp.sum(gates[:, :, None] * collect(returned), axis=1)
    output = (middle + moe).astype(jnp.bfloat16)
    upstream = output_gradient.astype(jnp.float32)
    grad_parts = (
        (gates[:, :, None] * upstream[:, None, :])
        .astype(jnp.bfloat16)
        .reshape(rows_dev * TOPK, width)
    )
    grad_sent = lax.all_to_all(spread(grad_parts), "fsdp", split_axis=0, concat_axis=0, tiled=True)
    grad_hidden = jnp.einsum(
        "scd,hd->sch", grad_sent, slab_down, preferred_element_type=jnp.float32
    )
    sigmoid = jax.nn.sigmoid(gate_part)
    grad_gate = (grad_hidden * up_part * sigmoid * (1.0 + gate_part * (1.0 - sigmoid))).astype(
        jnp.bfloat16
    )
    grad_up = (grad_hidden * gate_part * sigmoid).astype(jnp.bfloat16)
    grad_inputs = jnp.einsum(
        "sch,dh->scd", grad_gate, slab_gate, preferred_element_type=jnp.float32
    )
    grad_inputs = (
        grad_inputs
        + jnp.einsum("sch,dh->scd", grad_up, slab_up, preferred_element_type=jnp.float32)
    ).astype(jnp.bfloat16)
    grad_back = lax.all_to_all(grad_inputs, "fsdp", split_axis=0, concat_axis=0, tiled=True)
    grad_ffn = jnp.sum(collect(grad_back), axis=1)
    grad_middle = upstream + rms_back(middle, ffn_scale, grad_ffn)
    grad_attn = grad_middle.astype(jnp.bfloat16)
    regathered = (
        lax.all_gather(query_weight, "fsdp", axis=0, tiled=True),
        lax.all_gather(key_weight, "fsdp", axis=0, tiled=True),
        lax.all_gather(value_weight, "fsdp", axis=0, tiled=True),
        lax.all_gather(output_weight, "fsdp", axis=0, tiled=True),
        lax.all_gather(adapter_down_factors, "fsdp", axis=2, tiled=True),
        lax.all_gather(adapter_up_factors, "fsdp", axis=3, tiled=True),
    )
    back_matrices = regathered[:4]
    back_down = pick(regathered[4], adapter)
    back_up = pick(regathered[5], adapter)

    def project_back(inputs, inner, upstream_low, index):
        grad_inner = matmul(upstream_low, back_up[index].T).astype(jnp.bfloat16)
        grad_input = matmul(upstream_low, back_matrices[index].T) + matmul(
            grad_inner, back_down[index].T
        )
        return (grad_input, matmul(inputs.T, grad_inner), matmul(inner.T, upstream_low))

    grad_mixed_full, down_output, up_output = project_back(mixed, out_inner, grad_attn, 3)
    grad_mixed = grad_mixed_full.astype(jnp.bfloat16).reshape(rows_dev, heads, HEAD_DIM)
    probs = jnp.exp(masked_scores() - log_total)
    grad_probs = jnp.einsum(
        "thd,shd->hts", grad_mixed, values_all, preferred_element_type=jnp.float32
    )
    grad_scores = (
        probs * (grad_probs - jnp.sum(probs * grad_probs, axis=-1, keepdims=True))
    ).astype(jnp.bfloat16)
    grad_query = (
        jnp.einsum("hts,shd->thd", grad_scores, keys_all, preferred_element_type=jnp.float32)
        * scale
    )
    grad_keys_part = (
        jnp.einsum("hts,thd->shd", grad_scores, query_rot, preferred_element_type=jnp.float32)
        * scale
    )
    grad_keys_part = grad_keys_part.reshape(group, rows_dev, width)
    grad_values_part = jnp.einsum(
        "hts,thd->shd", probs.astype(jnp.bfloat16), grad_mixed, preferred_element_type=jnp.float32
    )
    grad_values_part = grad_values_part.reshape(group, rows_dev, width)
    for level in reversed(range(level_list)):
        size_half = 1 << level
        upper_bit = place // size_half % 2 == 1
        keep_keys = jnp.where(upper_bit, grad_keys_part[size_half:], grad_keys_part[:size_half])
        send_keys = jnp.where(upper_bit, grad_keys_part[:size_half], grad_keys_part[size_half:])
        keep_values = jnp.where(
            upper_bit, grad_values_part[size_half:], grad_values_part[:size_half]
        )
        send_values = jnp.where(
            upper_bit, grad_values_part[:size_half], grad_values_part[size_half:]
        )
        got_keys, got_values = (
            from_partner(send_keys.astype(jnp.bfloat16), "fsdp", level).astype(send_keys.dtype),
            from_partner(send_values.astype(jnp.bfloat16), "fsdp", level).astype(send_values.dtype),
        )
        grad_keys_part = keep_keys + got_keys
        grad_values_part = keep_values + got_values
    grad_keys = grad_keys_part[0]
    grad_values = grad_values_part[0]
    grad_value_proj = grad_values.astype(jnp.bfloat16)
    grad_key_proj = rms_back(
        key_heads,
        key_scale,
        rotate_back(grad_keys.reshape(rows_dev, heads, HEAD_DIM), cosine, sine),
    )
    grad_key_proj = grad_key_proj.reshape(rows_dev, width).astype(jnp.bfloat16)
    grad_query_proj = rms_back(query_heads, query_scale, rotate_back(grad_query, cosine, sine))
    grad_query_proj = grad_query_proj.reshape(rows_dev, width).astype(jnp.bfloat16)
    grad_from_query, down_query, up_query = project_back(normed, query_inner, grad_query_proj, 0)
    grad_from_key, down_key, up_key = project_back(normed, key_inner, grad_key_proj, 1)
    grad_from_value, down_value, up_value = project_back(normed, value_inner, grad_value_proj, 2)
    grad_normed = grad_from_query + grad_from_key + grad_from_value
    grad_tokens = (grad_middle + rms_back(rows, attn_scale, grad_normed)).astype(jnp.bfloat16)
    down_terms = jnp.stack([down_query, down_key, down_value, down_output])
    up_terms = jnp.stack([up_query, up_key, up_value, up_output])
    selected = (jnp.arange(ADAPTER_COUNT, dtype=jnp.int32) == adapter).astype(jnp.float32)[
        :, None, None, None
    ]
    grad_down, grad_up = (
        lax.psum_scatter(selected * down_terms[None], "fsdp", scatter_dimension=2, tiled=True),
        lax.psum_scatter(selected * up_terms[None], "fsdp", scatter_dimension=3, tiled=True),
    )
    return (output, grad_tokens, grad_down, grad_up)


epsilon = 1e-06
MESH = pl.DeviceIdType.MESH
LEVELS = 4
CHIPS = 16


class Place:
    def __init__(self):
        self.me = me = lax.axis_index("fsdp")
        self.core = me % 2
        self.x = me // 2 % 2
        self.y = me // 4 % 2
        self.z = me // 8
        self.sibling = me + 1 - 2 * self.core
        self.across_x = me + 2 - 4 * self.x
        self.across_y = me + 4 - 8 * self.y

    def level(self, i):
        upper = self.z // 2
        inner = self.z * (1 - upper) + (3 - self.z) * upper
        turn = i + inner * (1 - 2 * i) * (1 - i // 2)
        return turn + upper * (3 - 2 * turn)

    def chip(self, half, side, level):
        flip = 1 - 2 * side
        y = self.y + (1 - half) * side * (1 - 2 * self.y)
        x = self.x + half * side * (1 - 2 * self.x)
        return level * 4 + y * 2 + x

    def chip_at(self, dx, dy, level):
        y = self.y + dy * (1 - 2 * self.y)
        x = self.x + dx * (1 - 2 * self.x)
        return level * 4 + y * 2 + x

    def first(self, half):
        return self.across_y * (1 - half) + self.across_x * half

    def last(self, half):
        return self.across_x * (1 - half) + self.across_y * half


def scatter_kernel(rows, work, source, out, own, sib, cross_out, cross_in, z_out, z_in, first_out, first_in, total,
                   own_sem, sib_send, sib_recv, cross_send, cross_recv, z_send, z_recv, first_send, first_recv):
    place = Place()
    half_rows = rows // 2
    f32, bf = jnp.float32, jnp.bfloat16

    def local(o):
        return pltpu.make_async_copy(source.at[2 * o + place.core], own.at[o], own_sem.at[o])

    def to_sibling(o):
        return pltpu.make_async_remote_copy(
            src_ref=source.at[2 * o + 1 - place.core], dst_ref=sib.at[o], send_sem=sib_send.at[o],
            recv_sem=sib_recv.at[o], device_id=(place.sibling,), device_id_type=MESH)

    def across(h, k, level):
        return pltpu.make_async_remote_copy(
            src_ref=cross_out.at[h, k, level], dst_ref=cross_in.at[h, k, level], send_sem=cross_send.at[h, k, level],
            recv_sem=cross_recv.at[h, k, level], device_id=(place.last(h),), device_id_type=MESH)

    def along(h, k, level, up):
        return pltpu.make_async_remote_copy(
            src_ref=z_out.at[h, k, level], dst_ref=z_in.at[up, h, k, level], send_sem=z_send.at[h, k, level],
            recv_sem=z_recv.at[up, h, k, level], device_id=(place.me - 8 + 16 * up,), device_id_type=MESH)

    def first(h):
        return pltpu.make_async_remote_copy(
            src_ref=first_out.at[h], dst_ref=first_in.at[h], send_sem=first_send.at[h],
            recv_sem=first_recv.at[h], device_id=(place.first(h),), device_id_type=MESH)

    def both(o, h):
        part = pl.ds(h * half_rows, half_rows)
        return own[o, part].astype(f32) + sib[o, part].astype(f32)

    @pl.loop(0, CHIPS)
    def _(q):
        o = place.chip_at(q % 2, q // 2 % 2, place.level(3 - q // 4))
        local(o).start()
        to_sibling(o).start()

    @pl.loop(0, CHIPS + 4)
    def _(t):
        @pl.when(t < CHIPS)
        def _():
            level = place.level(3 - t // 4)
            dx, dy = t % 2, t // 2 % 2
            o = place.chip_at(dx, dy, level)
            local(o).wait()
            to_sibling(o).wait_recv()
            for h, away, k in ((0, dx, dy), (1, dy, dx)):
                @pl.when(away == 1)
                def _():
                    cross_out[h, k, level] = both(o, h).astype(bf)
                    across(h, k, level).start()

        @pl.when(t >= 4)
        def _():
            i, h, k = (t - 4) // 4, t % 2, t // 2 % 2
            level = place.level(3 - i)
            o = place.chip(h, k, level)
            across(h, k, level).wait_recv()
            total[...] = both(o, h) + cross_in[h, k, level].astype(f32)

            @pl.when((level >= place.z) & (place.z > 0))
            def _():
                along(h, k, level, 1).wait_recv()
                total[...] += z_in[1, h, k, level].astype(f32)

            @pl.when((level <= place.z) & (place.z < LEVELS - 1))
            def _():
                along(h, k, level, 0).wait_recv()
                total[...] += z_in[0, h, k, level].astype(f32)

            @pl.when(level > place.z)
            def _():
                z_out[h, k, level] = total[...].astype(bf)
                along(h, k, level, 1).start()

            @pl.when(level < place.z)
            def _():
                z_out[h, k, level] = total[...].astype(bf)
                along(h, k, level, 0).start()

            @pl.when((level == place.z) & (k == 1))
            def _():
                first_out[h] = total[...].astype(bf)
                first(h).start()

            @pl.when((level == place.z) & (k == 0))
            def _():
                out[pl.ds(h * half_rows, half_rows)] = total[...]

        if work is not None:
            work(t)

    for h in range(2):
        first(h).wait_recv()
        out[pl.ds(h * half_rows, half_rows)] += first_in[h].astype(f32)

    @pl.loop(0, CHIPS)
    def _(q):
        o = place.chip_at(q % 2, q // 2 % 2, place.level(3 - q // 4))
        to_sibling(o).wait_send()
        h, k, level = q % 2, q // 2 % 2, q // 4
        across(h, k, level).wait_send()

        @pl.when(level > place.z)
        def _():
            along(h, k, level, 1).wait_send()

        @pl.when(level < place.z)
        def _():
            along(h, k, level, 0).wait_send()

    for h in range(2):
        first(h).wait_send()


def scatter_scratch(rows, width):
    bf = jnp.bfloat16
    dma = pltpu.SemaphoreType.DMA
    piece = (rows // 2, width)
    return [
        pltpu.VMEM((CHIPS, rows, width), bf),
        pltpu.VMEM((CHIPS, rows, width), bf),
        pltpu.VMEM((2, 2, LEVELS) + piece, bf),
        pltpu.VMEM((2, 2, LEVELS) + piece, bf),
        pltpu.VMEM((2, 2, LEVELS) + piece, bf),
        pltpu.VMEM((2, 2, 2, LEVELS) + piece, bf),
        pltpu.VMEM((2,) + piece, bf),
        pltpu.VMEM((2,) + piece, bf),
        pltpu.VMEM(piece, jnp.float32),
        dma((CHIPS,)), dma((CHIPS,)), dma((CHIPS,)),
        dma((2, 2, LEVELS)), dma((2, 2, LEVELS)),
        dma((2, 2, LEVELS)), dma((2, 2, 2, LEVELS)),
        dma((2,)), dma((2,)),
    ]


def scatter_all(partial):
    devices, rows, width = partial.shape
    return pl.pallas_call(
        functools.partial(scatter_kernel, rows, None),
        out_shape=jax.ShapeDtypeStruct((rows, width), jnp.float32),
        in_specs=[pl.BlockSpec(memory_space=pl.ANY)],
        out_specs=pl.BlockSpec(memory_space=pltpu.VMEM),
        scratch_shapes=scatter_scratch(rows, width),
        compiler_params=pltpu.CompilerParams(has_side_effects=True, vmem_limit_bytes=48 << 20),
        name="scatter_all",
    )(partial)


OUTER_STEPS = (
    278531, 8684081, 548864, 50372672, 13396561, 21889169, 33882149, 17581620, 9471010, 55600272, 39080084, 42346578,
    38601784, 34932793, 11887841, 63513731, 35729961, 39868579, 48350861, 36731452, 45215881, 61890111, 49625245,
    16334382, 37575933, 62463018, 50150443, 79059002, 44584191, 15537291, 48616602, 79246902, 35155759, 39409401,
    39735847, 35482347, 64378152, 78529191, 47859943, 77196578, 76957479, 126075168, 126075360, 126075360, 126075360,
    126075360, 126075360, 126075360, 126075360, 126075360, 126075360, 126075360,
)
INNER_STEPS = (
    51829, 9699843, 13936708, 551028, 51423780, 9996900, 10502711, 17092868, 8408709, 16838712, 12658837, 21033529,
    12912694, 11906089, 13410925, 27593879, 41985814, 35706924, 33850915, 8978567, 47562812, 39879804, 40139314,
    38052989, 45162741, 16585263, 39357567, 18733167, 12130482, 22616686, 16319635, 33115890, 22886442, 11390570,
    28079293, 38353539, 45742714, 15539854, 41500262, 32339182, 65596554, 40431279, 27123339, 78722744, 44953901,
    75851499, 63856430, 76173993, 78209769, 76435697, 76693803, 76959526,
)


def experts_kernel(rows, x_ref, up_ref, gate_w, up_w, down_w, coeff, out, part_out, gathered,
                   block, part_buf, result, sib, cross_out, cross_in, hold, z_in, first_out, first_in, total,
                   local_sem, load_sem, part_sem, send, recv, sib_send, sib_recv, cross_send, cross_recv,
                   z_send, z_recv, first_send, first_recv):
    place = Place()
    half = rows // 2
    f32, bf = jnp.float32, jnp.bfloat16
    flip = (((1,), (1,)), ((), ()))
    me, core = place.me, place.core
    upper = place.z // 2
    inner = place.z * (1 - upper) + (3 - place.z) * upper
    UP, DOWN, LAST, SIB, FIRST = range(5)

    def move(n, h, o, kind, target):
        piece = gathered.at[2 * o + core, h, n]
        return pltpu.make_async_remote_copy(
            src_ref=piece, dst_ref=piece, send_sem=send.at[kind, n, h, o],
            recv_sem=recv.at[1 if kind == SIB else 0, n, h, o], device_id=(target,), device_id_type=MESH)

    def arrived(n, h, o, sibling):
        piece = gathered.at[2 * o + (1 - core if sibling else core), h, n]
        pltpu.make_async_remote_copy(
            src_ref=piece, dst_ref=piece, send_sem=send.at[SIB, n, h, o],
            recv_sem=recv.at[1 if sibling else 0, n, h, o], device_id=(place.sibling,), device_id_type=MESH).wait_recv()

    def column(n, h, o, level, act):
        @pl.when((level <= place.z) & (place.z < LEVELS - 1))
        def _():
            act(move(n, h, o, UP, me + 8))

        @pl.when((level >= place.z) & (place.z > 0))
        def _():
            act(move(n, h, o, DOWN, me - 8))

    def spread(n, h, o, level, act):
        column(n, h, o, level, act)
        act(move(n, h, o, LAST, place.last(h)))
        act(move(n, h, o, SIB, place.sibling))

    def to_sibling(slot):
        return pltpu.make_async_remote_copy(
            src_ref=result.at[slot, 1 - core], dst_ref=sib.at[slot], send_sem=sib_send.at[slot],
            recv_sem=sib_recv.at[slot], device_id=(place.sibling,), device_id_type=MESH)

    def across(h, k, level):
        return pltpu.make_async_remote_copy(
            src_ref=cross_out.at[h, k, level], dst_ref=cross_in.at[h, k, level], send_sem=cross_send.at[h, k, level],
            recv_sem=cross_recv.at[h, k, level], device_id=(place.last(h),), device_id_type=MESH)

    def along(h, k, level, up, slot):
        return pltpu.make_async_remote_copy(
            src_ref=hold.at[h, k, level], dst_ref=z_in.at[h, k, slot], send_sem=z_send.at[h, k, level],
            recv_sem=z_recv.at[h, k, slot], device_id=(me - 8 + 16 * up,), device_id_type=MESH)

    def first(h):
        return pltpu.make_async_remote_copy(
            src_ref=first_out.at[h], dst_ref=first_in.at[h], send_sem=first_send.at[h],
            recv_sem=first_recv.at[h], device_id=(place.first(h),), device_id_type=MESH)

    def down_slot(level):
        ends = 1 - jnp.minimum(jnp.abs(level - (place.z - 1)), 1)
        return level + ends * (LEVELS - level)

    start = lambda copy: copy.start()
    done = lambda copy: copy.wait_send()
    mine = me // 2
    own = [
        pltpu.make_async_copy(ref.at[pl.ds(h * half, half)], gathered.at[me, h, n], local_sem.at[n, h])
        for n, ref in enumerate((x_ref, up_ref)) for h in range(2)
    ]
    for copy in own:
        copy.start()
    for copy in own:
        copy.wait()
    pieces = [(n, h) for n in range(2) for h in range(2)]
    def keep_part(o, slot):
        return pltpu.make_async_copy(part_buf.at[slot], part_out.at[o], part_sem.at[slot])

    def compute(o, slot, again):
        for n, h in pieces:
            arrived(n, h, o, True)
        load = pltpu.make_async_copy(gathered.at[pl.ds(2 * o, 2)], block, load_sem)
        load.start()

        @pl.when(again)
        def _():
            to_sibling(slot).wait_send()

        load.wait()
        c = coeff[pl.ds(2 * o, 2)].reshape(2 * rows, 1)
        x = block[:, :, 0].reshape(2 * rows, -1)
        gate = jnp.dot(x, gate_w[...], preferred_element_type=f32)
        up = jnp.dot(x, up_w[...], preferred_element_type=f32)
        sig = jax.nn.sigmoid(gate)
        silu = gate * sig
        hidden = (silu * up).astype(bf)
        part = (c * jnp.dot(hidden, down_w[...], preferred_element_type=f32)).astype(bf)
        part = part.reshape(2, 2, half, -1)
        result[slot, 0, 1] = part[0]
        result[slot, 1, 1] = part[1]
        upstream = (c * block[:, :, 1].reshape(2 * rows, -1).astype(f32)).astype(bf)
        grad_hidden = lax.dot_general(upstream, down_w[...], flip, preferred_element_type=f32)
        grad_gate = (grad_hidden * up * sig * (1.0 + gate * (1.0 - sig))).astype(bf)
        grad_up = (grad_hidden * silu).astype(bf)
        grad = lax.dot_general(grad_gate, gate_w[...], flip, preferred_element_type=f32)
        grad += lax.dot_general(grad_up, up_w[...], flip, preferred_element_type=f32)
        grad = grad.astype(bf).reshape(2, 2, half, -1)
        result[slot, 0, 0] = grad[0]
        result[slot, 1, 0] = grad[1]
        to_sibling(slot).start()

    def pair_sum(dx, dy, level, slot, again):
        to_sibling(slot).wait_recv()

        def pair(n, h):
            return (result[slot, core, n, h].astype(f32) + sib[slot, n, h].astype(f32)).astype(bf)

        for h, away, k in ((0, dx, dy), (1, dy, dx)):
            @pl.when(away == 1)
            def _():
                cross_out[h, k, level] = pair(0, h)
                across(h, k, level).start()

            @pl.when(away == 0)
            def _():
                hold[h, k, level] = pair(0, h)

        o = place.chip_at(dx, dy, level)

        @pl.when(again)
        def _():
            keep_part(o, slot).wait()

        for h in range(2):
            part_buf[slot, h] = pair(1, h)
        keep_part(o, slot).start()

    def column_sum(h, k, level):
        across(h, k, level).wait_recv()
        total[...] = hold[h, k, level].astype(f32) + cross_in[h, k, level].astype(f32)

        @pl.when((level >= place.z) & (place.z > 0))
        def _():
            along(h, k, level, 1, level).wait_recv()
            total[...] += z_in[h, k, level].astype(f32)

        @pl.when((level < place.z) & (place.z < LEVELS - 1))
        def _():
            along(h, k, level, 0, level).wait_recv()
            total[...] += z_in[h, k, level].astype(f32)

        @pl.when((level == place.z) & (place.z < LEVELS - 1))
        def _():
            along(h, k, level, 0, LEVELS).wait_recv()
            total[...] += z_in[h, k, LEVELS].astype(f32)

        @pl.when(level > place.z)
        def _():
            hold[h, k, level] = total[...].astype(bf)
            along(h, k, level, 1, level).start()

        @pl.when(level < place.z)
        def _():
            hold[h, k, level] = total[...].astype(bf)
            along(h, k, level, 0, down_slot(level)).start()

        @pl.when((level == place.z) & (k == 1))
        def _():
            first_out[h] = total[...].astype(bf)
            first(h).start()

        @pl.when((level == place.z) & (k == 0))
        def _():
            out[h] = total[...]

    def step(code):
        kind, which = code // 32, code % 32
        h, k, n = which % 2, which // 2 % 2, which // 16
        turn = which // 4 % 4
        level = turn + upper * (3 - 2 * turn)
        o = place.chip(h, k, level)

        @pl.when(kind == 0)
        def _():
            move(which // 2 % 2, h, mine, FIRST, place.first(h)).start()

        @pl.when(kind == 1)
        def _():
            @pl.when((k == 1) | (level != place.z))
            def _():
                arrived(n, h, o, False)

            move(n, h, o, LAST, place.last(h)).start()
            move(n, h, o, SIB, place.sibling).start()

        @pl.when((kind == 2) | (kind == 3))
        def _():
            down = (kind + upper) % 2
            piece = gathered.at[2 * o + core, h, n]
            pltpu.make_async_remote_copy(
                src_ref=piece, dst_ref=piece, send_sem=send.at[down, n, h, o], recv_sem=recv.at[0, n, h, o],
                device_id=(me + 8 - 16 * down,), device_id_type=MESH).start()

        @pl.when(kind == 4)
        def _():
            away = place.chip_at(1 - h + h * k, k + h - h * k, level)
            arrived(n, h, away, False)
            move(n, h, away, SIB, place.sibling).start()

        dx, dy = which % 2, which // 2 % 2

        @pl.when((kind == 5) | (kind == 6))
        def _():
            compute(place.chip_at(dx, dy, level), which // 16, kind == 5)

        @pl.when((kind == 7) | (kind == 8))
        def _():
            pair_sum(dx, dy, level, which // 16, kind == 7)

        @pl.when(kind == 9)
        def _():
            column_sum(h, k, level)

    @pl.loop(0, len(OUTER_STEPS))
    def _(i):
        word = 0
        for at, (outer_word, inner_word) in enumerate(zip(OUTER_STEPS, INNER_STEPS)):
            word = jnp.where(i == at, jnp.where(inner == 0, outer_word, inner_word), word)

        def one(_, rest):
            step(rest % 512)
            return rest // 512

        lax.fori_loop(0, 3, one, word)

    for h in range(2):
        first(h).wait_recv()
        out[h] += first_in[h].astype(f32)

    for n, h in pieces:
        move(n, h, mine, FIRST, place.first(h)).wait_send()
        spread(n, h, mine, place.z, done)
        spread(n, h, place.chip(h, 1, place.z), place.z, done)
    for h in range(2):
        first(h).wait_send()
    for slot in range(2):
        to_sibling(slot).wait_send()
        keep_part(0, slot).wait()

    @pl.loop(0, CHIPS)
    def _(t):
        h, k = t % 2, t // 2 % 2

        @pl.when(t < CHIPS - 4)
        def _():
            level = place.level(1 + t // 4)
            for n in range(2):
                spread(n, h, place.chip(h, k, level), level, done)

        dx, dy = t % 2, t // 2 % 2
        o = place.chip_at(dx, dy, t // 4)
        for side, away in ((0, dx), (1, dy)):
            @pl.when(away == 1)
            def _():
                for n in range(2):
                    move(n, side, o, SIB, place.sibling).wait_send()

        level = t // 4
        across(h, k, level).wait_send()

        @pl.when(level > place.z)
        def _():
            along(h, k, level, 1, level).wait_send()

        @pl.when(level < place.z)
        def _():
            along(h, k, level, 0, down_slot(level)).wait_send()


def experts_pass(x, upstream, gate_w, up_w, down_w, coeff):
    rows, width = x.shape
    devices = coeff.shape[0]
    half = rows // 2
    bf, f32 = jnp.bfloat16, jnp.float32
    dma = pltpu.SemaphoreType.DMA
    vmem, anywhere = pl.BlockSpec(memory_space=pltpu.VMEM), pl.BlockSpec(memory_space=pl.ANY)
    piece = (half, width)
    grad, part, _ = pl.pallas_call(
        functools.partial(experts_kernel, rows),
        out_shape=(
            jax.ShapeDtypeStruct((2,) + piece, f32),
            jax.ShapeDtypeStruct((CHIPS, 2) + piece, bf),
            jax.ShapeDtypeStruct((devices, 2, 2) + piece, bf),
        ),
        in_specs=[anywhere, anywhere, vmem, vmem, vmem, vmem],
        out_specs=(vmem, anywhere, anywhere),
        scratch_shapes=[
            pltpu.VMEM((2, 2, 2) + piece, bf),
            pltpu.VMEM((2, 2) + piece, bf),
            pltpu.VMEM((2, 2, 2, 2) + piece, bf),
            pltpu.VMEM((2, 2, 2) + piece, bf),
            pltpu.VMEM((2, 2, LEVELS) + piece, bf),
            pltpu.VMEM((2, 2, LEVELS) + piece, bf),
            pltpu.VMEM((2, 2, LEVELS) + piece, bf),
            pltpu.VMEM((2, 2, LEVELS + 1) + piece, bf),
            pltpu.VMEM((2,) + piece, bf),
            pltpu.VMEM((2,) + piece, bf),
            pltpu.VMEM(piece, f32),
            dma((2, 2)), dma, dma((2,)), dma((5, 2, 2, CHIPS)), dma((2, 2, 2, CHIPS)), dma((2,)), dma((2,)),
            dma((2, 2, LEVELS)), dma((2, 2, LEVELS)),
            dma((2, 2, LEVELS)), dma((2, 2, LEVELS + 1)), dma((2,)), dma((2,)),
        ],
        compiler_params=pltpu.CompilerParams(has_side_effects=True, vmem_limit_bytes=56 << 20),
        name="experts",
    )(x, upstream, gate_w, up_w, down_w, coeff)
    return grad.reshape(rows, width), part


def front_kernel(rows, rank, picked, tokens, rows_gain, heads_w, downs, ups, routes, gates, out_w, near, far_turn,
                 query_gain, key_gain, ffn_gain, q_seg, k_seg,
                 middle, normed_ffn, normed, mixed, out_inner, weights, query_out, key_out, value_out,
                 query_proj, key_proj, inner_out, coeff_out, cosine, sine, out_all,
                 held, mixed_buf, pair, coeff, wo,
                 local_sem, send, recv, w_send, w_recv, pair_send, pair_recv, c_send, c_recv, m_send, m_recv, m_local,
                 g_send, g_recv, keep_sem):
    place = Place()
    f32, bf = jnp.float32, jnp.bfloat16
    me, core = place.me, place.core
    group = held.shape[0]
    base, p = me // group * group, me % group
    other = (me + group) % (2 * group)
    other_base = group - base
    half = rows // 2
    depth = weights.shape[1]
    wide = 3 * 128
    z = place.z % 2
    across_z = me + 8 - 16 * z
    chip = p // 2

    FIRST, ALONG, LAST, SIB = range(4)

    def chip_at(h, k, far):
        flip = place.chip(h, k, 0)
        zz = z + far * (1 - 2 * z)
        return zz * 4 + flip

    def move(h, o, kind, target):
        piece = held.at[2 * o + core, pl.ds(h * half, half)]
        return pltpu.make_async_remote_copy(
            src_ref=piece, dst_ref=piece, send_sem=send.at[kind, h, o],
            recv_sem=recv.at[1 if kind == SIB else 0, h, o], device_id=(target,), device_id_type=MESH)

    def arrived(h, o, sibling):
        piece = held.at[2 * o + (1 - core if sibling else core), pl.ds(h * half, half)]
        pltpu.make_async_remote_copy(
            src_ref=piece, dst_ref=piece, send_sem=send.at[SIB, h, o],
            recv_sem=recv.at[1 if sibling else 0, h, o], device_id=(place.sibling,), device_id_type=MESH).wait_recv()

    def to_heads(q):
        return pltpu.make_async_remote_copy(
            src_ref=heads_w.at[q % group], dst_ref=weights.at[me, :, pl.ds(0, wide)], send_sem=w_send.at[q],
            recv_sem=w_recv.at[me], device_id=(q,), device_id_type=MESH)

    def to_expert(q):
        return pltpu.make_async_remote_copy(
            src_ref=coeff.at[q // 2], dst_ref=coeff_out.at[me], send_sem=c_send.at[q],
            recv_sem=c_recv.at[me], device_id=(q,), device_id_type=MESH)

    def pair_over(q, side):
        row = (me + side * group) % (2 * group)
        piece = weights.at[row, :, pl.ds(wide, 128)]
        return pltpu.make_async_remote_copy(
            src_ref=piece, dst_ref=piece, send_sem=pair_send.at[side, q],
            recv_sem=pair_recv.at[row], device_id=(base + q,), device_id_type=MESH)

    pair_other = pltpu.make_async_remote_copy(
        src_ref=pair.at[other // group], dst_ref=weights.at[me, :, pl.ds(wide, 128)], send_sem=pair_send.at[2, 0],
        recv_sem=pair_recv.at[me], device_id=(other,), device_id_type=MESH)
    UP, DOWN, G_LAST, G_SIB, G_FIRST = range(5)

    def g_move(h, o, kind, target):
        piece = wo.at[2 * o + core, h]
        return pltpu.make_async_remote_copy(
            src_ref=piece, dst_ref=piece, send_sem=g_send.at[kind, h, o],
            recv_sem=g_recv.at[1 if kind == G_SIB else 0, h, o], device_id=(target,), device_id_type=MESH)

    def g_arrived(h, o, sibling):
        piece = wo.at[2 * o + (1 - core if sibling else core), h]
        pltpu.make_async_remote_copy(
            src_ref=piece, dst_ref=piece, send_sem=g_send.at[G_SIB, h, o],
            recv_sem=g_recv.at[1 if sibling else 0, h, o], device_id=(place.sibling,), device_id_type=MESH).wait_recv()

    def g_column(h, o, level, act):
        @pl.when((level <= place.z) & (place.z < LEVELS - 1))
        def _():
            act(g_move(h, o, UP, me + 8))

        @pl.when((level >= place.z) & (place.z > 0))
        def _():
            act(g_move(h, o, DOWN, me - 8))

    def g_spread(h, o, level, act):
        g_column(h, o, level, act)
        act(g_move(h, o, G_LAST, place.last(h)))
        act(g_move(h, o, G_SIB, place.sibling))

    def g_level(t):
        level, h, k = place.level(1 + t // 4), t % 2, t // 2 % 2
        o = place.chip(h, k, level)
        g_arrived(h, o, False)
        g_spread(h, o, level, start)

    def g_cross(q):
        dx, dy = q % 2, q // 2 % 2
        o = place.chip_at(dx, dy, place.level(q // 4))
        for h, away in ((0, dx), (1, dy)):
            @pl.when(away == 1)
            def _():
                g_arrived(h, o, False)
                g_move(h, o, G_SIB, place.sibling).start()

    start = lambda copy: copy.start()
    done = lambda copy: copy.wait_send()
    own_chip = me // 2
    own_copies = [
        pltpu.make_async_copy(heads_w.at[p], weights.at[me, :, pl.ds(0, wide)], local_sem.at[0]),
        pltpu.make_async_copy(out_w.at[pl.ds(0, depth // 2)], wo.at[me, 0], local_sem.at[1]),
        pltpu.make_async_copy(out_w.at[pl.ds(depth // 2, depth // 2)], wo.at[me, 1], local_sem.at[2]),
    ]
    for copy in own_copies:
        copy.start()
    ours = tokens[...].astype(f32)
    low = (ours * lax.rsqrt(jnp.mean(ours * ours, axis=-1, keepdims=True) + epsilon) * rows_gain[...]).astype(bf)
    held[p] = low
    normed[...] = low
    for h in range(2):
        move(h, chip, FIRST, place.first(h)).start()
        move(h, chip, ALONG, across_z).start()
    for h in range(2):
        move(h, chip, LAST, place.last(h)).start()
        move(h, chip, SIB, place.sibling).start()

    for s in range(2):
        down, up = downs[picked[s]].astype(f32), ups[picked[s]].astype(f32)
        down = jnp.concatenate([down[j] for j in range(4)], axis=1)
        up = jnp.concatenate([up[j] for j in range(4)], axis=0).T
        pair[s] = jnp.concatenate([down, up], axis=1).astype(bf)
    weights[me, :, wide:] = pair[me // group]
    pair_other.start()

    @pl.loop(0, group)
    def _(i):
        to_heads(other_base + (p + i) % group).start()

    lane = lax.broadcasted_iota(jnp.int32, (rows, 128), 1)
    gate = jnp.zeros((rows, 128), f32)
    for k in range(routes.shape[1]):
        gate += jnp.where(lane == routes[:, k : k + 1], gates[:, k : k + 1], 0.0)
    gate = gate.T
    for e in range(coeff.shape[0]):
        coeff[e] = gate[e : e + 1]
    coeff_out[me] = coeff[me // 2]

    @pl.loop(1, group)
    def _(i):
        pair_over((p + i) % group, 0).start()
        to_heads(base + (p + i) % group).start()

    @pl.loop(1, 2 * group)
    def _(i):
        to_expert((me + i) % (2 * group)).start()

    for copy in own_copies[1:]:
        copy.wait()
    for h in range(2):
        g_column(h, own_chip, place.z, start)
        g_move(h, own_chip, G_FIRST, place.first(h)).start()
    for h in range(2):
        g_move(h, own_chip, G_LAST, place.last(h)).start()
        g_move(h, own_chip, G_SIB, place.sibling).start()

    pltpu.make_async_remote_copy(
        src_ref=pair.at[0], dst_ref=weights.at[other, :, pl.ds(wide, 128)], send_sem=pair_send.at[2, 0],
        recv_sem=pair_recv.at[other], device_id=(other,), device_id_type=MESH).wait_recv()

    @pl.loop(1, group)
    def _(i):
        pair_over((p + i) % group, 1).start()

    for h in range(2):
        o = chip_at(h, 1, 0)
        arrived(h, o, False)
        move(h, o, ALONG, across_z).start()
        move(h, o, LAST, place.last(h)).start()
        move(h, o, SIB, place.sibling).start()
    for k in range(2):
        for h in range(2):
            o = chip_at(h, k, 1)
            arrived(h, o, False)
            move(h, o, LAST, place.last(h)).start()
            move(h, o, SIB, place.sibling).start()
    for h in range(2):
        o = place.chip(h, 1, place.z)
        g_arrived(h, o, False)
        g_spread(h, o, place.z, start)

    @pl.loop(0, group)
    def _(i):
        at = pl.ds(pl.multiple_of(i * rows, rows), rows)
        c, s = far_turn[0, pl.ds(i, 1)], far_turn[1, pl.ds(i, 1)]
        cosine[at] = c * near[0] - s * near[1]
        turn = s * near[0] + c * near[1]
        sine[at] = jnp.where(lane < 64, -turn, turn)

    for far in range(2):
        for k in range(2):
            for h in range(2):
                dx, dy = (1, k) if h == 0 else (k, 1)
                o = (z + far * (1 - 2 * z)) * 4 + place.chip_at(dx, dy, 0)
                arrived(h, o, False)
                move(h, o, SIB, place.sibling).start()
    own_copies[0].wait()

    @pl.loop(0, 4)
    def _(t):
        g_level(t)


    @pl.loop(1, 2 * group)
    def _(i):
        q = (me + i) % (2 * group)
        pltpu.make_async_remote_copy(
            src_ref=heads_w.at[0], dst_ref=weights.at[q, :, pl.ds(0, wide)], send_sem=w_send.at[q],
            recv_sem=w_recv.at[q], device_id=(q,), device_id_type=MESH).wait_recv()
        pltpu.make_async_remote_copy(
            src_ref=coeff.at[0], dst_ref=coeff_out.at[q], send_sem=c_send.at[q],
            recv_sem=c_recv.at[q], device_id=(q,), device_id_type=MESH).wait_recv()

        @pl.when(q != other)
        def _():
            pltpu.make_async_remote_copy(
                src_ref=pair.at[0], dst_ref=weights.at[q, :, pl.ds(wide, 128)], send_sem=pair_send.at[2, 0],
                recv_sem=pair_recv.at[q], device_id=(other,), device_id_type=MESH).wait_recv()

    @pl.loop(0, group // 2)
    def _(o):
        for h in range(2):
            arrived(h, o, True)

    @pl.loop(4, 8)
    def _(t):
        g_level(t)

    span = 2 * rows
    seq = group * rows
    up_own = weights[pl.ds(2 * p, 2), :, pl.ds(wide, 128)].reshape(2 * depth, 128)
    up_own = pltpu.roll(up_own.astype(f32), 64, 1).astype(bf)
    flip = (((1,), (1,)), ((), ()))
    scale = 1.0 / math.sqrt(128)

    @pl.loop(0, group // 2)
    def _(b):
        at = pl.ds(pl.multiple_of(b * span, span), span)
        x = held[pl.ds(2 * b, 2)].reshape(span, -1)
        acc = jnp.dot(x, weights[...].reshape(2 * group * depth, wide + 128), preferred_element_type=f32)
        inner = acc[:, wide:].astype(bf)
        inner_out[at] = inner
        owner = lax.broadcasted_iota(jnp.int32, inner.shape, 1) // rank

        def projected(j):
            low = jnp.where(owner == j, inner.astype(f32), 0.0).astype(bf)
            return acc[:, j * 128 : (j + 1) * 128] + lax.dot_general(low, up_own, flip, preferred_element_type=f32)

        for j, (gain, raw, rot) in enumerate(((query_gain, query_proj, query_out), (key_gain, key_proj, key_out))):
            value = projected(j)
            raw[at] = value
            unit = value * lax.rsqrt(jnp.mean(value * value, axis=-1, keepdims=True) + epsilon) * gain[...]
            rot[at] = (unit * cosine[at] + pltpu.roll(unit, 64, 1) * sine[at]).astype(bf)
        value_out[at] = projected(2).astype(bf)

        @pl.when(b % 2 == 0)
        def _():
            g_level(8 + b // 2)

    def to_token(q):
        return pltpu.make_async_remote_copy(
            src_ref=mixed_buf.at[q], dst_ref=mixed.at[:, pl.ds(p * 128, 128)], send_sem=m_send.at[q],
            recv_sem=m_recv.at[p], device_id=(base + q,), device_id_type=MESH)

    keep = pltpu.make_async_copy(mixed_buf.at[p], mixed.at[:, pl.ds(p * 128, 128)], m_local)

    @pl.loop(0, group // 2)
    def _(b):
        at = pl.ds(pl.multiple_of(b * span, span), span)
        scores = lax.dot_general(query_out[at], key_out[...], flip, preferred_element_type=f32)
        weight = jnp.where(q_seg[at] == k_seg[...], jnp.exp2(scores * (scale * math.log2(math.e))), 0.0)
        total = jnp.sum(weight, axis=-1, keepdims=True)
        value = jnp.dot(weight.astype(bf), value_out[...], preferred_element_type=f32) / total
        mixed_buf[pl.ds(2 * b, 2)] = value.astype(bf).reshape(2, rows, 128)
        for side in range(2):
            q = 2 * b + side

            @pl.when(q != p)
            def _():
                to_token(q).start()

            @pl.when(q == p)
            def _():
                keep.start()

        g_cross(2 * b)
        g_cross(2 * b + 1)

    keep.wait()

    @pl.loop(1, group)
    def _(i):
        q = (p + i) % group
        pltpu.make_async_remote_copy(
            src_ref=mixed_buf.at[q], dst_ref=mixed.at[:, pl.ds(q * 128, 128)], send_sem=m_send.at[q],
            recv_sem=m_recv.at[q], device_id=(base + q,), device_id_type=MESH).wait_recv()

    @pl.loop(0, CHIPS)
    def _(o):
        for h in range(2):
            g_arrived(h, o, True)

    keep_out = pltpu.make_async_copy(wo, out_all, keep_sem)
    keep_out.start()
    ours = mixed[...]
    matrix = weights[:, :, wide:].reshape(2 * group * depth, 128)
    lane = lax.broadcasted_iota(jnp.int32, (rows, 128), 1)
    inner = jnp.dot(ours, matrix, preferred_element_type=f32)
    inner = jnp.where(lane // rank == 3, inner, 0.0).astype(bf)
    out_inner[...] = inner
    shifted = pltpu.roll(inner.astype(f32), 64, 1).astype(bf)
    total = tokens[...].astype(f32) + jnp.dot(ours, wo[...].reshape(2 * group * depth, -1), preferred_element_type=f32)
    total = total + lax.dot_general(shifted, matrix, flip, preferred_element_type=f32)
    middle[...] = total
    unit = total * lax.rsqrt(jnp.mean(total * total, axis=-1, keepdims=True) + epsilon)
    normed_ffn[...] = (unit * ffn_gain[...]).astype(bf)

    keep_out.wait()
    for h in range(2):
        g_move(h, own_chip, G_FIRST, place.first(h)).wait_send()
        g_spread(h, own_chip, place.z, done)
        g_spread(h, place.chip(h, 1, place.z), place.z, done)

    @pl.loop(0, CHIPS)
    def _(t):
        @pl.when(t < CHIPS - 4)
        def _():
            level, h, k = place.level(1 + t // 4), t % 2, t // 2 % 2
            g_spread(h, place.chip(h, k, level), level, done)

        dx, dy = t % 2, t // 2 % 2
        o = place.chip_at(dx, dy, place.level(t // 4))
        for h, away in ((0, dx), (1, dy)):
            @pl.when(away == 1)
            def _():
                g_move(h, o, G_SIB, place.sibling).wait_send()

    pair_other.wait_send()
    for h in range(2):
        move(h, chip, FIRST, place.first(h)).wait_send()
        for far in range(2):
            for k in range(2):
                o = chip_at(h, k, far)
                if far == 0:
                    move(h, o, ALONG, across_z).wait_send()
                move(h, o, LAST, place.last(h)).wait_send()
                move(h, o, SIB, place.sibling).wait_send()
                dx, dy = (1, k) if h == 0 else (k, 1)
                o = (z + far * (1 - 2 * z)) * 4 + place.chip_at(dx, dy, 0)
                move(h, o, SIB, place.sibling).wait_send()

    @pl.loop(1, group)
    def _(i):
        q = (p + i) % group
        pair_over(q, 0).wait_send()
        pair_over(q, 1).wait_send()
        to_token(q).wait_send()

    @pl.loop(1, 2 * group)
    def _(i):
        q = (me + i) % (2 * group)
        to_heads(q).wait_send()
        to_expert(q).wait_send()


def turn_tables(rows, group):
    frequency = rope_base ** (-(np.arange(64, dtype=np.float32) * np.float32(2.0 / 128)))
    frequency = np.concatenate([frequency, frequency]).astype(np.float64)
    tables = []
    for positions in (np.arange(rows), np.arange(group) * rows):
        angle = positions[:, None] * frequency[None, :]
        tables.append(np.stack([np.cos(angle), np.sin(angle)]).astype(np.float32))
    return tables


def front(picked, tokens, rows_gain, heads_w, downs, ups, routes, gates, out_w, query_gain, key_gain, ffn_gain, q_seg, k_seg):
    rows, width = tokens.shape
    group, depth = heads_w.shape[0], heads_w.shape[1]
    rank = downs.shape[3]
    devices, seq = 2 * group, rows * group
    bf, f32 = jnp.bfloat16, jnp.float32
    dma = pltpu.SemaphoreType.DMA
    vmem, anywhere = pl.BlockSpec(memory_space=pltpu.VMEM), pl.BlockSpec(memory_space=pl.ANY)
    head = jax.ShapeDtypeStruct((seq, 128), bf)
    raw = jax.ShapeDtypeStruct((seq, 128), f32)
    mine = jax.ShapeDtypeStruct((rows, width), bf)
    near, far_turn = turn_tables(rows, group)
    return pl.pallas_call(
        functools.partial(front_kernel, rows, rank),
        out_shape=(
            jax.ShapeDtypeStruct((rows, width), f32), mine, mine, mine,
            jax.ShapeDtypeStruct((rows, 128), bf),
            jax.ShapeDtypeStruct((devices, depth, 512), bf),
            head, head, head, raw, raw, head,
            jax.ShapeDtypeStruct((devices, 1, rows), f32),
            raw, raw,
            jax.ShapeDtypeStruct((devices, 2, depth // 2, width), bf),
        ),
        in_specs=[pl.BlockSpec(memory_space=pltpu.SMEM), vmem, vmem, anywhere, vmem, vmem, vmem, vmem, anywhere]
        + [vmem] * 7,
        out_specs=(vmem,) * 15 + (anywhere,),
        scratch_shapes=[
            pltpu.VMEM((group, rows, width), bf),
            pltpu.VMEM((group, rows, 128), bf),
            pltpu.VMEM((2, depth, 128), bf),
            pltpu.VMEM((group, 1, rows), f32),
            pltpu.VMEM((devices, 2, depth // 2, width), bf),
            dma((3,)), dma((4, 2, group // 2)), dma((2, 2, group // 2)),
            dma((devices,)), dma((devices,)), dma((3, group)), dma((devices,)),
            dma((devices,)), dma((devices,)), dma((group,)), dma((group,)), dma,
            dma((5, 2, CHIPS)), dma((2, 2, CHIPS)), dma,
        ],
        compiler_params=pltpu.CompilerParams(has_side_effects=True, vmem_limit_bytes=60 << 20),
        name="front",
    )(picked, tokens, rows_gain, heads_w, downs, ups, routes, gates, out_w, jnp.asarray(near), jnp.asarray(far_turn),
      query_gain, key_gain, ffn_gain, q_seg, k_seg)


def back_kernel(rows, rank, grad_mixed, part, weights, query, key, value, query_proj, key_proj, inner, cosine, sine,
                query_gain, key_gain, q_seg, k_seg, rows_in, normed, rows_gain, grad_middle, middle, early,
                grad_rows, output, factors, out, up_terms, part_sum, late, early_in, late_in, owned,
                e_send, e_recv, l_send, l_recv, f_send, f_recv, t_local,
                grads, key_t, grad_key, grad_value, heads, result, sib, cross_out, cross_in, z_out, z_in, first_out, first_in,
                held, part_in, part_z, part_total, part_first_out, part_first_in,
                held_sem, pc_send, pc_recv, pz_send, pz_recv, pf_send, pf_recv,
                a_send, a_recv, a_local, sib_send, sib_recv, cross_send, cross_recv, z_send, z_recv, first_send, first_recv):
    place = Place()
    f32, bf = jnp.float32, jnp.bfloat16
    me, core = place.me, place.core
    group = grads.shape[0]
    depth = weights.shape[1]
    base, p = me // group * group, me % group
    half, span, seq = rows // 2, 2 * rows, rows * group
    width = out.shape[1] - 128
    z = place.z % 2
    across_z = me + 8 - 16 * z
    flip = (((1,), (1,)), ((), ()))
    tall = (((0,), (0,)), ((), ()))
    scale = 1.0 / math.sqrt(128)

    def keep_piece(h, k, level):
        return pltpu.make_async_copy(part.at[place.chip(h, k, level), h], held.at[h, k, level], held_sem.at[h, k, level])

    def part_across(h, k, level):
        dx, dy = (1, k) if h == 0 else (k, 1)
        return pltpu.make_async_remote_copy(
            src_ref=part.at[place.chip_at(dx, dy, level), h], dst_ref=part_in.at[h, k, level],
            send_sem=pc_send.at[h, k, level], recv_sem=pc_recv.at[h, k, level],
            device_id=(place.last(h),), device_id_type=MESH)

    def crossed(h, k, level):
        return pltpu.make_async_remote_copy(
            src_ref=held.at[h, k, level], dst_ref=part_in.at[h, k, level], send_sem=pc_send.at[h, k, level],
            recv_sem=pc_recv.at[h, k, level], device_id=(place.last(h),), device_id_type=MESH)

    def part_along(h, k, level, up, slot):
        return pltpu.make_async_remote_copy(
            src_ref=held.at[h, k, level], dst_ref=part_z.at[h, k, slot], send_sem=pz_send.at[h, k, level],
            recv_sem=pz_recv.at[h, k, slot], device_id=(me - 8 + 16 * up,), device_id_type=MESH)

    def part_first(h):
        return pltpu.make_async_remote_copy(
            src_ref=part_first_out.at[h], dst_ref=part_first_in.at[h], send_sem=pf_send.at[h],
            recv_sem=pf_recv.at[h], device_id=(place.first(h),), device_id_type=MESH)

    def down_slot(level):
        ends = 1 - jnp.minimum(jnp.abs(level - (place.z - 1)), 1)
        return level + ends * (LEVELS - level)

    def part_event(e):
        h, k, level = e % 2, e // 2 % 2, place.level(3 - e // 4)
        keep_piece(h, k, level).wait()
        crossed(h, k, level).wait_recv()
        total = held[h, k, level].astype(f32) + part_in[h, k, level].astype(f32)
        part_total[...] = total

        @pl.when((level >= place.z) & (place.z > 0))
        def _():
            part_along(h, k, level, 1, level).wait_recv()
            part_total[...] += part_z[h, k, level].astype(f32)

        @pl.when((level < place.z) & (place.z < LEVELS - 1))
        def _():
            part_along(h, k, level, 0, level).wait_recv()
            part_total[...] += part_z[h, k, level].astype(f32)

        @pl.when((level == place.z) & (place.z < LEVELS - 1))
        def _():
            part_along(h, k, level, 0, LEVELS).wait_recv()
            part_total[...] += part_z[h, k, LEVELS].astype(f32)

        @pl.when(level > place.z)
        def _():
            held[h, k, level] = part_total[...].astype(bf)
            part_along(h, k, level, 1, level).start()

        @pl.when(level < place.z)
        def _():
            held[h, k, level] = part_total[...].astype(bf)
            part_along(h, k, level, 0, down_slot(level)).start()

        @pl.when((level == place.z) & (k == 1))
        def _():
            part_first_out[h] = part_total[...].astype(bf)
            part_first(h).start()

        @pl.when((level == place.z) & (k == 0))
        def _():
            part_sum[h] = part_total[...]

    def to_head(q):
        return pltpu.make_async_remote_copy(
            src_ref=grad_mixed.at[:, pl.ds(q * 128, 128)], dst_ref=grads.at[p], send_sem=a_send.at[q],
            recv_sem=a_recv.at[p], device_id=(base + q,), device_id_type=MESH)

    def from_token(q):
        return pltpu.make_async_remote_copy(
            src_ref=grad_mixed.at[:, pl.ds(q * 128, 128)], dst_ref=grads.at[q], send_sem=a_send.at[q],
            recv_sem=a_recv.at[q], device_id=(base + q,), device_id_type=MESH)

    keep = pltpu.make_async_copy(grad_mixed.at[:, pl.ds(p * 128, 128)], grads.at[p], a_local)
    keep.start()

    def early_to(q, frm):
        return pltpu.make_async_remote_copy(
            src_ref=early.at[:, pl.ds(q * 128, 128)], dst_ref=early_in.at[frm], send_sem=e_send.at[q],
            recv_sem=e_recv.at[frm], device_id=(base + q,), device_id_type=MESH)

    def late_to(q, frm):
        return pltpu.make_async_remote_copy(
            src_ref=late.at[:, pl.ds(q * 128, 128)], dst_ref=late_in.at[frm], send_sem=l_send.at[q],
            recv_sem=l_recv.at[frm], device_id=(base + q,), device_id_type=MESH)

    def to_owner(side, q, frm):
        return pltpu.make_async_remote_copy(
            src_ref=owned, dst_ref=factors.at[frm], send_sem=f_send.at[side],
            recv_sem=f_recv.at[frm], device_id=(q,), device_id_type=MESH)

    early_keep = pltpu.make_async_copy(early.at[:, pl.ds(p * 128, 128)], early_in.at[p], t_local.at[0])
    late_keep = pltpu.make_async_copy(late.at[:, pl.ds(p * 128, 128)], late_in.at[p], t_local.at[1])
    owned_keep = pltpu.make_async_copy(owned, factors.at[me // group], t_local.at[2])
    early_keep.start()

    @pl.loop(1, group)
    def _(i):
        to_head((p + i) % group).start()

    @pl.loop(1, group)
    def _(i):
        early_to((p + i) % group, p).start()

    @pl.loop(0, 4)
    def _(i):
        level = place.level(3 - i)
        for k in range(2):
            for h in range(2):
                part_across(h, k, level).start()
                keep_piece(h, k, level).start()

    key_t[...] = key[...].astype(f32).T.astype(bf)
    grad_key[...] = jnp.zeros_like(grad_key)
    grad_value[...] = jnp.zeros_like(grad_value)
    keep.wait()

    def raw_grad(raw, gain, turned, at):
        back = turned * cosine[at] - pltpu.roll(turned, 64, 1) * sine[at]
        rows_ = raw[at]
        inverse = lax.rsqrt(jnp.mean(rows_ * rows_, axis=-1, keepdims=True) + epsilon)
        unit = rows_ * inverse
        scaled = back * gain[...]
        return (inverse * (scaled - unit * jnp.mean(scaled * unit, axis=-1, keepdims=True))).astype(bf)

    @pl.loop(0, group // 2)
    def _(b):
        at = pl.ds(pl.multiple_of(b * span, span), span)
        for side in range(2):
            q = 2 * b + side

            @pl.when(q != p)
            def _():
                from_token(q).wait_recv()

        ours = query[at]
        grad = grads[pl.ds(2 * b, 2)].reshape(span, 128)
        scores = lax.dot_general(key[...], ours, flip, preferred_element_type=f32)
        weight = jnp.where(k_seg[...] == q_seg[:, at], jnp.exp2(scores * (scale * math.log2(math.e))), 0.0)
        probs = weight * (1.0 / jnp.sum(weight, axis=0, keepdims=True))
        grad_probs = lax.dot_general(value[...], grad, flip, preferred_element_type=f32)
        mean = jnp.sum(probs * grad_probs, axis=0, keepdims=True)
        grad_scores = (probs * (grad_probs - mean)).astype(bf)
        grad_key[...] += jnp.dot(grad_scores, ours, preferred_element_type=f32)
        grad_value[...] += jnp.dot(probs.astype(bf), grad, preferred_element_type=f32)
        grad_query = jnp.dot(key_t[...], grad_scores, preferred_element_type=f32).T * scale
        heads[at, 0:128] = raw_grad(query_proj, query_gain, grad_query, at)

        @pl.when((b >= 2) & (b % 2 == 0))
        def _():
            part_event(b // 2 - 1)

    up_own = weights[pl.ds(2 * p, 2), :, 384:512].reshape(2 * depth, 128)
    up_own = pltpu.roll(up_own.astype(f32), 64, 1).astype(bf)

    @pl.loop(0, group // 2)
    def _(b):
        at = pl.ds(pl.multiple_of(b * span, span), span)
        heads[at, 128:256] = raw_grad(key_proj, key_gain, grad_key[at] * scale, at)
        heads[at, 256:384] = grad_value[at].astype(bf)

    def to_sibling(c):
        return pltpu.make_async_remote_copy(
            src_ref=result.at[c, 1 - core], dst_ref=sib.at[c], send_sem=sib_send.at[c],
            recv_sem=sib_recv.at[c], device_id=(place.sibling,), device_id_type=MESH)

    def across(h, k, far):
        return pltpu.make_async_remote_copy(
            src_ref=cross_out.at[h, k, far], dst_ref=cross_in.at[h, k, far], send_sem=cross_send.at[h, k, far],
            recv_sem=cross_recv.at[h, k, far], device_id=(place.last(h),), device_id_type=MESH)

    def along(h, k):
        return pltpu.make_async_remote_copy(
            src_ref=z_out.at[h, k], dst_ref=z_in.at[h, k], send_sem=z_send.at[h, k],
            recv_sem=z_recv.at[h, k], device_id=(across_z,), device_id_type=MESH)

    def first(h):
        return pltpu.make_async_remote_copy(
            src_ref=first_out.at[h], dst_ref=first_in.at[h], send_sem=first_send.at[h],
            recv_sem=first_recv.at[h], device_id=(place.first(h),), device_id_type=MESH)

    def both(c, h):
        part = pl.ds(h * half, half)
        return result[c, core, part].astype(f32) + sib[c, part].astype(f32)

    def pair_sum(c):
        far, dx, dy = 1 - c // 4, c % 2, c // 2 % 2
        to_sibling(c).wait_recv()
        for h, away, k in ((0, dx, dy), (1, dy, dx)):
            @pl.when(away == 1)
            def _():
                cross_out[h, k, far] = both(c, h).astype(bf)
                across(h, k, far).start()

    @pl.loop(0, group // 2 + 1)
    def _(c):
        @pl.when(c < group // 2)
        def _():
            far, dx, dy = 1 - c // 4, c % 2, c // 2 % 2
            o = (z + far * (1 - 2 * z)) * 4 + place.chip_at(dx, dy, 0)
            mine = heads[pl.ds(pl.multiple_of(o * span, span), span), :]
            matrix = weights[...].reshape(2 * group * depth, 512)[:, 0:384]
            part = lax.dot_general(mine, matrix, flip, preferred_element_type=f32)
            result[c, :, :, 0:width] = part.astype(bf).reshape(2, rows, width)
            low = jnp.zeros((span, 128), f32)
            owner = lax.broadcasted_iota(jnp.int32, low.shape, 1) // rank
            for j in range(3):
                term = jnp.dot(mine[:, j * 128 : (j + 1) * 128], up_own, preferred_element_type=f32)
                low = jnp.where(owner == j, term, low)
            result[c, :, :, width:] = low.astype(bf).reshape(2, rows, 128)
            to_sibling(c).start()

        @pl.when(c >= 1)
        def _():
            pair_sum(c - 1)

        @pl.when(c % 2 == 0)
        def _():
            part_event(3 + c // 2)

    @pl.loop(0, group // 2)
    def _(e):
        far, k, h = 1 - e // 4, e // 2 % 2, e % 2
        c = (1 - far) * 4 + k * (2 - h)
        across(h, k, far).wait_recv()
        total = both(c, h) + cross_in[h, k, far].astype(f32)

        @pl.when(far == 1)
        def _():
            z_out[h, k] = total.astype(bf)
            along(h, k).start()

        @pl.when(far == 0)
        def _():
            along(h, k).wait_recv()
            whole = total + z_in[h, k].astype(f32)

            @pl.when(k == 1)
            def _():
                first_out[h] = whole.astype(bf)
                first(h).start()

            @pl.when(k == 0)
            def _():
                out[pl.ds(h * half, half)] = whole

        @pl.when(e % 2 == 1)
        def _():
            part_event(8 + e // 2)

    owner = lax.broadcasted_iota(jnp.int32, (128, 128), 0) // rank
    up = jnp.zeros((128, 128), f32)
    for j in range(3):
        term = lax.dot_general(inner[...], heads[:, j * 128 : (j + 1) * 128], tall, preferred_element_type=f32)
        up = jnp.where(owner == j, term, up)
    up_terms[...] = up
    for h in range(2):
        first(h).wait_recv()
        out[pl.ds(h * half, half)] += first_in[h].astype(f32)
    lane = lax.broadcasted_iota(jnp.int32, (rows, 128), 1)
    grad_inner = jnp.where(lane < 3 * rank, out[:, width:], 0.0).astype(bf)
    late[...] = lax.dot_general(grad_inner, normed[...], tall, preferred_element_type=f32)[: 3 * rank]
    late_keep.start()

    @pl.loop(1, group)
    def _(i):
        late_to((p + i) % group, p).start()

    downs = weights[:, :, 384:512].reshape(2 * group * depth, 128)
    grad_normed = out[:, 0:width] + lax.dot_general(grad_inner, downs, flip, preferred_element_type=f32)
    ours = rows_in[...].astype(f32)
    inverse = lax.rsqrt(jnp.mean(ours * ours, axis=-1, keepdims=True) + epsilon)
    unit = ours * inverse
    scaled = grad_normed * rows_gain[...]
    grad = inverse * (scaled - unit * jnp.mean(scaled * unit, axis=-1, keepdims=True))
    grad_rows[...] = (grad_middle[...] + grad).astype(bf)
    early_keep.wait()
    late_keep.wait()

    @pl.loop(1, group)
    def _(i):
        q = (p + i) % group
        early_to(q, q).wait_recv()
        late_to(q, q).wait_recv()

    sums = jnp.sum(early_in[...], axis=0)
    owned[0 : 3 * rank] = jnp.sum(late_in[...], axis=0)
    owned[3 * rank : 4 * rank] = sums[:rank]
    owned[4 * rank : 7 * rank] = up_terms[0 : 3 * rank]
    owned[7 * rank : 8 * rank] = sums[rank:]
    for side in range(2):
        q = 2 * p + side

        @pl.when(q != me)
        def _():
            to_owner(side, q, me // group).start()

        @pl.when(q == me)
        def _():
            owned_keep.start()

    @pl.loop(12, CHIPS)
    def _(e):
        part_event(e)

    for h in range(2):
        part_first(h).wait_recv()
        side = pl.ds(h * half, half)
        output[side] = (middle[side] + part_sum[h] + part_first_in[h].astype(f32)).astype(bf)
    for s in range(2):
        source = s * group + me // 2

        @pl.when(source != me)
        def _():
            to_owner(0, source, s).wait_recv()

        @pl.when(source == me)
        def _():
            owned_keep.wait()

    @pl.loop(1, group)
    def _(i):
        to_head((p + i) % group).wait_send()
        early_to((p + i) % group, p).wait_send()
        late_to((p + i) % group, p).wait_send()

    for side in range(2):
        @pl.when(2 * p + side != me)
        def _():
            to_owner(side, 2 * p + side, me // group).wait_send()

    for h in range(2):
        part_first(h).wait_send()

    @pl.loop(0, 4)
    def _(level):
        for k in range(2):
            for h in range(2):
                part_across(h, k, level).wait_send()

                @pl.when(level > place.z)
                def _():
                    part_along(h, k, level, 1, level).wait_send()

                @pl.when(level < place.z)
                def _():
                    part_along(h, k, level, 0, down_slot(level)).wait_send()

    @pl.loop(0, group // 2)
    def _(c):
        to_sibling(c).wait_send()
        across(c % 2, c // 2 % 2, c // 4).wait_send()

        @pl.when(c < 4)
        def _():
            along(c % 2, c // 2).wait_send()

        @pl.when(c < 2)
        def _():
            first(c).wait_send()


def back(grad_mixed, part, weights, query, key, value, query_proj, key_proj, inner, cosine, sine,
         query_gain, key_gain, q_seg, k_seg, rows_in, normed, rows_gain, grad_middle, middle, early, rank):
    rows, width = grad_mixed.shape
    seq = query.shape[0]
    group = seq // rows
    bf, f32 = jnp.bfloat16, jnp.float32
    dma = pltpu.SemaphoreType.DMA
    vmem = pl.BlockSpec(memory_space=pltpu.VMEM)
    wide = width + 128
    piece = (rows // 2, wide)
    own = part.shape[2:]
    return pl.pallas_call(
        functools.partial(back_kernel, rows, rank),
        out_shape=(
            jax.ShapeDtypeStruct((rows, width), bf),
            jax.ShapeDtypeStruct((rows, width), bf),
            jax.ShapeDtypeStruct((2, 8 * rank, 128), f32),
        ),
        in_specs=[vmem, pl.BlockSpec(memory_space=pl.ANY)] + [vmem] * 19,
        out_specs=(vmem, vmem, vmem),
        scratch_shapes=[
            pltpu.VMEM((rows, wide), f32),
            pltpu.VMEM((128, 128), f32),
            pltpu.VMEM((2,) + own, f32),
            pltpu.VMEM((3 * rank, width), f32),
            pltpu.VMEM((group, 2 * rank, 128), f32),
            pltpu.VMEM((group, 3 * rank, 128), f32),
            pltpu.VMEM((8 * rank, 128), f32),
            dma((group,)), dma((group,)), dma((group,)), dma((group,)), dma((2,)), dma((2,)), dma((3,)),
            pltpu.VMEM((group, rows, 128), bf),
            pltpu.VMEM((128, seq), bf),
            pltpu.VMEM((seq, 128), f32),
            pltpu.VMEM((seq, 128), f32),
            pltpu.VMEM((seq, 384), bf),
            pltpu.VMEM((group // 2, 2, rows, wide), bf),
            pltpu.VMEM((group // 2, rows, wide), bf),
            pltpu.VMEM((2, 2, 2) + piece, bf),
            pltpu.VMEM((2, 2, 2) + piece, bf),
            pltpu.VMEM((2, 2) + piece, bf),
            pltpu.VMEM((2, 2) + piece, bf),
            pltpu.VMEM((2,) + piece, bf),
            pltpu.VMEM((2,) + piece, bf),
            pltpu.VMEM((2, 2, LEVELS) + own, bf),
            pltpu.VMEM((2, 2, LEVELS) + own, bf),
            pltpu.VMEM((2, 2, LEVELS + 1) + own, bf),
            pltpu.VMEM(own, f32),
            pltpu.VMEM((2,) + own, bf),
            pltpu.VMEM((2,) + own, bf),
            dma((2, 2, LEVELS)), dma((2, 2, LEVELS)), dma((2, 2, LEVELS)), dma((2, 2, LEVELS)), dma((2, 2, LEVELS + 1)),
            dma((2,)), dma((2,)),
            dma((group,)), dma((group,)), dma, dma((group // 2,)), dma((group // 2,)),
            dma((2, 2, 2)), dma((2, 2, 2)), dma((2, 2)), dma((2, 2)), dma((2,)), dma((2,)),
        ],
        compiler_params=pltpu.CompilerParams(has_side_effects=True, vmem_limit_bytes=63 << 20),
        name="back",
    )(grad_mixed, part, weights, query, key, value, query_proj, key_proj, inner, cosine, sine,
      query_gain, key_gain, q_seg, k_seg, rows_in, normed, rows_gain, grad_middle, middle, early)


def heads_plan(
    tokens,
    segments,
    routes,
    gates,
    sequence_adapter_index,
    attention_norm_gain,
    query_norm_gain,
    key_norm_gain,
    query_weight,
    key_weight,
    value_weight,
    output_weight,
    adapter_down_factors,
    adapter_up_factors,
    expert_norm_gain,
    expert_gate_weight,
    expert_up_weight,
    expert_down_weight,
    output_gradient,
):
    bf, f32 = jnp.bfloat16, jnp.float32
    devices = lax.axis_size("fsdp")
    rows_dev, width = tokens.shape
    group = SEQ_LEN // rows_dev
    seqs = segments.shape[0]
    rank = adapter_down_factors.shape[3]
    slots = 4 * rank
    own_rows = query_weight.shape[0]
    device = lax.axis_index("fsdp")
    sequence = device // group
    segment_row = pick(segments, sequence)
    attn_scale = attention_norm_gain.astype(f32)
    query_scale = query_norm_gain.astype(f32)
    key_scale = key_norm_gain.astype(f32)
    ffn_scale = expert_norm_gain.astype(f32)

    heads_w = jnp.concatenate(
        [
            weight.reshape(own_rows, group, HEAD_DIM)
            for weight in (query_weight, key_weight, value_weight)
        ],
        axis=2,
    ).transpose(1, 0, 2)
    head_gains = (query_scale.reshape(1, HEAD_DIM), key_scale.reshape(1, HEAD_DIM))
    tall, flat = segment_row.reshape(SEQ_LEN, 1), segment_row.reshape(1, SEQ_LEN)
    (middle, normed_ffn, normed, mixed, out_inner, head_weights, query, key, value, query_proj, key_proj, inner_all,
     coeff_own, *turns, output_matrix) = front(
        sequence_adapter_index, tokens, attn_scale.reshape(1, width), heads_w, adapter_down_factors,
        adapter_up_factors, routes, gates, output_weight, *head_gains, ffn_scale.reshape(1, width), tall, flat,
    )
    output_matrix = output_matrix.reshape(width, width)
    out_inner = out_inner[:, 3 * rank : slots]
    weights = head_weights.reshape(width, 4 * HEAD_DIM)
    down_out = weights[:, 3 * HEAD_DIM + 3 * rank : 3 * HEAD_DIM + slots]
    up_out = weights[:, 3 * HEAD_DIM + slots + 3 * rank :]

    slab_gate = expert_gate_weight[0]
    slab_up = expert_up_weight[0]
    slab_down = expert_down_weight[0]
    coeff_own = coeff_own.reshape(devices, rows_dev, 1)
    grad_ffn, part = experts_pass(normed_ffn, output_gradient, slab_gate, slab_up, slab_down, coeff_own)
    upstream = output_gradient.astype(f32)
    grad_middle = upstream + rms_back(middle, ffn_scale, grad_ffn)
    grad_attn = grad_middle.astype(bf)

    grad_inner_out = matmul(grad_attn, up_out).astype(bf)
    grad_mixed = matmul(grad_attn, output_matrix.T) + matmul(grad_inner_out, down_out.T)
    grad_mixed = grad_mixed.astype(bf)
    up_out_terms = matmul(out_inner.T, grad_attn)
    down_out_terms = matmul(grad_inner_out.T, mixed)

    grad_tokens, output, terms = back(
        grad_mixed, part, head_weights, query, key, value, query_proj, key_proj, inner_all,
        *turns, *head_gains, flat, tall,
        tokens, normed, attn_scale.reshape(1, width), grad_middle, middle,
        jnp.concatenate([down_out_terms, up_out_terms], axis=0), rank,
    )
    terms = lax.dynamic_slice_in_dim(terms, device % 2 * own_rows, own_rows, 2)
    selected = (
        jnp.arange(ADAPTER_COUNT, dtype=jnp.int32)[:, None] == sequence_adapter_index[None, :]
    ).astype(f32)
    spread = jnp.sum(selected[:, :, None, None] * terms[None], axis=1)
    spread = spread.reshape(ADAPTER_COUNT, 2, 4, rank, own_rows)
    grad_down = spread[:, 0].transpose(0, 1, 3, 2)
    grad_up = spread[:, 1]
    return (output, grad_tokens, grad_down, grad_up)


def solution(mesh):
    plan = heads_plan if mesh.shape["fsdp"] == LEVELS * 8 else shards
    in_specs = (
        P("fsdp", None),
        P(),
        P("fsdp", None),
        P("fsdp", None),
        P(),
        P(),
        P(),
        P(),
        P("fsdp", None),
        P("fsdp", None),
        P("fsdp", None),
        P("fsdp", None),
        P(None, None, "fsdp", None),
        P(None, None, None, "fsdp"),
        P(),
        P("fsdp", None, None),
        P("fsdp", None, None),
        P("fsdp", None, None),
        P("fsdp", None),
    )
    out_specs = (
        P("fsdp", None),
        P("fsdp", None),
        P(None, None, "fsdp", None),
        P(None, None, None, "fsdp"),
    )
    return jax.shard_map(plan, mesh=mesh, in_specs=in_specs, out_specs=out_specs, check_vma=False)
```

```python
import functools
import math

import jax
import jax.numpy as jnp
import numpy as np
from jax import lax
from jax.experimental import pallas as pl
from jax.experimental.pallas import tpu as pltpu
from jax.sharding import PartitionSpec as P

HEAD_DIM = 128
TOPK = 8
ADAPTER_COUNT = 8
SEQ_LEN = 2048


epsilon = 1e-06
rope_base = 50000.0


def from_partner(value, axis, distance):
    mask = 2**distance
    pairs = [(source, source ^ mask) for source in range(lax.axis_size(axis))]
    return lax.ppermute(value, axis, pairs)


def matmul(left, right):
    return jnp.dot(left, right, preferred_element_type=jnp.float32)


def rms_scale(rows, gain):
    return rows * lax.rsqrt(jnp.mean(rows * rows, axis=-1, keepdims=True) + epsilon) * gain


def rms_back(rows, gain, upstream):
    inverse = lax.rsqrt(jnp.mean(rows * rows, axis=-1, keepdims=True) + epsilon)
    unit = rows * inverse
    scaled = upstream * gain
    return inverse * (scaled - unit * jnp.mean(scaled * unit, axis=-1, keepdims=True))


def rope_tables(positions):
    half = HEAD_DIM // 2
    frequency = rope_base ** (-(jnp.arange(half, dtype=jnp.float32) * 2.0 / HEAD_DIM))
    angle = positions[:, None] * frequency[None, :]
    return (jnp.cos(angle)[:, None, :], jnp.sin(angle)[:, None, :])


def rotate(rows, cosine, sine):
    half = rows.shape[-1] // 2
    first = rows[..., :half]
    second = rows[..., half:]
    return jnp.concatenate(
        [first * cosine - second * sine, second * cosine + first * sine], axis=-1
    )


def rotate_back(upstream, cosine, sine):
    half = upstream.shape[-1] // 2
    first = upstream[..., :half]
    second = upstream[..., half:]
    return jnp.concatenate(
        [first * cosine + second * sine, second * cosine - first * sine], axis=-1
    )


def pick(table, index):
    return lax.dynamic_index_in_dim(table, index, 0, keepdims=False)


def shards(
    tokens,
    segments,
    routes,
    gates,
    sequence_adapter_index,
    attention_norm_gain,
    query_norm_gain,
    key_norm_gain,
    query_weight,
    key_weight,
    value_weight,
    output_weight,
    adapter_down_factors,
    adapter_up_factors,
    expert_norm_gain,
    expert_gate_weight,
    expert_up_weight,
    expert_down_weight,
    output_gradient,
):
    rows_dev = tokens.shape[0]
    width = tokens.shape[1]
    heads = width // HEAD_DIM
    group = SEQ_LEN // rows_dev
    level_list = group.bit_length() - 1
    device = lax.axis_index("fsdp")
    place = device % group
    sequence = device // group
    segment_row = pick(segments, sequence)
    own_segment = lax.dynamic_slice_in_dim(segment_row, place * rows_dev, rows_dev)
    adapter = pick(sequence_adapter_index, sequence)
    scale = 1.0 / math.sqrt(HEAD_DIM)
    cosine, sine = rope_tables(
        (place * rows_dev + jnp.arange(rows_dev, dtype=jnp.int32)).astype(jnp.float32)
    )
    attn_scale = attention_norm_gain.astype(jnp.float32)
    query_scale = query_norm_gain.astype(jnp.float32)
    key_scale = key_norm_gain.astype(jnp.float32)
    ffn_scale = expert_norm_gain.astype(jnp.float32)
    gathered = (
        lax.all_gather(query_weight, "fsdp", axis=0, tiled=True),
        lax.all_gather(key_weight, "fsdp", axis=0, tiled=True),
        lax.all_gather(value_weight, "fsdp", axis=0, tiled=True),
        lax.all_gather(output_weight, "fsdp", axis=0, tiled=True),
        lax.all_gather(adapter_down_factors, "fsdp", axis=2, tiled=True),
        lax.all_gather(adapter_up_factors, "fsdp", axis=3, tiled=True),
    )
    matrices = gathered[:4]
    down_own = pick(gathered[4], adapter)
    up_own = pick(gathered[5], adapter)

    def project(inputs, index):
        inner = matmul(inputs, down_own[index]).astype(jnp.bfloat16)
        return (matmul(inputs, matrices[index]) + matmul(inner, up_own[index]), inner)

    rows = tokens.astype(jnp.float32)
    normed = rms_scale(rows, attn_scale).astype(jnp.bfloat16)
    query_proj, query_inner = project(normed, 0)
    key_proj, key_inner = project(normed, 1)
    value_proj, value_inner = project(normed, 2)
    query_heads = query_proj.reshape(rows_dev, heads, HEAD_DIM)
    key_heads = key_proj.reshape(rows_dev, heads, HEAD_DIM)
    query_rot = rotate(rms_scale(query_heads, query_scale), cosine, sine).astype(jnp.bfloat16)
    key_rot = (
        rotate(rms_scale(key_heads, key_scale), cosine, sine)
        .astype(jnp.bfloat16)
        .reshape(rows_dev, width)
    )
    value_low = value_proj.astype(jnp.bfloat16)
    held_keys = key_rot
    held_values = value_low
    for level in range(level_list):
        other_keys, other_values = from_partner((held_keys, held_values), "fsdp", level)
        upper_bit = place // (1 << level) % 2 == 1
        held_keys = jnp.where(
            upper_bit,
            jnp.concatenate([other_keys, held_keys], axis=0),
            jnp.concatenate([held_keys, other_keys], axis=0),
        )
        held_values = jnp.where(
            upper_bit,
            jnp.concatenate([other_values, held_values], axis=0),
            jnp.concatenate([held_values, other_values], axis=0),
        )
    keys_all = held_keys.reshape(SEQ_LEN, heads, HEAD_DIM)
    values_all = held_values.reshape(SEQ_LEN, heads, HEAD_DIM)
    allowed = (own_segment[:, None] == segment_row[None, :])[None]

    def masked_scores():
        raw = (
            jnp.einsum("thd,shd->hts", query_rot, keys_all, preferred_element_type=jnp.float32)
            * scale
        )
        return jnp.where(allowed, raw, -1e30)

    scores = masked_scores()
    maximum = jnp.max(scores, axis=-1, keepdims=True)
    weights = jnp.exp(scores - maximum)
    total = jnp.sum(weights, axis=-1, keepdims=True)
    probs = weights / total
    log_total = maximum + jnp.log(total)
    mixed = jnp.einsum(
        "hts,shd->thd", probs.astype(jnp.bfloat16), values_all, preferred_element_type=jnp.float32
    )
    mixed = mixed.astype(jnp.bfloat16).reshape(rows_dev, width)
    attn_proj, out_inner = project(mixed, 3)
    middle = rows + attn_proj
    normed_ffn = rms_scale(middle, ffn_scale).astype(jnp.bfloat16)
    experts = lax.axis_size("fsdp") // 2
    capacity = 2 * rows_dev * TOPK // experts
    flat_routes = routes.reshape(-1)
    onehot = (flat_routes[:, None] == jnp.arange(experts, dtype=jnp.int32)[None, :]).astype(
        jnp.int32
    )
    slot = jnp.sum(jnp.cumsum(onehot, axis=0) * onehot, axis=1) - 1
    target = flat_routes * capacity + slot

    def spread(entries):
        buffer = jnp.zeros((experts * capacity, width), jnp.bfloat16).at[target].set(entries)
        buffer = buffer.reshape(experts, 1, capacity, width)
        return jnp.broadcast_to(buffer, (experts, 2, capacity, width)).reshape(
            2 * experts, capacity, width
        )

    def collect(returned):
        halves = returned.reshape(experts, 2, capacity, width).astype(jnp.float32)
        summed = (halves[:, 0] + halves[:, 1]).reshape(experts * capacity, width)
        return summed[target].reshape(rows_dev, TOPK, width)

    slab_gate = expert_gate_weight[0]
    slab_up = expert_up_weight[0]
    slab_down = expert_down_weight[0]
    dispatched = lax.all_to_all(
        spread(jnp.repeat(normed_ffn, TOPK, axis=0)),
        "fsdp",
        split_axis=0,
        concat_axis=0,
        tiled=True,
    )
    gate_part = jnp.einsum("scd,dh->sch", dispatched, slab_gate, preferred_element_type=jnp.float32)
    up_part = jnp.einsum("scd,dh->sch", dispatched, slab_up, preferred_element_type=jnp.float32)
    hidden = (jax.nn.silu(gate_part) * up_part).astype(jnp.bfloat16)
    produced = jnp.einsum(
        "sch,hd->scd", hidden, slab_down, preferred_element_type=jnp.float32
    ).astype(jnp.bfloat16)
    returned = lax.all_to_all(produced, "fsdp", split_axis=0, concat_axis=0, tiled=True)
    moe = jnp.sum(gates[:, :, None] * collect(returned), axis=1)
    output = (middle + moe).astype(jnp.bfloat16)
    upstream = output_gradient.astype(jnp.float32)
    grad_parts = (
        (gates[:, :, None] * upstream[:, None, :])
        .astype(jnp.bfloat16)
        .reshape(rows_dev * TOPK, width)
    )
    grad_sent = lax.all_to_all(spread(grad_parts), "fsdp", split_axis=0, concat_axis=0, tiled=True)
    grad_hidden = jnp.einsum(
        "scd,hd->sch", grad_sent, slab_down, preferred_element_type=jnp.float32
    )
    sigmoid = jax.nn.sigmoid(gate_part)
    grad_gate = (grad_hidden * up_part * sigmoid * (1.0 + gate_part * (1.0 - sigmoid))).astype(
        jnp.bfloat16
    )
    grad_up = (grad_hidden * gate_part * sigmoid).astype(jnp.bfloat16)
    grad_inputs = jnp.einsum(
        "sch,dh->scd", grad_gate, slab_gate, preferred_element_type=jnp.float32
    )
    grad_inputs = (
        grad_inputs
        + jnp.einsum("sch,dh->scd", grad_up, slab_up, preferred_element_type=jnp.float32)
    ).astype(jnp.bfloat16)
    grad_back = lax.all_to_all(grad_inputs, "fsdp", split_axis=0, concat_axis=0, tiled=True)
    grad_ffn = jnp.sum(collect(grad_back), axis=1)
    grad_middle = upstream + rms_back(middle, ffn_scale, grad_ffn)
    grad_attn = grad_middle.astype(jnp.bfloat16)
    regathered = (
        lax.all_gather(query_weight, "fsdp", axis=0, tiled=True),
        lax.all_gather(key_weight, "fsdp", axis=0, tiled=True),
        lax.all_gather(value_weight, "fsdp", axis=0, tiled=True),
        lax.all_gather(output_weight, "fsdp", axis=0, tiled=True),
        lax.all_gather(adapter_down_factors, "fsdp", axis=2, tiled=True),
        lax.all_gather(adapter_up_factors, "fsdp", axis=3, tiled=True),
    )
    back_matrices = regathered[:4]
    back_down = pick(regathered[4], adapter)
    back_up = pick(regathered[5], adapter)

    def project_back(inputs, inner, upstream_low, index):
        grad_inner = matmul(upstream_low, back_up[index].T).astype(jnp.bfloat16)
        grad_input = matmul(upstream_low, back_matrices[index].T) + matmul(
            grad_inner, back_down[index].T
        )
        return (grad_input, matmul(inputs.T, grad_inner), matmul(inner.T, upstream_low))

    grad_mixed_full, down_output, up_output = project_back(mixed, out_inner, grad_attn, 3)
    grad_mixed = grad_mixed_full.astype(jnp.bfloat16).reshape(rows_dev, heads, HEAD_DIM)
    probs = jnp.exp(masked_scores() - log_total)
    grad_probs = jnp.einsum(
        "thd,shd->hts", grad_mixed, values_all, preferred_element_type=jnp.float32
    )
    grad_scores = (
        probs * (grad_probs - jnp.sum(probs * grad_probs, axis=-1, keepdims=True))
    ).astype(jnp.bfloat16)
    grad_query = (
        jnp.einsum("hts,shd->thd", grad_scores, keys_all, preferred_element_type=jnp.float32)
        * scale
    )
    grad_keys_part = (
        jnp.einsum("hts,thd->shd", grad_scores, query_rot, preferred_element_type=jnp.float32)
        * scale
    )
    grad_keys_part = grad_keys_part.reshape(group, rows_dev, width)
    grad_values_part = jnp.einsum(
        "hts,thd->shd", probs.astype(jnp.bfloat16), grad_mixed, preferred_element_type=jnp.float32
    )
    grad_values_part = grad_values_part.reshape(group, rows_dev, width)
    for level in reversed(range(level_list)):
        size_half = 1 << level
        upper_bit = place // size_half % 2 == 1
        keep_keys = jnp.where(upper_bit, grad_keys_part[size_half:], grad_keys_part[:size_half])
        send_keys = jnp.where(upper_bit, grad_keys_part[:size_half], grad_keys_part[size_half:])
        keep_values = jnp.where(
            upper_bit, grad_values_part[size_half:], grad_values_part[:size_half]
        )
        send_values = jnp.where(
            upper_bit, grad_values_part[:size_half], grad_values_part[size_half:]
        )
        got_keys, got_values = (
            from_partner(send_keys.astype(jnp.bfloat16), "fsdp", level).astype(send_keys.dtype),
            from_partner(send_values.astype(jnp.bfloat16), "fsdp", level).astype(send_values.dtype),
        )
        grad_keys_part = keep_keys + got_keys
        grad_values_part = keep_values + got_values
    grad_keys = grad_keys_part[0]
    grad_values = grad_values_part[0]
    grad_value_proj = grad_values.astype(jnp.bfloat16)
    grad_key_proj = rms_back(
        key_heads,
        key_scale,
        rotate_back(grad_keys.reshape(rows_dev, heads, HEAD_DIM), cosine, sine),
    )
    grad_key_proj = grad_key_proj.reshape(rows_dev, width).astype(jnp.bfloat16)
    grad_query_proj = rms_back(query_heads, query_scale, rotate_back(grad_query, cosine, sine))
    grad_query_proj = grad_query_proj.reshape(rows_dev, width).astype(jnp.bfloat16)
    grad_from_query, down_query, up_query = project_back(normed, query_inner, grad_query_proj, 0)
    grad_from_key, down_key, up_key = project_back(normed, key_inner, grad_key_proj, 1)
    grad_from_value, down_value, up_value = project_back(normed, value_inner, grad_value_proj, 2)
    grad_normed = grad_from_query + grad_from_key + grad_from_value
    grad_tokens = (grad_middle + rms_back(rows, attn_scale, grad_normed)).astype(jnp.bfloat16)
    down_terms = jnp.stack([down_query, down_key, down_value, down_output])
    up_terms = jnp.stack([up_query, up_key, up_value, up_output])
    selected = (jnp.arange(ADAPTER_COUNT, dtype=jnp.int32) == adapter).astype(jnp.float32)[
        :, None, None, None
    ]
    grad_down, grad_up = (
        lax.psum_scatter(selected * down_terms[None], "fsdp", scatter_dimension=2, tiled=True),
        lax.psum_scatter(selected * up_terms[None], "fsdp", scatter_dimension=3, tiled=True),
    )
    return (output, grad_tokens, grad_down, grad_up)


epsilon = 1e-06
MESH = pl.DeviceIdType.MESH
LEVELS = 4
CHIPS = 16


def greet_all(me, devices):
    barrier = pltpu.get_barrier_semaphore()

    @pl.loop(1, devices)
    def _(i):
        pl.semaphore_signal(barrier, inc=1, device_id=((me + i) % devices,), device_id_type=MESH)


def segments_at(segs, sequence, at):
    row = segs[0:1, at]
    for s in range(1, segs.shape[0]):
        row = jnp.where(sequence == s, segs[s : s + 1, at], row)
    return row.astype(jnp.float32)


class Place:
    def __init__(self):
        self.me = me = lax.axis_index("fsdp")
        self.core = me % 2
        self.x = me // 2 % 2
        self.y = me // 4 % 2
        self.z = me // 8
        self.sibling = me + 1 - 2 * self.core
        self.across_x = me + 2 - 4 * self.x
        self.across_y = me + 4 - 8 * self.y

    def level(self, i):
        upper = self.z // 2
        inner = self.z * (1 - upper) + (3 - self.z) * upper
        turn = i + inner * (1 - 2 * i) * (1 - i // 2)
        return turn + upper * (3 - 2 * turn)

    def chip(self, half, side, level):
        flip = 1 - 2 * side
        y = self.y + (1 - half) * side * (1 - 2 * self.y)
        x = self.x + half * side * (1 - 2 * self.x)
        return level * 4 + y * 2 + x

    def chip_at(self, dx, dy, level):
        y = self.y + dy * (1 - 2 * self.y)
        x = self.x + dx * (1 - 2 * self.x)
        return level * 4 + y * 2 + x

    def first(self, half):
        return self.across_y * (1 - half) + self.across_x * half

    def last(self, half):
        return self.across_x * (1 - half) + self.across_y * half


OUTER_STEPS = (
    819265, 8651264, 12861442, 50372656, 8931409, 17432627, 13697571, 13172803, 37790773, 54809233, 34645544,
    42607251, 15008899, 14756500, 11890914, 65086601, 16013475, 59585160, 15800984, 41180860, 12187788, 16326300,
    37256878, 49626350, 11353642, 15294205, 36592266, 15561967, 40523830, 79254266, 10041135, 49140263, 35279415,
    65867414, 77672101, 60178981, 78533815, 43118213, 76663074, 64638646, 75646758, 126075173, 126075360, 126075360,
    126075360, 126075360, 126075360, 126075360, 126075360, 126075360, 126075360, 126075360,
)
INNER_STEPS = (
    297029, 30459904, 543235, 9464372, 51440213, 10266665, 8704550, 8409348, 14486081, 12612200, 14231616, 14705273,
    39127121, 11903096, 8953965, 71373446, 11568294, 35459180, 17594915, 13173376, 47565949, 15754834, 37812375,
    42247925, 18406959, 28859544, 39395993, 16349409, 36998782, 66092674, 22609570, 41228375, 34395178, 49923218,
    28071580, 66659898, 15529128, 37297787, 31027944, 26819743, 36265721, 62723687, 78966458, 26555547, 75847418,
    79259371, 77945587, 77716258, 78737199, 78507818, 76693795, 76959015,
)


def experts_kernel(rows, rank, x_ref, up_ref, gate_w, up_w, down_w, coeff, own_up, middle, gain, matrix, weights, out_inner, mixed,
                   grad_middle, grad_mixed, early, part_out, gathered,
                   out, held_w, pairs, tail_sem,
                   block, part_buf, result, sib, cross_out, cross_in, hold, z_in, first_out, first_in, total,
                   local_sem, load_sem, part_sem, send, recv, sib_send, sib_recv, cross_send, cross_recv,
                   z_send, z_recv, first_send, first_recv):
    place = Place()
    half = rows // 2
    f32, bf = jnp.float32, jnp.bfloat16
    flip = (((1,), (1,)), ((), ()))
    me, core = place.me, place.core
    upper = place.z // 2
    inner = place.z * (1 - upper) + (3 - place.z) * upper
    UP, DOWN, LAST, SIB, FIRST = range(5)

    def move(n, h, o, kind, target):
        piece = gathered.at[2 * o + core, h, n]
        return pltpu.make_async_remote_copy(
            src_ref=piece, dst_ref=piece, send_sem=send.at[kind, n, h, o],
            recv_sem=recv.at[1 if kind == SIB else 0, n, h, o], device_id=(target,), device_id_type=MESH)

    def arrived(n, h, o, sibling):
        piece = gathered.at[2 * o + (1 - core if sibling else core), h, n]
        pltpu.make_async_remote_copy(
            src_ref=piece, dst_ref=piece, send_sem=send.at[SIB, n, h, o],
            recv_sem=recv.at[1 if sibling else 0, n, h, o], device_id=(place.sibling,), device_id_type=MESH).wait_recv()

    def column(n, h, o, level, act):
        @pl.when((level <= place.z) & (place.z < LEVELS - 1))
        def _():
            act(move(n, h, o, UP, me + 8))

        @pl.when((level >= place.z) & (place.z > 0))
        def _():
            act(move(n, h, o, DOWN, me - 8))

    def spread(n, h, o, level, act):
        column(n, h, o, level, act)
        act(move(n, h, o, LAST, place.last(h)))
        act(move(n, h, o, SIB, place.sibling))

    def to_sibling(slot):
        return pltpu.make_async_remote_copy(
            src_ref=result.at[slot, 1 - core], dst_ref=sib.at[slot], send_sem=sib_send.at[slot],
            recv_sem=sib_recv.at[slot], device_id=(place.sibling,), device_id_type=MESH)

    def across(h, k, level):
        return pltpu.make_async_remote_copy(
            src_ref=cross_out.at[h, k, level], dst_ref=cross_in.at[h, k, level], send_sem=cross_send.at[h, k, level],
            recv_sem=cross_recv.at[h, k, level], device_id=(place.last(h),), device_id_type=MESH)

    def along(h, k, level, up, slot):
        return pltpu.make_async_remote_copy(
            src_ref=hold.at[h, k, level], dst_ref=z_in.at[h, k, slot], send_sem=z_send.at[h, k, level],
            recv_sem=z_recv.at[h, k, slot], device_id=(me - 8 + 16 * up,), device_id_type=MESH)

    def first(h):
        return pltpu.make_async_remote_copy(
            src_ref=first_out.at[h], dst_ref=first_in.at[h], send_sem=first_send.at[h],
            recv_sem=first_recv.at[h], device_id=(place.first(h),), device_id_type=MESH)

    def down_slot(level):
        ends = 1 - jnp.minimum(jnp.abs(level - (place.z - 1)), 1)
        return level + ends * (LEVELS - level)

    start = lambda copy: copy.start()
    done = lambda copy: copy.wait_send()
    mine = me // 2
    barrier = pltpu.get_barrier_semaphore()

    def greet(other):
        pl.semaphore_signal(barrier, inc=1, device_id=(other,), device_id_type=MESH)

    for other in (place.sibling, place.across_x, place.across_y):
        greet(other)

    @pl.when(place.z < LEVELS - 1)
    def _():
        greet(me + 8)

    @pl.when(place.z > 0)
    def _():
        greet(me - 8)

    tail = [
        pltpu.make_async_copy(matrix, held_w, tail_sem.at[0]),
        pltpu.make_async_copy(weights.at[:, :, pl.ds(384, 128)], pairs, tail_sem.at[1]),
    ]
    for copy in tail:
        copy.start()
    own = [
        pltpu.make_async_copy(ref.at[pl.ds(h * half, half)], gathered.at[me, h, n], local_sem.at[n, h])
        for n, ref in enumerate((x_ref, up_ref)) for h in range(2)
    ]
    for copy in own:
        copy.start()
    for copy in own:
        copy.wait()
    pl.semaphore_wait(barrier, 4 + inner)
    pieces = [(n, h) for n in range(2) for h in range(2)]
    def keep_part(o, slot):
        return pltpu.make_async_copy(part_buf.at[slot], part_out.at[o], part_sem.at[slot])

    def compute(o, slot, again):
        for n, h in pieces:
            arrived(n, h, o, True)
        load = pltpu.make_async_copy(gathered.at[pl.ds(2 * o, 2)], block, load_sem)
        load.start()

        @pl.when(again)
        def _():
            to_sibling(slot).wait_send()

        load.wait()
        c = [jnp.broadcast_to(coeff[2 * o + side], (rows, rows)).T[:, 0:1] for side in range(2)]
        c = jnp.concatenate(c, axis=0)
        x = block[:, :, 0].reshape(2 * rows, -1)
        gate = jnp.dot(x, gate_w[...], preferred_element_type=f32)
        up = jnp.dot(x, up_w[...], preferred_element_type=f32)
        sig = jax.nn.sigmoid(gate)
        silu = gate * sig
        hidden = (silu * up).astype(bf)
        part = (c * jnp.dot(hidden, down_w[...], preferred_element_type=f32)).astype(bf)
        part = part.reshape(2, 2, half, -1)
        result[slot, 0, 1] = part[0]
        result[slot, 1, 1] = part[1]
        upstream = (c * block[:, :, 1].reshape(2 * rows, -1).astype(f32)).astype(bf)
        grad_hidden = lax.dot_general(upstream, down_w[...], flip, preferred_element_type=f32)
        grad_gate = (grad_hidden * up * sig * (1.0 + gate * (1.0 - sig))).astype(bf)
        grad_up = (grad_hidden * silu).astype(bf)
        grad = lax.dot_general(grad_gate, gate_w[...], flip, preferred_element_type=f32)
        grad += lax.dot_general(grad_up, up_w[...], flip, preferred_element_type=f32)
        grad = grad.astype(bf).reshape(2, 2, half, -1)
        result[slot, 0, 0] = grad[0]
        result[slot, 1, 0] = grad[1]
        to_sibling(slot).start()

    def pair_sum(dx, dy, level, slot, again):
        to_sibling(slot).wait_recv()

        def pair(n, h):
            return (result[slot, core, n, h].astype(f32) + sib[slot, n, h].astype(f32)).astype(bf)

        for h, away, k in ((0, dx, dy), (1, dy, dx)):
            @pl.when(away == 1)
            def _():
                cross_out[h, k, level] = pair(0, h)
                across(h, k, level).start()

            @pl.when(away == 0)
            def _():
                hold[h, k, level] = pair(0, h)

        o = place.chip_at(dx, dy, level)

        @pl.when(again)
        def _():
            keep_part(o, slot).wait()

        for h in range(2):
            part_buf[slot, h] = pair(1, h)
        keep_part(o, slot).start()

    def column_sum(h, k, level):
        across(h, k, level).wait_recv()
        total[...] = hold[h, k, level].astype(f32) + cross_in[h, k, level].astype(f32)

        @pl.when((level >= place.z) & (place.z > 0))
        def _():
            along(h, k, level, 1, level).wait_recv()
            total[...] += z_in[h, k, level].astype(f32)

        @pl.when((level < place.z) & (place.z < LEVELS - 1))
        def _():
            along(h, k, level, 0, level).wait_recv()
            total[...] += z_in[h, k, level].astype(f32)

        @pl.when((level == place.z) & (place.z < LEVELS - 1))
        def _():
            along(h, k, level, 0, LEVELS).wait_recv()
            total[...] += z_in[h, k, LEVELS].astype(f32)

        @pl.when(level > place.z)
        def _():
            hold[h, k, level] = total[...].astype(bf)
            along(h, k, level, 1, level).start()

        @pl.when(level < place.z)
        def _():
            hold[h, k, level] = total[...].astype(bf)
            along(h, k, level, 0, down_slot(level)).start()

        @pl.when((level == place.z) & (k == 1))
        def _():
            first_out[h] = total[...].astype(bf)
            first(h).start()

        @pl.when((level == place.z) & (k == 0))
        def _():
            out[pl.ds(h * half, half)] = total[...]

    def step(code):
        kind, which = code // 32, code % 32
        h, k, n = which % 2, which // 2 % 2, which // 16
        turn = which // 4 % 4
        level = turn + upper * (3 - 2 * turn)
        o = place.chip(h, k, level)

        @pl.when(kind == 0)
        def _():
            move(which // 2 % 2, h, mine, FIRST, place.first(h)).start()

        @pl.when(kind == 1)
        def _():
            @pl.when((k == 1) | (level != place.z))
            def _():
                arrived(n, h, o, False)

            move(n, h, o, LAST, place.last(h)).start()
            move(n, h, o, SIB, place.sibling).start()

        @pl.when((kind == 2) | (kind == 3))
        def _():
            down = (kind + upper) % 2
            piece = gathered.at[2 * o + core, h, n]
            pltpu.make_async_remote_copy(
                src_ref=piece, dst_ref=piece, send_sem=send.at[down, n, h, o], recv_sem=recv.at[0, n, h, o],
                device_id=(me + 8 - 16 * down,), device_id_type=MESH).start()

        @pl.when(kind == 4)
        def _():
            away = place.chip_at(1 - h + h * k, k + h - h * k, level)
            arrived(n, h, away, False)
            move(n, h, away, SIB, place.sibling).start()

        dx, dy = which % 2, which // 2 % 2

        @pl.when((kind == 5) | (kind == 6))
        def _():
            compute(place.chip_at(dx, dy, level), which // 16, kind == 5)

        @pl.when((kind == 7) | (kind == 8))
        def _():
            pair_sum(dx, dy, level, which // 16, kind == 7)

        @pl.when(kind == 9)
        def _():
            column_sum(h, k, level)

    @pl.loop(0, len(OUTER_STEPS))
    def _(i):
        word = 0
        for at, (outer_word, inner_word) in enumerate(zip(OUTER_STEPS, INNER_STEPS)):
            word = jnp.where(i == at, jnp.where(inner == 0, outer_word, inner_word), word)

        def one(_, rest):
            step(rest % 512)
            return rest // 512

        lax.fori_loop(0, 3, one, word)

    for h in range(2):
        first(h).wait_recv()
        out[pl.ds(h * half, half)] += first_in[h].astype(f32)
    for copy in tail:
        copy.wait()

    ours = middle[...]
    inverse = lax.rsqrt(jnp.mean(ours * ours, axis=-1, keepdims=True) + epsilon)
    unit = ours * inverse
    scaled = out[...] * gain[...]
    grad = inverse * (scaled - unit * jnp.mean(scaled * unit, axis=-1, keepdims=True))
    grad = own_up[...].astype(f32) + grad
    grad_middle[...] = grad
    grad = grad.astype(bf)
    adapters = pairs[...].reshape(-1, 128)
    lane = lax.broadcasted_iota(jnp.int32, (rows, 128), 1)
    low = jnp.dot(grad, adapters, preferred_element_type=f32)
    low = jnp.where(lane // rank == 7, low, 0.0).astype(bf)
    low = pltpu.roll(low.astype(f32), 64, 1).astype(bf)
    back = lax.dot_general(grad, held_w[...], flip, preferred_element_type=f32)
    back += lax.dot_general(low, adapters, flip, preferred_element_type=f32)
    grad_mixed[...] = back.astype(bf)
    tall = (((0,), (0,)), ((), ()))
    early[0:rank] = lax.dot_general(low, mixed[...], tall, preferred_element_type=f32)[3 * rank : 4 * rank]
    early[rank:] = lax.dot_general(out_inner[...], grad, tall, preferred_element_type=f32)[3 * rank : 4 * rank]

    for n, h in pieces:
        move(n, h, mine, FIRST, place.first(h)).wait_send()
        spread(n, h, mine, place.z, done)
        spread(n, h, place.chip(h, 1, place.z), place.z, done)
    for h in range(2):
        first(h).wait_send()
    for slot in range(2):
        to_sibling(slot).wait_send()
        keep_part(0, slot).wait()

    @pl.loop(0, CHIPS)
    def _(t):
        h, k = t % 2, t // 2 % 2

        @pl.when(t < CHIPS - 4)
        def _():
            level = place.level(1 + t // 4)
            for n in range(2):
                spread(n, h, place.chip(h, k, level), level, done)

        dx, dy = t % 2, t // 2 % 2
        o = place.chip_at(dx, dy, t // 4)
        for side, away in ((0, dx), (1, dy)):
            @pl.when(away == 1)
            def _():
                for n in range(2):
                    move(n, side, o, SIB, place.sibling).wait_send()

        level = t // 4
        across(h, k, level).wait_send()

        @pl.when(level > place.z)
        def _():
            along(h, k, level, 1, level).wait_send()

        @pl.when(level < place.z)
        def _():
            along(h, k, level, 0, down_slot(level)).wait_send()


def experts_pass(x, upstream, gate_w, up_w, down_w, coeff, middle, gain, matrix, weights, out_inner, mixed, rank):
    rows, width = x.shape
    devices = coeff.shape[0]
    half = rows // 2
    bf, f32 = jnp.bfloat16, jnp.float32
    dma = pltpu.SemaphoreType.DMA
    vmem, anywhere = pl.BlockSpec(memory_space=pltpu.VMEM), pl.BlockSpec(memory_space=pl.ANY)
    piece = (half, width)
    return pl.pallas_call(
        functools.partial(experts_kernel, rows, rank),
        out_shape=(
            jax.ShapeDtypeStruct((rows, width), f32),
            jax.ShapeDtypeStruct((rows, width), bf),
            jax.ShapeDtypeStruct((2 * rank, width), f32),
            jax.ShapeDtypeStruct((CHIPS, 2) + piece, bf),
            jax.ShapeDtypeStruct((devices, 2, 2) + piece, bf),
        ),
        in_specs=[anywhere, anywhere] + [vmem] * 7 + [anywhere, anywhere, vmem, vmem],
        out_specs=(vmem, vmem, vmem, anywhere, anywhere),
        scratch_shapes=[
            pltpu.VMEM((rows, width), f32),
            pltpu.VMEM(matrix.shape, bf),
            pltpu.VMEM(weights.shape[:2] + (128,), bf),
            dma((2,)),
            pltpu.VMEM((2, 2, 2) + piece, bf),
            pltpu.VMEM((2, 2) + piece, bf),
            pltpu.VMEM((2, 2, 2, 2) + piece, bf),
            pltpu.VMEM((2, 2, 2) + piece, bf),
            pltpu.VMEM((2, 2, LEVELS) + piece, bf),
            pltpu.VMEM((2, 2, LEVELS) + piece, bf),
            pltpu.VMEM((2, 2, LEVELS) + piece, bf),
            pltpu.VMEM((2, 2, LEVELS + 1) + piece, bf),
            pltpu.VMEM((2,) + piece, bf),
            pltpu.VMEM((2,) + piece, bf),
            pltpu.VMEM(piece, f32),
            dma((2, 2)), dma, dma((2,)), dma((5, 2, 2, CHIPS)), dma((2, 2, 2, CHIPS)), dma((2,)), dma((2,)),
            dma((2, 2, LEVELS)), dma((2, 2, LEVELS)),
            dma((2, 2, LEVELS)), dma((2, 2, LEVELS + 1)), dma((2,)), dma((2,)),
        ],
        compiler_params=pltpu.CompilerParams(collective_id=1, has_side_effects=True, vmem_limit_bytes=62 << 20),
        name="experts",
    )(x, upstream, gate_w, up_w, down_w, coeff, upstream, middle, gain, matrix, weights, out_inner, mixed)


def front_kernel(rows, rank, picked, tokens, rows_gain, query_w, key_w, value_w, segs, downs, ups, routes, gates, out_w, near, far_turn,
                 query_gain, key_gain, ffn_gain,
                 middle, normed_ffn, normed, mixed, out_inner, weights, query_out, key_out, value_out,
                 query_proj, key_proj, inner_out, coeff_out, cosine, sine, out_all,
                 held, mixed_buf, pair, coeff, wo, heads_w,
                 local_sem, send, recv, w_send, w_recv, pair_send, pair_recv, c_send, c_recv, m_send, m_recv, m_local,
                 g_send, g_recv, keep_sem):
    place = Place()
    f32, bf = jnp.float32, jnp.bfloat16
    me, core = place.me, place.core
    group = held.shape[0]
    base, p = me // group * group, me % group
    other = (me + group) % (2 * group)
    other_base = group - base
    half = rows // 2
    depth = weights.shape[1]
    wide = 3 * 128
    z = place.z % 2
    across_z = me + 8 - 16 * z
    chip = p // 2

    FIRST, ALONG, LAST, SIB = range(4)

    def chip_at(h, k, far):
        flip = place.chip(h, k, 0)
        zz = z + far * (1 - 2 * z)
        return zz * 4 + flip

    def move(h, o, kind, target):
        piece = held.at[2 * o + core, pl.ds(h * half, half)]
        return pltpu.make_async_remote_copy(
            src_ref=piece, dst_ref=piece, send_sem=send.at[kind, h, o],
            recv_sem=recv.at[1 if kind == SIB else 0, h, o], device_id=(target,), device_id_type=MESH)

    def arrived(h, o, sibling):
        piece = held.at[2 * o + (1 - core if sibling else core), pl.ds(h * half, half)]
        pltpu.make_async_remote_copy(
            src_ref=piece, dst_ref=piece, send_sem=send.at[SIB, h, o],
            recv_sem=recv.at[1 if sibling else 0, h, o], device_id=(place.sibling,), device_id_type=MESH).wait_recv()

    def to_heads(q):
        return pltpu.make_async_remote_copy(
            src_ref=heads_w.at[q % group], dst_ref=weights.at[me, :, pl.ds(0, wide)], send_sem=w_send.at[q],
            recv_sem=w_recv.at[me], device_id=(q,), device_id_type=MESH)

    def to_expert(q):
        return pltpu.make_async_remote_copy(
            src_ref=coeff.at[q // 2], dst_ref=coeff_out.at[me], send_sem=c_send.at[q],
            recv_sem=c_recv.at[me], device_id=(q,), device_id_type=MESH)

    def pair_over(q, side):
        row = (me + side * group) % (2 * group)
        piece = weights.at[row, :, pl.ds(wide, 128)]
        return pltpu.make_async_remote_copy(
            src_ref=piece, dst_ref=piece, send_sem=pair_send.at[side, q],
            recv_sem=pair_recv.at[row], device_id=(base + q,), device_id_type=MESH)

    pair_other = pltpu.make_async_remote_copy(
        src_ref=pair.at[other // group], dst_ref=weights.at[me, :, pl.ds(wide, 128)], send_sem=pair_send.at[2, 0],
        recv_sem=pair_recv.at[me], device_id=(other,), device_id_type=MESH)
    greet_all(me, 2 * group)

    UP, DOWN, G_LAST, G_SIB, G_FIRST = range(5)

    def g_move(h, o, kind, target):
        piece = wo.at[2 * o + core, h]
        return pltpu.make_async_remote_copy(
            src_ref=piece, dst_ref=piece, send_sem=g_send.at[kind, h, o],
            recv_sem=g_recv.at[1 if kind == G_SIB else 0, h, o], device_id=(target,), device_id_type=MESH)

    def g_arrived(h, o, sibling):
        piece = wo.at[2 * o + (1 - core if sibling else core), h]
        pltpu.make_async_remote_copy(
            src_ref=piece, dst_ref=piece, send_sem=g_send.at[G_SIB, h, o],
            recv_sem=g_recv.at[1 if sibling else 0, h, o], device_id=(place.sibling,), device_id_type=MESH).wait_recv()

    def g_column(h, o, level, act):
        @pl.when((level <= place.z) & (place.z < LEVELS - 1))
        def _():
            act(g_move(h, o, UP, me + 8))

        @pl.when((level >= place.z) & (place.z > 0))
        def _():
            act(g_move(h, o, DOWN, me - 8))

    def g_spread(h, o, level, act):
        g_column(h, o, level, act)
        act(g_move(h, o, G_LAST, place.last(h)))
        act(g_move(h, o, G_SIB, place.sibling))

    def g_level(t):
        level, h, k = place.level(1 + t // 4), t % 2, t // 2 % 2
        o = place.chip(h, k, level)
        g_arrived(h, o, False)
        g_spread(h, o, level, start)

    def g_cross(q):
        dx, dy = q % 2, q // 2 % 2
        o = place.chip_at(dx, dy, place.level(q // 4))
        for h, away in ((0, dx), (1, dy)):
            @pl.when(away == 1)
            def _():
                g_arrived(h, o, False)
                g_move(h, o, G_SIB, place.sibling).start()

    start = lambda copy: copy.start()
    done = lambda copy: copy.wait_send()
    own_chip = me // 2
    own_copies = [
        pltpu.make_async_copy(heads_w.at[p], weights.at[me, :, pl.ds(0, wide)], local_sem.at[0]),
        pltpu.make_async_copy(out_w.at[pl.ds(0, depth // 2)], wo.at[me, 0], local_sem.at[1]),
        pltpu.make_async_copy(out_w.at[pl.ds(depth // 2, depth // 2)], wo.at[me, 1], local_sem.at[2]),
    ]
    for q in range(group):
        for j, matrix in enumerate((query_w, key_w, value_w)):
            heads_w[q, :, j * 128 : (j + 1) * 128] = matrix[:, q * 128 : (q + 1) * 128]
    for copy in own_copies:
        copy.start()
    ours = tokens[...].astype(f32)
    low = (ours * lax.rsqrt(jnp.mean(ours * ours, axis=-1, keepdims=True) + epsilon) * rows_gain[...]).astype(bf)
    held[p] = low
    normed[...] = low
    pl.semaphore_wait(pltpu.get_barrier_semaphore(), 2 * group - 1)
    for h in range(2):
        move(h, chip, ALONG, across_z).start()
        move(h, chip, FIRST, place.first(h)).start()
    for h in range(2):
        move(h, chip, LAST, place.last(h)).start()
        move(h, chip, SIB, place.sibling).start()

    for s in range(2):
        down, up = downs[picked[s]].astype(f32), ups[picked[s]].astype(f32)
        down = jnp.concatenate([down[j] for j in range(4)], axis=1)
        up = jnp.concatenate([up[j] for j in range(4)], axis=0).T
        pair[s] = jnp.concatenate([down, up], axis=1).astype(bf)
    weights[me, :, wide:] = pair[me // group]
    pair_other.start()

    @pl.loop(0, group)
    def _(i):
        to_heads(other_base + (p + i) % group).start()

    lane = lax.broadcasted_iota(jnp.int32, (rows, 128), 1)
    gate = jnp.zeros((rows, 128), f32)
    for k in range(routes.shape[1]):
        gate += jnp.where(lane == routes[:, k : k + 1], gates[:, k : k + 1], 0.0)
    gate = gate.T
    for e in range(coeff.shape[0]):
        coeff[e] = gate[e : e + 1]
    coeff_out[me] = coeff[me // 2]

    @pl.loop(1, group)
    def _(i):
        pair_over((p + i) % group, 0).start()
        to_heads(base + (p + i) % group).start()

    @pl.loop(1, 2 * group)
    def _(i):
        to_expert((me + i) % (2 * group)).start()

    for copy in own_copies[1:]:
        copy.wait()
    for h in range(2):
        g_column(h, own_chip, place.z, start)
        g_move(h, own_chip, G_FIRST, place.first(h)).start()
    for h in range(2):
        g_move(h, own_chip, G_LAST, place.last(h)).start()
        g_move(h, own_chip, G_SIB, place.sibling).start()

    pltpu.make_async_remote_copy(
        src_ref=pair.at[0], dst_ref=weights.at[other, :, pl.ds(wide, 128)], send_sem=pair_send.at[2, 0],
        recv_sem=pair_recv.at[other], device_id=(other,), device_id_type=MESH).wait_recv()

    @pl.loop(1, group)
    def _(i):
        pair_over((p + i) % group, 1).start()

    for h in range(2):
        o = chip_at(h, 0, 1)
        arrived(h, o, False)
        move(h, o, FIRST, place.first(h)).start()
        move(h, o, LAST, place.last(h)).start()
        move(h, o, SIB, place.sibling).start()
    for far in range(2):
        for h in range(2):
            o = chip_at(h, 1, far)
            arrived(h, o, False)
            move(h, o, LAST, place.last(h)).start()
            move(h, o, SIB, place.sibling).start()
    for h in range(2):
        o = place.chip(h, 1, place.z)
        g_arrived(h, o, False)
        g_spread(h, o, place.z, start)

    @pl.loop(0, group)
    def _(i):
        at = pl.ds(pl.multiple_of(i * rows, rows), rows)
        c, s = far_turn[0, pl.ds(i, 1)], far_turn[1, pl.ds(i, 1)]
        cosine[at] = c * near[0] - s * near[1]
        turn = s * near[0] + c * near[1]
        sine[at] = jnp.where(lane < 64, -turn, turn)

    for far in range(2):
        for k in range(2):
            for h in range(2):
                dx, dy = (1, k) if h == 0 else (k, 1)
                o = (z + far * (1 - 2 * z)) * 4 + place.chip_at(dx, dy, 0)
                arrived(h, o, False)
                move(h, o, SIB, place.sibling).start()
    own_copies[0].wait()

    @pl.loop(0, 4)
    def _(t):
        g_level(t)


    @pl.loop(1, 2 * group)
    def _(i):
        q = (me + i) % (2 * group)
        pltpu.make_async_remote_copy(
            src_ref=heads_w.at[0], dst_ref=weights.at[q, :, pl.ds(0, wide)], send_sem=w_send.at[q],
            recv_sem=w_recv.at[q], device_id=(q,), device_id_type=MESH).wait_recv()
        pltpu.make_async_remote_copy(
            src_ref=coeff.at[0], dst_ref=coeff_out.at[q], send_sem=c_send.at[q],
            recv_sem=c_recv.at[q], device_id=(q,), device_id_type=MESH).wait_recv()

        @pl.when(q != other)
        def _():
            pltpu.make_async_remote_copy(
                src_ref=pair.at[0], dst_ref=weights.at[q, :, pl.ds(wide, 128)], send_sem=pair_send.at[2, 0],
                recv_sem=pair_recv.at[q], device_id=(other,), device_id_type=MESH).wait_recv()

    @pl.loop(0, group // 2)
    def _(o):
        for h in range(2):
            arrived(h, o, True)

    @pl.loop(4, 8)
    def _(t):
        g_level(t)

    span = 2 * rows
    seq = group * rows
    up_own = weights[pl.ds(2 * p, 2), :, pl.ds(wide, 128)].reshape(2 * depth, 128)
    up_own = pltpu.roll(up_own.astype(f32), 64, 1).astype(bf)
    flip = (((1,), (1,)), ((), ()))
    scale = 1.0 / math.sqrt(128)

    @pl.loop(0, group // 2)
    def _(b):
        at = pl.ds(pl.multiple_of(b * span, span), span)
        x = held[pl.ds(2 * b, 2)].reshape(span, -1)
        acc = jnp.dot(x, weights[...].reshape(2 * group * depth, wide + 128), preferred_element_type=f32)
        inner = acc[:, wide:].astype(bf)
        inner_out[at] = inner
        owner = lax.broadcasted_iota(jnp.int32, inner.shape, 1) // rank

        def projected(j):
            low = jnp.where(owner == j, inner.astype(f32), 0.0).astype(bf)
            return acc[:, j * 128 : (j + 1) * 128] + lax.dot_general(low, up_own, flip, preferred_element_type=f32)

        for j, (gain, raw, rot) in enumerate(((query_gain, query_proj, query_out), (key_gain, key_proj, key_out))):
            value = projected(j)
            raw[at] = value
            unit = value * lax.rsqrt(jnp.mean(value * value, axis=-1, keepdims=True) + epsilon) * gain[...]
            rot[at] = (unit * cosine[at] + pltpu.roll(unit, 64, 1) * sine[at]).astype(bf)
        value_out[at] = projected(2).astype(bf)

        @pl.when(b % 2 == 0)
        def _():
            g_level(8 + b // 2)

    def to_token(q):
        return pltpu.make_async_remote_copy(
            src_ref=mixed_buf.at[q], dst_ref=mixed.at[:, pl.ds(p * 128, 128)], send_sem=m_send.at[q],
            recv_sem=m_recv.at[p], device_id=(base + q,), device_id_type=MESH)

    keep = pltpu.make_async_copy(mixed_buf.at[p], mixed.at[:, pl.ds(p * 128, 128)], m_local)

    @pl.loop(0, group // 2)
    def _(b):
        at = pl.ds(pl.multiple_of(b * span, span), span)
        scores = lax.dot_general(query_out[at], key_out[...], flip, preferred_element_type=f32)
        own_seg = [
            jnp.broadcast_to(segments_at(segs, me // group, pl.ds(pl.multiple_of(b * span + i, 128), 128)), (128, 128)).T
            for i in range(0, span, 128)
        ]
        own_seg = jnp.concatenate(own_seg, axis=0)[:, 0:1]
        weight = jnp.where(own_seg == segments_at(segs, me // group, slice(None)), jnp.exp2(scores * (scale * math.log2(math.e))), 0.0)
        total = jnp.sum(weight, axis=-1, keepdims=True)
        value = jnp.dot(weight.astype(bf), value_out[...], preferred_element_type=f32) / total
        mixed_buf[pl.ds(2 * b, 2)] = value.astype(bf).reshape(2, rows, 128)
        for side in range(2):
            q = 2 * b + side

            @pl.when(q != p)
            def _():
                to_token(q).start()

            @pl.when(q == p)
            def _():
                keep.start()

        g_cross(2 * b)
        g_cross(2 * b + 1)

    keep.wait()

    @pl.loop(1, group)
    def _(i):
        q = (p + i) % group
        pltpu.make_async_remote_copy(
            src_ref=mixed_buf.at[q], dst_ref=mixed.at[:, pl.ds(q * 128, 128)], send_sem=m_send.at[q],
            recv_sem=m_recv.at[q], device_id=(base + q,), device_id_type=MESH).wait_recv()

    @pl.loop(0, CHIPS)
    def _(o):
        for h in range(2):
            g_arrived(h, o, True)

    keep_out = pltpu.make_async_copy(wo, out_all, keep_sem)
    keep_out.start()
    ours = mixed[...]
    matrix = weights[:, :, wide:].reshape(2 * group * depth, 128)
    lane = lax.broadcasted_iota(jnp.int32, (rows, 128), 1)
    inner = jnp.dot(ours, matrix, preferred_element_type=f32)
    inner = jnp.where(lane // rank == 3, inner, 0.0).astype(bf)
    out_inner[...] = inner
    shifted = pltpu.roll(inner.astype(f32), 64, 1).astype(bf)
    total = tokens[...].astype(f32) + jnp.dot(ours, wo[...].reshape(2 * group * depth, -1), preferred_element_type=f32)
    total = total + lax.dot_general(shifted, matrix, flip, preferred_element_type=f32)
    middle[...] = total
    unit = total * lax.rsqrt(jnp.mean(total * total, axis=-1, keepdims=True) + epsilon)
    normed_ffn[...] = (unit * ffn_gain[...]).astype(bf)

    keep_out.wait()
    for h in range(2):
        g_move(h, own_chip, G_FIRST, place.first(h)).wait_send()
        g_spread(h, own_chip, place.z, done)
        g_spread(h, place.chip(h, 1, place.z), place.z, done)

    @pl.loop(0, CHIPS)
    def _(t):
        @pl.when(t < CHIPS - 4)
        def _():
            level, h, k = place.level(1 + t // 4), t % 2, t // 2 % 2
            g_spread(h, place.chip(h, k, level), level, done)

        dx, dy = t % 2, t // 2 % 2
        o = place.chip_at(dx, dy, place.level(t // 4))
        for h, away in ((0, dx), (1, dy)):
            @pl.when(away == 1)
            def _():
                g_move(h, o, G_SIB, place.sibling).wait_send()

    pair_other.wait_send()
    for h in range(2):
        move(h, chip, ALONG, across_z).wait_send()
        for far in range(2):
            for k in range(2):
                o = chip_at(h, k, far)
                if k == 0:
                    move(h, o, FIRST, place.first(h)).wait_send()
                move(h, o, LAST, place.last(h)).wait_send()
                move(h, o, SIB, place.sibling).wait_send()
                dx, dy = (1, k) if h == 0 else (k, 1)
                o = (z + far * (1 - 2 * z)) * 4 + place.chip_at(dx, dy, 0)
                move(h, o, SIB, place.sibling).wait_send()

    @pl.loop(1, group)
    def _(i):
        q = (p + i) % group
        pair_over(q, 0).wait_send()
        pair_over(q, 1).wait_send()
        to_token(q).wait_send()

    @pl.loop(1, 2 * group)
    def _(i):
        q = (me + i) % (2 * group)
        to_heads(q).wait_send()
        to_expert(q).wait_send()


def turn_tables(rows, group):
    frequency = rope_base ** (-(np.arange(64, dtype=np.float32) * np.float32(2.0 / 128)))
    frequency = np.concatenate([frequency, frequency]).astype(np.float64)
    tables = []
    for positions in (np.arange(rows), np.arange(group) * rows):
        angle = positions[:, None] * frequency[None, :]
        tables.append(np.stack([np.cos(angle), np.sin(angle)]).astype(np.float32))
    return tables


def front(picked, tokens, rows_gain, query_w, key_w, value_w, segs, downs, ups, routes, gates, out_w,
          query_gain, key_gain, ffn_gain):
    rows, width = tokens.shape
    group, depth = SEQ_LEN // rows, out_w.shape[0]
    rank = downs.shape[3]
    devices, seq = 2 * group, rows * group
    bf, f32 = jnp.bfloat16, jnp.float32
    dma = pltpu.SemaphoreType.DMA
    vmem, anywhere = pl.BlockSpec(memory_space=pltpu.VMEM), pl.BlockSpec(memory_space=pl.ANY)
    head = jax.ShapeDtypeStruct((seq, 128), bf)
    raw = jax.ShapeDtypeStruct((seq, 128), f32)
    mine = jax.ShapeDtypeStruct((rows, width), bf)
    near, far_turn = turn_tables(rows, group)
    return pl.pallas_call(
        functools.partial(front_kernel, rows, rank),
        out_shape=(
            jax.ShapeDtypeStruct((rows, width), f32), mine, mine, mine,
            jax.ShapeDtypeStruct((rows, 128), bf),
            jax.ShapeDtypeStruct((devices, depth, 512), bf),
            head, head, head, raw, raw, head,
            jax.ShapeDtypeStruct((devices, 1, rows), f32),
            raw, raw,
            jax.ShapeDtypeStruct((devices, 2, depth // 2, width), bf),
        ),
        in_specs=[pl.BlockSpec(memory_space=pltpu.SMEM)] + [vmem] * 10 + [anywhere] + [vmem] * 5,
        out_specs=(vmem,) * 15 + (anywhere,),
        scratch_shapes=[
            pltpu.VMEM((group, rows, width), bf),
            pltpu.VMEM((group, rows, 128), bf),
            pltpu.VMEM((2, depth, 128), bf),
            pltpu.VMEM((group, 1, rows), f32),
            pltpu.VMEM((devices, 2, depth // 2, width), bf),
            pltpu.VMEM((group, depth, 384), bf),
            dma((3,)), dma((4, 2, group // 2)), dma((2, 2, group // 2)),
            dma((devices,)), dma((devices,)), dma((3, group)), dma((devices,)),
            dma((devices,)), dma((devices,)), dma((group,)), dma((group,)), dma,
            dma((5, 2, CHIPS)), dma((2, 2, CHIPS)), dma,
        ],
        compiler_params=pltpu.CompilerParams(collective_id=0, has_side_effects=True, vmem_limit_bytes=60 << 20),
        name="front",
    )(picked, tokens, rows_gain, query_w, key_w, value_w, segs, downs, ups, routes, gates, out_w, jnp.asarray(near), jnp.asarray(far_turn),
      query_gain, key_gain, ffn_gain)


OUTER_DONE = (0, 1, 2, 2, 3, 4, 4, 5, 5, 6, 7, 9, 9, 9, 9, 9, 9, 9, 9, 9, 9, 11, 11, 12, 13, 13, 14, 14, 16)
INNER_DONE = (0, 0, 0, 0, 0, 0, 0, 0, 0, 0, 0, 0, 0, 0, 0, 0, 0, 0, 6, 6, 6, 11, 11, 13, 13, 14, 14, 14, 16)


def back_kernel(rows, rank, grad_mixed, part, weights, query, key, value, query_proj, key_proj, inner, cosine, sine,
                query_gain, key_gain, segs, rows_in, normed, rows_gain, grad_middle, middle, early,
                grad_rows, output, factors, out, up_terms, part_sum, late, early_in, late_in, owned,
                e_send, e_recv, l_send, l_recv, f_send, f_recv, t_local,
                grads, key_seg, key_t, grad_key, grad_value, heads, result, sib, cross_out, cross_in, z_out, z_in, first_out, first_in,
                held, part_in, part_z, part_total, part_first_out, part_first_in,
                held_sem, pc_send, pc_recv, pz_send, pz_recv, pf_send, pf_recv,
                a_send, a_recv, a_local, sib_send, sib_recv, cross_send, cross_recv, z_send, z_recv, first_send, first_recv):
    place = Place()
    f32, bf = jnp.float32, jnp.bfloat16
    me, core = place.me, place.core
    group = grads.shape[0]
    depth = weights.shape[1]
    base, p = me // group * group, me % group
    half, span, seq = rows // 2, 2 * rows, rows * group
    width = out.shape[1] - 128
    z = place.z % 2
    across_z = me + 8 - 16 * z
    flip = (((1,), (1,)), ((), ()))
    tall = (((0,), (0,)), ((), ()))
    scale = 1.0 / math.sqrt(128)

    def keep_piece(h, k, level):
        return pltpu.make_async_copy(part.at[place.chip(h, k, level), h], held.at[h, k, level], held_sem.at[h, k, level])

    def part_across(h, k, level):
        dx, dy = (1, k) if h == 0 else (k, 1)
        return pltpu.make_async_remote_copy(
            src_ref=part.at[place.chip_at(dx, dy, level), h], dst_ref=part_in.at[h, k, level],
            send_sem=pc_send.at[h, k, level], recv_sem=pc_recv.at[h, k, level],
            device_id=(place.last(h),), device_id_type=MESH)

    def crossed(h, k, level):
        return pltpu.make_async_remote_copy(
            src_ref=held.at[h, k, level], dst_ref=part_in.at[h, k, level], send_sem=pc_send.at[h, k, level],
            recv_sem=pc_recv.at[h, k, level], device_id=(place.last(h),), device_id_type=MESH)

    def part_along(h, k, level, up, slot):
        return pltpu.make_async_remote_copy(
            src_ref=held.at[h, k, level], dst_ref=part_z.at[h, k, slot], send_sem=pz_send.at[h, k, level],
            recv_sem=pz_recv.at[h, k, slot], device_id=(me - 8 + 16 * up,), device_id_type=MESH)

    def part_first(h):
        return pltpu.make_async_remote_copy(
            src_ref=part_first_out.at[h], dst_ref=part_first_in.at[h], send_sem=pf_send.at[h],
            recv_sem=pf_recv.at[h], device_id=(place.first(h),), device_id_type=MESH)

    def down_slot(level):
        ends = 1 - jnp.minimum(jnp.abs(level - (place.z - 1)), 1)
        return level + ends * (LEVELS - level)

    def part_event(e):
        h, k, level = e % 2, e // 2 % 2, place.level(3 - e // 4)
        keep_piece(h, k, level).wait()
        crossed(h, k, level).wait_recv()
        total = held[h, k, level].astype(f32) + part_in[h, k, level].astype(f32)
        part_total[...] = total

        @pl.when((level >= place.z) & (place.z > 0))
        def _():
            part_along(h, k, level, 1, level).wait_recv()
            part_total[...] += part_z[h, k, level].astype(f32)

        @pl.when((level < place.z) & (place.z < LEVELS - 1))
        def _():
            part_along(h, k, level, 0, level).wait_recv()
            part_total[...] += part_z[h, k, level].astype(f32)

        @pl.when((level == place.z) & (place.z < LEVELS - 1))
        def _():
            part_along(h, k, level, 0, LEVELS).wait_recv()
            part_total[...] += part_z[h, k, LEVELS].astype(f32)

        @pl.when(level > place.z)
        def _():
            held[h, k, level] = part_total[...].astype(bf)
            part_along(h, k, level, 1, level).start()

        @pl.when(level < place.z)
        def _():
            held[h, k, level] = part_total[...].astype(bf)
            part_along(h, k, level, 0, down_slot(level)).start()

        @pl.when((level == place.z) & (k == 1))
        def _():
            part_first_out[h] = part_total[...].astype(bf)
            part_first(h).start()

        @pl.when((level == place.z) & (k == 0))
        def _():
            part_sum[h] = part_total[...]

    upper = place.z // 2
    inner_level = place.z * (1 - upper) + (3 - place.z) * upper

    def part_steps(slot):
        def bound(at):
            if isinstance(at, int):
                return OUTER_DONE[at] + inner_level * (INNER_DONE[at] - OUTER_DONE[at])
            count = 0
            for i, (outer, inside) in enumerate(zip(OUTER_DONE, INNER_DONE)):
                count = jnp.where(at == i, jnp.where(inner_level == 0, outer, inside), count)
            return count

        def one(e, none):
            part_event(e)
            return none

        lax.fori_loop(bound(slot), bound(slot + 1), one, 0)

    def to_head(q):
        return pltpu.make_async_remote_copy(
            src_ref=grad_mixed.at[:, pl.ds(q * 128, 128)], dst_ref=grads.at[p], send_sem=a_send.at[q],
            recv_sem=a_recv.at[p], device_id=(base + q,), device_id_type=MESH)

    def from_token(q):
        return pltpu.make_async_remote_copy(
            src_ref=grad_mixed.at[:, pl.ds(q * 128, 128)], dst_ref=grads.at[q], send_sem=a_send.at[q],
            recv_sem=a_recv.at[q], device_id=(base + q,), device_id_type=MESH)

    keep = pltpu.make_async_copy(grad_mixed.at[:, pl.ds(p * 128, 128)], grads.at[p], a_local)
    keep.start()
    greet_all(me, 2 * group)
    @pl.loop(0, group)
    def _(i):
        at = pl.ds(pl.multiple_of(i * 128, 128), 128)
        key_seg[at] = jnp.broadcast_to(segments_at(segs, me // group, at), (128, 128)).T

    key_t[...] = key[...].astype(f32).T.astype(bf)
    pl.semaphore_wait(pltpu.get_barrier_semaphore(), 2 * group - 1)

    def early_to(q, frm):
        return pltpu.make_async_remote_copy(
            src_ref=early.at[:, pl.ds(q * 128, 128)], dst_ref=early_in.at[frm], send_sem=e_send.at[q],
            recv_sem=e_recv.at[frm], device_id=(base + q,), device_id_type=MESH)

    def late_to(q, frm):
        return pltpu.make_async_remote_copy(
            src_ref=late.at[:, pl.ds(q * 128, 128)], dst_ref=late_in.at[frm], send_sem=l_send.at[q],
            recv_sem=l_recv.at[frm], device_id=(base + q,), device_id_type=MESH)

    def to_owner(side, q, frm):
        return pltpu.make_async_remote_copy(
            src_ref=owned, dst_ref=factors.at[frm], send_sem=f_send.at[side],
            recv_sem=f_recv.at[frm], device_id=(q,), device_id_type=MESH)

    early_keep = pltpu.make_async_copy(early.at[:, pl.ds(p * 128, 128)], early_in.at[p], t_local.at[0])
    late_keep = pltpu.make_async_copy(late.at[:, pl.ds(p * 128, 128)], late_in.at[p], t_local.at[1])
    owned_keep = pltpu.make_async_copy(owned, factors.at[me // group], t_local.at[2])
    early_keep.start()

    @pl.loop(1, group)
    def _(i):
        to_head((p + i) % group).start()

    @pl.loop(1, group)
    def _(i):
        early_to((p + i) % group, p).start()

    @pl.loop(0, 4)
    def _(i):
        level = place.level(3 - i)
        for k in range(2):
            for h in range(2):
                part_across(h, k, level).start()
                keep_piece(h, k, level).start()

    grad_key[...] = jnp.zeros_like(grad_key)
    grad_value[...] = jnp.zeros_like(grad_value)
    keep.wait()

    def raw_grad(raw, gain, turned, at):
        back = turned * cosine[at] - pltpu.roll(turned, 64, 1) * sine[at]
        rows_ = raw[at]
        inverse = lax.rsqrt(jnp.mean(rows_ * rows_, axis=-1, keepdims=True) + epsilon)
        unit = rows_ * inverse
        scaled = back * gain[...]
        return (inverse * (scaled - unit * jnp.mean(scaled * unit, axis=-1, keepdims=True))).astype(bf)

    @pl.loop(0, group // 2)
    def _(b):
        at = pl.ds(pl.multiple_of(b * span, span), span)
        for side in range(2):
            q = 2 * b + side

            @pl.when(q != p)
            def _():
                from_token(q).wait_recv()

        ours = query[at]
        grad = grads[pl.ds(2 * b, 2)].reshape(span, 128)
        scores = lax.dot_general(key[...], ours, flip, preferred_element_type=f32)
        own_seg = segments_at(segs, me // group, at)
        weight = jnp.where(key_seg[:, 0:1] == own_seg, jnp.exp2(scores * (scale * math.log2(math.e))), 0.0)
        probs = weight * (1.0 / jnp.sum(weight, axis=0, keepdims=True))
        grad_probs = lax.dot_general(value[...], grad, flip, preferred_element_type=f32)
        mean = jnp.sum(probs * grad_probs, axis=0, keepdims=True)
        grad_scores = (probs * (grad_probs - mean)).astype(bf)
        grad_key[...] += jnp.dot(grad_scores, ours, preferred_element_type=f32)
        grad_value[...] += jnp.dot(probs.astype(bf), grad, preferred_element_type=f32)
        grad_query = jnp.dot(key_t[...], grad_scores, preferred_element_type=f32).T * scale
        heads[at, 0:128] = raw_grad(query_proj, query_gain, grad_query, at)
        part_steps(b)

    up_own = weights[pl.ds(2 * p, 2), :, 384:512].reshape(2 * depth, 128)
    up_own = pltpu.roll(up_own.astype(f32), 64, 1).astype(bf)

    @pl.loop(0, group // 2)
    def _(b):
        at = pl.ds(pl.multiple_of(b * span, span), span)
        heads[at, 128:256] = raw_grad(key_proj, key_gain, grad_key[at] * scale, at)
        heads[at, 256:384] = grad_value[at].astype(bf)

    def to_sibling(c):
        return pltpu.make_async_remote_copy(
            src_ref=result.at[c, 1 - core], dst_ref=sib.at[c], send_sem=sib_send.at[c],
            recv_sem=sib_recv.at[c], device_id=(place.sibling,), device_id_type=MESH)

    def across(h, k, far):
        return pltpu.make_async_remote_copy(
            src_ref=cross_out.at[h, k, far], dst_ref=cross_in.at[h, k, far], send_sem=cross_send.at[h, k, far],
            recv_sem=cross_recv.at[h, k, far], device_id=(place.last(h),), device_id_type=MESH)

    def along(h, k):
        return pltpu.make_async_remote_copy(
            src_ref=z_out.at[h, k], dst_ref=z_in.at[h, k], send_sem=z_send.at[h, k],
            recv_sem=z_recv.at[h, k], device_id=(across_z,), device_id_type=MESH)

    def first(h):
        return pltpu.make_async_remote_copy(
            src_ref=first_out.at[h], dst_ref=first_in.at[h], send_sem=first_send.at[h],
            recv_sem=first_recv.at[h], device_id=(place.first(h),), device_id_type=MESH)

    def both(c, h):
        part = pl.ds(h * half, half)
        return result[c, core, part].astype(f32) + sib[c, part].astype(f32)

    def pair_sum(c):
        far, dx, dy = 1 - c // 4, c % 2, c // 2 % 2
        to_sibling(c).wait_recv()
        for h, away, k in ((0, dx, dy), (1, dy, dx)):
            @pl.when(away == 1)
            def _():
                cross_out[h, k, far] = both(c, h).astype(bf)
                across(h, k, far).start()

    @pl.loop(0, group // 2 + 1)
    def _(c):
        @pl.when(c < group // 2)
        def _():
            far, dx, dy = 1 - c // 4, c % 2, c // 2 % 2
            o = (z + far * (1 - 2 * z)) * 4 + place.chip_at(dx, dy, 0)
            mine = heads[pl.ds(pl.multiple_of(o * span, span), span), :]
            matrix = weights[...].reshape(2 * group * depth, 512)[:, 0:384]
            part = lax.dot_general(mine, matrix, flip, preferred_element_type=f32)
            result[c, :, :, 0:width] = part.astype(bf).reshape(2, rows, width)
            low = jnp.zeros((span, 128), f32)
            owner = lax.broadcasted_iota(jnp.int32, low.shape, 1) // rank
            for j in range(3):
                term = jnp.dot(mine[:, j * 128 : (j + 1) * 128], up_own, preferred_element_type=f32)
                low = jnp.where(owner == j, term, low)
            result[c, :, :, width:] = low.astype(bf).reshape(2, rows, 128)
            to_sibling(c).start()

        @pl.when(c >= 1)
        def _():
            pair_sum(c - 1)

        part_steps(group // 2 + c)

    @pl.loop(0, group // 2)
    def _(e):
        far, k, h = 1 - e // 4, e // 2 % 2, e % 2
        c = (1 - far) * 4 + k * (2 - h)
        across(h, k, far).wait_recv()
        total = both(c, h) + cross_in[h, k, far].astype(f32)

        @pl.when(far == 1)
        def _():
            z_out[h, k] = total.astype(bf)
            along(h, k).start()

        @pl.when(far == 0)
        def _():
            along(h, k).wait_recv()
            whole = total + z_in[h, k].astype(f32)

            @pl.when(k == 1)
            def _():
                first_out[h] = whole.astype(bf)
                first(h).start()

            @pl.when(k == 0)
            def _():
                out[pl.ds(h * half, half)] = whole

        part_steps(group + 1 + e)

    part_steps(25)

    owner = lax.broadcasted_iota(jnp.int32, (128, 128), 0) // rank
    up = jnp.zeros((128, 128), f32)
    for j in range(3):
        term = lax.dot_general(inner[...], heads[:, j * 128 : (j + 1) * 128], tall, preferred_element_type=f32)
        up = jnp.where(owner == j, term, up)
    up_terms[...] = up
    for h in range(2):
        first(h).wait_recv()
        out[pl.ds(h * half, half)] += first_in[h].astype(f32)
    part_steps(26)
    lane = lax.broadcasted_iota(jnp.int32, (rows, 128), 1)
    grad_inner = jnp.where(lane < 3 * rank, out[:, width:], 0.0).astype(bf)
    late[...] = lax.dot_general(grad_inner, normed[...], tall, preferred_element_type=f32)[: 3 * rank]
    late_keep.start()

    @pl.loop(1, group)
    def _(i):
        late_to((p + i) % group, p).start()

    downs = weights[:, :, 384:512].reshape(2 * group * depth, 128)
    grad_normed = out[:, 0:width] + lax.dot_general(grad_inner, downs, flip, preferred_element_type=f32)
    ours = rows_in[...].astype(f32)
    inverse = lax.rsqrt(jnp.mean(ours * ours, axis=-1, keepdims=True) + epsilon)
    unit = ours * inverse
    scaled = grad_normed * rows_gain[...]
    grad = inverse * (scaled - unit * jnp.mean(scaled * unit, axis=-1, keepdims=True))
    grad_rows[...] = (grad_middle[...] + grad).astype(bf)
    part_steps(27)
    early_keep.wait()
    late_keep.wait()

    @pl.loop(1, group)
    def _(i):
        q = (p + i) % group
        early_to(q, q).wait_recv()
        late_to(q, q).wait_recv()

    sums = jnp.sum(early_in[...], axis=0)
    owned[0 : 3 * rank] = jnp.sum(late_in[...], axis=0)
    owned[3 * rank : 4 * rank] = sums[:rank]
    owned[4 * rank : 7 * rank] = up_terms[0 : 3 * rank]
    owned[7 * rank : 8 * rank] = sums[rank:]
    for side in range(2):
        q = 2 * p + side

        @pl.when(q != me)
        def _():
            to_owner(side, q, me // group).start()

        @pl.when(q == me)
        def _():
            owned_keep.start()

    for h in range(2):
        part_first(h).wait_recv()
        side = pl.ds(h * half, half)
        output[side] = (middle[side] + part_sum[h] + part_first_in[h].astype(f32)).astype(bf)
    for s in range(2):
        source = s * group + me // 2

        @pl.when(source != me)
        def _():
            to_owner(0, source, s).wait_recv()

        @pl.when(source == me)
        def _():
            owned_keep.wait()

    @pl.loop(1, group)
    def _(i):
        to_head((p + i) % group).wait_send()
        early_to((p + i) % group, p).wait_send()
        late_to((p + i) % group, p).wait_send()

    for side in range(2):
        @pl.when(2 * p + side != me)
        def _():
            to_owner(side, 2 * p + side, me // group).wait_send()

    for h in range(2):
        part_first(h).wait_send()

    @pl.loop(0, 4)
    def _(level):
        for k in range(2):
            for h in range(2):
                part_across(h, k, level).wait_send()

                @pl.when(level > place.z)
                def _():
                    part_along(h, k, level, 1, level).wait_send()

                @pl.when(level < place.z)
                def _():
                    part_along(h, k, level, 0, down_slot(level)).wait_send()

    @pl.loop(0, group // 2)
    def _(c):
        to_sibling(c).wait_send()
        across(c % 2, c // 2 % 2, c // 4).wait_send()

        @pl.when(c < 4)
        def _():
            along(c % 2, c // 2).wait_send()

        @pl.when(c < 2)
        def _():
            first(c).wait_send()


def back(grad_mixed, part, weights, query, key, value, query_proj, key_proj, inner, cosine, sine,
         query_gain, key_gain, segs, rows_in, normed, rows_gain, grad_middle, middle, early, rank):
    rows, width = grad_mixed.shape
    seq = query.shape[0]
    group = seq // rows
    bf, f32 = jnp.bfloat16, jnp.float32
    dma = pltpu.SemaphoreType.DMA
    vmem = pl.BlockSpec(memory_space=pltpu.VMEM)
    wide = width + 128
    piece = (rows // 2, wide)
    own = part.shape[2:]
    return pl.pallas_call(
        functools.partial(back_kernel, rows, rank),
        out_shape=(
            jax.ShapeDtypeStruct((rows, width), bf),
            jax.ShapeDtypeStruct((rows, width), bf),
            jax.ShapeDtypeStruct((2, 8 * rank, 128), f32),
        ),
        in_specs=[vmem, pl.BlockSpec(memory_space=pl.ANY)] + [vmem] * 18,
        out_specs=(vmem, vmem, vmem),
        scratch_shapes=[
            pltpu.VMEM((rows, wide), f32),
            pltpu.VMEM((128, 128), f32),
            pltpu.VMEM((2,) + own, f32),
            pltpu.VMEM((3 * rank, width), f32),
            pltpu.VMEM((group, 2 * rank, 128), f32),
            pltpu.VMEM((group, 3 * rank, 128), f32),
            pltpu.VMEM((8 * rank, 128), f32),
            dma((group,)), dma((group,)), dma((group,)), dma((group,)), dma((2,)), dma((2,)), dma((3,)),
            pltpu.VMEM((group, rows, 128), bf),
            pltpu.VMEM((seq, 128), f32),
            pltpu.VMEM((128, seq), bf),
            pltpu.VMEM((seq, 128), f32),
            pltpu.VMEM((seq, 128), f32),
            pltpu.VMEM((seq, 384), bf),
            pltpu.VMEM((group // 2, 2, rows, wide), bf),
            pltpu.VMEM((group // 2, rows, wide), bf),
            pltpu.VMEM((2, 2, 2) + piece, bf),
            pltpu.VMEM((2, 2, 2) + piece, bf),
            pltpu.VMEM((2, 2) + piece, bf),
            pltpu.VMEM((2, 2) + piece, bf),
            pltpu.VMEM((2,) + piece, bf),
            pltpu.VMEM((2,) + piece, bf),
            pltpu.VMEM((2, 2, LEVELS) + own, bf),
            pltpu.VMEM((2, 2, LEVELS) + own, bf),
            pltpu.VMEM((2, 2, LEVELS + 1) + own, bf),
            pltpu.VMEM(own, f32),
            pltpu.VMEM((2,) + own, bf),
            pltpu.VMEM((2,) + own, bf),
            dma((2, 2, LEVELS)), dma((2, 2, LEVELS)), dma((2, 2, LEVELS)), dma((2, 2, LEVELS)), dma((2, 2, LEVELS + 1)),
            dma((2,)), dma((2,)),
            dma((group,)), dma((group,)), dma, dma((group // 2,)), dma((group // 2,)),
            dma((2, 2, 2)), dma((2, 2, 2)), dma((2, 2)), dma((2, 2)), dma((2,)), dma((2,)),
        ],
        compiler_params=pltpu.CompilerParams(collective_id=2, has_side_effects=True, vmem_limit_bytes=63 << 20),
        name="back",
    )(grad_mixed, part, weights, query, key, value, query_proj, key_proj, inner, cosine, sine,
      query_gain, key_gain, segs, rows_in, normed, rows_gain, grad_middle, middle, early)


def heads_plan(
    tokens,
    segments,
    routes,
    gates,
    sequence_adapter_index,
    attention_norm_gain,
    query_norm_gain,
    key_norm_gain,
    query_weight,
    key_weight,
    value_weight,
    output_weight,
    adapter_down_factors,
    adapter_up_factors,
    expert_norm_gain,
    expert_gate_weight,
    expert_up_weight,
    expert_down_weight,
    output_gradient,
):
    bf, f32 = jnp.bfloat16, jnp.float32
    devices = lax.axis_size("fsdp")
    rows_dev, width = tokens.shape
    seqs = segments.shape[0]
    rank = adapter_down_factors.shape[3]
    slots = 4 * rank
    own_rows = query_weight.shape[0]
    device = lax.axis_index("fsdp")
    attn_scale = attention_norm_gain.astype(f32)
    query_scale = query_norm_gain.astype(f32)
    key_scale = key_norm_gain.astype(f32)
    ffn_scale = expert_norm_gain.astype(f32)

    head_gains = (query_scale.reshape(1, HEAD_DIM), key_scale.reshape(1, HEAD_DIM))
    (middle, normed_ffn, normed, mixed, out_inner, head_weights, query, key, value, query_proj, key_proj, inner_all,
     coeff_own, *turns, output_matrix) = front(
        sequence_adapter_index, tokens, attn_scale.reshape(1, width), query_weight, key_weight, value_weight,
        segments, adapter_down_factors,
        adapter_up_factors, routes, gates, output_weight, *head_gains, ffn_scale.reshape(1, width),
    )
    slab_gate = expert_gate_weight[0]
    slab_up = expert_up_weight[0]
    slab_down = expert_down_weight[0]
    grad_middle, grad_mixed, early, part, _ = experts_pass(
        normed_ffn, output_gradient, slab_gate, slab_up, slab_down, coeff_own, middle, ffn_scale.reshape(1, width),
        output_matrix.reshape(width, width), head_weights, out_inner, mixed, rank,
    )

    grad_tokens, output, terms = back(
        grad_mixed, part, head_weights, query, key, value, query_proj, key_proj, inner_all,
        *turns, *head_gains, segments,
        tokens, normed, attn_scale.reshape(1, width), grad_middle, middle,
        early, rank,
    )
    terms = lax.dynamic_slice_in_dim(terms, device % 2 * own_rows, own_rows, 2)
    selected = (
        jnp.arange(ADAPTER_COUNT, dtype=jnp.int32)[:, None] == sequence_adapter_index[None, :]
    ).astype(f32)
    spread = jnp.sum(selected[:, :, None, None] * terms[None], axis=1)
    spread = spread.reshape(ADAPTER_COUNT, 2, 4, rank, own_rows)
    grad_down = spread[:, 0].transpose(0, 1, 3, 2)
    grad_up = spread[:, 1]
    return (output, grad_tokens, grad_down, grad_up)


def solution(mesh):
    plan = heads_plan if mesh.shape["fsdp"] == LEVELS * 8 else shards
    in_specs = (
        P("fsdp", None),
        P(),
        P("fsdp", None),
        P("fsdp", None),
        P(),
        P(),
        P(),
        P(),
        P("fsdp", None),
        P("fsdp", None),
        P("fsdp", None),
        P("fsdp", None),
        P(None, None, "fsdp", None),
        P(None, None, None, "fsdp"),
        P(),
        P("fsdp", None, None),
        P("fsdp", None, None),
        P("fsdp", None, None),
        P("fsdp", None),
    )
    out_specs = (
        P("fsdp", None),
        P("fsdp", None),
        P(None, None, "fsdp", None),
        P(None, None, None, "fsdp"),
    )
    return jax.shard_map(plan, mesh=mesh, in_specs=in_specs, out_specs=out_specs, check_vma=False)
```

```python
import functools
import math

import jax
import jax.numpy as jnp
import numpy as np
from jax import lax
from jax.experimental import pallas as pl
from jax.experimental.pallas import tpu as pltpu
from jax.sharding import PartitionSpec as P

HEAD_DIM = 128
TOPK = 8
ADAPTER_COUNT = 8
SEQ_LEN = 2048


epsilon = 1e-06
rope_base = 50000.0


def from_partner(value, axis, distance):
    mask = 2**distance
    pairs = [(source, source ^ mask) for source in range(lax.axis_size(axis))]
    return lax.ppermute(value, axis, pairs)


def matmul(left, right):
    return jnp.dot(left, right, preferred_element_type=jnp.float32)


def rms_scale(rows, gain):
    return rows * lax.rsqrt(jnp.mean(rows * rows, axis=-1, keepdims=True) + epsilon) * gain


def rms_back(rows, gain, upstream):
    inverse = lax.rsqrt(jnp.mean(rows * rows, axis=-1, keepdims=True) + epsilon)
    unit = rows * inverse
    scaled = upstream * gain
    return inverse * (scaled - unit * jnp.mean(scaled * unit, axis=-1, keepdims=True))


def rope_tables(positions):
    half = HEAD_DIM // 2
    frequency = rope_base ** (-(jnp.arange(half, dtype=jnp.float32) * 2.0 / HEAD_DIM))
    angle = positions[:, None] * frequency[None, :]
    return (jnp.cos(angle)[:, None, :], jnp.sin(angle)[:, None, :])


def rotate(rows, cosine, sine):
    half = rows.shape[-1] // 2
    first = rows[..., :half]
    second = rows[..., half:]
    return jnp.concatenate(
        [first * cosine - second * sine, second * cosine + first * sine], axis=-1
    )


def rotate_back(upstream, cosine, sine):
    half = upstream.shape[-1] // 2
    first = upstream[..., :half]
    second = upstream[..., half:]
    return jnp.concatenate(
        [first * cosine + second * sine, second * cosine - first * sine], axis=-1
    )


def pick(table, index):
    return lax.dynamic_index_in_dim(table, index, 0, keepdims=False)


def shards(
    tokens,
    segments,
    routes,
    gates,
    sequence_adapter_index,
    attention_norm_gain,
    query_norm_gain,
    key_norm_gain,
    query_weight,
    key_weight,
    value_weight,
    output_weight,
    adapter_down_factors,
    adapter_up_factors,
    expert_norm_gain,
    expert_gate_weight,
    expert_up_weight,
    expert_down_weight,
    output_gradient,
):
    rows_dev = tokens.shape[0]
    width = tokens.shape[1]
    heads = width // HEAD_DIM
    group = SEQ_LEN // rows_dev
    level_list = group.bit_length() - 1
    device = lax.axis_index("fsdp")
    place = device % group
    sequence = device // group
    segment_row = pick(segments, sequence)
    own_segment = lax.dynamic_slice_in_dim(segment_row, place * rows_dev, rows_dev)
    adapter = pick(sequence_adapter_index, sequence)
    scale = 1.0 / math.sqrt(HEAD_DIM)
    cosine, sine = rope_tables(
        (place * rows_dev + jnp.arange(rows_dev, dtype=jnp.int32)).astype(jnp.float32)
    )
    attn_scale = attention_norm_gain.astype(jnp.float32)
    query_scale = query_norm_gain.astype(jnp.float32)
    key_scale = key_norm_gain.astype(jnp.float32)
    ffn_scale = expert_norm_gain.astype(jnp.float32)
    gathered = (
        lax.all_gather(query_weight, "fsdp", axis=0, tiled=True),
        lax.all_gather(key_weight, "fsdp", axis=0, tiled=True),
        lax.all_gather(value_weight, "fsdp", axis=0, tiled=True),
        lax.all_gather(output_weight, "fsdp", axis=0, tiled=True),
        lax.all_gather(adapter_down_factors, "fsdp", axis=2, tiled=True),
        lax.all_gather(adapter_up_factors, "fsdp", axis=3, tiled=True),
    )
    matrices = gathered[:4]
    down_own = pick(gathered[4], adapter)
    up_own = pick(gathered[5], adapter)

    def project(inputs, index):
        inner = matmul(inputs, down_own[index]).astype(jnp.bfloat16)
        return (matmul(inputs, matrices[index]) + matmul(inner, up_own[index]), inner)

    rows = tokens.astype(jnp.float32)
    normed = rms_scale(rows, attn_scale).astype(jnp.bfloat16)
    query_proj, query_inner = project(normed, 0)
    key_proj, key_inner = project(normed, 1)
    value_proj, value_inner = project(normed, 2)
    query_heads = query_proj.reshape(rows_dev, heads, HEAD_DIM)
    key_heads = key_proj.reshape(rows_dev, heads, HEAD_DIM)
    query_rot = rotate(rms_scale(query_heads, query_scale), cosine, sine).astype(jnp.bfloat16)
    key_rot = (
        rotate(rms_scale(key_heads, key_scale), cosine, sine)
        .astype(jnp.bfloat16)
        .reshape(rows_dev, width)
    )
    value_low = value_proj.astype(jnp.bfloat16)
    held_keys = key_rot
    held_values = value_low
    for level in range(level_list):
        other_keys, other_values = from_partner((held_keys, held_values), "fsdp", level)
        upper_bit = place // (1 << level) % 2 == 1
        held_keys = jnp.where(
            upper_bit,
            jnp.concatenate([other_keys, held_keys], axis=0),
            jnp.concatenate([held_keys, other_keys], axis=0),
        )
        held_values = jnp.where(
            upper_bit,
            jnp.concatenate([other_values, held_values], axis=0),
            jnp.concatenate([held_values, other_values], axis=0),
        )
    keys_all = held_keys.reshape(SEQ_LEN, heads, HEAD_DIM)
    values_all = held_values.reshape(SEQ_LEN, heads, HEAD_DIM)
    allowed = (own_segment[:, None] == segment_row[None, :])[None]

    def masked_scores():
        raw = (
            jnp.einsum("thd,shd->hts", query_rot, keys_all, preferred_element_type=jnp.float32)
            * scale
        )
        return jnp.where(allowed, raw, -1e30)

    scores = masked_scores()
    maximum = jnp.max(scores, axis=-1, keepdims=True)
    weights = jnp.exp(scores - maximum)
    total = jnp.sum(weights, axis=-1, keepdims=True)
    probs = weights / total
    log_total = maximum + jnp.log(total)
    mixed = jnp.einsum(
        "hts,shd->thd", probs.astype(jnp.bfloat16), values_all, preferred_element_type=jnp.float32
    )
    mixed = mixed.astype(jnp.bfloat16).reshape(rows_dev, width)
    attn_proj, out_inner = project(mixed, 3)
    middle = rows + attn_proj
    normed_ffn = rms_scale(middle, ffn_scale).astype(jnp.bfloat16)
    experts = lax.axis_size("fsdp") // 2
    capacity = 2 * rows_dev * TOPK // experts
    flat_routes = routes.reshape(-1)
    onehot = (flat_routes[:, None] == jnp.arange(experts, dtype=jnp.int32)[None, :]).astype(
        jnp.int32
    )
    slot = jnp.sum(jnp.cumsum(onehot, axis=0) * onehot, axis=1) - 1
    target = flat_routes * capacity + slot

    def spread(entries):
        buffer = jnp.zeros((experts * capacity, width), jnp.bfloat16).at[target].set(entries)
        buffer = buffer.reshape(experts, 1, capacity, width)
        return jnp.broadcast_to(buffer, (experts, 2, capacity, width)).reshape(
            2 * experts, capacity, width
        )

    def collect(returned):
        halves = returned.reshape(experts, 2, capacity, width).astype(jnp.float32)
        summed = (halves[:, 0] + halves[:, 1]).reshape(experts * capacity, width)
        return summed[target].reshape(rows_dev, TOPK, width)

    slab_gate = expert_gate_weight[0]
    slab_up = expert_up_weight[0]
    slab_down = expert_down_weight[0]
    dispatched = lax.all_to_all(
        spread(jnp.repeat(normed_ffn, TOPK, axis=0)),
        "fsdp",
        split_axis=0,
        concat_axis=0,
        tiled=True,
    )
    gate_part = jnp.einsum("scd,dh->sch", dispatched, slab_gate, preferred_element_type=jnp.float32)
    up_part = jnp.einsum("scd,dh->sch", dispatched, slab_up, preferred_element_type=jnp.float32)
    hidden = (jax.nn.silu(gate_part) * up_part).astype(jnp.bfloat16)
    produced = jnp.einsum(
        "sch,hd->scd", hidden, slab_down, preferred_element_type=jnp.float32
    ).astype(jnp.bfloat16)
    returned = lax.all_to_all(produced, "fsdp", split_axis=0, concat_axis=0, tiled=True)
    moe = jnp.sum(gates[:, :, None] * collect(returned), axis=1)
    output = (middle + moe).astype(jnp.bfloat16)
    upstream = output_gradient.astype(jnp.float32)
    grad_parts = (
        (gates[:, :, None] * upstream[:, None, :])
        .astype(jnp.bfloat16)
        .reshape(rows_dev * TOPK, width)
    )
    grad_sent = lax.all_to_all(spread(grad_parts), "fsdp", split_axis=0, concat_axis=0, tiled=True)
    grad_hidden = jnp.einsum(
        "scd,hd->sch", grad_sent, slab_down, preferred_element_type=jnp.float32
    )
    sigmoid = jax.nn.sigmoid(gate_part)
    grad_gate = (grad_hidden * up_part * sigmoid * (1.0 + gate_part * (1.0 - sigmoid))).astype(
        jnp.bfloat16
    )
    grad_up = (grad_hidden * gate_part * sigmoid).astype(jnp.bfloat16)
    grad_inputs = jnp.einsum(
        "sch,dh->scd", grad_gate, slab_gate, preferred_element_type=jnp.float32
    )
    grad_inputs = (
        grad_inputs
        + jnp.einsum("sch,dh->scd", grad_up, slab_up, preferred_element_type=jnp.float32)
    ).astype(jnp.bfloat16)
    grad_back = lax.all_to_all(grad_inputs, "fsdp", split_axis=0, concat_axis=0, tiled=True)
    grad_ffn = jnp.sum(collect(grad_back), axis=1)
    grad_middle = upstream + rms_back(middle, ffn_scale, grad_ffn)
    grad_attn = grad_middle.astype(jnp.bfloat16)
    regathered = (
        lax.all_gather(query_weight, "fsdp", axis=0, tiled=True),
        lax.all_gather(key_weight, "fsdp", axis=0, tiled=True),
        lax.all_gather(value_weight, "fsdp", axis=0, tiled=True),
        lax.all_gather(output_weight, "fsdp", axis=0, tiled=True),
        lax.all_gather(adapter_down_factors, "fsdp", axis=2, tiled=True),
        lax.all_gather(adapter_up_factors, "fsdp", axis=3, tiled=True),
    )
    back_matrices = regathered[:4]
    back_down = pick(regathered[4], adapter)
    back_up = pick(regathered[5], adapter)

    def project_back(inputs, inner, upstream_low, index):
        grad_inner = matmul(upstream_low, back_up[index].T).astype(jnp.bfloat16)
        grad_input = matmul(upstream_low, back_matrices[index].T) + matmul(
            grad_inner, back_down[index].T
        )
        return (grad_input, matmul(inputs.T, grad_inner), matmul(inner.T, upstream_low))

    grad_mixed_full, down_output, up_output = project_back(mixed, out_inner, grad_attn, 3)
    grad_mixed = grad_mixed_full.astype(jnp.bfloat16).reshape(rows_dev, heads, HEAD_DIM)
    probs = jnp.exp(masked_scores() - log_total)
    grad_probs = jnp.einsum(
        "thd,shd->hts", grad_mixed, values_all, preferred_element_type=jnp.float32
    )
    grad_scores = (
        probs * (grad_probs - jnp.sum(probs * grad_probs, axis=-1, keepdims=True))
    ).astype(jnp.bfloat16)
    grad_query = (
        jnp.einsum("hts,shd->thd", grad_scores, keys_all, preferred_element_type=jnp.float32)
        * scale
    )
    grad_keys_part = (
        jnp.einsum("hts,thd->shd", grad_scores, query_rot, preferred_element_type=jnp.float32)
        * scale
    )
    grad_keys_part = grad_keys_part.reshape(group, rows_dev, width)
    grad_values_part = jnp.einsum(
        "hts,thd->shd", probs.astype(jnp.bfloat16), grad_mixed, preferred_element_type=jnp.float32
    )
    grad_values_part = grad_values_part.reshape(group, rows_dev, width)
    for level in reversed(range(level_list)):
        size_half = 1 << level
        upper_bit = place // size_half % 2 == 1
        keep_keys = jnp.where(upper_bit, grad_keys_part[size_half:], grad_keys_part[:size_half])
        send_keys = jnp.where(upper_bit, grad_keys_part[:size_half], grad_keys_part[size_half:])
        keep_values = jnp.where(
            upper_bit, grad_values_part[size_half:], grad_values_part[:size_half]
        )
        send_values = jnp.where(
            upper_bit, grad_values_part[:size_half], grad_values_part[size_half:]
        )
        got_keys, got_values = (
            from_partner(send_keys.astype(jnp.bfloat16), "fsdp", level).astype(send_keys.dtype),
            from_partner(send_values.astype(jnp.bfloat16), "fsdp", level).astype(send_values.dtype),
        )
        grad_keys_part = keep_keys + got_keys
        grad_values_part = keep_values + got_values
    grad_keys = grad_keys_part[0]
    grad_values = grad_values_part[0]
    grad_value_proj = grad_values.astype(jnp.bfloat16)
    grad_key_proj = rms_back(
        key_heads,
        key_scale,
        rotate_back(grad_keys.reshape(rows_dev, heads, HEAD_DIM), cosine, sine),
    )
    grad_key_proj = grad_key_proj.reshape(rows_dev, width).astype(jnp.bfloat16)
    grad_query_proj = rms_back(query_heads, query_scale, rotate_back(grad_query, cosine, sine))
    grad_query_proj = grad_query_proj.reshape(rows_dev, width).astype(jnp.bfloat16)
    grad_from_query, down_query, up_query = project_back(normed, query_inner, grad_query_proj, 0)
    grad_from_key, down_key, up_key = project_back(normed, key_inner, grad_key_proj, 1)
    grad_from_value, down_value, up_value = project_back(normed, value_inner, grad_value_proj, 2)
    grad_normed = grad_from_query + grad_from_key + grad_from_value
    grad_tokens = (grad_middle + rms_back(rows, attn_scale, grad_normed)).astype(jnp.bfloat16)
    down_terms = jnp.stack([down_query, down_key, down_value, down_output])
    up_terms = jnp.stack([up_query, up_key, up_value, up_output])
    selected = (jnp.arange(ADAPTER_COUNT, dtype=jnp.int32) == adapter).astype(jnp.float32)[
        :, None, None, None
    ]
    grad_down, grad_up = (
        lax.psum_scatter(selected * down_terms[None], "fsdp", scatter_dimension=2, tiled=True),
        lax.psum_scatter(selected * up_terms[None], "fsdp", scatter_dimension=3, tiled=True),
    )
    return (output, grad_tokens, grad_down, grad_up)


epsilon = 1e-06
MESH = pl.DeviceIdType.MESH
LEVELS = 4
CHIPS = 16


def greet_all(me, devices):
    barrier = pltpu.get_barrier_semaphore()

    @pl.loop(1, devices)
    def _(i):
        pl.semaphore_signal(barrier, inc=1, device_id=((me + i) % devices,), device_id_type=MESH)


def segments_at(segs, sequence, at):
    row = segs[0:1, at]
    for s in range(1, segs.shape[0]):
        row = jnp.where(sequence == s, segs[s : s + 1, at], row)
    return row.astype(jnp.float32)


class Place:
    def __init__(self):
        self.me = me = lax.axis_index("fsdp")
        self.core = me % 2
        self.x = me // 2 % 2
        self.y = me // 4 % 2
        self.z = me // 8
        self.sibling = me + 1 - 2 * self.core
        self.across_x = me + 2 - 4 * self.x
        self.across_y = me + 4 - 8 * self.y

    def level(self, i):
        upper = self.z // 2
        inner = self.z * (1 - upper) + (3 - self.z) * upper
        turn = i + inner * (1 - 2 * i) * (1 - i // 2)
        return turn + upper * (3 - 2 * turn)

    def chip(self, half, side, level):
        flip = 1 - 2 * side
        y = self.y + (1 - half) * side * (1 - 2 * self.y)
        x = self.x + half * side * (1 - 2 * self.x)
        return level * 4 + y * 2 + x

    def chip_at(self, dx, dy, level):
        y = self.y + dy * (1 - 2 * self.y)
        x = self.x + dx * (1 - 2 * self.x)
        return level * 4 + y * 2 + x

    def first(self, half):
        return self.across_y * (1 - half) + self.across_x * half

    def last(self, half):
        return self.across_x * (1 - half) + self.across_y * half


OUTER_STEPS = (
    819265, 8651264, 12861442, 50372656, 8931409, 17432627, 13697571, 13172803, 37790773, 54809233, 34645544,
    42607251, 15008899, 14756500, 11890914, 65086601, 16013475, 59585160, 15800984, 41180860, 12187788, 16326300,
    37256878, 49626350, 11353642, 15294205, 36592266, 15561967, 40523830, 79254266, 10041135, 49140263, 35279415,
    65867414, 77672101, 60178981, 78533815, 43118213, 76663074, 64638646, 75646758, 126075173, 126075360, 126075360,
    126075360, 126075360, 126075360, 126075360, 126075360, 126075360, 126075360, 126075360,
)
INNER_STEPS = (
    297029, 30459904, 543235, 9464372, 51440213, 10266665, 8704550, 8409348, 14486081, 12612200, 14231616, 14705273,
    39127121, 11903096, 8953965, 71373446, 11568294, 35459180, 17594915, 13173376, 47565949, 15754834, 37812375,
    42247925, 18406959, 28859544, 39395993, 16349409, 36998782, 66092674, 22609570, 41228375, 34395178, 49923218,
    28071580, 66659898, 15529128, 37297787, 31027944, 26819743, 36265721, 62723687, 78966458, 26555547, 75847418,
    79259371, 77945587, 77716258, 78737199, 78507818, 76693795, 76959015,
)


def experts_kernel(rows, rank, x_ref, up_ref, gate_w, up_w, down_w, coeff, own_up, middle, gains, matrix, weights, out_inner, mixed,
                   grad_middle, grad_mixed, early, part_out, gathered,
                   out, held_w, pairs, tail_sem,
                   block, part_buf, result, sib, cross_out, cross_in, hold, z_in, first_out, first_in, total,
                   local_sem, load_sem, part_sem, send, recv, sib_send, sib_recv, cross_send, cross_recv,
                   z_send, z_recv, first_send, first_recv):
    place = Place()
    half = rows // 2
    f32, bf = jnp.float32, jnp.bfloat16
    flip = (((1,), (1,)), ((), ()))
    me, core = place.me, place.core
    upper = place.z // 2
    inner = place.z * (1 - upper) + (3 - place.z) * upper
    UP, DOWN, LAST, SIB, FIRST = range(5)

    def move(n, h, o, kind, target):
        piece = gathered.at[2 * o + core, h, n]
        return pltpu.make_async_remote_copy(
            src_ref=piece, dst_ref=piece, send_sem=send.at[kind, n, h, o],
            recv_sem=recv.at[1 if kind == SIB else 0, n, h, o], device_id=(target,), device_id_type=MESH)

    def arrived(n, h, o, sibling):
        piece = gathered.at[2 * o + (1 - core if sibling else core), h, n]
        pltpu.make_async_remote_copy(
            src_ref=piece, dst_ref=piece, send_sem=send.at[SIB, n, h, o],
            recv_sem=recv.at[1 if sibling else 0, n, h, o], device_id=(place.sibling,), device_id_type=MESH).wait_recv()

    def column(n, h, o, level, act):
        @pl.when((level <= place.z) & (place.z < LEVELS - 1))
        def _():
            act(move(n, h, o, UP, me + 8))

        @pl.when((level >= place.z) & (place.z > 0))
        def _():
            act(move(n, h, o, DOWN, me - 8))

    def spread(n, h, o, level, act):
        column(n, h, o, level, act)
        act(move(n, h, o, LAST, place.last(h)))
        act(move(n, h, o, SIB, place.sibling))

    def to_sibling(slot):
        return pltpu.make_async_remote_copy(
            src_ref=result.at[slot, 1 - core], dst_ref=sib.at[slot], send_sem=sib_send.at[slot],
            recv_sem=sib_recv.at[slot], device_id=(place.sibling,), device_id_type=MESH)

    def across(h, k, level):
        return pltpu.make_async_remote_copy(
            src_ref=cross_out.at[h, k, level], dst_ref=cross_in.at[h, k, level], send_sem=cross_send.at[h, k, level],
            recv_sem=cross_recv.at[h, k, level], device_id=(place.last(h),), device_id_type=MESH)

    def along(h, k, level, up, slot):
        return pltpu.make_async_remote_copy(
            src_ref=hold.at[h, k, level], dst_ref=z_in.at[h, k, slot], send_sem=z_send.at[h, k, level],
            recv_sem=z_recv.at[h, k, slot], device_id=(me - 8 + 16 * up,), device_id_type=MESH)

    def first(h):
        return pltpu.make_async_remote_copy(
            src_ref=first_out.at[h], dst_ref=first_in.at[h], send_sem=first_send.at[h],
            recv_sem=first_recv.at[h], device_id=(place.first(h),), device_id_type=MESH)

    def down_slot(level):
        ends = 1 - jnp.minimum(jnp.abs(level - (place.z - 1)), 1)
        return level + ends * (LEVELS - level)

    start = lambda copy: copy.start()
    done = lambda copy: copy.wait_send()
    mine = me // 2
    barrier = pltpu.get_barrier_semaphore()

    def greet(other):
        pl.semaphore_signal(barrier, inc=1, device_id=(other,), device_id_type=MESH)

    for other in (place.sibling, place.across_x, place.across_y):
        greet(other)

    @pl.when(place.z < LEVELS - 1)
    def _():
        greet(me + 8)

    @pl.when(place.z > 0)
    def _():
        greet(me - 8)

    tail = [
        pltpu.make_async_copy(matrix, held_w, tail_sem.at[0]),
        pltpu.make_async_copy(weights.at[:, :, pl.ds(384, 128)], pairs, tail_sem.at[1]),
    ]
    for copy in tail:
        copy.start()
    own = [
        pltpu.make_async_copy(ref.at[pl.ds(h * half, half)], gathered.at[me, h, n], local_sem.at[n, h])
        for n, ref in enumerate((x_ref, up_ref)) for h in range(2)
    ]
    for copy in own:
        copy.start()
    for copy in own:
        copy.wait()
    pl.semaphore_wait(barrier, 4 + inner)
    pieces = [(n, h) for n in range(2) for h in range(2)]
    def keep_part(o, slot):
        return pltpu.make_async_copy(part_buf.at[slot], part_out.at[o], part_sem.at[slot])

    def compute(o, slot, again):
        for n, h in pieces:
            arrived(n, h, o, True)
        load = pltpu.make_async_copy(gathered.at[pl.ds(2 * o, 2)], block, load_sem)
        load.start()

        @pl.when(again)
        def _():
            to_sibling(slot).wait_send()

        load.wait()
        c = [jnp.broadcast_to(coeff[2 * o + side], (rows, rows)).T[:, 0:1] for side in range(2)]
        c = jnp.concatenate(c, axis=0)
        x = block[:, :, 0].reshape(2 * rows, -1)
        gate = jnp.dot(x, gate_w[...], preferred_element_type=f32)
        up = jnp.dot(x, up_w[...], preferred_element_type=f32)
        sig = jax.nn.sigmoid(gate)
        silu = gate * sig
        hidden = (silu * up).astype(bf)
        part = (c * jnp.dot(hidden, down_w[...], preferred_element_type=f32)).astype(bf)
        part = part.reshape(2, 2, half, -1)
        result[slot, 0, 1] = part[0]
        result[slot, 1, 1] = part[1]
        upstream = (c * block[:, :, 1].reshape(2 * rows, -1).astype(f32)).astype(bf)
        grad_hidden = lax.dot_general(upstream, down_w[...], flip, preferred_element_type=f32)
        grad_gate = (grad_hidden * up * sig * (1.0 + gate * (1.0 - sig))).astype(bf)
        grad_up = (grad_hidden * silu).astype(bf)
        grad = lax.dot_general(grad_gate, gate_w[...], flip, preferred_element_type=f32)
        grad += lax.dot_general(grad_up, up_w[...], flip, preferred_element_type=f32)
        grad = grad.astype(bf).reshape(2, 2, half, -1)
        result[slot, 0, 0] = grad[0]
        result[slot, 1, 0] = grad[1]
        to_sibling(slot).start()

    def pair_sum(dx, dy, level, slot, again):
        to_sibling(slot).wait_recv()

        def pair(n, h):
            return (result[slot, core, n, h].astype(f32) + sib[slot, n, h].astype(f32)).astype(bf)

        for h, away, k in ((0, dx, dy), (1, dy, dx)):
            @pl.when(away == 1)
            def _():
                cross_out[h, k, level] = pair(0, h)
                across(h, k, level).start()

            @pl.when(away == 0)
            def _():
                hold[h, k, level] = pair(0, h)

        o = place.chip_at(dx, dy, level)

        @pl.when(again)
        def _():
            keep_part(o, slot).wait()

        for h in range(2):
            part_buf[slot, h] = pair(1, h)
        keep_part(o, slot).start()

    def column_sum(h, k, level):
        across(h, k, level).wait_recv()
        total[...] = hold[h, k, level].astype(f32) + cross_in[h, k, level].astype(f32)

        @pl.when((level >= place.z) & (place.z > 0))
        def _():
            along(h, k, level, 1, level).wait_recv()
            total[...] += z_in[h, k, level].astype(f32)

        @pl.when((level < place.z) & (place.z < LEVELS - 1))
        def _():
            along(h, k, level, 0, level).wait_recv()
            total[...] += z_in[h, k, level].astype(f32)

        @pl.when((level == place.z) & (place.z < LEVELS - 1))
        def _():
            along(h, k, level, 0, LEVELS).wait_recv()
            total[...] += z_in[h, k, LEVELS].astype(f32)

        @pl.when(level > place.z)
        def _():
            hold[h, k, level] = total[...].astype(bf)
            along(h, k, level, 1, level).start()

        @pl.when(level < place.z)
        def _():
            hold[h, k, level] = total[...].astype(bf)
            along(h, k, level, 0, down_slot(level)).start()

        @pl.when((level == place.z) & (k == 1))
        def _():
            first_out[h] = total[...].astype(bf)
            first(h).start()

        @pl.when((level == place.z) & (k == 0))
        def _():
            out[pl.ds(h * half, half)] = total[...]

    def step(code):
        kind, which = code // 32, code % 32
        h, k, n = which % 2, which // 2 % 2, which // 16
        turn = which // 4 % 4
        level = turn + upper * (3 - 2 * turn)
        o = place.chip(h, k, level)

        @pl.when(kind == 0)
        def _():
            move(which // 2 % 2, h, mine, FIRST, place.first(h)).start()

        @pl.when(kind == 1)
        def _():
            @pl.when((k == 1) | (level != place.z))
            def _():
                arrived(n, h, o, False)

            move(n, h, o, LAST, place.last(h)).start()
            move(n, h, o, SIB, place.sibling).start()

        @pl.when((kind == 2) | (kind == 3))
        def _():
            down = (kind + upper) % 2
            piece = gathered.at[2 * o + core, h, n]
            pltpu.make_async_remote_copy(
                src_ref=piece, dst_ref=piece, send_sem=send.at[down, n, h, o], recv_sem=recv.at[0, n, h, o],
                device_id=(me + 8 - 16 * down,), device_id_type=MESH).start()

        @pl.when(kind == 4)
        def _():
            away = place.chip_at(1 - h + h * k, k + h - h * k, level)
            arrived(n, h, away, False)
            move(n, h, away, SIB, place.sibling).start()

        dx, dy = which % 2, which // 2 % 2

        @pl.when((kind == 5) | (kind == 6))
        def _():
            compute(place.chip_at(dx, dy, level), which // 16, kind == 5)

        @pl.when((kind == 7) | (kind == 8))
        def _():
            pair_sum(dx, dy, level, which // 16, kind == 7)

        @pl.when(kind == 9)
        def _():
            column_sum(h, k, level)

    @pl.loop(0, len(OUTER_STEPS))
    def _(i):
        word = 0
        for at, (outer_word, inner_word) in enumerate(zip(OUTER_STEPS, INNER_STEPS)):
            word = jnp.where(i == at, jnp.where(inner == 0, outer_word, inner_word), word)

        def one(_, rest):
            step(rest % 512)
            return rest // 512

        lax.fori_loop(0, 3, one, word)

    for h in range(2):
        first(h).wait_recv()
        out[pl.ds(h * half, half)] += first_in[h].astype(f32)
    for copy in tail:
        copy.wait()

    ours = middle[...]
    inverse = lax.rsqrt(jnp.mean(ours * ours, axis=-1, keepdims=True) + epsilon)
    unit = ours * inverse
    scaled = out[...] * gains[1:2]
    grad = inverse * (scaled - unit * jnp.mean(scaled * unit, axis=-1, keepdims=True))
    grad = own_up[...].astype(f32) + grad
    grad_middle[...] = grad
    grad = grad.astype(bf)
    adapters = pairs[...].reshape(-1, 128)
    lane = lax.broadcasted_iota(jnp.int32, (rows, 128), 1)
    low = jnp.dot(grad, adapters, preferred_element_type=f32)
    low = jnp.where(lane // rank == 7, low, 0.0).astype(bf)
    low = pltpu.roll(low.astype(f32), 64, 1).astype(bf)
    back = lax.dot_general(grad, held_w[...], flip, preferred_element_type=f32)
    back += lax.dot_general(low, adapters, flip, preferred_element_type=f32)
    grad_mixed[...] = back.astype(bf)
    tall = (((0,), (0,)), ((), ()))
    early[0:rank] = lax.dot_general(low, mixed[...], tall, preferred_element_type=f32)[3 * rank : 4 * rank]
    early[rank:] = lax.dot_general(out_inner[...], grad, tall, preferred_element_type=f32)[3 * rank : 4 * rank]

    for n, h in pieces:
        move(n, h, mine, FIRST, place.first(h)).wait_send()
        spread(n, h, mine, place.z, done)
        spread(n, h, place.chip(h, 1, place.z), place.z, done)
    for h in range(2):
        first(h).wait_send()
    for slot in range(2):
        to_sibling(slot).wait_send()
        keep_part(0, slot).wait()

    @pl.loop(0, CHIPS)
    def _(t):
        h, k = t % 2, t // 2 % 2

        @pl.when(t < CHIPS - 4)
        def _():
            level = place.level(1 + t // 4)
            for n in range(2):
                spread(n, h, place.chip(h, k, level), level, done)

        dx, dy = t % 2, t // 2 % 2
        o = place.chip_at(dx, dy, t // 4)
        for side, away in ((0, dx), (1, dy)):
            @pl.when(away == 1)
            def _():
                for n in range(2):
                    move(n, side, o, SIB, place.sibling).wait_send()

        level = t // 4
        across(h, k, level).wait_send()

        @pl.when(level > place.z)
        def _():
            along(h, k, level, 1, level).wait_send()

        @pl.when(level < place.z)
        def _():
            along(h, k, level, 0, down_slot(level)).wait_send()


def experts_pass(x, upstream, gate_w, up_w, down_w, coeff, middle, gains, matrix, weights, out_inner, mixed, rank):
    rows, width = x.shape
    devices = coeff.shape[0]
    half = rows // 2
    bf, f32 = jnp.bfloat16, jnp.float32
    dma = pltpu.SemaphoreType.DMA
    vmem, anywhere = pl.BlockSpec(memory_space=pltpu.VMEM), pl.BlockSpec(memory_space=pl.ANY)
    piece = (half, width)
    return pl.pallas_call(
        functools.partial(experts_kernel, rows, rank),
        out_shape=(
            jax.ShapeDtypeStruct((rows, width), f32),
            jax.ShapeDtypeStruct((rows, width), bf),
            jax.ShapeDtypeStruct((2 * rank, width), f32),
            jax.ShapeDtypeStruct((CHIPS, 2) + piece, bf),
            jax.ShapeDtypeStruct((devices, 2, 2) + piece, bf),
        ),
        in_specs=[anywhere, anywhere] + [vmem] * 7 + [anywhere, anywhere, vmem, vmem],
        out_specs=(vmem, vmem, vmem, anywhere, anywhere),
        scratch_shapes=[
            pltpu.VMEM((rows, width), f32),
            pltpu.VMEM(matrix.shape, bf),
            pltpu.VMEM(weights.shape[:2] + (128,), bf),
            dma((2,)),
            pltpu.VMEM((2, 2, 2) + piece, bf),
            pltpu.VMEM((2, 2) + piece, bf),
            pltpu.VMEM((2, 2, 2, 2) + piece, bf),
            pltpu.VMEM((2, 2, 2) + piece, bf),
            pltpu.VMEM((2, 2, LEVELS) + piece, bf),
            pltpu.VMEM((2, 2, LEVELS) + piece, bf),
            pltpu.VMEM((2, 2, LEVELS) + piece, bf),
            pltpu.VMEM((2, 2, LEVELS + 1) + piece, bf),
            pltpu.VMEM((2,) + piece, bf),
            pltpu.VMEM((2,) + piece, bf),
            pltpu.VMEM(piece, f32),
            dma((2, 2)), dma, dma((2,)), dma((5, 2, 2, CHIPS)), dma((2, 2, 2, CHIPS)), dma((2,)), dma((2,)),
            dma((2, 2, LEVELS)), dma((2, 2, LEVELS)),
            dma((2, 2, LEVELS)), dma((2, 2, LEVELS + 1)), dma((2,)), dma((2,)),
        ],
        compiler_params=pltpu.CompilerParams(collective_id=1, has_side_effects=True, vmem_limit_bytes=62 << 20),
        name="experts",
    )(x, upstream, gate_w, up_w, down_w, coeff, upstream, middle, gains, matrix, weights, out_inner, mixed)


def front_kernel(rows, rank, picked, tokens, gains, query_w, key_w, value_w, segs, downs, ups, routes, gates, out_w, near, far_turn,
                 query_gain, key_gain,
                 middle, normed_ffn, normed, mixed, out_inner, weights, query_out, key_out, value_out,
                 query_proj, key_proj, inner_out, coeff_out, cosine, sine, out_all,
                 held, mixed_buf, pair, coeff, wo, heads_w,
                 local_sem, send, recv, w_send, w_recv, pair_send, pair_recv, c_send, c_recv, m_send, m_recv, m_local,
                 g_send, g_recv, keep_sem):
    place = Place()
    f32, bf = jnp.float32, jnp.bfloat16
    me, core = place.me, place.core
    group = held.shape[0]
    base, p = me // group * group, me % group
    other = (me + group) % (2 * group)
    other_base = group - base
    half = rows // 2
    depth = weights.shape[1]
    wide = 3 * 128
    z = place.z % 2
    across_z = me + 8 - 16 * z
    chip = p // 2

    FIRST, ALONG, LAST, SIB = range(4)

    def chip_at(h, k, far):
        flip = place.chip(h, k, 0)
        zz = z + far * (1 - 2 * z)
        return zz * 4 + flip

    def move(h, o, kind, target):
        piece = held.at[2 * o + core, pl.ds(h * half, half)]
        return pltpu.make_async_remote_copy(
            src_ref=piece, dst_ref=piece, send_sem=send.at[kind, h, o],
            recv_sem=recv.at[1 if kind == SIB else 0, h, o], device_id=(target,), device_id_type=MESH)

    def arrived(h, o, sibling):
        piece = held.at[2 * o + (1 - core if sibling else core), pl.ds(h * half, half)]
        pltpu.make_async_remote_copy(
            src_ref=piece, dst_ref=piece, send_sem=send.at[SIB, h, o],
            recv_sem=recv.at[1 if sibling else 0, h, o], device_id=(place.sibling,), device_id_type=MESH).wait_recv()

    def to_heads(q):
        return pltpu.make_async_remote_copy(
            src_ref=heads_w.at[q % group], dst_ref=weights.at[me, :, pl.ds(0, wide)], send_sem=w_send.at[q],
            recv_sem=w_recv.at[me], device_id=(q,), device_id_type=MESH)

    def to_expert(q):
        return pltpu.make_async_remote_copy(
            src_ref=coeff.at[q // 2], dst_ref=coeff_out.at[me], send_sem=c_send.at[q],
            recv_sem=c_recv.at[me], device_id=(q,), device_id_type=MESH)

    def pair_over(q, side):
        row = (me + side * group) % (2 * group)
        piece = weights.at[row, :, pl.ds(wide, 128)]
        return pltpu.make_async_remote_copy(
            src_ref=piece, dst_ref=piece, send_sem=pair_send.at[side, q],
            recv_sem=pair_recv.at[row], device_id=(base + q,), device_id_type=MESH)

    pair_other = pltpu.make_async_remote_copy(
        src_ref=pair.at[other // group], dst_ref=weights.at[me, :, pl.ds(wide, 128)], send_sem=pair_send.at[2, 0],
        recv_sem=pair_recv.at[me], device_id=(other,), device_id_type=MESH)
    greet_all(me, 2 * group)

    UP, DOWN, G_LAST, G_SIB, G_FIRST = range(5)

    def g_move(h, o, kind, target):
        piece = wo.at[2 * o + core, h]
        return pltpu.make_async_remote_copy(
            src_ref=piece, dst_ref=piece, send_sem=g_send.at[kind, h, o],
            recv_sem=g_recv.at[1 if kind == G_SIB else 0, h, o], device_id=(target,), device_id_type=MESH)

    def g_arrived(h, o, sibling):
        piece = wo.at[2 * o + (1 - core if sibling else core), h]
        pltpu.make_async_remote_copy(
            src_ref=piece, dst_ref=piece, send_sem=g_send.at[G_SIB, h, o],
            recv_sem=g_recv.at[1 if sibling else 0, h, o], device_id=(place.sibling,), device_id_type=MESH).wait_recv()

    def g_column(h, o, level, act):
        @pl.when((level <= place.z) & (place.z < LEVELS - 1))
        def _():
            act(g_move(h, o, UP, me + 8))

        @pl.when((level >= place.z) & (place.z > 0))
        def _():
            act(g_move(h, o, DOWN, me - 8))

    def g_spread(h, o, level, act):
        g_column(h, o, level, act)
        act(g_move(h, o, G_LAST, place.last(h)))
        act(g_move(h, o, G_SIB, place.sibling))

    def g_level(t):
        level, h, k = place.level(1 + t // 4), t % 2, t // 2 % 2
        o = place.chip(h, k, level)
        g_arrived(h, o, False)
        g_spread(h, o, level, start)

    def g_cross(q):
        dx, dy = q % 2, q // 2 % 2
        o = place.chip_at(dx, dy, place.level(q // 4))
        for h, away in ((0, dx), (1, dy)):
            @pl.when(away == 1)
            def _():
                g_arrived(h, o, False)
                g_move(h, o, G_SIB, place.sibling).start()

    start = lambda copy: copy.start()
    done = lambda copy: copy.wait_send()
    own_chip = me // 2
    own_copies = [
        pltpu.make_async_copy(heads_w.at[p], weights.at[me, :, pl.ds(0, wide)], local_sem.at[0]),
        pltpu.make_async_copy(out_w.at[pl.ds(0, depth // 2)], wo.at[me, 0], local_sem.at[1]),
        pltpu.make_async_copy(out_w.at[pl.ds(depth // 2, depth // 2)], wo.at[me, 1], local_sem.at[2]),
    ]
    for q in range(group):
        for j, matrix in enumerate((query_w, key_w, value_w)):
            heads_w[q, :, j * 128 : (j + 1) * 128] = matrix[:, q * 128 : (q + 1) * 128]
    for copy in own_copies:
        copy.start()
    ours = tokens[...].astype(f32)
    low = (ours * lax.rsqrt(jnp.mean(ours * ours, axis=-1, keepdims=True) + epsilon) * gains[0:1]).astype(bf)
    held[p] = low
    normed[...] = low
    pl.semaphore_wait(pltpu.get_barrier_semaphore(), 2 * group - 1)
    for h in range(2):
        move(h, chip, ALONG, across_z).start()
        move(h, chip, FIRST, place.first(h)).start()
    for h in range(2):
        move(h, chip, LAST, place.last(h)).start()
        move(h, chip, SIB, place.sibling).start()

    for s in range(2):
        down, up = downs[picked[s]].astype(f32), ups[picked[s]].astype(f32)
        both = [jnp.concatenate([side[j] for j in range(4)], axis=0).T for side in (down, up)]
        pair[s] = jnp.concatenate(both, axis=1).astype(bf)
    weights[me, :, wide:] = pair[me // group]
    pair_other.start()

    @pl.loop(0, group)
    def _(i):
        to_heads(other_base + (p + i) % group).start()

    lane = lax.broadcasted_iota(jnp.int32, (rows, 128), 1)
    expert = lax.broadcasted_iota(jnp.int32, (coeff.shape[0], rows), 0)
    gate = jnp.zeros(expert.shape, f32)
    for k in range(routes.shape[0]):
        gate += jnp.where(expert == routes[k : k + 1], gates[k : k + 1], 0.0)
    for e in range(coeff.shape[0]):
        coeff[e] = gate[e : e + 1]
    coeff_out[me] = coeff[me // 2]

    @pl.loop(1, group)
    def _(i):
        pair_over((p + i) % group, 0).start()
        to_heads(base + (p + i) % group).start()

    @pl.loop(1, 2 * group)
    def _(i):
        to_expert((me + i) % (2 * group)).start()

    for copy in own_copies[1:]:
        copy.wait()
    for h in range(2):
        g_column(h, own_chip, place.z, start)
        g_move(h, own_chip, G_FIRST, place.first(h)).start()
    for h in range(2):
        g_move(h, own_chip, G_LAST, place.last(h)).start()
        g_move(h, own_chip, G_SIB, place.sibling).start()

    pltpu.make_async_remote_copy(
        src_ref=pair.at[0], dst_ref=weights.at[other, :, pl.ds(wide, 128)], send_sem=pair_send.at[2, 0],
        recv_sem=pair_recv.at[other], device_id=(other,), device_id_type=MESH).wait_recv()

    @pl.loop(1, group)
    def _(i):
        pair_over((p + i) % group, 1).start()

    for h in range(2):
        o = chip_at(h, 0, 1)
        arrived(h, o, False)
        move(h, o, FIRST, place.first(h)).start()
        move(h, o, LAST, place.last(h)).start()
        move(h, o, SIB, place.sibling).start()
    for far in range(2):
        for h in range(2):
            o = chip_at(h, 1, far)
            arrived(h, o, False)
            move(h, o, LAST, place.last(h)).start()
            move(h, o, SIB, place.sibling).start()
    for h in range(2):
        o = place.chip(h, 1, place.z)
        g_arrived(h, o, False)
        g_spread(h, o, place.z, start)

    @pl.loop(0, group)
    def _(i):
        at = pl.ds(pl.multiple_of(i * rows, rows), rows)
        c, s = far_turn[0, pl.ds(i, 1)], far_turn[1, pl.ds(i, 1)]
        cosine[at] = c * near[0] - s * near[1]
        turn = s * near[0] + c * near[1]
        sine[at] = jnp.where(lane < 64, -turn, turn)

    for far in range(2):
        for k in range(2):
            for h in range(2):
                dx, dy = (1, k) if h == 0 else (k, 1)
                o = (z + far * (1 - 2 * z)) * 4 + place.chip_at(dx, dy, 0)
                arrived(h, o, False)
                move(h, o, SIB, place.sibling).start()
    own_copies[0].wait()

    @pl.loop(0, 4)
    def _(t):
        g_level(t)


    @pl.loop(1, 2 * group)
    def _(i):
        q = (me + i) % (2 * group)
        pltpu.make_async_remote_copy(
            src_ref=heads_w.at[0], dst_ref=weights.at[q, :, pl.ds(0, wide)], send_sem=w_send.at[q],
            recv_sem=w_recv.at[q], device_id=(q,), device_id_type=MESH).wait_recv()
        pltpu.make_async_remote_copy(
            src_ref=coeff.at[0], dst_ref=coeff_out.at[q], send_sem=c_send.at[q],
            recv_sem=c_recv.at[q], device_id=(q,), device_id_type=MESH).wait_recv()

        @pl.when(q != other)
        def _():
            pltpu.make_async_remote_copy(
                src_ref=pair.at[0], dst_ref=weights.at[q, :, pl.ds(wide, 128)], send_sem=pair_send.at[2, 0],
                recv_sem=pair_recv.at[q], device_id=(other,), device_id_type=MESH).wait_recv()

    @pl.loop(0, group // 2)
    def _(o):
        for h in range(2):
            arrived(h, o, True)

    @pl.loop(4, 8)
    def _(t):
        g_level(t)

    span = 2 * rows
    seq = group * rows
    up_own = weights[pl.ds(2 * p, 2), :, pl.ds(wide, 128)].reshape(2 * depth, 128)
    up_own = pltpu.roll(up_own.astype(f32), 64, 1).astype(bf)
    flip = (((1,), (1,)), ((), ()))
    scale = 1.0 / math.sqrt(128)

    @pl.loop(0, group // 2)
    def _(b):
        at = pl.ds(pl.multiple_of(b * span, span), span)
        x = held[pl.ds(2 * b, 2)].reshape(span, -1)
        acc = jnp.dot(x, weights[...].reshape(2 * group * depth, wide + 128), preferred_element_type=f32)
        inner = acc[:, wide:].astype(bf)
        inner_out[at] = inner
        owner = lax.broadcasted_iota(jnp.int32, inner.shape, 1) // rank

        def projected(j):
            low = jnp.where(owner == j, inner.astype(f32), 0.0).astype(bf)
            return acc[:, j * 128 : (j + 1) * 128] + lax.dot_general(low, up_own, flip, preferred_element_type=f32)

        for j, (gain, raw, rot) in enumerate(((query_gain, query_proj, query_out), (key_gain, key_proj, key_out))):
            value = projected(j)
            raw[at] = value
            unit = value * lax.rsqrt(jnp.mean(value * value, axis=-1, keepdims=True) + epsilon) * gain[...]
            rot[at] = (unit * cosine[at] + pltpu.roll(unit, 64, 1) * sine[at]).astype(bf)
        value_out[at] = projected(2).astype(bf)

        @pl.when(b % 2 == 0)
        def _():
            g_level(8 + b // 2)

    def to_token(q):
        return pltpu.make_async_remote_copy(
            src_ref=mixed_buf.at[q], dst_ref=mixed.at[:, pl.ds(p * 128, 128)], send_sem=m_send.at[q],
            recv_sem=m_recv.at[p], device_id=(base + q,), device_id_type=MESH)

    keep = pltpu.make_async_copy(mixed_buf.at[p], mixed.at[:, pl.ds(p * 128, 128)], m_local)

    @pl.loop(0, group // 2)
    def _(b):
        at = pl.ds(pl.multiple_of(b * span, span), span)
        scores = lax.dot_general(query_out[at], key_out[...], flip, preferred_element_type=f32)
        own_seg = [
            jnp.broadcast_to(segments_at(segs, me // group, pl.ds(pl.multiple_of(b * span + i, 128), 128)), (128, 128)).T
            for i in range(0, span, 128)
        ]
        own_seg = jnp.concatenate(own_seg, axis=0)[:, 0:1]
        weight = jnp.where(own_seg == segments_at(segs, me // group, slice(None)), jnp.exp2(scores * (scale * math.log2(math.e))), 0.0)
        total = jnp.sum(weight, axis=-1, keepdims=True)
        value = jnp.dot(weight.astype(bf), value_out[...], preferred_element_type=f32) / total
        mixed_buf[pl.ds(2 * b, 2)] = value.astype(bf).reshape(2, rows, 128)
        for side in range(2):
            q = 2 * b + side

            @pl.when(q != p)
            def _():
                to_token(q).start()

            @pl.when(q == p)
            def _():
                keep.start()

        g_cross(2 * b)
        g_cross(2 * b + 1)

    keep.wait()

    @pl.loop(1, group)
    def _(i):
        q = (p + i) % group
        pltpu.make_async_remote_copy(
            src_ref=mixed_buf.at[q], dst_ref=mixed.at[:, pl.ds(q * 128, 128)], send_sem=m_send.at[q],
            recv_sem=m_recv.at[q], device_id=(base + q,), device_id_type=MESH).wait_recv()

    @pl.loop(0, CHIPS)
    def _(o):
        for h in range(2):
            g_arrived(h, o, True)

    keep_out = pltpu.make_async_copy(wo, out_all, keep_sem)
    keep_out.start()
    ours = mixed[...]
    matrix = weights[:, :, wide:].reshape(2 * group * depth, 128)
    lane = lax.broadcasted_iota(jnp.int32, (rows, 128), 1)
    inner = jnp.dot(ours, matrix, preferred_element_type=f32)
    inner = jnp.where(lane // rank == 3, inner, 0.0).astype(bf)
    out_inner[...] = inner
    shifted = pltpu.roll(inner.astype(f32), 64, 1).astype(bf)
    total = tokens[...].astype(f32) + jnp.dot(ours, wo[...].reshape(2 * group * depth, -1), preferred_element_type=f32)
    total = total + lax.dot_general(shifted, matrix, flip, preferred_element_type=f32)
    middle[...] = total
    unit = total * lax.rsqrt(jnp.mean(total * total, axis=-1, keepdims=True) + epsilon)
    normed_ffn[...] = (unit * gains[1:2]).astype(bf)

    keep_out.wait()
    for h in range(2):
        g_move(h, own_chip, G_FIRST, place.first(h)).wait_send()
        g_spread(h, own_chip, place.z, done)
        g_spread(h, place.chip(h, 1, place.z), place.z, done)

    @pl.loop(0, CHIPS)
    def _(t):
        @pl.when(t < CHIPS - 4)
        def _():
            level, h, k = place.level(1 + t // 4), t % 2, t // 2 % 2
            g_spread(h, place.chip(h, k, level), level, done)

        dx, dy = t % 2, t // 2 % 2
        o = place.chip_at(dx, dy, place.level(t // 4))
        for h, away in ((0, dx), (1, dy)):
            @pl.when(away == 1)
            def _():
                g_move(h, o, G_SIB, place.sibling).wait_send()

    pair_other.wait_send()
    for h in range(2):
        move(h, chip, ALONG, across_z).wait_send()
        for far in range(2):
            for k in range(2):
                o = chip_at(h, k, far)
                if k == 0:
                    move(h, o, FIRST, place.first(h)).wait_send()
                move(h, o, LAST, place.last(h)).wait_send()
                move(h, o, SIB, place.sibling).wait_send()
                dx, dy = (1, k) if h == 0 else (k, 1)
                o = (z + far * (1 - 2 * z)) * 4 + place.chip_at(dx, dy, 0)
                move(h, o, SIB, place.sibling).wait_send()

    @pl.loop(1, group)
    def _(i):
        q = (p + i) % group
        pair_over(q, 0).wait_send()
        pair_over(q, 1).wait_send()
        to_token(q).wait_send()

    @pl.loop(1, 2 * group)
    def _(i):
        q = (me + i) % (2 * group)
        to_heads(q).wait_send()
        to_expert(q).wait_send()


def turn_tables(rows, group):
    frequency = rope_base ** (-(np.arange(64, dtype=np.float32) * np.float32(2.0 / 128)))
    frequency = np.concatenate([frequency, frequency]).astype(np.float64)
    tables = []
    for positions in (np.arange(rows), np.arange(group) * rows):
        angle = positions[:, None] * frequency[None, :]
        tables.append(np.stack([np.cos(angle), np.sin(angle)]).astype(np.float32))
    return tables


def front(picked, tokens, gains, query_w, key_w, value_w, segs, downs, ups, routes, gates, out_w,
          query_gain, key_gain):
    rows, width = tokens.shape
    group, depth = SEQ_LEN // rows, out_w.shape[0]
    rank = downs.shape[2]
    devices, seq = 2 * group, rows * group
    bf, f32 = jnp.bfloat16, jnp.float32
    dma = pltpu.SemaphoreType.DMA
    vmem, anywhere = pl.BlockSpec(memory_space=pltpu.VMEM), pl.BlockSpec(memory_space=pl.ANY)
    head = jax.ShapeDtypeStruct((seq, 128), bf)
    raw = jax.ShapeDtypeStruct((seq, 128), f32)
    mine = jax.ShapeDtypeStruct((rows, width), bf)
    near, far_turn = turn_tables(rows, group)
    return pl.pallas_call(
        functools.partial(front_kernel, rows, rank),
        out_shape=(
            jax.ShapeDtypeStruct((rows, width), f32), mine, mine, mine,
            jax.ShapeDtypeStruct((rows, 128), bf),
            jax.ShapeDtypeStruct((devices, depth, 512), bf),
            head, head, head, raw, raw, head,
            jax.ShapeDtypeStruct((devices, 1, rows), f32),
            raw, raw,
            jax.ShapeDtypeStruct((devices, 2, depth // 2, width), bf),
        ),
        in_specs=[pl.BlockSpec(memory_space=pltpu.SMEM)] + [vmem] * 10 + [anywhere] + [vmem] * 4,
        out_specs=(vmem,) * 15 + (anywhere,),
        scratch_shapes=[
            pltpu.VMEM((group, rows, width), bf),
            pltpu.VMEM((group, rows, 128), bf),
            pltpu.VMEM((2, depth, 128), bf),
            pltpu.VMEM((group, 1, rows), f32),
            pltpu.VMEM((devices, 2, depth // 2, width), bf),
            pltpu.VMEM((group, depth, 384), bf),
            dma((3,)), dma((4, 2, group // 2)), dma((2, 2, group // 2)),
            dma((devices,)), dma((devices,)), dma((3, group)), dma((devices,)),
            dma((devices,)), dma((devices,)), dma((group,)), dma((group,)), dma,
            dma((5, 2, CHIPS)), dma((2, 2, CHIPS)), dma,
        ],
        compiler_params=pltpu.CompilerParams(collective_id=0, has_side_effects=True, vmem_limit_bytes=60 << 20),
        name="front",
    )(picked, tokens, gains, query_w, key_w, value_w, segs, downs, ups, routes, gates, out_w, jnp.asarray(near), jnp.asarray(far_turn),
      query_gain, key_gain)


OUTER_DONE = (0, 1, 2, 2, 3, 4, 4, 5, 5, 6, 7, 9, 9, 9, 9, 9, 9, 9, 9, 9, 9, 11, 11, 12, 13, 13, 14, 14, 16)
INNER_DONE = (0, 0, 0, 0, 0, 0, 0, 0, 0, 0, 0, 0, 0, 0, 0, 0, 0, 0, 6, 6, 6, 11, 11, 13, 13, 14, 14, 14, 16)


def back_kernel(rows, rank, grad_mixed, part, weights, query, key, value, query_proj, key_proj, inner, cosine, sine,
                query_gain, key_gain, segs, rows_in, normed, gains, grad_middle, middle, early,
                grad_rows, output, factors, out, up_terms, part_sum, late, early_in, late_in, owned,
                e_send, e_recv, l_send, l_recv, f_send, f_recv, t_local,
                grads, key_seg, key_t, grad_key, grad_value, heads, result, sib, cross_out, cross_in, z_out, z_in, first_out, first_in,
                held, part_in, part_z, part_total, part_first_out, part_first_in,
                held_sem, pc_send, pc_recv, pz_send, pz_recv, pf_send, pf_recv,
                a_send, a_recv, a_local, sib_send, sib_recv, cross_send, cross_recv, z_send, z_recv, first_send, first_recv):
    place = Place()
    f32, bf = jnp.float32, jnp.bfloat16
    me, core = place.me, place.core
    group = grads.shape[0]
    depth = weights.shape[1]
    base, p = me // group * group, me % group
    half, span, seq = rows // 2, 2 * rows, rows * group
    width = out.shape[1] - 128
    z = place.z % 2
    across_z = me + 8 - 16 * z
    flip = (((1,), (1,)), ((), ()))
    tall = (((0,), (0,)), ((), ()))
    scale = 1.0 / math.sqrt(128)

    def keep_piece(h, k, level):
        return pltpu.make_async_copy(part.at[place.chip(h, k, level), h], held.at[h, k, level], held_sem.at[h, k, level])

    def part_across(h, k, level):
        dx, dy = (1, k) if h == 0 else (k, 1)
        return pltpu.make_async_remote_copy(
            src_ref=part.at[place.chip_at(dx, dy, level), h], dst_ref=part_in.at[h, k, level],
            send_sem=pc_send.at[h, k, level], recv_sem=pc_recv.at[h, k, level],
            device_id=(place.last(h),), device_id_type=MESH)

    def crossed(h, k, level):
        return pltpu.make_async_remote_copy(
            src_ref=held.at[h, k, level], dst_ref=part_in.at[h, k, level], send_sem=pc_send.at[h, k, level],
            recv_sem=pc_recv.at[h, k, level], device_id=(place.last(h),), device_id_type=MESH)

    def part_along(h, k, level, up, slot):
        return pltpu.make_async_remote_copy(
            src_ref=held.at[h, k, level], dst_ref=part_z.at[h, k, slot], send_sem=pz_send.at[h, k, level],
            recv_sem=pz_recv.at[h, k, slot], device_id=(me - 8 + 16 * up,), device_id_type=MESH)

    def part_first(h):
        return pltpu.make_async_remote_copy(
            src_ref=part_first_out.at[h], dst_ref=part_first_in.at[h], send_sem=pf_send.at[h],
            recv_sem=pf_recv.at[h], device_id=(place.first(h),), device_id_type=MESH)

    def down_slot(level):
        ends = 1 - jnp.minimum(jnp.abs(level - (place.z - 1)), 1)
        return level + ends * (LEVELS - level)

    def part_event(e):
        h, k, level = e % 2, e // 2 % 2, place.level(3 - e // 4)
        keep_piece(h, k, level).wait()
        crossed(h, k, level).wait_recv()
        total = held[h, k, level].astype(f32) + part_in[h, k, level].astype(f32)
        part_total[...] = total

        @pl.when((level >= place.z) & (place.z > 0))
        def _():
            part_along(h, k, level, 1, level).wait_recv()
            part_total[...] += part_z[h, k, level].astype(f32)

        @pl.when((level < place.z) & (place.z < LEVELS - 1))
        def _():
            part_along(h, k, level, 0, level).wait_recv()
            part_total[...] += part_z[h, k, level].astype(f32)

        @pl.when((level == place.z) & (place.z < LEVELS - 1))
        def _():
            part_along(h, k, level, 0, LEVELS).wait_recv()
            part_total[...] += part_z[h, k, LEVELS].astype(f32)

        @pl.when(level > place.z)
        def _():
            held[h, k, level] = part_total[...].astype(bf)
            part_along(h, k, level, 1, level).start()

        @pl.when(level < place.z)
        def _():
            held[h, k, level] = part_total[...].astype(bf)
            part_along(h, k, level, 0, down_slot(level)).start()

        @pl.when((level == place.z) & (k == 1))
        def _():
            part_first_out[h] = part_total[...].astype(bf)
            part_first(h).start()

        @pl.when((level == place.z) & (k == 0))
        def _():
            part_sum[h] = part_total[...]

    upper = place.z // 2
    inner_level = place.z * (1 - upper) + (3 - place.z) * upper

    def part_steps(slot):
        def bound(at):
            if isinstance(at, int):
                return OUTER_DONE[at] + inner_level * (INNER_DONE[at] - OUTER_DONE[at])
            count = 0
            for i, (outer, inside) in enumerate(zip(OUTER_DONE, INNER_DONE)):
                count = jnp.where(at == i, jnp.where(inner_level == 0, outer, inside), count)
            return count

        def one(e, none):
            part_event(e)
            return none

        lax.fori_loop(bound(slot), bound(slot + 1), one, 0)

    def to_head(q):
        return pltpu.make_async_remote_copy(
            src_ref=grad_mixed.at[:, pl.ds(q * 128, 128)], dst_ref=grads.at[p], send_sem=a_send.at[q],
            recv_sem=a_recv.at[p], device_id=(base + q,), device_id_type=MESH)

    def from_token(q):
        return pltpu.make_async_remote_copy(
            src_ref=grad_mixed.at[:, pl.ds(q * 128, 128)], dst_ref=grads.at[q], send_sem=a_send.at[q],
            recv_sem=a_recv.at[q], device_id=(base + q,), device_id_type=MESH)

    keep = pltpu.make_async_copy(grad_mixed.at[:, pl.ds(p * 128, 128)], grads.at[p], a_local)
    keep.start()
    greet_all(me, 2 * group)
    @pl.loop(0, group)
    def _(i):
        at = pl.ds(pl.multiple_of(i * 128, 128), 128)
        key_seg[at] = jnp.broadcast_to(segments_at(segs, me // group, at), (128, 128)).T

    key_t[...] = key[...].astype(f32).T.astype(bf)
    pl.semaphore_wait(pltpu.get_barrier_semaphore(), 2 * group - 1)

    def early_to(q, frm):
        return pltpu.make_async_remote_copy(
            src_ref=early.at[:, pl.ds(q * 128, 128)], dst_ref=early_in.at[frm], send_sem=e_send.at[q],
            recv_sem=e_recv.at[frm], device_id=(base + q,), device_id_type=MESH)

    def late_to(q, frm):
        return pltpu.make_async_remote_copy(
            src_ref=late.at[:, pl.ds(q * 128, 128)], dst_ref=late_in.at[frm], send_sem=l_send.at[q],
            recv_sem=l_recv.at[frm], device_id=(base + q,), device_id_type=MESH)

    def to_owner(side, q, frm):
        return pltpu.make_async_remote_copy(
            src_ref=owned, dst_ref=factors.at[frm], send_sem=f_send.at[side],
            recv_sem=f_recv.at[frm], device_id=(q,), device_id_type=MESH)

    early_keep = pltpu.make_async_copy(early.at[:, pl.ds(p * 128, 128)], early_in.at[p], t_local.at[0])
    late_keep = pltpu.make_async_copy(late.at[:, pl.ds(p * 128, 128)], late_in.at[p], t_local.at[1])
    owned_keep = pltpu.make_async_copy(owned, factors.at[me // group], t_local.at[2])
    early_keep.start()

    @pl.loop(1, group)
    def _(i):
        to_head((p + i) % group).start()

    @pl.loop(1, group)
    def _(i):
        early_to((p + i) % group, p).start()

    @pl.loop(0, 4)
    def _(i):
        level = place.level(3 - i)
        for k in range(2):
            for h in range(2):
                part_across(h, k, level).start()
                keep_piece(h, k, level).start()

    grad_key[...] = jnp.zeros_like(grad_key)
    grad_value[...] = jnp.zeros_like(grad_value)
    keep.wait()

    def raw_grad(raw, gain, turned, at):
        back = turned * cosine[at] - pltpu.roll(turned, 64, 1) * sine[at]
        rows_ = raw[at]
        inverse = lax.rsqrt(jnp.mean(rows_ * rows_, axis=-1, keepdims=True) + epsilon)
        unit = rows_ * inverse
        scaled = back * gain[...]
        return (inverse * (scaled - unit * jnp.mean(scaled * unit, axis=-1, keepdims=True))).astype(bf)

    @pl.loop(0, group // 2)
    def _(b):
        at = pl.ds(pl.multiple_of(b * span, span), span)
        for side in range(2):
            q = 2 * b + side

            @pl.when(q != p)
            def _():
                from_token(q).wait_recv()

        ours = query[at]
        grad = grads[pl.ds(2 * b, 2)].reshape(span, 128)
        scores = lax.dot_general(key[...], ours, flip, preferred_element_type=f32)
        own_seg = segments_at(segs, me // group, at)
        weight = jnp.where(key_seg[:, 0:1] == own_seg, jnp.exp2(scores * (scale * math.log2(math.e))), 0.0)
        probs = weight * (1.0 / jnp.sum(weight, axis=0, keepdims=True))
        grad_probs = lax.dot_general(value[...], grad, flip, preferred_element_type=f32)
        mean = jnp.sum(probs * grad_probs, axis=0, keepdims=True)
        grad_scores = (probs * (grad_probs - mean)).astype(bf)
        grad_key[...] += jnp.dot(grad_scores, ours, preferred_element_type=f32)
        grad_value[...] += jnp.dot(probs.astype(bf), grad, preferred_element_type=f32)
        grad_query = jnp.dot(key_t[...], grad_scores, preferred_element_type=f32).T * scale
        heads[at, 0:128] = raw_grad(query_proj, query_gain, grad_query, at)
        part_steps(b)

    up_own = weights[pl.ds(2 * p, 2), :, 384:512].reshape(2 * depth, 128)
    up_own = pltpu.roll(up_own.astype(f32), 64, 1).astype(bf)

    @pl.loop(0, group // 2)
    def _(b):
        at = pl.ds(pl.multiple_of(b * span, span), span)
        heads[at, 128:256] = raw_grad(key_proj, key_gain, grad_key[at] * scale, at)
        heads[at, 256:384] = grad_value[at].astype(bf)

    def to_sibling(c):
        return pltpu.make_async_remote_copy(
            src_ref=result.at[c, 1 - core], dst_ref=sib.at[c], send_sem=sib_send.at[c],
            recv_sem=sib_recv.at[c], device_id=(place.sibling,), device_id_type=MESH)

    def across(h, k, far):
        return pltpu.make_async_remote_copy(
            src_ref=cross_out.at[h, k, far], dst_ref=cross_in.at[h, k, far], send_sem=cross_send.at[h, k, far],
            recv_sem=cross_recv.at[h, k, far], device_id=(place.last(h),), device_id_type=MESH)

    def along(h, k):
        return pltpu.make_async_remote_copy(
            src_ref=z_out.at[h, k], dst_ref=z_in.at[h, k], send_sem=z_send.at[h, k],
            recv_sem=z_recv.at[h, k], device_id=(across_z,), device_id_type=MESH)

    def first(h):
        return pltpu.make_async_remote_copy(
            src_ref=first_out.at[h], dst_ref=first_in.at[h], send_sem=first_send.at[h],
            recv_sem=first_recv.at[h], device_id=(place.first(h),), device_id_type=MESH)

    def both(c, h):
        part = pl.ds(h * half, half)
        return result[c, core, part].astype(f32) + sib[c, part].astype(f32)

    def pair_sum(c):
        far, dx, dy = 1 - c // 4, c % 2, c // 2 % 2
        to_sibling(c).wait_recv()
        for h, away, k in ((0, dx, dy), (1, dy, dx)):
            @pl.when(away == 1)
            def _():
                cross_out[h, k, far] = both(c, h).astype(bf)
                across(h, k, far).start()

    @pl.loop(0, group // 2 + 1)
    def _(c):
        @pl.when(c < group // 2)
        def _():
            far, dx, dy = 1 - c // 4, c % 2, c // 2 % 2
            o = (z + far * (1 - 2 * z)) * 4 + place.chip_at(dx, dy, 0)
            mine = heads[pl.ds(pl.multiple_of(o * span, span), span), :]
            matrix = weights[...].reshape(2 * group * depth, 512)[:, 0:384]
            part = lax.dot_general(mine, matrix, flip, preferred_element_type=f32)
            result[c, :, :, 0:width] = part.astype(bf).reshape(2, rows, width)
            low = jnp.zeros((span, 128), f32)
            owner = lax.broadcasted_iota(jnp.int32, low.shape, 1) // rank
            for j in range(3):
                term = jnp.dot(mine[:, j * 128 : (j + 1) * 128], up_own, preferred_element_type=f32)
                low = jnp.where(owner == j, term, low)
            result[c, :, :, width:] = low.astype(bf).reshape(2, rows, 128)
            to_sibling(c).start()

        @pl.when(c >= 1)
        def _():
            pair_sum(c - 1)

        part_steps(group // 2 + c)

    @pl.loop(0, group // 2)
    def _(e):
        far, k, h = 1 - e // 4, e // 2 % 2, e % 2
        c = (1 - far) * 4 + k * (2 - h)
        across(h, k, far).wait_recv()
        total = both(c, h) + cross_in[h, k, far].astype(f32)

        @pl.when(far == 1)
        def _():
            z_out[h, k] = total.astype(bf)
            along(h, k).start()

        @pl.when(far == 0)
        def _():
            along(h, k).wait_recv()
            whole = total + z_in[h, k].astype(f32)

            @pl.when(k == 1)
            def _():
                first_out[h] = whole.astype(bf)
                first(h).start()

            @pl.when(k == 0)
            def _():
                out[pl.ds(h * half, half)] = whole

        part_steps(group + 1 + e)

    part_steps(25)

    owner = lax.broadcasted_iota(jnp.int32, (128, 128), 0) // rank
    up = jnp.zeros((128, 128), f32)
    for j in range(3):
        term = lax.dot_general(inner[...], heads[:, j * 128 : (j + 1) * 128], tall, preferred_element_type=f32)
        up = jnp.where(owner == j, term, up)
    up_terms[...] = up
    for h in range(2):
        first(h).wait_recv()
        out[pl.ds(h * half, half)] += first_in[h].astype(f32)
    part_steps(26)
    lane = lax.broadcasted_iota(jnp.int32, (rows, 128), 1)
    grad_inner = jnp.where(lane < 3 * rank, out[:, width:], 0.0).astype(bf)
    late[...] = lax.dot_general(grad_inner, normed[...], tall, preferred_element_type=f32)[: 3 * rank]
    late_keep.start()

    @pl.loop(1, group)
    def _(i):
        late_to((p + i) % group, p).start()

    downs = weights[:, :, 384:512].reshape(2 * group * depth, 128)
    grad_normed = out[:, 0:width] + lax.dot_general(grad_inner, downs, flip, preferred_element_type=f32)
    ours = rows_in[...].astype(f32)
    inverse = lax.rsqrt(jnp.mean(ours * ours, axis=-1, keepdims=True) + epsilon)
    unit = ours * inverse
    scaled = grad_normed * gains[0:1]
    grad = inverse * (scaled - unit * jnp.mean(scaled * unit, axis=-1, keepdims=True))
    grad_rows[...] = (grad_middle[...] + grad).astype(bf)
    part_steps(27)
    early_keep.wait()
    late_keep.wait()

    @pl.loop(1, group)
    def _(i):
        q = (p + i) % group
        early_to(q, q).wait_recv()
        late_to(q, q).wait_recv()

    sums = jnp.sum(early_in[...], axis=0)
    owned[0 : 3 * rank] = jnp.sum(late_in[...], axis=0)
    owned[3 * rank : 4 * rank] = sums[:rank]
    owned[4 * rank : 7 * rank] = up_terms[0 : 3 * rank]
    owned[7 * rank : 8 * rank] = sums[rank:]
    for side in range(2):
        q = 2 * p + side

        @pl.when(q != me)
        def _():
            to_owner(side, q, me // group).start()

        @pl.when(q == me)
        def _():
            owned_keep.start()

    for h in range(2):
        part_first(h).wait_recv()
        side = pl.ds(h * half, half)
        output[side] = (middle[side] + part_sum[h] + part_first_in[h].astype(f32)).astype(bf)
    for s in range(2):
        source = s * group + me // 2

        @pl.when(source != me)
        def _():
            to_owner(0, source, s).wait_recv()

        @pl.when(source == me)
        def _():
            owned_keep.wait()

    @pl.loop(1, group)
    def _(i):
        to_head((p + i) % group).wait_send()
        early_to((p + i) % group, p).wait_send()
        late_to((p + i) % group, p).wait_send()

    for side in range(2):
        @pl.when(2 * p + side != me)
        def _():
            to_owner(side, 2 * p + side, me // group).wait_send()

    for h in range(2):
        part_first(h).wait_send()

    @pl.loop(0, 4)
    def _(level):
        for k in range(2):
            for h in range(2):
                part_across(h, k, level).wait_send()

                @pl.when(level > place.z)
                def _():
                    part_along(h, k, level, 1, level).wait_send()

                @pl.when(level < place.z)
                def _():
                    part_along(h, k, level, 0, down_slot(level)).wait_send()

    @pl.loop(0, group // 2)
    def _(c):
        to_sibling(c).wait_send()
        across(c % 2, c // 2 % 2, c // 4).wait_send()

        @pl.when(c < 4)
        def _():
            along(c % 2, c // 2).wait_send()

        @pl.when(c < 2)
        def _():
            first(c).wait_send()


def back(grad_mixed, part, weights, query, key, value, query_proj, key_proj, inner, cosine, sine,
         query_gain, key_gain, segs, rows_in, normed, gains, grad_middle, middle, early, rank):
    rows, width = grad_mixed.shape
    seq = query.shape[0]
    group = seq // rows
    bf, f32 = jnp.bfloat16, jnp.float32
    dma = pltpu.SemaphoreType.DMA
    vmem = pl.BlockSpec(memory_space=pltpu.VMEM)
    wide = width + 128
    piece = (rows // 2, wide)
    own = part.shape[2:]
    return pl.pallas_call(
        functools.partial(back_kernel, rows, rank),
        out_shape=(
            jax.ShapeDtypeStruct((rows, width), bf),
            jax.ShapeDtypeStruct((rows, width), bf),
            jax.ShapeDtypeStruct((2, 8 * rank, 128), f32),
        ),
        in_specs=[vmem, pl.BlockSpec(memory_space=pl.ANY)] + [vmem] * 18,
        out_specs=(vmem, vmem, vmem),
        scratch_shapes=[
            pltpu.VMEM((rows, wide), f32),
            pltpu.VMEM((128, 128), f32),
            pltpu.VMEM((2,) + own, f32),
            pltpu.VMEM((3 * rank, width), f32),
            pltpu.VMEM((group, 2 * rank, 128), f32),
            pltpu.VMEM((group, 3 * rank, 128), f32),
            pltpu.VMEM((8 * rank, 128), f32),
            dma((group,)), dma((group,)), dma((group,)), dma((group,)), dma((2,)), dma((2,)), dma((3,)),
            pltpu.VMEM((group, rows, 128), bf),
            pltpu.VMEM((seq, 128), f32),
            pltpu.VMEM((128, seq), bf),
            pltpu.VMEM((seq, 128), f32),
            pltpu.VMEM((seq, 128), f32),
            pltpu.VMEM((seq, 384), bf),
            pltpu.VMEM((group // 2, 2, rows, wide), bf),
            pltpu.VMEM((group // 2, rows, wide), bf),
            pltpu.VMEM((2, 2, 2) + piece, bf),
            pltpu.VMEM((2, 2, 2) + piece, bf),
            pltpu.VMEM((2, 2) + piece, bf),
            pltpu.VMEM((2, 2) + piece, bf),
            pltpu.VMEM((2,) + piece, bf),
            pltpu.VMEM((2,) + piece, bf),
            pltpu.VMEM((2, 2, LEVELS) + own, bf),
            pltpu.VMEM((2, 2, LEVELS) + own, bf),
            pltpu.VMEM((2, 2, LEVELS + 1) + own, bf),
            pltpu.VMEM(own, f32),
            pltpu.VMEM((2,) + own, bf),
            pltpu.VMEM((2,) + own, bf),
            dma((2, 2, LEVELS)), dma((2, 2, LEVELS)), dma((2, 2, LEVELS)), dma((2, 2, LEVELS)), dma((2, 2, LEVELS + 1)),
            dma((2,)), dma((2,)),
            dma((group,)), dma((group,)), dma, dma((group // 2,)), dma((group // 2,)),
            dma((2, 2, 2)), dma((2, 2, 2)), dma((2, 2)), dma((2, 2)), dma((2,)), dma((2,)),
        ],
        compiler_params=pltpu.CompilerParams(collective_id=2, has_side_effects=True, vmem_limit_bytes=63 << 20),
        name="back",
    )(grad_mixed, part, weights, query, key, value, query_proj, key_proj, inner, cosine, sine,
      query_gain, key_gain, segs, rows_in, normed, gains, grad_middle, middle, early)


def heads_plan(
    tokens,
    segments,
    routes,
    gates,
    sequence_adapter_index,
    attention_norm_gain,
    query_norm_gain,
    key_norm_gain,
    query_weight,
    key_weight,
    value_weight,
    output_weight,
    adapter_down_factors,
    adapter_up_factors,
    expert_norm_gain,
    expert_gate_weight,
    expert_up_weight,
    expert_down_weight,
    output_gradient,
):
    bf, f32 = jnp.bfloat16, jnp.float32
    devices = lax.axis_size("fsdp")
    rows_dev, width = tokens.shape
    seqs = segments.shape[0]
    rank = adapter_down_factors.shape[3]
    slots = 4 * rank
    own_rows = query_weight.shape[0]
    device = lax.axis_index("fsdp")
    gains = jnp.stack([attention_norm_gain, expert_norm_gain]).astype(f32)
    query_scale = query_norm_gain.astype(f32)
    key_scale = key_norm_gain.astype(f32)

    head_gains = (query_scale.reshape(1, HEAD_DIM), key_scale.reshape(1, HEAD_DIM))
    (middle, normed_ffn, normed, mixed, out_inner, head_weights, query, key, value, query_proj, key_proj, inner_all,
     coeff_own, *turns, output_matrix) = front(
        sequence_adapter_index, tokens, gains, query_weight, key_weight, value_weight,
        segments, adapter_down_factors.swapaxes(2, 3),
        adapter_up_factors, routes.T, gates.T, output_weight, *head_gains,
    )
    slab_gate = expert_gate_weight[0]
    slab_up = expert_up_weight[0]
    slab_down = expert_down_weight[0]
    grad_middle, grad_mixed, early, part, _ = experts_pass(
        normed_ffn, output_gradient, slab_gate, slab_up, slab_down, coeff_own, middle, gains,
        output_matrix.reshape(width, width), head_weights, out_inner, mixed, rank,
    )

    grad_tokens, output, terms = back(
        grad_mixed, part, head_weights, query, key, value, query_proj, key_proj, inner_all,
        *turns, *head_gains, segments,
        tokens, normed, gains, grad_middle, middle,
        early, rank,
    )
    terms = lax.dynamic_slice_in_dim(terms, device % 2 * own_rows, own_rows, 2)
    selected = (
        jnp.arange(ADAPTER_COUNT, dtype=jnp.int32)[:, None] == sequence_adapter_index[None, :]
    ).astype(f32)
    spread = jnp.sum(selected[:, :, None, None] * terms[None], axis=1)
    spread = spread.reshape(ADAPTER_COUNT, 2, 4, rank, own_rows)
    grad_down = spread[:, 0].transpose(0, 1, 3, 2)
    grad_up = spread[:, 1]
    return (output, grad_tokens, grad_down, grad_up)


def solution(mesh):
    plan = heads_plan if mesh.shape["fsdp"] == LEVELS * 8 else shards
    in_specs = (
        P("fsdp", None),
        P(),
        P("fsdp", None),
        P("fsdp", None),
        P(),
        P(),
        P(),
        P(),
        P("fsdp", None),
        P("fsdp", None),
        P("fsdp", None),
        P("fsdp", None),
        P(None, None, "fsdp", None),
        P(None, None, None, "fsdp"),
        P(),
        P("fsdp", None, None),
        P("fsdp", None, None),
        P("fsdp", None, None),
        P("fsdp", None),
    )
    out_specs = (
        P("fsdp", None),
        P("fsdp", None),
        P(None, None, "fsdp", None),
        P(None, None, None, "fsdp"),
    )
    return jax.shard_map(plan, mesh=mesh, in_specs=in_specs, out_specs=out_specs, check_vma=False)
```

```python
import functools
import math

import jax
import jax.numpy as jnp
import numpy as np
from jax import lax
from jax.experimental import pallas as pl
from jax.experimental.pallas import tpu as pltpu
from jax.sharding import PartitionSpec as P

HEAD_DIM = 128
TOPK = 8
ADAPTER_COUNT = 8
SEQ_LEN = 2048


epsilon = 1e-06
rope_base = 50000.0


def from_partner(value, axis, distance):
    mask = 2**distance
    pairs = [(source, source ^ mask) for source in range(lax.axis_size(axis))]
    return lax.ppermute(value, axis, pairs)


def matmul(left, right):
    return jnp.dot(left, right, preferred_element_type=jnp.float32)


def rms_scale(rows, gain):
    return rows * lax.rsqrt(jnp.mean(rows * rows, axis=-1, keepdims=True) + epsilon) * gain


def rms_back(rows, gain, upstream):
    inverse = lax.rsqrt(jnp.mean(rows * rows, axis=-1, keepdims=True) + epsilon)
    unit = rows * inverse
    scaled = upstream * gain
    return inverse * (scaled - unit * jnp.mean(scaled * unit, axis=-1, keepdims=True))


def rope_tables(positions):
    half = HEAD_DIM // 2
    frequency = rope_base ** (-(jnp.arange(half, dtype=jnp.float32) * 2.0 / HEAD_DIM))
    angle = positions[:, None] * frequency[None, :]
    return (jnp.cos(angle)[:, None, :], jnp.sin(angle)[:, None, :])


def rotate(rows, cosine, sine):
    half = rows.shape[-1] // 2
    first = rows[..., :half]
    second = rows[..., half:]
    return jnp.concatenate(
        [first * cosine - second * sine, second * cosine + first * sine], axis=-1
    )


def rotate_back(upstream, cosine, sine):
    half = upstream.shape[-1] // 2
    first = upstream[..., :half]
    second = upstream[..., half:]
    return jnp.concatenate(
        [first * cosine + second * sine, second * cosine - first * sine], axis=-1
    )


def pick(table, index):
    return lax.dynamic_index_in_dim(table, index, 0, keepdims=False)


def shards(
    tokens,
    segments,
    routes,
    gates,
    sequence_adapter_index,
    attention_norm_gain,
    query_norm_gain,
    key_norm_gain,
    query_weight,
    key_weight,
    value_weight,
    output_weight,
    adapter_down_factors,
    adapter_up_factors,
    expert_norm_gain,
    expert_gate_weight,
    expert_up_weight,
    expert_down_weight,
    output_gradient,
):
    rows_dev = tokens.shape[0]
    width = tokens.shape[1]
    heads = width // HEAD_DIM
    group = SEQ_LEN // rows_dev
    level_list = group.bit_length() - 1
    device = lax.axis_index("fsdp")
    place = device % group
    sequence = device // group
    segment_row = pick(segments, sequence)
    own_segment = lax.dynamic_slice_in_dim(segment_row, place * rows_dev, rows_dev)
    adapter = pick(sequence_adapter_index, sequence)
    scale = 1.0 / math.sqrt(HEAD_DIM)
    cosine, sine = rope_tables(
        (place * rows_dev + jnp.arange(rows_dev, dtype=jnp.int32)).astype(jnp.float32)
    )
    attn_scale = attention_norm_gain.astype(jnp.float32)
    query_scale = query_norm_gain.astype(jnp.float32)
    key_scale = key_norm_gain.astype(jnp.float32)
    ffn_scale = expert_norm_gain.astype(jnp.float32)
    gathered = (
        lax.all_gather(query_weight, "fsdp", axis=0, tiled=True),
        lax.all_gather(key_weight, "fsdp", axis=0, tiled=True),
        lax.all_gather(value_weight, "fsdp", axis=0, tiled=True),
        lax.all_gather(output_weight, "fsdp", axis=0, tiled=True),
        lax.all_gather(adapter_down_factors, "fsdp", axis=2, tiled=True),
        lax.all_gather(adapter_up_factors, "fsdp", axis=3, tiled=True),
    )
    matrices = gathered[:4]
    down_own = pick(gathered[4], adapter)
    up_own = pick(gathered[5], adapter)

    def project(inputs, index):
        inner = matmul(inputs, down_own[index]).astype(jnp.bfloat16)
        return (matmul(inputs, matrices[index]) + matmul(inner, up_own[index]), inner)

    rows = tokens.astype(jnp.float32)
    normed = rms_scale(rows, attn_scale).astype(jnp.bfloat16)
    query_proj, query_inner = project(normed, 0)
    key_proj, key_inner = project(normed, 1)
    value_proj, value_inner = project(normed, 2)
    query_heads = query_proj.reshape(rows_dev, heads, HEAD_DIM)
    key_heads = key_proj.reshape(rows_dev, heads, HEAD_DIM)
    query_rot = rotate(rms_scale(query_heads, query_scale), cosine, sine).astype(jnp.bfloat16)
    key_rot = (
        rotate(rms_scale(key_heads, key_scale), cosine, sine)
        .astype(jnp.bfloat16)
        .reshape(rows_dev, width)
    )
    value_low = value_proj.astype(jnp.bfloat16)
    held_keys = key_rot
    held_values = value_low
    for level in range(level_list):
        other_keys, other_values = from_partner((held_keys, held_values), "fsdp", level)
        upper_bit = place // (1 << level) % 2 == 1
        held_keys = jnp.where(
            upper_bit,
            jnp.concatenate([other_keys, held_keys], axis=0),
            jnp.concatenate([held_keys, other_keys], axis=0),
        )
        held_values = jnp.where(
            upper_bit,
            jnp.concatenate([other_values, held_values], axis=0),
            jnp.concatenate([held_values, other_values], axis=0),
        )
    keys_all = held_keys.reshape(SEQ_LEN, heads, HEAD_DIM)
    values_all = held_values.reshape(SEQ_LEN, heads, HEAD_DIM)
    allowed = (own_segment[:, None] == segment_row[None, :])[None]

    def masked_scores():
        raw = (
            jnp.einsum("thd,shd->hts", query_rot, keys_all, preferred_element_type=jnp.float32)
            * scale
        )
        return jnp.where(allowed, raw, -1e30)

    scores = masked_scores()
    maximum = jnp.max(scores, axis=-1, keepdims=True)
    weights = jnp.exp(scores - maximum)
    total = jnp.sum(weights, axis=-1, keepdims=True)
    probs = weights / total
    log_total = maximum + jnp.log(total)
    mixed = jnp.einsum(
        "hts,shd->thd", probs.astype(jnp.bfloat16), values_all, preferred_element_type=jnp.float32
    )
    mixed = mixed.astype(jnp.bfloat16).reshape(rows_dev, width)
    attn_proj, out_inner = project(mixed, 3)
    middle = rows + attn_proj
    normed_ffn = rms_scale(middle, ffn_scale).astype(jnp.bfloat16)
    experts = lax.axis_size("fsdp") // 2
    capacity = 2 * rows_dev * TOPK // experts
    flat_routes = routes.reshape(-1)
    onehot = (flat_routes[:, None] == jnp.arange(experts, dtype=jnp.int32)[None, :]).astype(
        jnp.int32
    )
    slot = jnp.sum(jnp.cumsum(onehot, axis=0) * onehot, axis=1) - 1
    target = flat_routes * capacity + slot

    def spread(entries):
        buffer = jnp.zeros((experts * capacity, width), jnp.bfloat16).at[target].set(entries)
        buffer = buffer.reshape(experts, 1, capacity, width)
        return jnp.broadcast_to(buffer, (experts, 2, capacity, width)).reshape(
            2 * experts, capacity, width
        )

    def collect(returned):
        halves = returned.reshape(experts, 2, capacity, width).astype(jnp.float32)
        summed = (halves[:, 0] + halves[:, 1]).reshape(experts * capacity, width)
        return summed[target].reshape(rows_dev, TOPK, width)

    slab_gate = expert_gate_weight[0]
    slab_up = expert_up_weight[0]
    slab_down = expert_down_weight[0]
    dispatched = lax.all_to_all(
        spread(jnp.repeat(normed_ffn, TOPK, axis=0)),
        "fsdp",
        split_axis=0,
        concat_axis=0,
        tiled=True,
    )
    gate_part = jnp.einsum("scd,dh->sch", dispatched, slab_gate, preferred_element_type=jnp.float32)
    up_part = jnp.einsum("scd,dh->sch", dispatched, slab_up, preferred_element_type=jnp.float32)
    hidden = (jax.nn.silu(gate_part) * up_part).astype(jnp.bfloat16)
    produced = jnp.einsum(
        "sch,hd->scd", hidden, slab_down, preferred_element_type=jnp.float32
    ).astype(jnp.bfloat16)
    returned = lax.all_to_all(produced, "fsdp", split_axis=0, concat_axis=0, tiled=True)
    moe = jnp.sum(gates[:, :, None] * collect(returned), axis=1)
    output = (middle + moe).astype(jnp.bfloat16)
    upstream = output_gradient.astype(jnp.float32)
    grad_parts = (
        (gates[:, :, None] * upstream[:, None, :])
        .astype(jnp.bfloat16)
        .reshape(rows_dev * TOPK, width)
    )
    grad_sent = lax.all_to_all(spread(grad_parts), "fsdp", split_axis=0, concat_axis=0, tiled=True)
    grad_hidden = jnp.einsum(
        "scd,hd->sch", grad_sent, slab_down, preferred_element_type=jnp.float32
    )
    sigmoid = jax.nn.sigmoid(gate_part)
    grad_gate = (grad_hidden * up_part * sigmoid * (1.0 + gate_part * (1.0 - sigmoid))).astype(
        jnp.bfloat16
    )
    grad_up = (grad_hidden * gate_part * sigmoid).astype(jnp.bfloat16)
    grad_inputs = jnp.einsum(
        "sch,dh->scd", grad_gate, slab_gate, preferred_element_type=jnp.float32
    )
    grad_inputs = (
        grad_inputs
        + jnp.einsum("sch,dh->scd", grad_up, slab_up, preferred_element_type=jnp.float32)
    ).astype(jnp.bfloat16)
    grad_back = lax.all_to_all(grad_inputs, "fsdp", split_axis=0, concat_axis=0, tiled=True)
    grad_ffn = jnp.sum(collect(grad_back), axis=1)
    grad_middle = upstream + rms_back(middle, ffn_scale, grad_ffn)
    grad_attn = grad_middle.astype(jnp.bfloat16)
    regathered = (
        lax.all_gather(query_weight, "fsdp", axis=0, tiled=True),
        lax.all_gather(key_weight, "fsdp", axis=0, tiled=True),
        lax.all_gather(value_weight, "fsdp", axis=0, tiled=True),
        lax.all_gather(output_weight, "fsdp", axis=0, tiled=True),
        lax.all_gather(adapter_down_factors, "fsdp", axis=2, tiled=True),
        lax.all_gather(adapter_up_factors, "fsdp", axis=3, tiled=True),
    )
    back_matrices = regathered[:4]
    back_down = pick(regathered[4], adapter)
    back_up = pick(regathered[5], adapter)

    def project_back(inputs, inner, upstream_low, index):
        grad_inner = matmul(upstream_low, back_up[index].T).astype(jnp.bfloat16)
        grad_input = matmul(upstream_low, back_matrices[index].T) + matmul(
            grad_inner, back_down[index].T
        )
        return (grad_input, matmul(inputs.T, grad_inner), matmul(inner.T, upstream_low))

    grad_mixed_full, down_output, up_output = project_back(mixed, out_inner, grad_attn, 3)
    grad_mixed = grad_mixed_full.astype(jnp.bfloat16).reshape(rows_dev, heads, HEAD_DIM)
    probs = jnp.exp(masked_scores() - log_total)
    grad_probs = jnp.einsum(
        "thd,shd->hts", grad_mixed, values_all, preferred_element_type=jnp.float32
    )
    grad_scores = (
        probs * (grad_probs - jnp.sum(probs * grad_probs, axis=-1, keepdims=True))
    ).astype(jnp.bfloat16)
    grad_query = (
        jnp.einsum("hts,shd->thd", grad_scores, keys_all, preferred_element_type=jnp.float32)
        * scale
    )
    grad_keys_part = (
        jnp.einsum("hts,thd->shd", grad_scores, query_rot, preferred_element_type=jnp.float32)
        * scale
    )
    grad_keys_part = grad_keys_part.reshape(group, rows_dev, width)
    grad_values_part = jnp.einsum(
        "hts,thd->shd", probs.astype(jnp.bfloat16), grad_mixed, preferred_element_type=jnp.float32
    )
    grad_values_part = grad_values_part.reshape(group, rows_dev, width)
    for level in reversed(range(level_list)):
        size_half = 1 << level
        upper_bit = place // size_half % 2 == 1
        keep_keys = jnp.where(upper_bit, grad_keys_part[size_half:], grad_keys_part[:size_half])
        send_keys = jnp.where(upper_bit, grad_keys_part[:size_half], grad_keys_part[size_half:])
        keep_values = jnp.where(
            upper_bit, grad_values_part[size_half:], grad_values_part[:size_half]
        )
        send_values = jnp.where(
            upper_bit, grad_values_part[:size_half], grad_values_part[size_half:]
        )
        got_keys, got_values = (
            from_partner(send_keys.astype(jnp.bfloat16), "fsdp", level).astype(send_keys.dtype),
            from_partner(send_values.astype(jnp.bfloat16), "fsdp", level).astype(send_values.dtype),
        )
        grad_keys_part = keep_keys + got_keys
        grad_values_part = keep_values + got_values
    grad_keys = grad_keys_part[0]
    grad_values = grad_values_part[0]
    grad_value_proj = grad_values.astype(jnp.bfloat16)
    grad_key_proj = rms_back(
        key_heads,
        key_scale,
        rotate_back(grad_keys.reshape(rows_dev, heads, HEAD_DIM), cosine, sine),
    )
    grad_key_proj = grad_key_proj.reshape(rows_dev, width).astype(jnp.bfloat16)
    grad_query_proj = rms_back(query_heads, query_scale, rotate_back(grad_query, cosine, sine))
    grad_query_proj = grad_query_proj.reshape(rows_dev, width).astype(jnp.bfloat16)
    grad_from_query, down_query, up_query = project_back(normed, query_inner, grad_query_proj, 0)
    grad_from_key, down_key, up_key = project_back(normed, key_inner, grad_key_proj, 1)
    grad_from_value, down_value, up_value = project_back(normed, value_inner, grad_value_proj, 2)
    grad_normed = grad_from_query + grad_from_key + grad_from_value
    grad_tokens = (grad_middle + rms_back(rows, attn_scale, grad_normed)).astype(jnp.bfloat16)
    down_terms = jnp.stack([down_query, down_key, down_value, down_output])
    up_terms = jnp.stack([up_query, up_key, up_value, up_output])
    selected = (jnp.arange(ADAPTER_COUNT, dtype=jnp.int32) == adapter).astype(jnp.float32)[
        :, None, None, None
    ]
    grad_down, grad_up = (
        lax.psum_scatter(selected * down_terms[None], "fsdp", scatter_dimension=2, tiled=True),
        lax.psum_scatter(selected * up_terms[None], "fsdp", scatter_dimension=3, tiled=True),
    )
    return (output, grad_tokens, grad_down, grad_up)


epsilon = 1e-06
MESH = pl.DeviceIdType.MESH
LEVELS = 4
CHIPS = 16


def greet_all(me, devices):
    barrier = pltpu.get_barrier_semaphore()

    @pl.loop(1, devices)
    def _(i):
        pl.semaphore_signal(barrier, inc=1, device_id=((me + i) % devices,), device_id_type=MESH)


def segments_at(segs, sequence, at):
    row = segs[0:1, at]
    for s in range(1, segs.shape[0]):
        row = jnp.where(sequence == s, segs[s : s + 1, at], row)
    return row.astype(jnp.float32)


class Place:
    def __init__(self):
        self.me = me = lax.axis_index("fsdp")
        self.core = me % 2
        self.x = me // 2 % 2
        self.y = me // 4 % 2
        self.z = me // 8
        self.sibling = me + 1 - 2 * self.core
        self.across_x = me + 2 - 4 * self.x
        self.across_y = me + 4 - 8 * self.y

    def level(self, i):
        upper = self.z // 2
        inner = self.z * (1 - upper) + (3 - self.z) * upper
        turn = i + inner * (1 - 2 * i) * (1 - i // 2)
        return turn + upper * (3 - 2 * turn)

    def chip(self, half, side, level):
        flip = 1 - 2 * side
        y = self.y + (1 - half) * side * (1 - 2 * self.y)
        x = self.x + half * side * (1 - 2 * self.x)
        return level * 4 + y * 2 + x

    def chip_at(self, dx, dy, level):
        y = self.y + dy * (1 - 2 * self.y)
        x = self.x + dx * (1 - 2 * self.x)
        return level * 4 + y * 2 + x

    def first(self, half):
        return self.across_y * (1 - half) + self.across_x * half

    def last(self, half):
        return self.across_x * (1 - half) + self.across_y * half


OUTER_STEPS = (
    819265, 8651264, 12861442, 50372656, 8931409, 17432627, 13697571, 13172803, 37790773, 54809233, 34645544,
    42607251, 15008899, 14756500, 11890914, 65086601, 16013475, 59585160, 15800984, 41180860, 12187788, 16326300,
    37256878, 49626350, 11353642, 15294205, 36592266, 15561967, 40523830, 79254266, 10041135, 49140263, 35279415,
    65867414, 77672101, 60178981, 78533815, 43118213, 76663074, 64638646, 75646758, 126075173, 126075360, 126075360,
    126075360, 126075360, 126075360, 126075360, 126075360, 126075360, 126075360, 126075360,
)
INNER_STEPS = (
    297029, 30459904, 543235, 9464372, 51440213, 10266665, 8704550, 8409348, 14486081, 12612200, 14231616, 14705273,
    39127121, 11903096, 8953965, 71373446, 11568294, 35459180, 17594915, 13173376, 47565949, 15754834, 37812375,
    42247925, 18406959, 28859544, 39395993, 16349409, 36998782, 66092674, 22609570, 41228375, 34395178, 49923218,
    28071580, 66659898, 15529128, 37297787, 31027944, 26819743, 36265721, 62723687, 78966458, 26555547, 75847418,
    79259371, 77945587, 77716258, 78737199, 78507818, 76693795, 76959015,
)


def experts_kernel(rows, rank, x_ref, up_ref, gate_w, up_w, down_w, coeff, own_up, middle, gains, matrix, weights, out_inner, mixed,
                   grad_middle, grad_mixed, early, part_out, gathered,
                   out, held_w, pairs, tail_sem,
                   block, part_buf, result, sib, cross_out, cross_in, hold, z_in, first_out, first_in, total,
                   local_sem, load_sem, part_sem, send, recv, sib_send, sib_recv, cross_send, cross_recv,
                   z_send, z_recv, first_send, first_recv):
    place = Place()
    half = rows // 2
    f32, bf = jnp.float32, jnp.bfloat16
    flip = (((1,), (1,)), ((), ()))
    me, core = place.me, place.core
    upper = place.z // 2
    inner = place.z * (1 - upper) + (3 - place.z) * upper
    UP, DOWN, LAST, SIB, FIRST = range(5)

    def move(n, h, o, kind, target):
        piece = gathered.at[2 * o + core, h, n]
        return pltpu.make_async_remote_copy(
            src_ref=piece, dst_ref=piece, send_sem=send.at[kind, n, h, o],
            recv_sem=recv.at[1 if kind == SIB else 0, n, h, o], device_id=(target,), device_id_type=MESH)

    def arrived(n, h, o, sibling):
        piece = gathered.at[2 * o + (1 - core if sibling else core), h, n]
        pltpu.make_async_remote_copy(
            src_ref=piece, dst_ref=piece, send_sem=send.at[SIB, n, h, o],
            recv_sem=recv.at[1 if sibling else 0, n, h, o], device_id=(place.sibling,), device_id_type=MESH).wait_recv()

    def column(n, h, o, level, act):
        @pl.when((level <= place.z) & (place.z < LEVELS - 1))
        def _():
            act(move(n, h, o, UP, me + 8))

        @pl.when((level >= place.z) & (place.z > 0))
        def _():
            act(move(n, h, o, DOWN, me - 8))

    def spread(n, h, o, level, act):
        column(n, h, o, level, act)
        act(move(n, h, o, LAST, place.last(h)))
        act(move(n, h, o, SIB, place.sibling))

    def to_sibling(slot):
        return pltpu.make_async_remote_copy(
            src_ref=result.at[slot, 1 - core], dst_ref=sib.at[slot], send_sem=sib_send.at[slot],
            recv_sem=sib_recv.at[slot], device_id=(place.sibling,), device_id_type=MESH)

    def across(h, k, level):
        return pltpu.make_async_remote_copy(
            src_ref=cross_out.at[h, k, level], dst_ref=cross_in.at[h, k, level], send_sem=cross_send.at[h, k, level],
            recv_sem=cross_recv.at[h, k, level], device_id=(place.last(h),), device_id_type=MESH)

    def along(h, k, level, up, slot):
        return pltpu.make_async_remote_copy(
            src_ref=hold.at[h, k, level], dst_ref=z_in.at[h, k, slot], send_sem=z_send.at[h, k, level],
            recv_sem=z_recv.at[h, k, slot], device_id=(me - 8 + 16 * up,), device_id_type=MESH)

    def first(h):
        return pltpu.make_async_remote_copy(
            src_ref=first_out.at[h], dst_ref=first_in.at[h], send_sem=first_send.at[h],
            recv_sem=first_recv.at[h], device_id=(place.first(h),), device_id_type=MESH)

    def down_slot(level):
        ends = 1 - jnp.minimum(jnp.abs(level - (place.z - 1)), 1)
        return level + ends * (LEVELS - level)

    start = lambda copy: copy.start()
    done = lambda copy: copy.wait_send()
    mine = me // 2
    barrier = pltpu.get_barrier_semaphore()

    def greet(other):
        pl.semaphore_signal(barrier, inc=1, device_id=(other,), device_id_type=MESH)

    for other in (place.sibling, place.across_x, place.across_y):
        greet(other)

    @pl.when(place.z < LEVELS - 1)
    def _():
        greet(me + 8)

    @pl.when(place.z > 0)
    def _():
        greet(me - 8)

    tail = [
        pltpu.make_async_copy(matrix, held_w, tail_sem.at[0]),
        pltpu.make_async_copy(weights.at[:, :, pl.ds(384, 128)], pairs, tail_sem.at[1]),
    ]
    for copy in tail:
        copy.start()
    own = [
        pltpu.make_async_copy(ref.at[pl.ds(h * half, half)], gathered.at[me, h, n], local_sem.at[n, h])
        for n, ref in enumerate((x_ref, up_ref)) for h in range(2)
    ]
    for copy in own:
        copy.start()
    for copy in own:
        copy.wait()
    pl.semaphore_wait(barrier, 4 + inner)
    pieces = [(n, h) for n in range(2) for h in range(2)]
    def keep_part(o, slot):
        return pltpu.make_async_copy(part_buf.at[slot], part_out.at[o], part_sem.at[slot])

    def compute(o, slot, again):
        def load(n, sibling):
            side = 1 - core if sibling else core
            return pltpu.make_async_copy(
                gathered.at[2 * o + side, :, n], block.at[side, :, n], load_sem.at[n, 1 if sibling else 0])

        for n in range(2):
            load(n, False).start()
        for n in range(2):
            for h in range(2):
                arrived(n, h, o, True)
            load(n, True).start()

        @pl.when(again)
        def _():
            to_sibling(slot).wait_send()

        load(0, False).wait()
        load(0, True).wait()
        c = [jnp.broadcast_to(coeff[2 * o + side], (rows, rows)).T[:, 0:1] for side in range(2)]
        c = jnp.concatenate(c, axis=0)
        x = block[:, :, 0].reshape(2 * rows, -1)
        gate = jnp.dot(x, gate_w[...], preferred_element_type=f32)
        up = jnp.dot(x, up_w[...], preferred_element_type=f32)
        sig = jax.nn.sigmoid(gate)
        silu = gate * sig
        hidden = (silu * up).astype(bf)
        part = (c * jnp.dot(hidden, down_w[...], preferred_element_type=f32)).astype(bf)
        part = part.reshape(2, 2, half, -1)
        result[slot, 0, 1] = part[0]
        result[slot, 1, 1] = part[1]
        load(1, False).wait()
        load(1, True).wait()
        upstream = (c * block[:, :, 1].reshape(2 * rows, -1).astype(f32)).astype(bf)
        grad_hidden = lax.dot_general(upstream, down_w[...], flip, preferred_element_type=f32)
        grad_gate = (grad_hidden * up * sig * (1.0 + gate * (1.0 - sig))).astype(bf)
        grad_up = (grad_hidden * silu).astype(bf)
        grad = lax.dot_general(grad_gate, gate_w[...], flip, preferred_element_type=f32)
        grad += lax.dot_general(grad_up, up_w[...], flip, preferred_element_type=f32)
        grad = grad.astype(bf).reshape(2, 2, half, -1)
        result[slot, 0, 0] = grad[0]
        result[slot, 1, 0] = grad[1]
        to_sibling(slot).start()

    def pair_sum(dx, dy, level, slot, again):
        to_sibling(slot).wait_recv()

        def pair(n, h):
            return (result[slot, core, n, h].astype(f32) + sib[slot, n, h].astype(f32)).astype(bf)

        for h, away, k in ((0, dx, dy), (1, dy, dx)):
            @pl.when(away == 1)
            def _():
                cross_out[h, k, level] = pair(0, h)
                across(h, k, level).start()

            @pl.when(away == 0)
            def _():
                hold[h, k, level] = pair(0, h)

        o = place.chip_at(dx, dy, level)

        @pl.when(again)
        def _():
            keep_part(o, slot).wait()

        for h in range(2):
            part_buf[slot, h] = pair(1, h)
        keep_part(o, slot).start()

    def column_sum(h, k, level):
        across(h, k, level).wait_recv()
        total[...] = hold[h, k, level].astype(f32) + cross_in[h, k, level].astype(f32)

        @pl.when((level >= place.z) & (place.z > 0))
        def _():
            along(h, k, level, 1, level).wait_recv()
            total[...] += z_in[h, k, level].astype(f32)

        @pl.when((level < place.z) & (place.z < LEVELS - 1))
        def _():
            along(h, k, level, 0, level).wait_recv()
            total[...] += z_in[h, k, level].astype(f32)

        @pl.when((level == place.z) & (place.z < LEVELS - 1))
        def _():
            along(h, k, level, 0, LEVELS).wait_recv()
            total[...] += z_in[h, k, LEVELS].astype(f32)

        @pl.when(level > place.z)
        def _():
            hold[h, k, level] = total[...].astype(bf)
            along(h, k, level, 1, level).start()

        @pl.when(level < place.z)
        def _():
            hold[h, k, level] = total[...].astype(bf)
            along(h, k, level, 0, down_slot(level)).start()

        @pl.when((level == place.z) & (k == 1))
        def _():
            first_out[h] = total[...].astype(bf)
            first(h).start()

        @pl.when((level == place.z) & (k == 0))
        def _():
            out[pl.ds(h * half, half)] = total[...]

    def step(code):
        kind, which = code // 32, code % 32
        h, k, n = which % 2, which // 2 % 2, which // 16
        turn = which // 4 % 4
        level = turn + upper * (3 - 2 * turn)
        o = place.chip(h, k, level)

        @pl.when(kind == 0)
        def _():
            move(which // 2 % 2, h, mine, FIRST, place.first(h)).start()

        @pl.when(kind == 1)
        def _():
            @pl.when((k == 1) | (level != place.z))
            def _():
                arrived(n, h, o, False)

            move(n, h, o, LAST, place.last(h)).start()
            move(n, h, o, SIB, place.sibling).start()

        @pl.when((kind == 2) | (kind == 3))
        def _():
            down = (kind + upper) % 2
            piece = gathered.at[2 * o + core, h, n]
            pltpu.make_async_remote_copy(
                src_ref=piece, dst_ref=piece, send_sem=send.at[down, n, h, o], recv_sem=recv.at[0, n, h, o],
                device_id=(me + 8 - 16 * down,), device_id_type=MESH).start()

        @pl.when(kind == 4)
        def _():
            away = place.chip_at(1 - h + h * k, k + h - h * k, level)
            arrived(n, h, away, False)
            move(n, h, away, SIB, place.sibling).start()

        dx, dy = which % 2, which // 2 % 2

        @pl.when((kind == 5) | (kind == 6))
        def _():
            compute(place.chip_at(dx, dy, level), which // 16, kind == 5)

        @pl.when((kind == 7) | (kind == 8))
        def _():
            pair_sum(dx, dy, level, which // 16, kind == 7)

        @pl.when(kind == 9)
        def _():
            column_sum(h, k, level)

    @pl.loop(0, len(OUTER_STEPS))
    def _(i):
        word = 0
        for at, (outer_word, inner_word) in enumerate(zip(OUTER_STEPS, INNER_STEPS)):
            word = jnp.where(i == at, jnp.where(inner == 0, outer_word, inner_word), word)

        def one(_, rest):
            step(rest % 512)
            return rest // 512

        lax.fori_loop(0, 3, one, word)

    for h in range(2):
        first(h).wait_recv()
        out[pl.ds(h * half, half)] += first_in[h].astype(f32)
    for copy in tail:
        copy.wait()

    ours = middle[...]
    inverse = lax.rsqrt(jnp.mean(ours * ours, axis=-1, keepdims=True) + epsilon)
    unit = ours * inverse
    scaled = out[...] * gains[1:2]
    grad = inverse * (scaled - unit * jnp.mean(scaled * unit, axis=-1, keepdims=True))
    grad = own_up[...].astype(f32) + grad
    grad_middle[...] = grad
    grad = grad.astype(bf)
    adapters = pairs[...].reshape(-1, 128)
    lane = lax.broadcasted_iota(jnp.int32, (rows, 128), 1)
    low = jnp.dot(grad, adapters, preferred_element_type=f32)
    low = jnp.where(lane // rank == 7, low, 0.0).astype(bf)
    low = pltpu.roll(low.astype(f32), 64, 1).astype(bf)
    back = lax.dot_general(grad, held_w[...], flip, preferred_element_type=f32)
    back += lax.dot_general(low, adapters, flip, preferred_element_type=f32)
    grad_mixed[...] = back.astype(bf)
    tall = (((0,), (0,)), ((), ()))
    early[0:rank] = lax.dot_general(low, mixed[...], tall, preferred_element_type=f32)[3 * rank : 4 * rank]
    early[rank:] = lax.dot_general(out_inner[...], grad, tall, preferred_element_type=f32)[3 * rank : 4 * rank]

    for n, h in pieces:
        move(n, h, mine, FIRST, place.first(h)).wait_send()
        spread(n, h, mine, place.z, done)
        spread(n, h, place.chip(h, 1, place.z), place.z, done)
    for h in range(2):
        first(h).wait_send()
    for slot in range(2):
        to_sibling(slot).wait_send()
        keep_part(0, slot).wait()

    @pl.loop(0, CHIPS)
    def _(t):
        h, k = t % 2, t // 2 % 2

        @pl.when(t < CHIPS - 4)
        def _():
            level = place.level(1 + t // 4)
            for n in range(2):
                spread(n, h, place.chip(h, k, level), level, done)

        dx, dy = t % 2, t // 2 % 2
        o = place.chip_at(dx, dy, t // 4)
        for side, away in ((0, dx), (1, dy)):
            @pl.when(away == 1)
            def _():
                for n in range(2):
                    move(n, side, o, SIB, place.sibling).wait_send()

        level = t // 4
        across(h, k, level).wait_send()

        @pl.when(level > place.z)
        def _():
            along(h, k, level, 1, level).wait_send()

        @pl.when(level < place.z)
        def _():
            along(h, k, level, 0, down_slot(level)).wait_send()


def experts_pass(x, upstream, gate_w, up_w, down_w, coeff, middle, gains, matrix, weights, out_inner, mixed, rank):
    rows, width = x.shape
    devices = coeff.shape[0]
    half = rows // 2
    bf, f32 = jnp.bfloat16, jnp.float32
    dma = pltpu.SemaphoreType.DMA
    vmem, anywhere = pl.BlockSpec(memory_space=pltpu.VMEM), pl.BlockSpec(memory_space=pl.ANY)
    piece = (half, width)
    return pl.pallas_call(
        functools.partial(experts_kernel, rows, rank),
        out_shape=(
            jax.ShapeDtypeStruct((rows, width), f32),
            jax.ShapeDtypeStruct((rows, width), bf),
            jax.ShapeDtypeStruct((2 * rank, width), f32),
            jax.ShapeDtypeStruct((CHIPS, 2) + piece, bf),
            jax.ShapeDtypeStruct((devices, 2, 2) + piece, bf),
        ),
        in_specs=[anywhere, anywhere] + [vmem] * 7 + [anywhere, anywhere, vmem, vmem],
        out_specs=(vmem, vmem, vmem, anywhere, anywhere),
        scratch_shapes=[
            pltpu.VMEM((rows, width), f32),
            pltpu.VMEM(matrix.shape, bf),
            pltpu.VMEM(weights.shape[:2] + (128,), bf),
            dma((2,)),
            pltpu.VMEM((2, 2, 2) + piece, bf),
            pltpu.VMEM((2, 2) + piece, bf),
            pltpu.VMEM((2, 2, 2, 2) + piece, bf),
            pltpu.VMEM((2, 2, 2) + piece, bf),
            pltpu.VMEM((2, 2, LEVELS) + piece, bf),
            pltpu.VMEM((2, 2, LEVELS) + piece, bf),
            pltpu.VMEM((2, 2, LEVELS) + piece, bf),
            pltpu.VMEM((2, 2, LEVELS + 1) + piece, bf),
            pltpu.VMEM((2,) + piece, bf),
            pltpu.VMEM((2,) + piece, bf),
            pltpu.VMEM(piece, f32),
            dma((2, 2)), dma((2, 2)), dma((2,)), dma((5, 2, 2, CHIPS)), dma((2, 2, 2, CHIPS)), dma((2,)), dma((2,)),
            dma((2, 2, LEVELS)), dma((2, 2, LEVELS)),
            dma((2, 2, LEVELS)), dma((2, 2, LEVELS + 1)), dma((2,)), dma((2,)),
        ],
        compiler_params=pltpu.CompilerParams(collective_id=1, has_side_effects=True, vmem_limit_bytes=62 << 20),
        name="experts",
    )(x, upstream, gate_w, up_w, down_w, coeff, upstream, middle, gains, matrix, weights, out_inner, mixed)


def front_kernel(rows, rank, picked, tokens, gains, query_w, key_w, value_w, segs, downs, ups, routes, gates, out_w, near, far_turn,
                 query_gain, key_gain,
                 middle, normed_ffn, normed, mixed, out_inner, weights, query_out, key_out, value_out,
                 query_proj, key_proj, inner_out, coeff_out, cosine, sine, out_all,
                 held, mixed_buf, pair, coeff, wo, heads_w,
                 local_sem, send, recv, w_send, w_recv, pair_send, pair_recv, c_send, c_recv, m_send, m_recv, m_local,
                 g_send, g_recv, keep_sem):
    place = Place()
    f32, bf = jnp.float32, jnp.bfloat16
    me, core = place.me, place.core
    group = held.shape[0]
    base, p = me // group * group, me % group
    other = (me + group) % (2 * group)
    other_base = group - base
    half = rows // 2
    depth = weights.shape[1]
    wide = 3 * 128
    z = place.z % 2
    across_z = me + 8 - 16 * z
    chip = p // 2

    FIRST, ALONG, LAST, SIB = range(4)

    def chip_at(h, k, far):
        flip = place.chip(h, k, 0)
        zz = z + far * (1 - 2 * z)
        return zz * 4 + flip

    def move(h, o, kind, target):
        piece = held.at[2 * o + core, pl.ds(h * half, half)]
        return pltpu.make_async_remote_copy(
            src_ref=piece, dst_ref=piece, send_sem=send.at[kind, h, o],
            recv_sem=recv.at[1 if kind == SIB else 0, h, o], device_id=(target,), device_id_type=MESH)

    def arrived(h, o, sibling):
        piece = held.at[2 * o + (1 - core if sibling else core), pl.ds(h * half, half)]
        pltpu.make_async_remote_copy(
            src_ref=piece, dst_ref=piece, send_sem=send.at[SIB, h, o],
            recv_sem=recv.at[1 if sibling else 0, h, o], device_id=(place.sibling,), device_id_type=MESH).wait_recv()

    def to_heads(q):
        return pltpu.make_async_remote_copy(
            src_ref=heads_w.at[q % group], dst_ref=weights.at[me, :, pl.ds(0, wide)], send_sem=w_send.at[q],
            recv_sem=w_recv.at[me], device_id=(q,), device_id_type=MESH)

    def to_expert(q):
        return pltpu.make_async_remote_copy(
            src_ref=coeff.at[q // 2], dst_ref=coeff_out.at[me], send_sem=c_send.at[q],
            recv_sem=c_recv.at[me], device_id=(q,), device_id_type=MESH)

    def pair_over(q, side):
        row = (me + side * group) % (2 * group)
        piece = weights.at[row, :, pl.ds(wide, 128)]
        return pltpu.make_async_remote_copy(
            src_ref=piece, dst_ref=piece, send_sem=pair_send.at[side, q],
            recv_sem=pair_recv.at[row], device_id=(base + q,), device_id_type=MESH)

    pair_other = pltpu.make_async_remote_copy(
        src_ref=pair.at[other // group], dst_ref=weights.at[me, :, pl.ds(wide, 128)], send_sem=pair_send.at[2, 0],
        recv_sem=pair_recv.at[me], device_id=(other,), device_id_type=MESH)
    greet_all(me, 2 * group)

    UP, DOWN, G_LAST, G_SIB, G_FIRST = range(5)

    def g_move(h, o, kind, target):
        piece = wo.at[2 * o + core, h]
        return pltpu.make_async_remote_copy(
            src_ref=piece, dst_ref=piece, send_sem=g_send.at[kind, h, o],
            recv_sem=g_recv.at[1 if kind == G_SIB else 0, h, o], device_id=(target,), device_id_type=MESH)

    def g_arrived(h, o, sibling):
        piece = wo.at[2 * o + (1 - core if sibling else core), h]
        pltpu.make_async_remote_copy(
            src_ref=piece, dst_ref=piece, send_sem=g_send.at[G_SIB, h, o],
            recv_sem=g_recv.at[1 if sibling else 0, h, o], device_id=(place.sibling,), device_id_type=MESH).wait_recv()

    def g_column(h, o, level, act):
        @pl.when((level <= place.z) & (place.z < LEVELS - 1))
        def _():
            act(g_move(h, o, UP, me + 8))

        @pl.when((level >= place.z) & (place.z > 0))
        def _():
            act(g_move(h, o, DOWN, me - 8))

    def g_spread(h, o, level, act):
        g_column(h, o, level, act)
        act(g_move(h, o, G_LAST, place.last(h)))
        act(g_move(h, o, G_SIB, place.sibling))

    def g_level(t):
        level, h, k = place.level(1 + t // 4), t % 2, t // 2 % 2
        o = place.chip(h, k, level)
        g_arrived(h, o, False)
        g_spread(h, o, level, start)

    def g_cross(q):
        dx, dy = q % 2, q // 2 % 2
        o = place.chip_at(dx, dy, place.level(q // 4))
        for h, away in ((0, dx), (1, dy)):
            @pl.when(away == 1)
            def _():
                g_arrived(h, o, False)
                g_move(h, o, G_SIB, place.sibling).start()

    start = lambda copy: copy.start()
    done = lambda copy: copy.wait_send()
    own_chip = me // 2
    own_copies = [
        pltpu.make_async_copy(heads_w.at[p], weights.at[me, :, pl.ds(0, wide)], local_sem.at[0]),
        pltpu.make_async_copy(out_w.at[pl.ds(0, depth // 2)], wo.at[me, 0], local_sem.at[1]),
        pltpu.make_async_copy(out_w.at[pl.ds(depth // 2, depth // 2)], wo.at[me, 1], local_sem.at[2]),
    ]
    for q in range(group):
        for j, matrix in enumerate((query_w, key_w, value_w)):
            heads_w[q, :, j * 128 : (j + 1) * 128] = matrix[:, q * 128 : (q + 1) * 128]
    for copy in own_copies:
        copy.start()
    ours = tokens[...].astype(f32)
    low = (ours * lax.rsqrt(jnp.mean(ours * ours, axis=-1, keepdims=True) + epsilon) * gains[0:1]).astype(bf)
    held[p] = low
    normed[...] = low
    pl.semaphore_wait(pltpu.get_barrier_semaphore(), 2 * group - 1)
    for h in range(2):
        move(h, chip, ALONG, across_z).start()
        move(h, chip, FIRST, place.first(h)).start()
    for h in range(2):
        move(h, chip, LAST, place.last(h)).start()
        move(h, chip, SIB, place.sibling).start()

    @pl.loop(0, group)
    def _(i):
        to_heads(other_base + (p + i) % group).start()

    for s in range(2):
        down, up = downs[picked[s]].astype(f32), ups[picked[s]].astype(f32)
        both = [jnp.concatenate([side[j] for j in range(4)], axis=0).T for side in (down, up)]
        pair[s] = jnp.concatenate(both, axis=1).astype(bf)
    weights[me, :, wide:] = pair[me // group]
    pair_other.start()

    lane = lax.broadcasted_iota(jnp.int32, (rows, 128), 1)
    expert = lax.broadcasted_iota(jnp.int32, (coeff.shape[0], rows), 0)
    gate = jnp.zeros(expert.shape, f32)
    for k in range(routes.shape[0]):
        gate += jnp.where(expert == routes[k : k + 1], gates[k : k + 1], 0.0)
    for e in range(coeff.shape[0]):
        coeff[e] = gate[e : e + 1]
    coeff_out[me] = coeff[me // 2]

    @pl.loop(1, group)
    def _(i):
        pair_over((p + i) % group, 0).start()
        to_heads(base + (p + i) % group).start()

    @pl.loop(1, 2 * group)
    def _(i):
        to_expert((me + i) % (2 * group)).start()

    for copy in own_copies[1:]:
        copy.wait()
    for h in range(2):
        g_column(h, own_chip, place.z, start)
        g_move(h, own_chip, G_FIRST, place.first(h)).start()
    for h in range(2):
        g_move(h, own_chip, G_LAST, place.last(h)).start()
        g_move(h, own_chip, G_SIB, place.sibling).start()

    pltpu.make_async_remote_copy(
        src_ref=pair.at[0], dst_ref=weights.at[other, :, pl.ds(wide, 128)], send_sem=pair_send.at[2, 0],
        recv_sem=pair_recv.at[other], device_id=(other,), device_id_type=MESH).wait_recv()

    @pl.loop(1, group)
    def _(i):
        pair_over((p + i) % group, 1).start()

    for h in range(2):
        o = chip_at(h, 0, 1)
        arrived(h, o, False)
        move(h, o, FIRST, place.first(h)).start()
        move(h, o, LAST, place.last(h)).start()
        move(h, o, SIB, place.sibling).start()
    for far in range(2):
        for h in range(2):
            o = chip_at(h, 1, far)
            arrived(h, o, False)
            move(h, o, LAST, place.last(h)).start()
            move(h, o, SIB, place.sibling).start()
    for h in range(2):
        o = place.chip(h, 1, place.z)
        g_arrived(h, o, False)
        g_spread(h, o, place.z, start)

    @pl.loop(0, group)
    def _(i):
        at = pl.ds(pl.multiple_of(i * rows, rows), rows)
        c, s = far_turn[0, pl.ds(i, 1)], far_turn[1, pl.ds(i, 1)]
        cosine[at] = c * near[0] - s * near[1]
        turn = s * near[0] + c * near[1]
        sine[at] = jnp.where(lane < 64, -turn, turn)

    for far in range(2):
        for k in range(2):
            for h in range(2):
                dx, dy = (1, k) if h == 0 else (k, 1)
                o = (z + far * (1 - 2 * z)) * 4 + place.chip_at(dx, dy, 0)
                arrived(h, o, False)
                move(h, o, SIB, place.sibling).start()
    own_copies[0].wait()

    @pl.loop(0, 4)
    def _(t):
        g_level(t)


    @pl.loop(1, 2 * group)
    def _(i):
        q = (me + i) % (2 * group)
        pltpu.make_async_remote_copy(
            src_ref=heads_w.at[0], dst_ref=weights.at[q, :, pl.ds(0, wide)], send_sem=w_send.at[q],
            recv_sem=w_recv.at[q], device_id=(q,), device_id_type=MESH).wait_recv()
        pltpu.make_async_remote_copy(
            src_ref=coeff.at[0], dst_ref=coeff_out.at[q], send_sem=c_send.at[q],
            recv_sem=c_recv.at[q], device_id=(q,), device_id_type=MESH).wait_recv()

        @pl.when(q != other)
        def _():
            pltpu.make_async_remote_copy(
                src_ref=pair.at[0], dst_ref=weights.at[q, :, pl.ds(wide, 128)], send_sem=pair_send.at[2, 0],
                recv_sem=pair_recv.at[q], device_id=(other,), device_id_type=MESH).wait_recv()

    @pl.loop(0, group // 2)
    def _(o):
        for h in range(2):
            arrived(h, o, True)

    @pl.loop(4, 8)
    def _(t):
        g_level(t)

    span = 2 * rows
    seq = group * rows
    up_own = weights[pl.ds(2 * p, 2), :, pl.ds(wide, 128)].reshape(2 * depth, 128)
    up_own = pltpu.roll(up_own.astype(f32), 64, 1).astype(bf)
    flip = (((1,), (1,)), ((), ()))
    scale = 1.0 / math.sqrt(128)

    @pl.loop(0, group // 2)
    def _(b):
        at = pl.ds(pl.multiple_of(b * span, span), span)
        x = held[pl.ds(2 * b, 2)].reshape(span, -1)
        acc = jnp.dot(x, weights[...].reshape(2 * group * depth, wide + 128), preferred_element_type=f32)
        inner = acc[:, wide:].astype(bf)
        inner_out[at] = inner
        owner = lax.broadcasted_iota(jnp.int32, inner.shape, 1) // rank

        def projected(j):
            low = jnp.where(owner == j, inner.astype(f32), 0.0).astype(bf)
            return acc[:, j * 128 : (j + 1) * 128] + lax.dot_general(low, up_own, flip, preferred_element_type=f32)

        for j, (gain, raw, rot) in enumerate(((query_gain, query_proj, query_out), (key_gain, key_proj, key_out))):
            value = projected(j)
            raw[at] = value
            unit = value * lax.rsqrt(jnp.mean(value * value, axis=-1, keepdims=True) + epsilon) * gain[...]
            rot[at] = (unit * cosine[at] + pltpu.roll(unit, 64, 1) * sine[at]).astype(bf)
        value_out[at] = projected(2).astype(bf)

        @pl.when(b % 2 == 0)
        def _():
            g_level(8 + b // 2)

    def to_token(q):
        return pltpu.make_async_remote_copy(
            src_ref=mixed_buf.at[q], dst_ref=mixed.at[:, pl.ds(p * 128, 128)], send_sem=m_send.at[q],
            recv_sem=m_recv.at[p], device_id=(base + q,), device_id_type=MESH)

    keep = pltpu.make_async_copy(mixed_buf.at[p], mixed.at[:, pl.ds(p * 128, 128)], m_local)

    @pl.loop(0, group // 2)
    def _(b):
        at = pl.ds(pl.multiple_of(b * span, span), span)
        scores = lax.dot_general(query_out[at], key_out[...], flip, preferred_element_type=f32)
        own_seg = [
            jnp.broadcast_to(segments_at(segs, me // group, pl.ds(pl.multiple_of(b * span + i, 128), 128)), (128, 128)).T
            for i in range(0, span, 128)
        ]
        own_seg = jnp.concatenate(own_seg, axis=0)[:, 0:1]
        weight = jnp.where(own_seg == segments_at(segs, me // group, slice(None)), jnp.exp2(scores * (scale * math.log2(math.e))), 0.0)
        total = jnp.sum(weight, axis=-1, keepdims=True)
        value = jnp.dot(weight.astype(bf), value_out[...], preferred_element_type=f32) / total
        mixed_buf[pl.ds(2 * b, 2)] = value.astype(bf).reshape(2, rows, 128)
        for side in range(2):
            q = 2 * b + side

            @pl.when(q != p)
            def _():
                to_token(q).start()

            @pl.when(q == p)
            def _():
                keep.start()

        g_cross(2 * b)
        g_cross(2 * b + 1)

    keep.wait()

    @pl.loop(1, group)
    def _(i):
        q = (p + i) % group
        pltpu.make_async_remote_copy(
            src_ref=mixed_buf.at[q], dst_ref=mixed.at[:, pl.ds(q * 128, 128)], send_sem=m_send.at[q],
            recv_sem=m_recv.at[q], device_id=(base + q,), device_id_type=MESH).wait_recv()

    @pl.loop(0, CHIPS)
    def _(o):
        for h in range(2):
            g_arrived(h, o, True)

    keep_out = pltpu.make_async_copy(wo, out_all, keep_sem)
    keep_out.start()
    ours = mixed[...]
    matrix = weights[:, :, wide:].reshape(2 * group * depth, 128)
    lane = lax.broadcasted_iota(jnp.int32, (rows, 128), 1)
    inner = jnp.dot(ours, matrix, preferred_element_type=f32)
    inner = jnp.where(lane // rank == 3, inner, 0.0).astype(bf)
    out_inner[...] = inner
    shifted = pltpu.roll(inner.astype(f32), 64, 1).astype(bf)
    total = tokens[...].astype(f32) + jnp.dot(ours, wo[...].reshape(2 * group * depth, -1), preferred_element_type=f32)
    total = total + lax.dot_general(shifted, matrix, flip, preferred_element_type=f32)
    middle[...] = total
    unit = total * lax.rsqrt(jnp.mean(total * total, axis=-1, keepdims=True) + epsilon)
    normed_ffn[...] = (unit * gains[1:2]).astype(bf)

    keep_out.wait()
    for h in range(2):
        g_move(h, own_chip, G_FIRST, place.first(h)).wait_send()
        g_spread(h, own_chip, place.z, done)
        g_spread(h, place.chip(h, 1, place.z), place.z, done)

    @pl.loop(0, CHIPS)
    def _(t):
        @pl.when(t < CHIPS - 4)
        def _():
            level, h, k = place.level(1 + t // 4), t % 2, t // 2 % 2
            g_spread(h, place.chip(h, k, level), level, done)

        dx, dy = t % 2, t // 2 % 2
        o = place.chip_at(dx, dy, place.level(t // 4))
        for h, away in ((0, dx), (1, dy)):
            @pl.when(away == 1)
            def _():
                g_move(h, o, G_SIB, place.sibling).wait_send()

    pair_other.wait_send()
    for h in range(2):
        move(h, chip, ALONG, across_z).wait_send()
        for far in range(2):
            for k in range(2):
                o = chip_at(h, k, far)
                if k == 0:
                    move(h, o, FIRST, place.first(h)).wait_send()
                move(h, o, LAST, place.last(h)).wait_send()
                move(h, o, SIB, place.sibling).wait_send()
                dx, dy = (1, k) if h == 0 else (k, 1)
                o = (z + far * (1 - 2 * z)) * 4 + place.chip_at(dx, dy, 0)
                move(h, o, SIB, place.sibling).wait_send()

    @pl.loop(1, group)
    def _(i):
        q = (p + i) % group
        pair_over(q, 0).wait_send()
        pair_over(q, 1).wait_send()
        to_token(q).wait_send()

    @pl.loop(1, 2 * group)
    def _(i):
        q = (me + i) % (2 * group)
        to_heads(q).wait_send()
        to_expert(q).wait_send()


def turn_tables(rows, group):
    frequency = rope_base ** (-(np.arange(64, dtype=np.float32) * np.float32(2.0 / 128)))
    frequency = np.concatenate([frequency, frequency]).astype(np.float64)
    tables = []
    for positions in (np.arange(rows), np.arange(group) * rows):
        angle = positions[:, None] * frequency[None, :]
        tables.append(np.stack([np.cos(angle), np.sin(angle)]).astype(np.float32))
    return tables


def front(picked, tokens, gains, query_w, key_w, value_w, segs, downs, ups, routes, gates, out_w,
          query_gain, key_gain):
    rows, width = tokens.shape
    group, depth = SEQ_LEN // rows, out_w.shape[0]
    rank = downs.shape[2]
    devices, seq = 2 * group, rows * group
    bf, f32 = jnp.bfloat16, jnp.float32
    dma = pltpu.SemaphoreType.DMA
    vmem, anywhere = pl.BlockSpec(memory_space=pltpu.VMEM), pl.BlockSpec(memory_space=pl.ANY)
    head = jax.ShapeDtypeStruct((seq, 128), bf)
    raw = jax.ShapeDtypeStruct((seq, 128), f32)
    mine = jax.ShapeDtypeStruct((rows, width), bf)
    near, far_turn = turn_tables(rows, group)
    return pl.pallas_call(
        functools.partial(front_kernel, rows, rank),
        out_shape=(
            jax.ShapeDtypeStruct((rows, width), f32), mine, mine, mine,
            jax.ShapeDtypeStruct((rows, 128), bf),
            jax.ShapeDtypeStruct((devices, depth, 512), bf),
            head, head, head, raw, raw, head,
            jax.ShapeDtypeStruct((devices, 1, rows), f32),
            raw, raw,
            jax.ShapeDtypeStruct((devices, 2, depth // 2, width), bf),
        ),
        in_specs=[pl.BlockSpec(memory_space=pltpu.SMEM)] + [vmem] * 10 + [anywhere] + [vmem] * 4,
        out_specs=(vmem,) * 15 + (anywhere,),
        scratch_shapes=[
            pltpu.VMEM((group, rows, width), bf),
            pltpu.VMEM((group, rows, 128), bf),
            pltpu.VMEM((2, depth, 128), bf),
            pltpu.VMEM((group, 1, rows), f32),
            pltpu.VMEM((devices, 2, depth // 2, width), bf),
            pltpu.VMEM((group, depth, 384), bf),
            dma((3,)), dma((4, 2, group // 2)), dma((2, 2, group // 2)),
            dma((devices,)), dma((devices,)), dma((3, group)), dma((devices,)),
            dma((devices,)), dma((devices,)), dma((group,)), dma((group,)), dma,
            dma((5, 2, CHIPS)), dma((2, 2, CHIPS)), dma,
        ],
        compiler_params=pltpu.CompilerParams(collective_id=0, has_side_effects=True, vmem_limit_bytes=60 << 20),
        name="front",
    )(picked, tokens, gains, query_w, key_w, value_w, segs, downs, ups, routes, gates, out_w, jnp.asarray(near), jnp.asarray(far_turn),
      query_gain, key_gain)


OUTER_DONE = (0, 1, 2, 2, 3, 4, 4, 5, 5, 6, 7, 9, 9, 9, 9, 9, 9, 9, 9, 9, 9, 11, 11, 12, 13, 13, 14, 14, 16)
INNER_DONE = (0, 0, 0, 0, 0, 0, 0, 0, 0, 0, 0, 0, 0, 0, 0, 0, 0, 0, 6, 6, 6, 11, 11, 13, 13, 14, 14, 14, 16)


def back_kernel(rows, rank, grad_mixed, part, weights, query, key, value, query_proj, key_proj, inner, cosine, sine,
                query_gain, key_gain, segs, rows_in, normed, gains, grad_middle, middle, early,
                grad_rows, output, factors, out, up_terms, part_sum, late, early_in, late_in, owned,
                e_send, e_recv, l_send, l_recv, f_send, f_recv, t_local,
                grads, key_seg, key_t, grad_key, grad_value, heads, result, sib, cross_out, cross_in, z_out, z_in, first_out, first_in,
                held, part_in, part_z, part_total, part_first_out, part_first_in,
                held_sem, pc_send, pc_recv, pz_send, pz_recv, pf_send, pf_recv,
                a_send, a_recv, a_local, sib_send, sib_recv, cross_send, cross_recv, z_send, z_recv, first_send, first_recv):
    place = Place()
    f32, bf = jnp.float32, jnp.bfloat16
    me, core = place.me, place.core
    group = grads.shape[0]
    depth = weights.shape[1]
    base, p = me // group * group, me % group
    half, span, seq = rows // 2, 2 * rows, rows * group
    width = out.shape[1] - 128
    z = place.z % 2
    across_z = me + 8 - 16 * z
    flip = (((1,), (1,)), ((), ()))
    tall = (((0,), (0,)), ((), ()))
    scale = 1.0 / math.sqrt(128)

    def keep_piece(h, k, level):
        return pltpu.make_async_copy(part.at[place.chip(h, k, level), h], held.at[h, k, level], held_sem.at[h, k, level])

    def part_across(h, k, level):
        dx, dy = (1, k) if h == 0 else (k, 1)
        return pltpu.make_async_remote_copy(
            src_ref=part.at[place.chip_at(dx, dy, level), h], dst_ref=part_in.at[h, k, level],
            send_sem=pc_send.at[h, k, level], recv_sem=pc_recv.at[h, k, level],
            device_id=(place.last(h),), device_id_type=MESH)

    def crossed(h, k, level):
        return pltpu.make_async_remote_copy(
            src_ref=held.at[h, k, level], dst_ref=part_in.at[h, k, level], send_sem=pc_send.at[h, k, level],
            recv_sem=pc_recv.at[h, k, level], device_id=(place.last(h),), device_id_type=MESH)

    def part_along(h, k, level, up, slot):
        return pltpu.make_async_remote_copy(
            src_ref=held.at[h, k, level], dst_ref=part_z.at[h, k, slot], send_sem=pz_send.at[h, k, level],
            recv_sem=pz_recv.at[h, k, slot], device_id=(me - 8 + 16 * up,), device_id_type=MESH)

    def part_first(h):
        return pltpu.make_async_remote_copy(
            src_ref=part_first_out.at[h], dst_ref=part_first_in.at[h], send_sem=pf_send.at[h],
            recv_sem=pf_recv.at[h], device_id=(place.first(h),), device_id_type=MESH)

    def down_slot(level):
        ends = 1 - jnp.minimum(jnp.abs(level - (place.z - 1)), 1)
        return level + ends * (LEVELS - level)

    def part_event(e):
        h, k, level = e % 2, e // 2 % 2, place.level(3 - e // 4)
        keep_piece(h, k, level).wait()
        crossed(h, k, level).wait_recv()
        total = held[h, k, level].astype(f32) + part_in[h, k, level].astype(f32)
        part_total[...] = total

        @pl.when((level >= place.z) & (place.z > 0))
        def _():
            part_along(h, k, level, 1, level).wait_recv()
            part_total[...] += part_z[h, k, level].astype(f32)

        @pl.when((level < place.z) & (place.z < LEVELS - 1))
        def _():
            part_along(h, k, level, 0, level).wait_recv()
            part_total[...] += part_z[h, k, level].astype(f32)

        @pl.when((level == place.z) & (place.z < LEVELS - 1))
        def _():
            part_along(h, k, level, 0, LEVELS).wait_recv()
            part_total[...] += part_z[h, k, LEVELS].astype(f32)

        @pl.when(level > place.z)
        def _():
            held[h, k, level] = part_total[...].astype(bf)
            part_along(h, k, level, 1, level).start()

        @pl.when(level < place.z)
        def _():
            held[h, k, level] = part_total[...].astype(bf)
            part_along(h, k, level, 0, down_slot(level)).start()

        @pl.when((level == place.z) & (k == 1))
        def _():
            part_first_out[h] = part_total[...].astype(bf)
            part_first(h).start()

        @pl.when((level == place.z) & (k == 0))
        def _():
            part_sum[h] = part_total[...]

    upper = place.z // 2
    inner_level = place.z * (1 - upper) + (3 - place.z) * upper

    def part_steps(slot):
        def bound(at):
            if isinstance(at, int):
                return OUTER_DONE[at] + inner_level * (INNER_DONE[at] - OUTER_DONE[at])
            count = 0
            for i, (outer, inside) in enumerate(zip(OUTER_DONE, INNER_DONE)):
                count = jnp.where(at == i, jnp.where(inner_level == 0, outer, inside), count)
            return count

        def one(e, none):
            part_event(e)
            return none

        lax.fori_loop(bound(slot), bound(slot + 1), one, 0)

    def to_head(q):
        return pltpu.make_async_remote_copy(
            src_ref=grad_mixed.at[:, pl.ds(q * 128, 128)], dst_ref=grads.at[p], send_sem=a_send.at[q],
            recv_sem=a_recv.at[p], device_id=(base + q,), device_id_type=MESH)

    def from_token(q):
        return pltpu.make_async_remote_copy(
            src_ref=grad_mixed.at[:, pl.ds(q * 128, 128)], dst_ref=grads.at[q], send_sem=a_send.at[q],
            recv_sem=a_recv.at[q], device_id=(base + q,), device_id_type=MESH)

    keep = pltpu.make_async_copy(grad_mixed.at[:, pl.ds(p * 128, 128)], grads.at[p], a_local)
    keep.start()
    greet_all(me, 2 * group)
    @pl.loop(0, group)
    def _(i):
        at = pl.ds(pl.multiple_of(i * 128, 128), 128)
        key_seg[at] = jnp.broadcast_to(segments_at(segs, me // group, at), (128, 128)).T

    key_t[...] = key[...].astype(f32).T.astype(bf)
    pl.semaphore_wait(pltpu.get_barrier_semaphore(), 2 * group - 1)

    def early_to(q, frm):
        return pltpu.make_async_remote_copy(
            src_ref=early.at[:, pl.ds(q * 128, 128)], dst_ref=early_in.at[frm], send_sem=e_send.at[q],
            recv_sem=e_recv.at[frm], device_id=(base + q,), device_id_type=MESH)

    def late_to(q, frm):
        return pltpu.make_async_remote_copy(
            src_ref=late.at[:, pl.ds(q * 128, 128)], dst_ref=late_in.at[frm], send_sem=l_send.at[q],
            recv_sem=l_recv.at[frm], device_id=(base + q,), device_id_type=MESH)

    def to_owner(side, q, frm):
        return pltpu.make_async_remote_copy(
            src_ref=owned, dst_ref=factors.at[frm], send_sem=f_send.at[side],
            recv_sem=f_recv.at[frm], device_id=(q,), device_id_type=MESH)

    early_keep = pltpu.make_async_copy(early.at[:, pl.ds(p * 128, 128)], early_in.at[p], t_local.at[0])
    late_keep = pltpu.make_async_copy(late.at[:, pl.ds(p * 128, 128)], late_in.at[p], t_local.at[1])
    owned_keep = pltpu.make_async_copy(owned, factors.at[me // group], t_local.at[2])
    early_keep.start()

    @pl.loop(1, group)
    def _(i):
        to_head((p + i) % group).start()

    @pl.loop(1, group)
    def _(i):
        early_to((p + i) % group, p).start()

    @pl.loop(0, 4)
    def _(i):
        level = place.level(3 - i)
        for k in range(2):
            for h in range(2):
                part_across(h, k, level).start()
                keep_piece(h, k, level).start()

    grad_key[...] = jnp.zeros_like(grad_key)
    grad_value[...] = jnp.zeros_like(grad_value)
    keep.wait()

    def raw_grad(raw, gain, turned, at):
        back = turned * cosine[at] - pltpu.roll(turned, 64, 1) * sine[at]
        rows_ = raw[at]
        inverse = lax.rsqrt(jnp.mean(rows_ * rows_, axis=-1, keepdims=True) + epsilon)
        unit = rows_ * inverse
        scaled = back * gain[...]
        return (inverse * (scaled - unit * jnp.mean(scaled * unit, axis=-1, keepdims=True))).astype(bf)

    @pl.loop(0, group // 2)
    def _(b):
        at = pl.ds(pl.multiple_of(b * span, span), span)
        for side in range(2):
            q = 2 * b + side

            @pl.when(q != p)
            def _():
                from_token(q).wait_recv()

        ours = query[at]
        grad = grads[pl.ds(2 * b, 2)].reshape(span, 128)
        scores = lax.dot_general(key[...], ours, flip, preferred_element_type=f32)
        own_seg = segments_at(segs, me // group, at)
        weight = jnp.where(key_seg[:, 0:1] == own_seg, jnp.exp2(scores * (scale * math.log2(math.e))), 0.0)
        probs = weight * (1.0 / jnp.sum(weight, axis=0, keepdims=True))
        grad_probs = lax.dot_general(value[...], grad, flip, preferred_element_type=f32)
        mean = jnp.sum(probs * grad_probs, axis=0, keepdims=True)
        grad_scores = (probs * (grad_probs - mean)).astype(bf)
        grad_key[...] += jnp.dot(grad_scores, ours, preferred_element_type=f32)
        grad_value[...] += jnp.dot(probs.astype(bf), grad, preferred_element_type=f32)
        grad_query = jnp.dot(key_t[...], grad_scores, preferred_element_type=f32).T * scale
        heads[at, 0:128] = raw_grad(query_proj, query_gain, grad_query, at)
        part_steps(b)

    up_own = weights[pl.ds(2 * p, 2), :, 384:512].reshape(2 * depth, 128)
    up_own = pltpu.roll(up_own.astype(f32), 64, 1).astype(bf)

    @pl.loop(0, group // 2)
    def _(b):
        at = pl.ds(pl.multiple_of(b * span, span), span)
        heads[at, 128:256] = raw_grad(key_proj, key_gain, grad_key[at] * scale, at)
        heads[at, 256:384] = grad_value[at].astype(bf)

    def to_sibling(c):
        return pltpu.make_async_remote_copy(
            src_ref=result.at[c, 1 - core], dst_ref=sib.at[c], send_sem=sib_send.at[c],
            recv_sem=sib_recv.at[c], device_id=(place.sibling,), device_id_type=MESH)

    def across(h, k, far):
        return pltpu.make_async_remote_copy(
            src_ref=cross_out.at[h, k, far], dst_ref=cross_in.at[h, k, far], send_sem=cross_send.at[h, k, far],
            recv_sem=cross_recv.at[h, k, far], device_id=(place.last(h),), device_id_type=MESH)

    def along(h, k):
        return pltpu.make_async_remote_copy(
            src_ref=z_out.at[h, k], dst_ref=z_in.at[h, k], send_sem=z_send.at[h, k],
            recv_sem=z_recv.at[h, k], device_id=(across_z,), device_id_type=MESH)

    def first(h):
        return pltpu.make_async_remote_copy(
            src_ref=first_out.at[h], dst_ref=first_in.at[h], send_sem=first_send.at[h],
            recv_sem=first_recv.at[h], device_id=(place.first(h),), device_id_type=MESH)

    def both(c, h):
        part = pl.ds(h * half, half)
        return result[c, core, part].astype(f32) + sib[c, part].astype(f32)

    def pair_sum(c):
        far, dx, dy = 1 - c // 4, c % 2, c // 2 % 2
        to_sibling(c).wait_recv()
        for h, away, k in ((0, dx, dy), (1, dy, dx)):
            @pl.when(away == 1)
            def _():
                cross_out[h, k, far] = both(c, h).astype(bf)
                across(h, k, far).start()

    @pl.loop(0, group // 2 + 1)
    def _(c):
        @pl.when(c < group // 2)
        def _():
            far, dx, dy = 1 - c // 4, c % 2, c // 2 % 2
            o = (z + far * (1 - 2 * z)) * 4 + place.chip_at(dx, dy, 0)
            mine = heads[pl.ds(pl.multiple_of(o * span, span), span), :]
            matrix = weights[...].reshape(2 * group * depth, 512)[:, 0:384]
            part = lax.dot_general(mine, matrix, flip, preferred_element_type=f32)
            result[c, :, :, 0:width] = part.astype(bf).reshape(2, rows, width)
            low = jnp.zeros((span, 128), f32)
            owner = lax.broadcasted_iota(jnp.int32, low.shape, 1) // rank
            for j in range(3):
                term = jnp.dot(mine[:, j * 128 : (j + 1) * 128], up_own, preferred_element_type=f32)
                low = jnp.where(owner == j, term, low)
            result[c, :, :, width:] = low.astype(bf).reshape(2, rows, 128)
            to_sibling(c).start()

        @pl.when(c >= 1)
        def _():
            pair_sum(c - 1)

        part_steps(group // 2 + c)

    @pl.loop(0, group // 2)
    def _(e):
        far, k, h = 1 - e // 4, e // 2 % 2, e % 2
        c = (1 - far) * 4 + k * (2 - h)
        across(h, k, far).wait_recv()
        total = both(c, h) + cross_in[h, k, far].astype(f32)

        @pl.when(far == 1)
        def _():
            z_out[h, k] = total.astype(bf)
            along(h, k).start()

        @pl.when(far == 0)
        def _():
            along(h, k).wait_recv()
            whole = total + z_in[h, k].astype(f32)

            @pl.when(k == 1)
            def _():
                first_out[h] = whole.astype(bf)
                first(h).start()

            @pl.when(k == 0)
            def _():
                out[pl.ds(h * half, half)] = whole

        part_steps(group + 1 + e)

    part_steps(25)

    owner = lax.broadcasted_iota(jnp.int32, (128, 128), 0) // rank
    up = jnp.zeros((128, 128), f32)
    for j in range(3):
        term = lax.dot_general(inner[...], heads[:, j * 128 : (j + 1) * 128], tall, preferred_element_type=f32)
        up = jnp.where(owner == j, term, up)
    up_terms[...] = up
    for h in range(2):
        first(h).wait_recv()
        out[pl.ds(h * half, half)] += first_in[h].astype(f32)
    part_steps(26)
    lane = lax.broadcasted_iota(jnp.int32, (rows, 128), 1)
    grad_inner = jnp.where(lane < 3 * rank, out[:, width:], 0.0).astype(bf)
    late[...] = lax.dot_general(grad_inner, normed[...], tall, preferred_element_type=f32)[: 3 * rank]
    late_keep.start()

    @pl.loop(1, group)
    def _(i):
        late_to((p + i) % group, p).start()

    downs = weights[:, :, 384:512].reshape(2 * group * depth, 128)
    grad_normed = out[:, 0:width] + lax.dot_general(grad_inner, downs, flip, preferred_element_type=f32)
    ours = rows_in[...].astype(f32)
    inverse = lax.rsqrt(jnp.mean(ours * ours, axis=-1, keepdims=True) + epsilon)
    unit = ours * inverse
    scaled = grad_normed * gains[0:1]
    grad = inverse * (scaled - unit * jnp.mean(scaled * unit, axis=-1, keepdims=True))
    grad_rows[...] = (grad_middle[...] + grad).astype(bf)
    part_steps(27)
    early_keep.wait()
    late_keep.wait()

    @pl.loop(1, group)
    def _(i):
        q = (p + i) % group
        early_to(q, q).wait_recv()
        late_to(q, q).wait_recv()

    sums = jnp.sum(early_in[...], axis=0)
    owned[0 : 3 * rank] = jnp.sum(late_in[...], axis=0)
    owned[3 * rank : 4 * rank] = sums[:rank]
    owned[4 * rank : 7 * rank] = up_terms[0 : 3 * rank]
    owned[7 * rank : 8 * rank] = sums[rank:]
    for side in range(2):
        q = 2 * p + side

        @pl.when(q != me)
        def _():
            to_owner(side, q, me // group).start()

        @pl.when(q == me)
        def _():
            owned_keep.start()

    for h in range(2):
        part_first(h).wait_recv()
        side = pl.ds(h * half, half)
        output[side] = (middle[side] + part_sum[h] + part_first_in[h].astype(f32)).astype(bf)
    for s in range(2):
        source = s * group + me // 2

        @pl.when(source != me)
        def _():
            to_owner(0, source, s).wait_recv()

        @pl.when(source == me)
        def _():
            owned_keep.wait()

    @pl.loop(1, group)
    def _(i):
        to_head((p + i) % group).wait_send()
        early_to((p + i) % group, p).wait_send()
        late_to((p + i) % group, p).wait_send()

    for side in range(2):
        @pl.when(2 * p + side != me)
        def _():
            to_owner(side, 2 * p + side, me // group).wait_send()

    for h in range(2):
        part_first(h).wait_send()

    @pl.loop(0, 4)
    def _(level):
        for k in range(2):
            for h in range(2):
                part_across(h, k, level).wait_send()

                @pl.when(level > place.z)
                def _():
                    part_along(h, k, level, 1, level).wait_send()

                @pl.when(level < place.z)
                def _():
                    part_along(h, k, level, 0, down_slot(level)).wait_send()

    @pl.loop(0, group // 2)
    def _(c):
        to_sibling(c).wait_send()
        across(c % 2, c // 2 % 2, c // 4).wait_send()

        @pl.when(c < 4)
        def _():
            along(c % 2, c // 2).wait_send()

        @pl.when(c < 2)
        def _():
            first(c).wait_send()


def back(grad_mixed, part, weights, query, key, value, query_proj, key_proj, inner, cosine, sine,
         query_gain, key_gain, segs, rows_in, normed, gains, grad_middle, middle, early, rank):
    rows, width = grad_mixed.shape
    seq = query.shape[0]
    group = seq // rows
    bf, f32 = jnp.bfloat16, jnp.float32
    dma = pltpu.SemaphoreType.DMA
    vmem = pl.BlockSpec(memory_space=pltpu.VMEM)
    wide = width + 128
    piece = (rows // 2, wide)
    own = part.shape[2:]
    return pl.pallas_call(
        functools.partial(back_kernel, rows, rank),
        out_shape=(
            jax.ShapeDtypeStruct((rows, width), bf),
            jax.ShapeDtypeStruct((rows, width), bf),
            jax.ShapeDtypeStruct((2, 8 * rank, 128), f32),
        ),
        in_specs=[vmem, pl.BlockSpec(memory_space=pl.ANY)] + [vmem] * 18,
        out_specs=(vmem, vmem, vmem),
        scratch_shapes=[
            pltpu.VMEM((rows, wide), f32),
            pltpu.VMEM((128, 128), f32),
            pltpu.VMEM((2,) + own, f32),
            pltpu.VMEM((3 * rank, width), f32),
            pltpu.VMEM((group, 2 * rank, 128), f32),
            pltpu.VMEM((group, 3 * rank, 128), f32),
            pltpu.VMEM((8 * rank, 128), f32),
            dma((group,)), dma((group,)), dma((group,)), dma((group,)), dma((2,)), dma((2,)), dma((3,)),
            pltpu.VMEM((group, rows, 128), bf),
            pltpu.VMEM((seq, 128), f32),
            pltpu.VMEM((128, seq), bf),
            pltpu.VMEM((seq, 128), f32),
            pltpu.VMEM((seq, 128), f32),
            pltpu.VMEM((seq, 384), bf),
            pltpu.VMEM((group // 2, 2, rows, wide), bf),
            pltpu.VMEM((group // 2, rows, wide), bf),
            pltpu.VMEM((2, 2, 2) + piece, bf),
            pltpu.VMEM((2, 2, 2) + piece, bf),
            pltpu.VMEM((2, 2) + piece, bf),
            pltpu.VMEM((2, 2) + piece, bf),
            pltpu.VMEM((2,) + piece, bf),
            pltpu.VMEM((2,) + piece, bf),
            pltpu.VMEM((2, 2, LEVELS) + own, bf),
            pltpu.VMEM((2, 2, LEVELS) + own, bf),
            pltpu.VMEM((2, 2, LEVELS + 1) + own, bf),
            pltpu.VMEM(own, f32),
            pltpu.VMEM((2,) + own, bf),
            pltpu.VMEM((2,) + own, bf),
            dma((2, 2, LEVELS)), dma((2, 2, LEVELS)), dma((2, 2, LEVELS)), dma((2, 2, LEVELS)), dma((2, 2, LEVELS + 1)),
            dma((2,)), dma((2,)),
            dma((group,)), dma((group,)), dma, dma((group // 2,)), dma((group // 2,)),
            dma((2, 2, 2)), dma((2, 2, 2)), dma((2, 2)), dma((2, 2)), dma((2,)), dma((2,)),
        ],
        compiler_params=pltpu.CompilerParams(collective_id=2, has_side_effects=True, vmem_limit_bytes=63 << 20),
        name="back",
    )(grad_mixed, part, weights, query, key, value, query_proj, key_proj, inner, cosine, sine,
      query_gain, key_gain, segs, rows_in, normed, gains, grad_middle, middle, early)


def heads_plan(
    tokens,
    segments,
    routes,
    gates,
    sequence_adapter_index,
    attention_norm_gain,
    query_norm_gain,
    key_norm_gain,
    query_weight,
    key_weight,
    value_weight,
    output_weight,
    adapter_down_factors,
    adapter_up_factors,
    expert_norm_gain,
    expert_gate_weight,
    expert_up_weight,
    expert_down_weight,
    output_gradient,
):
    bf, f32 = jnp.bfloat16, jnp.float32
    devices = lax.axis_size("fsdp")
    rows_dev, width = tokens.shape
    seqs = segments.shape[0]
    rank = adapter_down_factors.shape[3]
    slots = 4 * rank
    own_rows = query_weight.shape[0]
    device = lax.axis_index("fsdp")
    gains = jnp.stack([attention_norm_gain, expert_norm_gain]).astype(f32)
    query_scale = query_norm_gain.astype(f32)
    key_scale = key_norm_gain.astype(f32)

    head_gains = (query_scale.reshape(1, HEAD_DIM), key_scale.reshape(1, HEAD_DIM))
    (middle, normed_ffn, normed, mixed, out_inner, head_weights, query, key, value, query_proj, key_proj, inner_all,
     coeff_own, *turns, output_matrix) = front(
        sequence_adapter_index, tokens, gains, query_weight, key_weight, value_weight,
        segments, adapter_down_factors.swapaxes(2, 3),
        adapter_up_factors, routes.T, gates.T, output_weight, *head_gains,
    )
    slab_gate = expert_gate_weight[0]
    slab_up = expert_up_weight[0]
    slab_down = expert_down_weight[0]
    grad_middle, grad_mixed, early, part, _ = experts_pass(
        normed_ffn, output_gradient, slab_gate, slab_up, slab_down, coeff_own, middle, gains,
        output_matrix.reshape(width, width), head_weights, out_inner, mixed, rank,
    )

    grad_tokens, output, terms = back(
        grad_mixed, part, head_weights, query, key, value, query_proj, key_proj, inner_all,
        *turns, *head_gains, segments,
        tokens, normed, gains, grad_middle, middle,
        early, rank,
    )
    terms = lax.dynamic_slice_in_dim(terms, device % 2 * own_rows, own_rows, 2)
    selected = (
        jnp.arange(ADAPTER_COUNT, dtype=jnp.int32)[:, None] == sequence_adapter_index[None, :]
    ).astype(f32)
    spread = jnp.sum(selected[:, :, None, None] * terms[None], axis=1)
    spread = spread.reshape(ADAPTER_COUNT, 2, 4, rank, own_rows)
    grad_down = spread[:, 0].transpose(0, 1, 3, 2)
    grad_up = spread[:, 1]
    return (output, grad_tokens, grad_down, grad_up)


def solution(mesh):
    plan = heads_plan if mesh.shape["fsdp"] == LEVELS * 8 else shards
    in_specs = (
        P("fsdp", None),
        P(),
        P("fsdp", None),
        P("fsdp", None),
        P(),
        P(),
        P(),
        P(),
        P("fsdp", None),
        P("fsdp", None),
        P("fsdp", None),
        P("fsdp", None),
        P(None, None, "fsdp", None),
        P(None, None, None, "fsdp"),
        P(),
        P("fsdp", None, None),
        P("fsdp", None, None),
        P("fsdp", None, None),
        P("fsdp", None),
    )
    out_specs = (
        P("fsdp", None),
        P("fsdp", None),
        P(None, None, "fsdp", None),
        P(None, None, None, "fsdp"),
    )
    return jax.shard_map(plan, mesh=mesh, in_specs=in_specs, out_specs=out_specs, check_vma=False)
```
